32 devices in a mesh: dp: 8 (over y, x, core), seq: 4 (over z).
Axes of the slice: x: 2, y: 2, z: 4, core: 2. Of those that a mesh axis runs over, the one named last changes fastest.
Arguments:
- tokens: bfloat16 [96, 200, 512], P('dp', 'seq'), may hold values from -6 to 6
- ln1_gain: bfloat16 [512], P('dp'), may hold values from 0.5 to 1.5
- ln1_bias: bfloat16 [512], P('dp'), may hold values from -1 to 1
- w_qkv: bfloat16 [512, 1536], P('dp'), may hold values from -0.25 to 0.25
- w_out: bfloat16 [512, 512], P('dp'), may hold values from -1.75 to 1.75
- ln2_gain: bfloat16 [512], P('dp'), may hold values from 0.5 to 1.5
- ln2_bias: bfloat16 [512], P('dp'), may hold values from -1 to 1
- w_router: bfloat16 [512, 8], P('dp'), may hold values from -0.1875 to 0.1875
- expert_in: bfloat16 [8, 512, 2048], P('dp', None, 'seq'), may hold values from -0.25 to 0.25
- expert_out: bfloat16 [8, 2048, 512], P('dp', 'seq'), may hold values from -3 to 3
- routes: int32 [96, 200, 2], P('dp', 'seq'), may hold values from 0 to 7, all different within a row; in each aligned block of 50 rows (0 to 49, 50 to 99, ..., all dimensions but the last counted through in order) at most 14 rows name the same one
- targets: bfloat16 [96, 200, 512], P('dp', 'seq'), may hold values from -6 to 6
Outputs:
- mixed: bfloat16 [96, 200, 512], P('dp', 'seq')
- grad_tokens: float32 [96, 200, 512], P('dp', 'seq')
- grad_ln1_gain: float32 [512], P('dp')
- grad_ln1_bias: float32 [512], P('dp')
- grad_qkv: float32 [512, 1536], P('dp')
- grad_out: float32 [512, 512], P('dp')
- grad_ln2_gain: float32 [512], P('dp')
- grad_ln2_bias: float32 [512], P('dp')
- grad_router: float32 [512, 8], P('dp')
- grad_expert_in: float32 [8, 512, 2048], P('dp', None, 'seq')
- grad_expert_out: float32 [8, 2048, 512], P('dp', 'seq')
The draws below stay inside these ranges and needn't reach their ends.
Inputs may be any that keep to these rules, and one draw needn't show every extreme that they name: `routes`: each slot names two different experts. In each aligned block of 50 rows (one image's slots on one device), no expert is named more than 14 times, and some expert reaches 14.
All inputs are finite; a program needn't handle non-finite values.
Results may differ from the reference program's by a relative error of at most 0.013.
Values may be sent and summed in bfloat16 or wider, within the bound.
A program may use at most 128 MiB of HBM per device.

```python
import math
import jax
import jax.numpy as jnp
import numpy as np
from jax import lax

D = 512
H = 8
HD = 64
F = 2048
S = 200
VALID = 197
EXPERTS = 8
IMAGES = 96
MOST = 14
N_SEQ = 4


def block_levels(rng, dims, shards, least, top_value):
    def one(axis_at, parts):
        draws = jax.random.uniform(jax.random.fold_in(jax.random.fold_in(rng, 6), axis_at), (parts,), jnp.float32, least / len(shards), top_value / len(shards))
        return jnp.repeat(jnp.exp(draws), dims[axis_at] // parts).reshape((-1,) + (1,) * (len(dims) - axis_at - 1))

    level = one(*shards[0])
    for cut in shards[1:]:
        level = level * one(*cut)
    return level


def shared_out(key, own, number, rows, amount, top, limit, lean):
    order = jax.random.permutation(key, amount)
    crowded, common = load_shares(amount, rows * top, limit, lean, True), load_shares(amount, rows * top, limit, lean, False)
    places = jnp.arange(amount)

    def named(tallies, rotation):
        used = int((tallies > 0).sum())
        fixed = max(1, used // 4)
        passed = fixed + (places - fixed + rotation * (used - fixed)) % max(1, amount - fixed)
        return jnp.zeros((amount,), jnp.int32).at[order[jnp.where(places < fixed, places, passed)]].set(jnp.asarray(tallies, jnp.int32))

    tallies = jnp.where(number % 4 == 0, named(crowded, number // 4), named(common, number - number // 4 - 1))
    mixed = jax.random.permutation(jax.random.fold_in(own, 3), amount)
    source_of, taker = mixed[0:amount // 2 * 2:2], mixed[1:amount // 2 * 2:2]
    slack = jnp.minimum(tallies[source_of] - 1, limit - tallies[taker]) // 2
    slack = jnp.where((source_of == order[0]) | (taker == order[0]) | (tallies[taker] == 0), 0, jnp.maximum(slack, 0))
    passed = jax.random.randint(jax.random.fold_in(own, 4), (amount // 2,), 0, 1 << 20) % (slack + 1)
    tallies = tallies.at[source_of].add(-passed).at[taker].add(passed)
    items = jnp.searchsorted(jnp.cumsum(tallies), jnp.arange(rows * top), side="right").astype(jnp.int32)
    listing = items.reshape(top, rows).T
    listing = listing[jax.random.permutation(jax.random.fold_in(own, 1), rows)]
    rotation = jax.random.randint(jax.random.fold_in(own, 2), (rows, 1), 0, top)
    return jnp.take_along_axis(listing, (jnp.arange(top)[None, :] + rotation) % top, axis=1)


def load_shares(count, total, limit, lean, full):
    weights = [(1 << 20) // math.isqrt(rank ** lean) + 1 for rank in range(1, count + 1)]
    largest = limit if full else min(limit, max(-(-total // count), total * weights[0] // sum(weights)))
    least = 1 if total - largest >= count - 1 else 0
    holding, spare = [largest] + [least] * (count - 1), total - largest - least * (count - 1)
    while spare > 0:
        free = [i for i in range(1, count) if holding[i] < largest] or [i for i in range(1, count) if holding[i] < limit]
        whole, budget = sum([weights[i] for i in free]), spare
        for i in free:
            addition = min(limit - holding[i], max(1, budget * weights[i] // whole), spare)
            holding[i] = holding[i] + addition
            spare = spare - addition
    return np.array(holding)


def centred(rng, shape, deviation, limit, pieces=(), kind=jnp.bfloat16):
    array = deviation * jax.random.normal(rng, shape, jnp.float32)
    if pieces:
        array = array * block_levels(rng, shape, pieces, -0.22, 0.18)
    return jnp.clip(array, -limit, limit).astype(kind)


def setup_inputs(seed: int = 0) -> dict:
    key_of = jax.random.split(jax.random.key(seed), 13)
    tokens = centred(key_of[0], (IMAGES, S, D), 1.0, 6.0, ((0, 8), (1, 4)))
    ln1_gain = jnp.clip(1.0 + 0.1 * jax.random.normal(key_of[1], (D,), jnp.float32), 0.5, 1.5).astype(jnp.bfloat16)
    ln1_bias = centred(key_of[2], (D,), 0.2, 1.0, ((0, 8),))
    w_qkv = centred(key_of[3], (D, 3 * D), D ** -0.5, 0.25, ((0, 8),))
    w_out = centred(key_of[4], (D, D), (D // 40 + 1) ** -0.5, 1.75, ((0, 8),))
    ln2_gain = jnp.clip(1.0 + 0.1 * jax.random.normal(key_of[5], (D,), jnp.float32), 0.5, 1.5).astype(jnp.bfloat16)
    ln2_bias = centred(key_of[6], (D,), 0.2, 1.0, ((0, 8),))
    w_router = centred(key_of[7], (D, EXPERTS), (2 * D) ** -0.5, 0.1875, ((0, 8),))
    expert_in = centred(key_of[8], (EXPERTS, D, F), D ** -0.5, 0.25, ((0, 8), (2, 4)))
    expert_out = centred(key_of[9], (EXPERTS, F, D), (F // 640 + 1) ** -0.5, 3.0, ((0, 8), (1, 4)))
    routes_keys = jax.random.split(jax.random.fold_in(key_of[10], 1), IMAGES * S // (S // N_SEQ))
    routes_turns = jax.random.permutation(jax.random.fold_in(key_of[10], 3), IMAGES * S // (S // N_SEQ))
    routes = jax.vmap(lambda own, number: shared_out(jax.random.fold_in(key_of[10], 2), own, number, S // N_SEQ, EXPERTS, 2, MOST, 1))(routes_keys, routes_turns).reshape((IMAGES, S, 2))
    targets = centred(key_of[11], (IMAGES, S, D), 1.0, 6.0, ((0, 8), (1, 4)))
    return {"tokens": tokens, "ln1_gain": ln1_gain, "ln1_bias": ln1_bias, "w_qkv": w_qkv, "w_out": w_out, "ln2_gain": ln2_gain, "ln2_bias": ln2_bias, "w_router": w_router, "expert_in": expert_in, "expert_out": expert_out, "routes": routes, "targets": targets}


@jax.custom_vjp
def low(v):
    return lax.optimization_barrier(v.astype(jnp.bfloat16)).astype(jnp.float32)

@jax.custom_vjp
def low_back(v):
    return v

def low_keep(v):
    return (low(v), None)

def low_pass(kept, grad):
    return (grad,)

def back_keep(v):
    return (v, None)

def back_low(kept, grad):
    return (low(grad),)
low.defvjp(low_keep, low_pass)
low_back.defvjp(back_keep, back_low)

def layer_norm(values, gain_vec, bias_vec):
    centre = values - lax.optimization_barrier(jnp.mean(values, axis=-1, keepdims=True))
    spread = lax.optimization_barrier(jnp.mean(centre * centre, axis=-1, keepdims=True))
    return centre * lax.rsqrt(spread + 1e-06) * gain_vec + bias_vec

def attend_group(group):
    highest = lax.Precision.HIGHEST
    queries, keys_in, values = group
    raw_scores = jnp.einsum('bqhd,bkhd->bhqk', queries, keys_in, precision=highest) * 0.125
    scores = low_back(raw_scores)
    key_valid = jnp.arange(S) < VALID
    scores = jnp.where(key_valid[None, None, None, :], scores, -1e+30)
    prob_rows = jax.nn.softmax(scores, axis=-1)
    return jnp.einsum('bhqk,bkhd->bqhd', low(prob_rows), values, precision=highest)

def forward(tokens, gain_one, bias_one, qkv_weight, out_weight, gain_two, bias_two, router_weight, expert_in, expert_out, routes):
    highest = lax.Precision.HIGHEST
    image_count = tokens.shape[0]
    row_count = image_count * S
    token_rows = tokens.reshape(row_count, D)
    normed_one = low(layer_norm(token_rows, gain_one, bias_one))
    mixed_qkv = low(low_back(jnp.dot(normed_one, qkv_weight, precision=highest)))
    group_size = math.gcd(image_count, 16)
    grouped = mixed_qkv.reshape(image_count // group_size, group_size, S, 3, H, HD)
    attended = lax.map(jax.checkpoint(attend_group), (grouped[:, :, :, 0], grouped[:, :, :, 1], grouped[:, :, :, 2]))
    attended = low(low_back(attended.reshape(row_count, D)))
    residual_two = token_rows + low_back(jnp.dot(attended, out_weight, precision=highest))
    normed_two = low(layer_norm(residual_two, gain_two, bias_two))
    logits = low_back(jnp.dot(normed_two, router_weight, precision=highest))
    prob_rows = jax.nn.softmax(logits, axis=-1)
    route_rows = routes.reshape(row_count, 2).astype(jnp.int32)
    gate_values = jnp.take_along_axis(prob_rows, route_rows, axis=1).reshape(row_count * 2)
    valid_slots = jnp.arange(row_count) % S < VALID
    live_picks = jnp.repeat(valid_slots, 2)
    route_flat = route_rows.reshape(row_count * 2)
    capacity = image_count * N_SEQ * MOST

    def expert_term(expert_id, normed_rows, gate_flat):
        expert_hit = (route_flat == expert_id) & live_picks
        slot_index = jnp.nonzero(expert_hit, size=capacity, fill_value=-1)[0].astype(jnp.int32)
        slot_used = slot_index >= 0
        safe_index = jnp.maximum(slot_index, 0)
        token_pick = safe_index // 2
        picked = low_back(normed_rows[token_pick])
        hidden_pre = low_back(jnp.dot(picked, expert_in[expert_id], precision=highest))
        activated = low(jax.nn.gelu(hidden_pre))
        produced = low(low_back(jnp.dot(activated, expert_out[expert_id], precision=highest)))
        weighting = jnp.where(slot_used, gate_flat[safe_index], 0.0)
        return jnp.zeros((row_count, D), jnp.float32).at[token_pick].add(produced * weighting[:, None])

    def add_expert(running, expert_id):
        return (running + jax.checkpoint(expert_term)(expert_id, normed_two, gate_values), None)
    moe_rows = lax.scan(add_expert, jnp.zeros((row_count, D), jnp.float32), jnp.arange(EXPERTS, dtype=jnp.int32))[0]
    return residual_two + moe_rows

def reference(tokens, ln1_gain, ln1_bias, w_qkv, w_out, ln2_gain, ln2_bias, w_router, expert_in, expert_out, routes, targets):
    floats = [member.astype(jnp.float32) for member in (tokens, ln1_gain, ln1_bias, w_qkv, w_out, ln2_gain, ln2_bias, w_router, expert_in, expert_out)]
    valid_slots = (jnp.arange(IMAGES * S) % S < VALID).astype(jnp.float32)
    target_rows = targets.astype(jnp.float32).reshape(IMAGES * S, D)

    def scaled_loss(*params):
        mixed_rows = forward(*params, routes)
        error = (mixed_rows - target_rows) * valid_slots[:, None]
        return (0.5 * jnp.sum(error * error), mixed_rows)
    loss, back_fn, mixed_rows = jax.vjp(scaled_loss, *floats, has_aux=True)
    grads = back_fn(jnp.ones_like(loss))
    mixed = mixed_rows.astype(jnp.bfloat16).reshape(IMAGES, S, D)
    return (mixed, grads[0], grads[1], grads[2], grads[3], grads[4], grads[5], grads[6], grads[7], grads[8], grads[9])
```

```python
import functools

import jax
import jax.numpy as jnp
from jax import lax
from jax.experimental import pallas as pl
from jax.experimental.pallas import tpu as pltpu
from jax.sharding import PartitionSpec as P

H = 8
S = 200
VALID = 197


def layer_norm(values, gain_vec, bias_vec):
    centre = values - jnp.mean(values, axis=-1, keepdims=True)
    spread = jnp.mean(centre * centre, axis=-1, keepdims=True)
    return centre * lax.rsqrt(spread + 1e-06) * gain_vec + bias_vec


def regroup_heads(values):
    return lax.all_to_all(values, "seq", split_axis=3, concat_axis=1, tiled=True)


def regroup_slots(values):
    return lax.all_to_all(values, "seq", split_axis=1, concat_axis=3, tiled=True)


def send_experts(values):
    return lax.all_to_all(values, "dp", split_axis=0, concat_axis=1, tiled=True)


def send_tokens(values):
    return lax.all_to_all(values, "dp", split_axis=1, concat_axis=0, tiled=True)


def masked_scores(queries, keys_in, key_valid):
    scores = (
        jnp.einsum("bqhd,bkhd->bhqk", queries, keys_in, preferred_element_type=jnp.float32) * 0.125
    )
    return jnp.where(key_valid, scores, -1e30)


def attention_forward(queries, keys_in, values, key_valid):
    scores = masked_scores(queries, keys_in, key_valid)
    row_top = jnp.max(scores, axis=-1, keepdims=True)
    exponent = jnp.exp(scores - row_top)
    row_total = jnp.sum(exponent, axis=-1, keepdims=True)
    prob_rows = exponent / row_total
    log_total = row_top + jnp.log(row_total)
    attended = jnp.einsum(
        "bhqk,bkhd->bqhd",
        prob_rows.astype(jnp.bfloat16),
        values,
        preferred_element_type=jnp.float32,
    )
    return (attended.astype(jnp.bfloat16), log_total)


def attention_backward(queries, keys_in, values, log_total, grad_attended, key_valid):
    scores = masked_scores(queries, keys_in, key_valid)
    prob_rows = jnp.exp(scores - log_total)
    grad_values = jnp.einsum(
        "bhqk,bqhd->bkhd",
        prob_rows.astype(jnp.bfloat16),
        grad_attended,
        preferred_element_type=jnp.float32,
    )
    grad_probs = jnp.einsum(
        "bqhd,bkhd->bhqk", grad_attended, values, preferred_element_type=jnp.float32
    )
    inner_sum = jnp.sum(prob_rows * grad_probs, axis=-1, keepdims=True)
    grad_scores = (prob_rows * (grad_probs - inner_sum)).astype(jnp.bfloat16)
    grad_queries = (
        jnp.einsum("bhqk,bkhd->bqhd", grad_scores, keys_in, preferred_element_type=jnp.float32)
        * 0.125
    )
    grad_keys = (
        jnp.einsum("bhqk,bqhd->bkhd", grad_scores, queries, preferred_element_type=jnp.float32)
        * 0.125
    )
    return jnp.stack([grad_queries, grad_keys, grad_values], axis=2)


def pick_block(total_rows):
    for candidate in (1024, 768, 512, 384, 256):
        if total_rows % candidate == 0:
            return candidate
    return total_rows


def by_heads(
    tokens,
    ln1_gain,
    ln1_bias,
    w_qkv,
    w_out,
    ln2_gain,
    ln2_bias,
    w_router,
    expert_in,
    expert_out,
    routes,
    targets,
):
    image_count, slot_count, model_width = tokens.shape
    seq_devices = lax.axis_size("seq")
    row_count = image_count * slot_count
    expert_count = w_router.shape[1]
    local_experts = expert_in.shape[0]
    slot_limit = 2 * S // (seq_devices * expert_count) + 2
    head_size = model_width // H
    gathered = (
        lax.all_gather(ln1_gain, "dp", axis=0, tiled=True),
        lax.all_gather(ln1_bias, "dp", axis=0, tiled=True),
        lax.all_gather(w_qkv, "dp", axis=0, tiled=True),
        lax.all_gather(w_out, "dp", axis=0, tiled=True),
        lax.all_gather(ln2_gain, "dp", axis=0, tiled=True),
        lax.all_gather(ln2_bias, "dp", axis=0, tiled=True),
        lax.all_gather(w_router, "dp", axis=0, tiled=True),
    )
    gain_one = gathered[0].astype(jnp.float32)
    bias_one = gathered[1].astype(jnp.float32)
    qkv_weight = gathered[2]
    out_weight = gathered[3]
    gain_two = gathered[4].astype(jnp.float32)
    bias_two = gathered[5].astype(jnp.float32)
    router_weight = gathered[6]
    slot_start = lax.axis_index("seq") * slot_count
    valid_slot = slot_start + jnp.arange(slot_count) < VALID
    valid_rows = jnp.tile(valid_slot, image_count)
    key_valid = (jnp.arange(S) < VALID)[None, None, None, :]
    token_rows = tokens.reshape(row_count, model_width).astype(jnp.float32)
    normed_one, norm_one_back = jax.vjp(layer_norm, token_rows, gain_one, bias_one)
    normed_one_b = normed_one.astype(jnp.bfloat16)
    mixed_qkv = jnp.dot(normed_one_b, qkv_weight, preferred_element_type=jnp.float32).astype(
        jnp.bfloat16
    )
    qkv_heads = regroup_heads(mixed_qkv.reshape(image_count, slot_count, 3, H, head_size))
    queries = qkv_heads[:, :, 0]
    keys_in = qkv_heads[:, :, 1]
    values = qkv_heads[:, :, 2]
    attended, log_total = attention_forward(queries, keys_in, values, key_valid)
    attended_rows = regroup_slots(attended[:, :, None]).reshape(row_count, model_width)
    residual_two = token_rows + jnp.dot(
        attended_rows, out_weight, preferred_element_type=jnp.float32
    )
    normed_two, norm_two_back = jax.vjp(layer_norm, residual_two, gain_two, bias_two)
    normed_two_b = normed_two.astype(jnp.bfloat16)
    logits = jnp.dot(normed_two_b, router_weight, preferred_element_type=jnp.float32)
    route_rows = routes.reshape(row_count, 2)
    chosen = (route_rows[:, :, None] == jnp.arange(expert_count)[None, None, :]) & valid_rows[
        :, None, None
    ]
    chosen_f = chosen.astype(jnp.float32)

    def gate_pick(logit_rows):
        return jnp.sum(jax.nn.softmax(logit_rows, axis=-1)[:, None, :] * chosen_f, axis=-1)

    gate_values, gate_back = jax.vjp(gate_pick, logits)
    pick_count = chosen.astype(jnp.int32).reshape(image_count, slot_count * 2, expert_count)
    before = jnp.cumsum(pick_count, axis=1) - pick_count
    place_hit = (before[..., None] == jnp.arange(slot_limit)) & (pick_count[..., None] > 0)
    dispatch = place_hit.astype(jnp.bfloat16).reshape(
        image_count, slot_count, 2, expert_count, slot_limit
    )
    normed_img = normed_two_b.reshape(image_count, slot_count, model_width)
    sent_rows = jnp.einsum(
        "bskem,bsd->ebmd", dispatch, normed_img, preferred_element_type=jnp.float32
    ).astype(jnp.bfloat16)
    received = send_experts(sent_rows.reshape(expert_count, image_count * slot_limit, model_width))
    weights_in, weights_out = (
        lax.all_gather(expert_in, "seq", axis=2, tiled=True),
        lax.all_gather(expert_out, "seq", axis=1, tiled=True),
    )
    total_rows = received.shape[1]
    block_rows = pick_block(total_rows)
    block_count = total_rows // block_rows

    def expert_step(block_index, produced):
        row_piece = lax.dynamic_slice_in_dim(received, block_index * block_rows, block_rows, 1)
        hidden_pre = jnp.einsum(
            "erd,edf->erf", row_piece, weights_in, preferred_element_type=jnp.float32
        )
        activated = jax.nn.gelu(hidden_pre).astype(jnp.bfloat16)
        result = jnp.einsum(
            "erf,efd->erd", activated, weights_out, preferred_element_type=jnp.float32
        ).astype(jnp.bfloat16)
        return lax.dynamic_update_slice_in_dim(produced, result, block_index * block_rows, 1)

    produced = lax.fori_loop(
        0,
        block_count,
        expert_step,
        jnp.zeros((local_experts, total_rows, model_width), jnp.bfloat16),
    )
    returned = send_tokens(produced).reshape(expert_count, image_count, slot_limit, model_width)
    per_choice = jnp.einsum(
        "bskem,ebmd->bskd", dispatch, returned, preferred_element_type=jnp.float32
    ).reshape(row_count, 2, model_width)
    mixed_rows = (
        residual_two
        + gate_values[:, 0:1] * per_choice[:, 0]
        + gate_values[:, 1:2] * per_choice[:, 1]
    )
    target_rows = targets.reshape(row_count, model_width).astype(jnp.float32)
    grad_mixed = (mixed_rows - target_rows) * valid_rows[:, None].astype(jnp.float32)
    grad_gates = jnp.sum(grad_mixed[:, None, :] * per_choice, axis=-1)
    grad_choice = (
        (gate_values[:, :, None] * grad_mixed[:, None, :])
        .astype(jnp.bfloat16)
        .reshape(image_count, slot_count, 2, model_width)
    )
    grad_sent = jnp.einsum(
        "bskem,bskd->ebmd", dispatch, grad_choice, preferred_element_type=jnp.float32
    ).astype(jnp.bfloat16)
    grad_received = send_experts(
        grad_sent.reshape(expert_count, image_count * slot_limit, model_width)
    )
    back_in, back_out = (
        lax.all_gather(expert_in, "seq", axis=2, tiled=True),
        lax.all_gather(expert_out, "seq", axis=1, tiled=True),
    )

    def expert_back(block_index, loop_carry):
        grad_in_sum, grad_out_sum, grad_rows = loop_carry
        row_piece = lax.dynamic_slice_in_dim(received, block_index * block_rows, block_rows, 1)
        grad_piece = lax.dynamic_slice_in_dim(
            grad_received, block_index * block_rows, block_rows, 1
        )
        hidden_pre = jnp.einsum(
            "erd,edf->erf", row_piece, back_in, preferred_element_type=jnp.float32
        )
        activated, gelu_back = jax.vjp(jax.nn.gelu, hidden_pre)
        grad_act = jnp.einsum(
            "erd,efd->erf", grad_piece, back_out, preferred_element_type=jnp.float32
        )
        grad_pre = gelu_back(grad_act)[0].astype(jnp.bfloat16)
        grad_out_sum = grad_out_sum + jnp.einsum(
            "erf,erd->efd",
            activated.astype(jnp.bfloat16),
            grad_piece,
            preferred_element_type=jnp.float32,
        )
        grad_in_sum = grad_in_sum + jnp.einsum(
            "erd,erf->edf", row_piece, grad_pre, preferred_element_type=jnp.float32
        )
        rows_back = jnp.einsum(
            "erf,edf->erd", grad_pre, back_in, preferred_element_type=jnp.float32
        ).astype(jnp.bfloat16)
        grad_rows = lax.dynamic_update_slice_in_dim(
            grad_rows, rows_back, block_index * block_rows, 1
        )
        return (grad_in_sum, grad_out_sum, grad_rows)

    start_carry = (
        jnp.zeros(back_in.shape, jnp.float32),
        jnp.zeros(back_out.shape, jnp.float32),
        jnp.zeros((local_experts, total_rows, model_width), jnp.bfloat16),
    )
    grad_in_sum, grad_out_sum, grad_rows = lax.fori_loop(0, block_count, expert_back, start_carry)
    grad_returned = send_tokens(grad_rows).reshape(
        expert_count, image_count, slot_limit, model_width
    )
    grad_normed_two = jnp.einsum(
        "bskem,ebmd->bsd", dispatch, grad_returned, preferred_element_type=jnp.float32
    ).reshape(row_count, model_width)
    grad_logits = gate_back(grad_gates)[0].astype(jnp.bfloat16)
    grad_router = jnp.einsum(
        "rd,re->de", normed_two_b, grad_logits, preferred_element_type=jnp.float32
    )
    grad_normed_two = grad_normed_two + jnp.einsum(
        "re,de->rd", grad_logits, router_weight, preferred_element_type=jnp.float32
    )
    grad_res_two, grad_gain_two, grad_bias_two = norm_two_back(grad_normed_two)
    grad_residual = grad_mixed + grad_res_two
    grad_branch = grad_residual.astype(jnp.bfloat16)
    grad_out_weight = jnp.einsum(
        "rd,re->de", attended_rows, grad_branch, preferred_element_type=jnp.float32
    )
    grad_attended = jnp.einsum(
        "re,de->rd", grad_branch, out_weight, preferred_element_type=jnp.float32
    ).astype(jnp.bfloat16)
    grad_heads = regroup_heads(grad_attended.reshape(image_count, slot_count, 1, H, head_size))[
        :, :, 0
    ]
    grad_qkv_heads = attention_backward(
        queries, keys_in, values, log_total, grad_heads, key_valid
    ).astype(jnp.bfloat16)
    grad_qkv_rows = regroup_slots(grad_qkv_heads).reshape(row_count, 3 * model_width)
    grad_qkv_weight = jnp.einsum(
        "rd,rf->df", normed_one_b, grad_qkv_rows, preferred_element_type=jnp.float32
    )
    grad_normed_one = jnp.einsum(
        "rf,df->rd", grad_qkv_rows, qkv_weight, preferred_element_type=jnp.float32
    )
    grad_token_ln, grad_gain_one, grad_bias_one = norm_one_back(grad_normed_one)
    grad_tokens = grad_residual + grad_token_ln
    dense_grads = (
        grad_gain_one,
        grad_bias_one,
        grad_qkv_weight,
        grad_out_weight,
        grad_gain_two,
        grad_bias_two,
        grad_router,
    )
    dense_grads = (
        lax.psum(dense_grads[0].astype(jnp.bfloat16), "seq").astype(jnp.float32),
        lax.psum(dense_grads[1].astype(jnp.bfloat16), "seq").astype(jnp.float32),
        lax.psum(dense_grads[2].astype(jnp.bfloat16), "seq").astype(jnp.float32),
        lax.psum(dense_grads[3].astype(jnp.bfloat16), "seq").astype(jnp.float32),
        lax.psum(dense_grads[4].astype(jnp.bfloat16), "seq").astype(jnp.float32),
        lax.psum(dense_grads[5].astype(jnp.bfloat16), "seq").astype(jnp.float32),
        lax.psum(dense_grads[6].astype(jnp.bfloat16), "seq").astype(jnp.float32),
    )
    dense_grads = (
        lax.psum_scatter(
            dense_grads[0].astype(jnp.bfloat16), "dp", scatter_dimension=0, tiled=True
        ).astype(jnp.float32),
        lax.psum_scatter(
            dense_grads[1].astype(jnp.bfloat16), "dp", scatter_dimension=0, tiled=True
        ).astype(jnp.float32),
        lax.psum_scatter(
            dense_grads[2].astype(jnp.bfloat16), "dp", scatter_dimension=0, tiled=True
        ).astype(jnp.float32),
        lax.psum_scatter(
            dense_grads[3].astype(jnp.bfloat16), "dp", scatter_dimension=0, tiled=True
        ).astype(jnp.float32),
        lax.psum_scatter(
            dense_grads[4].astype(jnp.bfloat16), "dp", scatter_dimension=0, tiled=True
        ).astype(jnp.float32),
        lax.psum_scatter(
            dense_grads[5].astype(jnp.bfloat16), "dp", scatter_dimension=0, tiled=True
        ).astype(jnp.float32),
        lax.psum_scatter(
            dense_grads[6].astype(jnp.bfloat16), "dp", scatter_dimension=0, tiled=True
        ).astype(jnp.float32),
    )
    expert_in_grad, expert_out_grad = (
        lax.psum_scatter(
            grad_in_sum.astype(jnp.bfloat16), "seq", scatter_dimension=2, tiled=True
        ).astype(jnp.float32),
        lax.psum_scatter(
            grad_out_sum.astype(jnp.bfloat16), "seq", scatter_dimension=1, tiled=True
        ).astype(jnp.float32),
    )
    mixed = mixed_rows.astype(jnp.bfloat16).reshape(image_count, slot_count, model_width)
    return (
        mixed,
        grad_tokens.reshape(image_count, slot_count, model_width),
        dense_grads[0],
        dense_grads[1],
        dense_grads[2],
        dense_grads[3],
        dense_grads[4],
        dense_grads[5],
        dense_grads[6],
        expert_in_grad,
        expert_out_grad,
    )


BF = jnp.bfloat16
F32 = jnp.float32
MESH_ID = pl.DeviceIdType.MESH
NEG = -1e30
BP = 64
VMEM_LIMIT = 64 * 1000 * 1024


def nn(a, b):
    return lax.dot_general(a, b, (((1,), (0,)), ((), ())), preferred_element_type=F32)


def nt(a, b):
    return lax.dot_general(a, b, (((1,), (1,)), ((), ())), preferred_element_type=F32)


def tn(a, b):
    return lax.dot_general(a, b, (((0,), (0,)), ((), ())), preferred_element_type=F32)


def remote(src, dst, send_sem, recv_sem, dp, z):
    return pltpu.make_async_remote_copy(
        src_ref=src,
        dst_ref=dst,
        send_sem=send_sem,
        recv_sem=recv_sem,
        device_id=(dp, z),
        device_id_type=MESH_ID,
    )


def entry_barrier(me, z, n_dp, n_z, use_dp, use_z):
    barrier = pltpu.get_barrier_semaphore()
    count = 0
    if use_dp:
        for k in range(1, n_dp):
            pl.semaphore_signal(
                barrier, inc=1, device_id=(lax.rem(me + k, n_dp), z), device_id_type=MESH_ID
            )
            count += 1
    if use_z:
        for k in range(1, n_z):
            pl.semaphore_signal(
                barrier, inc=1, device_id=(me, lax.rem(z + k, n_z)), device_id_type=MESH_ID
            )
            count += 1
    pl.semaphore_wait(barrier, count)


def rows_of(index, size):
    return pl.ds(pl.multiple_of(index * size, size), size)


def norm_parts(x):
    centre = x - jnp.mean(x, axis=-1, keepdims=True)
    scale = lax.rsqrt(jnp.mean(centre * centre, axis=-1, keepdims=True) + 1e-06)
    return centre * scale, scale


def norm_back(grad_hat, hat, scale):
    return scale * (
        grad_hat
        - jnp.mean(grad_hat, axis=-1, keepdims=True)
        - hat * jnp.mean(grad_hat * hat, axis=-1, keepdims=True)
    )


def half_masks():
    lane = lax.broadcasted_iota(jnp.int32, (1, 128), 1)
    low = jnp.where(lane < 64, 1.0, 0.0).astype(BF)
    high = jnp.where(lane < 64, 0.0, 1.0).astype(BF)
    return (low, high)


def key_mask(z_blocks, block):
    lane = lax.broadcasted_iota(jnp.int32, (1, z_blocks * BP), 1)
    return (lane % BP < block) & ((lane // BP) * block + lane % BP < VALID)


def row_mask(z_blocks, block):
    row = lax.broadcasted_iota(jnp.int32, (z_blocks * BP, 1), 0)
    return (row % BP < block) & ((row // BP) * block + row % BP < VALID)


def gather_step(step, z, n_z, me, sends):
    @pl.when(z >= step)
    def _():
        for full, send_sem, recv_sem in sends:
            slot = z - step
            remote(full.at[slot], full.at[slot], send_sem.at[0, step], recv_sem.at[slot], me, z).wait_recv()

            @pl.when(z < n_z - 1)
            def _():
                remote(
                    full.at[slot], full.at[slot], send_sem.at[0, step], recv_sem.at[slot], me, z + 1
                ).start()

    @pl.when(z + step < n_z)
    def _():
        for full, send_sem, recv_sem in sends:
            slot = z + step
            remote(full.at[slot], full.at[slot], send_sem.at[1, step], recv_sem.at[slot], me, z).wait_recv()

            @pl.when(z > 0)
            def _():
                remote(
                    full.at[slot], full.at[slot], send_sem.at[1, step], recv_sem.at[slot], me, z - 1
                ).start()


def gather_sends_done(z, n_z, me, sends):
    for step in range(n_z):

        @pl.when((z >= step) & (z < n_z - 1))
        def _():
            for full, send_sem, recv_sem in sends:
                remote(
                    full.at[0], full.at[0], send_sem.at[0, step], recv_sem.at[0], me, z
                ).wait_send()

        @pl.when((z + step < n_z) & (z > 0))
        def _():
            for full, send_sem, recv_sem in sends:
                remote(
                    full.at[0], full.at[0], send_sem.at[1, step], recv_sem.at[0], me, z
                ).wait_send()


def front_kernel(
    dims,
    tok, rts, wq, wo, vec, win, wout,
    recv, win_all, wout_all, wq_all, wo_all, vsum, xpad, x2s, n2s, qkvs, outs, gts, meta, metat, lses,
    xin, rin, vec_all, sbuf,
    tok_ss, tok_rs, rts_ss, rts_rs, den_ss, den_rs, fwd_ss, win_ss, win_rs, wout_ss, wout_rs,
    row_ss, row_rs, loc_sem,
):
    n_dp, n_z, im, block, cap, er = dims
    me, z = lax.axis_index("dp"), lax.axis_index("seq")
    sp = n_z * BP
    half = n_dp // 2
    entry_barrier(me, z, n_dp, n_z, True, True)
    for k in range(1, n_z):
        peer = lax.rem(z + k, n_z)
        remote(tok.at[pl.ds(peer * im, im)], xin.at[z], tok_ss.at[k], tok_rs.at[z], me, peer).start()
        remote(rts.at[pl.ds(peer * im, im)], rin.at[z], rts_ss.at[k], rts_rs.at[z], me, peer).start()
    core, chip = lax.rem(me, 2), me // 2
    partner = chip * 2 + 1 - core
    dense = ((wq, wq_all, 64), (wo, wo_all, 64))
    own_copies = [
        pltpu.make_async_copy(tok.at[pl.ds(z * im, im)], xin.at[z], loc_sem.at[0]),
        pltpu.make_async_copy(rts.at[pl.ds(z * im, im)], rin.at[z], loc_sem.at[1]),
        pltpu.make_async_copy(win, win_all.at[z], loc_sem.at[2]),
        pltpu.make_async_copy(wout, wout_all.at[z], loc_sem.at[3]),
        pltpu.make_async_copy(wq, wq_all.at[rows_of(me, 64)], loc_sem.at[4]),
        pltpu.make_async_copy(wo, wo_all.at[rows_of(me, 64)], loc_sem.at[5]),
        pltpu.make_async_copy(vec, vec_all.at[me], loc_sem.at[6]),
    ]
    for copy in own_copies:
        copy.start()

    def dense_slot(array, index):
        if array == 0:
            return wq_all.at[rows_of(index, 64)]
        if array == 1:
            return wo_all.at[rows_of(index, 64)]
        return vec_all.at[index]

    dense_in = (wq, wo, vec)
    for array in range(3):
        for k in range(1, half):
            peer = lax.rem(chip + k, half) * 2 + core
            remote(
                dense_in[array], dense_slot(array, me), den_ss.at[array, k], den_rs.at[array, me], peer, z
            ).start()
        remote(
            dense_in[array], dense_slot(array, me), den_ss.at[array, 0], den_rs.at[array, me], partner, z
        ).start()
    sends = ((win_all, win_ss, win_rs), (wout_all, wout_ss, wout_rs))
    for source, (full, send_sem, recv_sem) in zip((win, wout), sends):

        @pl.when(z < n_z - 1)
        def _():
            remote(source, full.at[z], send_sem.at[0, 0], recv_sem.at[z], me, z + 1).start()

        @pl.when(z > 0)
        def _():
            remote(source, full.at[z], send_sem.at[1, 0], recv_sem.at[z], me, z - 1).start()

    xpad[...] = jnp.zeros_like(xpad)
    for k in range(1, half):
        origin = lax.rem(chip + k, half) * 2 + core
        for array in range(3):
            slot = dense_slot(array, origin)
            remote(slot, slot, den_ss.at[array, 0], den_rs.at[array, origin], me, z).wait_recv()
            remote(slot, slot, fwd_ss.at[array, k], den_rs.at[array, origin], partner, z).start()
    for k in range(half):
        origin = lax.rem(chip + k, half) * 2 + 1 - core
        for array in range(3):
            slot = dense_slot(array, origin)
            remote(slot, slot, den_ss.at[array, 0], den_rs.at[array, origin], me, z).wait_recv()
    for copy in own_copies:
        copy.wait()
    total = vec_all[0].astype(F32)
    for k in range(1, n_dp):
        total = total + vec_all[k].astype(F32)
    vsum[...] = total
    for k in range(1, n_z):
        origin = lax.rem(z + k, n_z)
        remote(xin.at[origin], xin.at[origin], tok_ss.at[0], tok_rs.at[origin], me, z).wait_recv()
        remote(rin.at[origin], rin.at[origin], rts_ss.at[0], rts_rs.at[origin], me, z).wait_recv()

    masks = half_masks()
    keys_ok = key_mask(n_z, block)
    gain_one, bias_one = vsum[0:1, :], vsum[1:2, :]
    gain_two, bias_two = vsum[2:3, :], vsum[3:4, :]
    router_t = vsum[8:16, :].astype(BF)
    lane_low = lax.broadcasted_iota(jnp.int32, (sp, 128), 1) < 64
    lane_id = lax.broadcasted_iota(jnp.int32, (sp, 128), 1)
    before = lax.broadcasted_iota(jnp.int32, (sp, sp), 0)
    after = lax.broadcasted_iota(jnp.int32, (sp, sp), 1)
    prefix = jnp.where((before < after) & (before // BP == after // BP), 1.0, 0.0).astype(BF)
    expert_id = lax.broadcasted_iota(jnp.int32, (8, sp), 0)
    slot_lane = lax.broadcasted_iota(jnp.int32, (8, sp), 1)

    def image(i, carry):
        for b in range(n_z):
            xpad[i, b * BP : b * BP + block, :] = xin[b, i]
        x = xpad[i].astype(F32)
        hat, _ = norm_parts(x)
        normed = (hat * gain_one + bias_one).astype(BF)
        qkvs[i] = nn(normed, wq_all[...]).astype(BF)
        lse_all = jnp.zeros((sp, 128), F32)
        for pair in range(4):
            q2 = qkvs[i, :, pair * 128 : pair * 128 + 128]
            k2 = qkvs[i, :, 512 + pair * 128 : 512 + pair * 128 + 128]
            v2 = qkvs[i, :, 1024 + pair * 128 : 1024 + pair * 128 + 128]
            parts = []
            for side in range(2):
                scores = nt(q2 * masks[side], k2) * 0.125
                scores = jnp.where(keys_ok, scores, NEG)
                top = jnp.max(scores, axis=-1, keepdims=True)
                exponent = jnp.exp(scores - top)
                whole = jnp.sum(exponent, axis=-1, keepdims=True)
                lse_all = jnp.where(lane_id == pair * 2 + side, top + jnp.log(whole), lse_all)
                parts.append(nn((exponent / whole).astype(BF), v2))
            outs[i, :, pair * 128 : pair * 128 + 128] = jnp.where(lane_low, parts[0], parts[1]).astype(BF)
        lses[i] = lse_all
        x2 = x + nn(outs[i], wo_all[...])
        x2s[i] = x2
        hat2, _ = norm_parts(x2)
        n2 = (hat2 * gain_two + bias_two).astype(BF)
        n2s[i] = n2
        logits = nt(router_t, n2)
        raised = jnp.exp(logits - jnp.max(logits, axis=0, keepdims=True))
        share = raised / jnp.sum(raised, axis=0, keepdims=True)
        gts[i] = share
        lane8 = lax.broadcasted_iota(jnp.int32, (8, 128), 1)
        wide = jnp.concatenate([rin[0, i] + rin[1, i], rin[2, i] + rin[3, i]], axis=1)
        hits = [(expert_id + 1) == wide[j : j + 1, :] for j in range(2)]
        any_hit = jnp.where(hits[0] | hits[1], 1.0, 0.0)
        place = nn(any_hit.astype(BF), prefix)
        base = place + (expert_id * er + (slot_lane // BP) * cap + i * (n_z * cap) + 1).astype(F32)
        lines = [jnp.sum(jnp.where(hit, base, 0.0), axis=0, keepdims=True) - 1.0 for hit in hits]
        lines += [jnp.sum(jnp.where(hit, share, 0.0), axis=0, keepdims=True) for hit in hits]
        table = jnp.concatenate(lines + [jnp.zeros((124, sp), F32)], axis=0)
        meta[i] = table[0:8]
        metat[i] = jnp.transpose(table)
        return carry

    lax.fori_loop(0, im, image, 0)

    row_id = lax.broadcasted_iota(jnp.int32, (er, sp), 0)
    for k in range(n_dp):
        peer = lax.rem(me + k, n_dp)
        want = (row_id + peer * er).astype(F32)
        total = jnp.zeros((er, 512), F32)
        for i in range(im):
            pick = (want == meta[i, 0:1, :]) | (want == meta[i, 1:2, :])
            total = total + nn(jnp.where(pick, 1.0, 0.0).astype(BF), n2s[i])
        if k == 0:
            recv[rows_of(me, er)] = total.astype(BF)
        else:
            sbuf[k] = total.astype(BF)
            remote(
                sbuf.at[k], recv.at[rows_of(me, er)], row_ss.at[k], row_rs.at[me], peer, z
            ).start()
    for step in range(1, n_z):
        gather_step(step, z, n_z, me, sends)
    for k in range(1, n_dp):
        origin = lax.rem(me + k, n_dp)
        spot = recv.at[rows_of(origin, er)]
        remote(spot, spot, row_ss.at[0], row_rs.at[origin], me, z).wait_recv()
    gather_sends_done(z, n_z, me, sends)
    for k in range(1, n_dp):
        remote(sbuf.at[k], sbuf.at[k], row_ss.at[k], row_rs.at[0], me, z).wait_send()
    for k in range(1, n_z):
        remote(xin.at[0], xin.at[0], tok_ss.at[k], tok_rs.at[0], me, z).wait_send()
        remote(rin.at[0], rin.at[0], rts_ss.at[k], rts_rs.at[0], me, z).wait_send()
    for array in range(3):
        for k in range(half):
            remote(
                dense_in[array], dense_in[array], den_ss.at[array, k], den_rs.at[array, 0], me, z
            ).wait_send()
        for k in range(1, half):
            remote(
                dense_in[array], dense_in[array], fwd_ss.at[array, k], den_rs.at[array, 0], me, z
            ).wait_send()


GELU_C = 0.7978845608028654
GELU_K = 0.044715


def expert_kernel(
    dims,
    rows, win_all, wout_all, tgt,
    ret, acts, slopes, tin,
    ubuf,
    u_ss, u_rs, tgt_ss, tgt_rs, loc_sem,
):
    n_dp, n_z, im, block, cap, er = dims
    me, z = lax.axis_index("dp"), lax.axis_index("seq")
    entry_barrier(me, z, n_dp, n_z, True, True)
    for k in range(1, n_z):
        peer = lax.rem(z + k, n_z)
        remote(tgt.at[pl.ds(peer * im, im)], tin.at[z], tgt_ss.at[k], tgt_rs.at[z], me, peer).start()
    own = pltpu.make_async_copy(tgt.at[pl.ds(z * im, im)], tin.at[z], loc_sem)
    own.start()
    two = 2 * er

    def hidden(step, carry):
        shard, chunk = step // 8, lax.rem(step, 8)
        part, side = chunk // 2, lax.rem(chunk, 2)
        x = rows[rows_of(part, two)]
        for side in range(2):
            pre = nn(x, win_all[shard, :, side * 256 : side * 256 + 256])
            square = pre * pre
            tanh = jnp.tanh(pre * (GELU_C + (GELU_C * GELU_K) * square))
            gate = 0.5 + 0.5 * tanh
            acts[shard, rows_of(part, two), side * 256 : side * 256 + 256] = (pre * gate).astype(BF)
            slope = gate + pre * (0.5 - 0.5 * tanh * tanh) * (
                GELU_C + (3.0 * GELU_C * GELU_K) * square
            )
            slopes[shard, rows_of(part, two), side * 256 : side * 256 + 256] = slope.astype(BF)
        return carry

    def hidden_step(step, carry):
        return hidden((step // 4) * 8 + lax.rem(step, 4) * 2, carry)

    lax.fori_loop(0, 4 * n_z, hidden_step, 0)
    for k in range(n_dp // 2):
        part = lax.rem(me // 2 + k, n_dp // 2)
        total = jnp.zeros((two, 512), F32)
        for shard in range(n_z):
            total = total + nn(acts[shard, rows_of(part, two)], wout_all[shard])
        out = total.astype(BF)
        if k == 0:
            ubuf[0] = out[0:er]
            ubuf[1] = out[er:two]
            mine = lax.rem(me, 2)
            peer = (me // 2) * 2 + 1 - mine
            ret[rows_of(me, er)] = ubuf[mine]
            remote(
                ubuf.at[1 - mine], ret.at[rows_of(me, er)], u_ss.at[1], u_rs.at[me], peer, z
            ).start()
        else:
            for c in range(2):
                ubuf[2 * k + c] = out[c * er : c * er + er]
                remote(
                    ubuf.at[2 * k + c],
                    ret.at[rows_of(me, er)],
                    u_ss.at[2 * k + c],
                    u_rs.at[me],
                    part * 2 + c,
                    z,
                ).start()
    for k in range(1, n_dp):
        origin = lax.rem(me + k, n_dp)
        spot = ret.at[rows_of(origin, er)]
        remote(spot, spot, u_ss.at[0], u_rs.at[origin], me, z).wait_recv()
    for k in range(1, n_dp):
        remote(ubuf.at[k], ubuf.at[k], u_ss.at[k], u_rs.at[0], me, z).wait_send()
    own.wait()
    for k in range(1, n_z):
        origin = lax.rem(z + k, n_z)
        remote(tin.at[origin], tin.at[origin], tgt_ss.at[0], tgt_rs.at[origin], me, z).wait_recv()
    for k in range(1, n_z):
        remote(tin.at[0], tin.at[0], tgt_ss.at[k], tgt_rs.at[0], me, z).wait_send()


def mix_kernel(
    dims,
    ret, tin, x2s, n2s, meta, metat, gts,
    recv, mixed, dys, dlogs, grouter,
    mbuf, dus, sbuf,
    row_ss, row_rs, mix_ss, mix_rs, loc_sem,
):
    n_dp, n_z, im, block, cap, er = dims
    me, z = lax.axis_index("dp"), lax.axis_index("seq")
    sp = n_z * BP
    nr = n_dp * er
    entry_barrier(me, z, n_dp, n_z, True, True)
    rows_ok = row_mask(n_z, block)
    line = lax.broadcasted_iota(jnp.int32, (sp, nr), 1).astype(F32)
    lane_id = lax.broadcasted_iota(jnp.int32, (sp, 128), 1)

    def image(i, carry):
        cols = metat[i]
        picked = []
        for j in range(2):
            pick = jnp.where(line == cols[:, j : j + 1], 1.0, 0.0).astype(BF)
            picked.append(nn(pick, ret[...]))
        mix = x2s[i] + cols[:, 2:3] * picked[0] + cols[:, 3:4] * picked[1]
        mix_b = mix.astype(BF)
        for b in range(n_z):
            mbuf[b, i] = mix_b[b * BP : b * BP + block]
        for b in range(n_z):
            dys[i, b * BP : b * BP + block, :] = tin[b, i].astype(F32)
        dy = jnp.where(rows_ok, mix - dys[i], 0.0)
        dys[i] = dy
        dus[0, i] = (cols[:, 2:3] * dy).astype(BF)
        dus[1, i] = (cols[:, 3:4] * dy).astype(BF)
        slope = jnp.where(
            lane_id == 0, jnp.sum(dy * picked[0], axis=-1, keepdims=True), 0.0
        ) + jnp.where(lane_id == 1, jnp.sum(dy * picked[1], axis=-1, keepdims=True), 0.0)
        dlogs[i] = slope
        return carry

    lax.fori_loop(0, im, image, 0)
    row_id = lax.broadcasted_iota(jnp.int32, (er, sp), 0)
    for k in range(n_dp):
        peer = lax.rem(me + k, n_dp)
        want = (row_id + peer * er).astype(F32)
        total = jnp.zeros((er, 512), F32)
        for i in range(im):
            for j in range(2):
                pick = jnp.where(want == meta[i, j : j + 1, :], 1.0, 0.0).astype(BF)
                total = total + nn(pick, dus[j, i])
        if k == 0:
            recv[rows_of(me, er)] = total.astype(BF)
        else:
            sbuf[k] = total.astype(BF)
            remote(
                sbuf.at[k], recv.at[rows_of(me, er)], row_ss.at[k], row_rs.at[me], peer, z
            ).start()
    for k in range(1, n_z):
        peer = lax.rem(z + k, n_z)
        remote(mbuf.at[peer], mixed.at[pl.ds(z * im, im)], mix_ss.at[k], mix_rs.at[z], me, peer).start()
    own = pltpu.make_async_copy(mbuf.at[z], mixed.at[pl.ds(z * im, im)], loc_sem)
    own.start()
    expert_id = lax.broadcasted_iota(jnp.int32, (8, sp), 0).astype(F32)
    router = jnp.zeros((8, 512), F32)
    for i in range(im):
        flat = jnp.transpose(dlogs[i])
        at = [meta[i, j : j + 1, :] for j in range(2)]
        share = gts[i]
        grad = jnp.zeros((8, sp), F32)
        for j in range(2):
            inside = (at[j] >= expert_id * er) & (at[j] < expert_id * er + er)
            grad = grad + jnp.where(inside, flat[j : j + 1, :], 0.0)
        inner = jnp.sum(share * grad, axis=0, keepdims=True)
        dlog = (share * (grad - inner)).astype(BF)
        dlogs[i, 0:8, 0:128] = dlog[:, 0:128].astype(F32)
        dlogs[i, 8:16, 0:128] = dlog[:, 128:256].astype(F32)
        router = router + nn(dlog, n2s[i])
    grouter[...] = router
    for k in range(1, n_dp):
        origin = lax.rem(me + k, n_dp)
        spot = recv.at[rows_of(origin, er)]
        remote(spot, spot, row_ss.at[0], row_rs.at[origin], me, z).wait_recv()
    for k in range(1, n_dp):
        remote(sbuf.at[k], sbuf.at[k], row_ss.at[k], row_rs.at[0], me, z).wait_send()
    own.wait()
    for k in range(1, n_z):
        origin = lax.rem(z + k, n_z)
        spot = mixed.at[pl.ds(origin * im, im)]
        remote(spot, spot, mix_ss.at[0], mix_rs.at[origin], me, z).wait_recv()
    for k in range(1, n_z):
        remote(mbuf.at[0], mbuf.at[0], mix_ss.at[k], mix_rs.at[0], me, z).wait_send()


def expert_back_kernel(
    dims,
    rows, drows, acts, slopes, win_all, wout_all,
    ret, dws,
    dpres, ubuf,
    u_ss, u_rs,
):
    n_dp, n_z, im, block, cap, er = dims
    me, z = lax.axis_index("dp"), lax.axis_index("seq")
    entry_barrier(me, z, n_dp, n_z, True, False)
    two = 2 * er
    for k in range(n_dp // 2):
        part = lax.rem(me // 2 + k, n_dp // 2)
        at = rows_of(part, two)
        du = drows[at]
        total = jnp.zeros((two, 512), F32)
        for shard in range(n_z):
            dpre = (nt(du, wout_all[shard]) * slopes[shard, at].astype(F32)).astype(BF)
            dpres[shard, at] = dpre
            total = total + nt(dpre, win_all[shard])
        out = total.astype(BF)
        if k == 0:
            ubuf[0] = out[0:er]
            ubuf[1] = out[er:two]
            mine = lax.rem(me, 2)
            peer = (me // 2) * 2 + 1 - mine
            ret[rows_of(me, er)] = ubuf[mine]
            remote(
                ubuf.at[1 - mine], ret.at[rows_of(me, er)], u_ss.at[1], u_rs.at[me], peer, z
            ).start()
        else:
            for c in range(2):
                ubuf[2 * k + c] = out[c * er : c * er + er]
                remote(
                    ubuf.at[2 * k + c],
                    ret.at[rows_of(me, er)],
                    u_ss.at[2 * k + c],
                    u_rs.at[me],
                    part * 2 + c,
                    z,
                ).start()

    def weights(shard, carry):
        dws[shard, 0:512, :] = tn(rows[...], dpres[shard]).astype(BF)
        dws[shard, 512:1024, :] = tn(acts[shard], drows[...]).astype(BF)
        return carry

    lax.fori_loop(0, n_z, weights, 0)
    for k in range(1, n_dp):
        origin = lax.rem(me + k, n_dp)
        spot = ret.at[rows_of(origin, er)]
        remote(spot, spot, u_ss.at[0], u_rs.at[origin], me, z).wait_recv()
    for k in range(1, n_dp):
        remote(ubuf.at[k], ubuf.at[k], u_ss.at[k], u_rs.at[0], me, z).wait_send()


def back_kernel(
    dims,
    dret, dws, dys, dlogs, x2s, xpad, qkvs, outs, lses, metat, wq_all, wo_all, vsum,
    gtok, gbig, gvec, gin, gout,
    gacc, tbuf, from_left, from_right, to_right, to_left,
    tok_ss, tok_rs, r_ss, r_rs, l_ss, l_rs, loc_sem,
):
    n_dp, n_z, im, block, cap, er = dims
    me, z = lax.axis_index("dp"), lax.axis_index("seq")
    sp = n_z * BP
    nr = n_dp * er
    entry_barrier(me, z, n_dp, n_z, False, True)
    last = n_z - 1

    def pass_right(target):
        @pl.when(z < target)
        def _():
            @pl.when(z == 0)
            def _():
                remote(
                    dws.at[target], from_left.at[target], r_ss.at[target], r_rs.at[target], me, z + 1
                ).start()

            @pl.when(z > 0)
            def _():
                here = from_left.at[target]
                remote(here, here, r_ss.at[target], r_rs.at[target], me, z).wait_recv()

                def add(c, carry):
                    at = rows_of(c, 128)
                    to_right[target, at] = (
                        dws[target, at].astype(F32) + from_left[target, at].astype(F32)
                    ).astype(BF)
                    return carry

                lax.fori_loop(0, 8, add, 0)
                remote(
                    to_right.at[target], here, r_ss.at[target], r_rs.at[target], me, z + 1
                ).start()

    def pass_left(target):
        @pl.when(z > target)
        def _():
            @pl.when(z == last)
            def _():
                remote(
                    dws.at[target], from_right.at[target], l_ss.at[target], l_rs.at[target], me, z - 1
                ).start()

            @pl.when(z < last)
            def _():
                here = from_right.at[target]
                remote(here, here, l_ss.at[target], l_rs.at[target], me, z).wait_recv()

                def add(c, carry):
                    at = rows_of(c, 128)
                    to_left[target, at] = (
                        dws[target, at].astype(F32) + from_right[target, at].astype(F32)
                    ).astype(BF)
                    return carry

                lax.fori_loop(0, 8, add, 0)
                remote(
                    to_left.at[target], here, l_ss.at[target], l_rs.at[target], me, z - 1
                ).start()

    def pass_on(step, first):
        for way, target in ((pass_right, last - step), (pass_left, step)):
            edge = 0 if way is pass_right else last

            @pl.when((z == edge) if first else (z != edge))
            def _():
                way(target)

    for step in range(n_z - 1):
        pass_on(step, True)

    masks = half_masks()
    keys_ok = key_mask(n_z, block)
    gain_one, bias_one = vsum[0:1, :], vsum[1:2, :]
    gain_two = vsum[2:3, :]
    router_t = vsum[8:16, :].astype(BF)
    line = lax.broadcasted_iota(jnp.int32, (sp, nr), 1).astype(F32)
    lane_low = lax.broadcasted_iota(jnp.int32, (sp, 128), 1) < 64
    gacc[...] = jnp.zeros_like(gacc)
    gvec[...] = jnp.zeros_like(gvec)

    def image(i, carry):
        cols = metat[i]
        pick = jnp.where((line == cols[:, 0:1]) | (line == cols[:, 1:2]), 1.0, 0.0).astype(BF)
        dlog = jnp.concatenate([dlogs[i, 0:8, :], dlogs[i, 8:16, :]], axis=1).astype(BF)
        dn2 = nn(pick, dret[...]) + tn(dlog, router_t)
        hat2, scale2 = norm_parts(x2s[i])
        gvec[2:3, :] += jnp.sum(dn2 * hat2, axis=0, keepdims=True)
        gvec[3:4, :] += jnp.sum(dn2, axis=0, keepdims=True)
        dx2 = dys[i] + norm_back(dn2 * gain_two, hat2, scale2)
        da = dx2.astype(BF)
        gacc[:, 1536:2048] += tn(outs[i], da)
        do = nt(da, wo_all[...]).astype(BF)
        hat1, scale1 = norm_parts(xpad[i].astype(F32))
        n1 = (hat1 * gain_one + bias_one).astype(BF)
        dn1 = jnp.zeros((sp, 512), F32)
        for pair in range(4):
            at = pair * 128
            q2 = qkvs[i, :, at : at + 128]
            k2 = qkvs[i, :, 512 + at : 512 + at + 128]
            v2 = qkvs[i, :, 1024 + at : 1024 + at + 128]
            do2 = do[:, at : at + 128]
            grads = ([], [], [])
            for side in range(2):
                head = pair * 2 + side
                scores = nt(q2 * masks[side], k2) * 0.125
                scores = jnp.where(keys_ok, scores, NEG)
                prob = jnp.exp(scores - lses[i, :, head : head + 1])
                dprob = nt(do2 * masks[side], v2)
                inner = jnp.sum(prob * dprob, axis=-1, keepdims=True)
                ds = (prob * (dprob - inner)).astype(BF)
                grads[0].append(nn(ds, k2))
                grads[1].append(tn(ds, q2))
                grads[2].append(tn(prob.astype(BF), do2))
            for part in range(3):
                grad = jnp.where(lane_low, grads[part][0], grads[part][1])
                if part < 2:
                    grad = grad * 0.125
                grad = grad.astype(BF)
                col = part * 512 + at
                gacc[:, col : col + 128] += tn(n1, grad)
                dn1 = dn1 + nt(grad, wq_all[:, col : col + 128])
        gvec[0:1, :] += jnp.sum(dn1 * hat1, axis=0, keepdims=True)
        gvec[1:2, :] += jnp.sum(dn1, axis=0, keepdims=True)
        dx = (dx2 + norm_back(dn1 * gain_one, hat1, scale1)).astype(BF)
        for b in range(n_z):
            tbuf[b, i] = dx[b * BP : b * BP + block]
        return carry

    lax.fori_loop(0, im, image, 0)
    for k in range(1, n_z):
        peer = lax.rem(z + k, n_z)
        remote(tbuf.at[peer], gtok.at[pl.ds(z * im, im)], tok_ss.at[k], tok_rs.at[z], me, peer).start()
    own = pltpu.make_async_copy(tbuf.at[z], gtok.at[pl.ds(z * im, im)], loc_sem)
    own.start()
    gbig[...] = gacc[...].astype(BF)
    for step in range(n_z - 1):
        pass_on(step, False)

    @pl.when(z > 0)
    def _():
        here = from_left.at[z]
        remote(here, here, r_ss.at[0], r_rs.at[z], me, z).wait_recv()

    @pl.when(z < last)
    def _():
        here = from_right.at[z]
        remote(here, here, l_ss.at[0], l_rs.at[z], me, z).wait_recv()

    def finish(c, carry):
        at = rows_of(c, 128)
        left = jnp.where(z > 0, from_left[z, at].astype(F32), 0.0)
        right = jnp.where(z < last, from_right[z, at].astype(F32), 0.0)
        total = dws[z, at].astype(F32) + left + right

        @pl.when(c < 4)
        def _():
            gin[at] = total

        @pl.when(c >= 4)
        def _():
            gout[rows_of(c - 4, 128)] = total

        return carry

    lax.fori_loop(0, 8, finish, 0)
    own.wait()
    for k in range(1, n_z):
        origin = lax.rem(z + k, n_z)
        spot = gtok.at[pl.ds(origin * im, im)]
        remote(spot, spot, tok_ss.at[0], tok_rs.at[origin], me, z).wait_recv()
    for k in range(1, n_z):
        remote(tbuf.at[0], tbuf.at[0], tok_ss.at[k], tok_rs.at[0], me, z).wait_send()
    for target in range(n_z):

        @pl.when(z < target)
        def _():
            remote(dws.at[0], dws.at[0], r_ss.at[target], r_rs.at[0], me, z).wait_send()

        @pl.when(z > target)
        def _():
            remote(dws.at[0], dws.at[0], l_ss.at[target], l_rs.at[0], me, z).wait_send()


def dense_kernel(
    dims,
    gbig, gvec,
    big, small,
    brecv, vrecv, bz, vz, bsend, vsend,
    b_ss, b_rs, v_ss, v_rs, bz_ss, bz_rs, vz_ss, vz_rs,
):
    n_dp, n_z, im, block, cap, er = dims
    me, z = lax.axis_index("dp"), lax.axis_index("seq")
    entry_barrier(me, z, n_dp, n_z, True, True)
    for k in range(1, n_dp):
        peer = lax.rem(me + k, n_dp)
        remote(gbig.at[rows_of(peer, 64)], brecv.at[me], b_ss.at[k], b_rs.at[me], peer, z).start()
        remote(gvec, vrecv.at[me], v_ss.at[k], v_rs.at[me], peer, z).start()
    total = gbig[rows_of(me, 64)].astype(F32)
    vtotal = gvec[...].astype(F32)
    for k in range(1, n_dp):
        origin = lax.rem(me + k, n_dp)
        remote(brecv.at[origin], brecv.at[origin], b_ss.at[0], b_rs.at[origin], me, z).wait_recv()
        remote(vrecv.at[origin], vrecv.at[origin], v_ss.at[0], v_rs.at[origin], me, z).wait_recv()
        total = total + brecv[origin].astype(F32)
        vtotal = vtotal + vrecv[origin].astype(F32)
    bsend[...] = total.astype(BF)
    vsend[...] = vtotal.astype(BF)
    for k in range(1, n_z):
        peer = lax.rem(z + k, n_z)
        remote(bsend, bz.at[z], bz_ss.at[k], bz_rs.at[z], me, peer).start()
        remote(vsend, vz.at[z], vz_ss.at[k], vz_rs.at[z], me, peer).start()
    for k in range(1, n_z):
        origin = lax.rem(z + k, n_z)
        remote(bz.at[origin], bz.at[origin], bz_ss.at[0], bz_rs.at[origin], me, z).wait_recv()
        remote(vz.at[origin], vz.at[origin], vz_ss.at[0], vz_rs.at[origin], me, z).wait_recv()
        total = total + bz[origin].astype(F32)
        vtotal = vtotal + vz[origin].astype(F32)
    big[...] = total
    small[...] = vtotal
    for k in range(1, n_dp):
        remote(brecv.at[0], brecv.at[0], b_ss.at[k], b_rs.at[0], me, z).wait_send()
        remote(vrecv.at[0], vrecv.at[0], v_ss.at[k], v_rs.at[0], me, z).wait_send()
    for k in range(1, n_z):
        remote(bsend, bsend, bz_ss.at[k], bz_rs.at[0], me, z).wait_send()
        remote(vsend, vsend, vz_ss.at[k], vz_rs.at[0], me, z).wait_send()


def call(kernel, dims, collective_id, outs, scratch, name, *args):
    spec = pl.BlockSpec(memory_space=pltpu.VMEM)
    return pl.pallas_call(
        functools.partial(kernel, dims),
        out_shape=[jax.ShapeDtypeStruct(shape, kind) for shape, kind in outs],
        in_specs=[spec] * len(args),
        out_specs=[spec] * len(outs),
        scratch_shapes=scratch,
        compiler_params=pltpu.CompilerParams(
            collective_id=collective_id, has_side_effects=True, vmem_limit_bytes=VMEM_LIMIT
        ),
        name=name,
    )(*args)


def whole_images(
    tokens, ln1_gain, ln1_bias, w_qkv, w_out, ln2_gain, ln2_bias, w_router, expert_in, expert_out, routes, targets
):
    n_dp, n_z = lax.axis_size("dp"), lax.axis_size("seq")
    image_count, block, width = tokens.shape
    im = image_count // n_z
    cap = 2 * S // (n_z * w_router.shape[1]) + 2
    er = -(-(im * n_z * cap) // 16) * 16
    dims = (n_dp, n_z, im, block, cap, er)
    sp, nr = n_z * BP, n_dp * er
    me, z = lax.axis_index("dp"), lax.axis_index("seq")
    dma, vm = pltpu.SemaphoreType.DMA, pltpu.VMEM

    valid = z * block + jnp.arange(block) < VALID
    lines = jnp.where(valid[None, None, :], jnp.transpose(routes, (0, 2, 1)) + 1, 0)
    lines = jnp.pad(lines, ((0, 0), (0, 6), (0, BP - block)))
    odd = lax.rem(z, 2) == 1
    lines = jnp.concatenate([jnp.where(odd, 0, lines), jnp.where(odd, lines, 0)], axis=-1)
    vec = jnp.concatenate(
        [
            jnp.stack([ln1_gain, ln1_bias, ln2_gain, ln2_bias]),
            jnp.zeros((4, ln1_gain.shape[0]), BF),
            jnp.transpose(w_router),
        ],
        axis=0,
    )
    vec = lax.dynamic_update_slice(jnp.zeros((16, width), BF), vec, (0, me * ln1_gain.shape[0]))

    (recv, win_all, wout_all, wq_all, wo_all, vsum, xpad, x2s, n2s, qkvs, outs, gts, meta, metat, lses) = call(
        front_kernel, dims, 1,
        [
            ((nr, width), BF), ((n_z, 512, 512), BF), ((n_z, 512, 512), BF), ((width, 1536), BF), ((width, width), BF),
            ((16, width), F32), ((im, sp, width), BF), ((im, sp, width), F32), ((im, sp, width), BF),
            ((im, sp, 1536), BF), ((im, sp, width), BF), ((im, 8, sp), F32), ((im, 8, sp), F32), ((im, sp, 128), F32),
            ((im, sp, 128), F32),
        ],
        [
            vm((n_z, im, block, width), BF), vm((n_z, im, 8, 128), jnp.int32), vm((n_dp, 16, width), BF),
            vm((n_dp, er, width), BF),
            dma((n_z,)), dma((n_z,)), dma((n_z,)), dma((n_z,)), dma((3, n_dp // 2)), dma((3, n_dp)), dma((3, n_dp // 2)),
            dma((2, n_z)), dma((n_z,)), dma((2, n_z)), dma((n_z,)), dma((n_dp,)), dma((n_dp,)), dma((7,)),
        ],
        "front",
        tokens, lines, w_qkv, w_out, vec, expert_in[0], expert_out[0],
    )
    ret, acts, slopes, tin = call(
        expert_kernel, dims, 2,
        [((nr, width), BF), ((n_z, nr, 512), BF), ((n_z, nr, 512), BF), ((n_z, im, block, width), BF)],
        [vm((n_dp, er, width), BF), dma((n_dp,)), dma((n_dp,)), dma((n_z,)), dma((n_z,)), dma],
        "experts",
        recv, win_all, wout_all, targets,
    )
    drows, mixed, dys, dlogs, grouter = call(
        mix_kernel, dims, 3,
        [
            ((nr, width), BF), ((image_count, block, width), BF), ((im, sp, width), F32), ((im, sp, 128), F32),
            ((8, width), F32),
        ],
        [
            vm((n_z, im, block, width), BF), vm((2, im, sp, width), BF), vm((n_dp, er, width), BF),
            dma((n_dp,)), dma((n_dp,)), dma((n_z,)), dma((n_z,)), dma,
        ],
        "mix",
        ret, tin, x2s, n2s, meta, metat, gts,
    )
    dret, dws = call(
        expert_back_kernel, dims, 4,
        [((nr, width), BF), ((n_z, 1024, 512), BF)],
        [vm((n_z, nr, 512), BF), vm((n_dp, er, width), BF), dma((n_dp,)), dma((n_dp,))],
        "experts_back",
        recv, drows, acts, slopes, win_all, wout_all,
    )
    gtok, gbig, gvec, gin, gout = call(
        back_kernel, dims, 5,
        [
            ((image_count, block, width), BF), ((width, 2048), BF), ((8, width), F32), ((512, 512), F32),
            ((512, 512), F32),
        ],
        [
            vm((width, 2048), F32), vm((n_z, im, block, width), BF), vm((n_z, 1024, 512), BF), vm((n_z, 1024, 512), BF),
            vm((n_z, 1024, 512), BF), vm((n_z, 1024, 512), BF),
            dma((n_z,)), dma((n_z,)), dma((n_z,)), dma((n_z,)), dma((n_z,)), dma((n_z,)), dma,
        ],
        "back",
        dret, dws, dys, dlogs, x2s, xpad, qkvs, outs, lses, metat, wq_all, wo_all, vsum,
    )
    big, small = call(
        dense_kernel, dims, 6,
        [((64, 2048), F32), ((16, width), F32)],
        [
            vm((n_dp, 64, 2048), BF), vm((n_dp, 16, width), BF), vm((n_z, 64, 2048), BF), vm((n_z, 16, width), BF),
            vm((64, 2048), BF), vm((16, width), BF),
            dma((n_dp,)), dma((n_dp,)), dma((n_dp,)), dma((n_dp,)), dma((n_z,)), dma((n_z,)), dma((n_z,)), dma((n_z,)),
        ],
        "dense",
        gbig, jnp.concatenate([gvec, grouter], axis=0).astype(BF),
    )
    part = lax.dynamic_slice(small, (0, me * ln1_gain.shape[0]), (16, ln1_gain.shape[0]))
    return (
        mixed,
        gtok.astype(F32),
        part[0],
        part[1],
        big[:, 0:1536],
        big[:, 1536:2048],
        part[2],
        part[3],
        jnp.transpose(part[8:16]),
        gin[None],
        gout[None],
    )


def fits(tokens, w_qkv, w_router, expert_in):
    n_dp, n_z = lax.axis_size("dp"), lax.axis_size("seq")
    return (
        n_dp == 8
        and n_z == 4
        and tokens.shape[0] % n_z == 0
        and tokens.shape[1] <= BP
        and tokens.shape[2] == 512
        and w_qkv.shape == (64, 1536)
        and w_router.shape[1] == n_dp
        and expert_in.shape == (1, 512, 512)
    )


def local(*args):
    if fits(args[0], args[3], args[7], args[8]):
        return whole_images(*args)
    return by_heads(*args)


def solution(mesh):
    placed = (
        P("dp", "seq", None),
        P("dp"),
        P("dp"),
        P("dp", None),
        P("dp", None),
        P("dp"),
        P("dp"),
        P("dp", None),
        P("dp", None, "seq"),
        P("dp", "seq", None),
        P("dp", "seq", None),
        P("dp", "seq", None),
    )
    return jax.shard_map(
        local,
        mesh=mesh,
        in_specs=placed,
        out_specs=(
            P("dp", "seq", None),
            P("dp", "seq", None),
            P("dp"),
            P("dp"),
            P("dp", None),
            P("dp", None),
            P("dp"),
            P("dp"),
            P("dp", None),
            P("dp", None, "seq"),
            P("dp", "seq", None),
        ),
        check_vma=False,
    )
```

```python
import functools

import jax
import jax.numpy as jnp
from jax import lax
from jax.experimental import pallas as pl
from jax.experimental.pallas import tpu as pltpu
from jax.sharding import PartitionSpec as P

H = 8
S = 200
VALID = 197


def layer_norm(values, gain_vec, bias_vec):
    centre = values - jnp.mean(values, axis=-1, keepdims=True)
    spread = jnp.mean(centre * centre, axis=-1, keepdims=True)
    return centre * lax.rsqrt(spread + 1e-06) * gain_vec + bias_vec


def regroup_heads(values):
    return lax.all_to_all(values, "seq", split_axis=3, concat_axis=1, tiled=True)


def regroup_slots(values):
    return lax.all_to_all(values, "seq", split_axis=1, concat_axis=3, tiled=True)


def send_experts(values):
    return lax.all_to_all(values, "dp", split_axis=0, concat_axis=1, tiled=True)


def send_tokens(values):
    return lax.all_to_all(values, "dp", split_axis=1, concat_axis=0, tiled=True)


def masked_scores(queries, keys_in, key_valid):
    scores = (
        jnp.einsum("bqhd,bkhd->bhqk", queries, keys_in, preferred_element_type=jnp.float32) * 0.125
    )
    return jnp.where(key_valid, scores, -1e30)


def attention_forward(queries, keys_in, values, key_valid):
    scores = masked_scores(queries, keys_in, key_valid)
    row_top = jnp.max(scores, axis=-1, keepdims=True)
    exponent = jnp.exp(scores - row_top)
    row_total = jnp.sum(exponent, axis=-1, keepdims=True)
    prob_rows = exponent / row_total
    log_total = row_top + jnp.log(row_total)
    attended = jnp.einsum(
        "bhqk,bkhd->bqhd",
        prob_rows.astype(jnp.bfloat16),
        values,
        preferred_element_type=jnp.float32,
    )
    return (attended.astype(jnp.bfloat16), log_total)


def attention_backward(queries, keys_in, values, log_total, grad_attended, key_valid):
    scores = masked_scores(queries, keys_in, key_valid)
    prob_rows = jnp.exp(scores - log_total)
    grad_values = jnp.einsum(
        "bhqk,bqhd->bkhd",
        prob_rows.astype(jnp.bfloat16),
        grad_attended,
        preferred_element_type=jnp.float32,
    )
    grad_probs = jnp.einsum(
        "bqhd,bkhd->bhqk", grad_attended, values, preferred_element_type=jnp.float32
    )
    inner_sum = jnp.sum(prob_rows * grad_probs, axis=-1, keepdims=True)
    grad_scores = (prob_rows * (grad_probs - inner_sum)).astype(jnp.bfloat16)
    grad_queries = (
        jnp.einsum("bhqk,bkhd->bqhd", grad_scores, keys_in, preferred_element_type=jnp.float32)
        * 0.125
    )
    grad_keys = (
        jnp.einsum("bhqk,bqhd->bkhd", grad_scores, queries, preferred_element_type=jnp.float32)
        * 0.125
    )
    return jnp.stack([grad_queries, grad_keys, grad_values], axis=2)


def pick_block(total_rows):
    for candidate in (1024, 768, 512, 384, 256):
        if total_rows % candidate == 0:
            return candidate
    return total_rows


def by_heads(
    tokens,
    ln1_gain,
    ln1_bias,
    w_qkv,
    w_out,
    ln2_gain,
    ln2_bias,
    w_router,
    expert_in,
    expert_out,
    routes,
    targets,
):
    image_count, slot_count, model_width = tokens.shape
    seq_devices = lax.axis_size("seq")
    row_count = image_count * slot_count
    expert_count = w_router.shape[1]
    local_experts = expert_in.shape[0]
    slot_limit = 2 * S // (seq_devices * expert_count) + 2
    head_size = model_width // H
    gathered = (
        lax.all_gather(ln1_gain, "dp", axis=0, tiled=True),
        lax.all_gather(ln1_bias, "dp", axis=0, tiled=True),
        lax.all_gather(w_qkv, "dp", axis=0, tiled=True),
        lax.all_gather(w_out, "dp", axis=0, tiled=True),
        lax.all_gather(ln2_gain, "dp", axis=0, tiled=True),
        lax.all_gather(ln2_bias, "dp", axis=0, tiled=True),
        lax.all_gather(w_router, "dp", axis=0, tiled=True),
    )
    gain_one = gathered[0].astype(jnp.float32)
    bias_one = gathered[1].astype(jnp.float32)
    qkv_weight = gathered[2]
    out_weight = gathered[3]
    gain_two = gathered[4].astype(jnp.float32)
    bias_two = gathered[5].astype(jnp.float32)
    router_weight = gathered[6]
    slot_start = lax.axis_index("seq") * slot_count
    valid_slot = slot_start + jnp.arange(slot_count) < VALID
    valid_rows = jnp.tile(valid_slot, image_count)
    key_valid = (jnp.arange(S) < VALID)[None, None, None, :]
    token_rows = tokens.reshape(row_count, model_width).astype(jnp.float32)
    normed_one, norm_one_back = jax.vjp(layer_norm, token_rows, gain_one, bias_one)
    normed_one_b = normed_one.astype(jnp.bfloat16)
    mixed_qkv = jnp.dot(normed_one_b, qkv_weight, preferred_element_type=jnp.float32).astype(
        jnp.bfloat16
    )
    qkv_heads = regroup_heads(mixed_qkv.reshape(image_count, slot_count, 3, H, head_size))
    queries = qkv_heads[:, :, 0]
    keys_in = qkv_heads[:, :, 1]
    values = qkv_heads[:, :, 2]
    attended, log_total = attention_forward(queries, keys_in, values, key_valid)
    attended_rows = regroup_slots(attended[:, :, None]).reshape(row_count, model_width)
    residual_two = token_rows + jnp.dot(
        attended_rows, out_weight, preferred_element_type=jnp.float32
    )
    normed_two, norm_two_back = jax.vjp(layer_norm, residual_two, gain_two, bias_two)
    normed_two_b = normed_two.astype(jnp.bfloat16)
    logits = jnp.dot(normed_two_b, router_weight, preferred_element_type=jnp.float32)
    route_rows = routes.reshape(row_count, 2)
    chosen = (route_rows[:, :, None] == jnp.arange(expert_count)[None, None, :]) & valid_rows[
        :, None, None
    ]
    chosen_f = chosen.astype(jnp.float32)

    def gate_pick(logit_rows):
        return jnp.sum(jax.nn.softmax(logit_rows, axis=-1)[:, None, :] * chosen_f, axis=-1)

    gate_values, gate_back = jax.vjp(gate_pick, logits)
    pick_count = chosen.astype(jnp.int32).reshape(image_count, slot_count * 2, expert_count)
    before = jnp.cumsum(pick_count, axis=1) - pick_count
    place_hit = (before[..., None] == jnp.arange(slot_limit)) & (pick_count[..., None] > 0)
    dispatch = place_hit.astype(jnp.bfloat16).reshape(
        image_count, slot_count, 2, expert_count, slot_limit
    )
    normed_img = normed_two_b.reshape(image_count, slot_count, model_width)
    sent_rows = jnp.einsum(
        "bskem,bsd->ebmd", dispatch, normed_img, preferred_element_type=jnp.float32
    ).astype(jnp.bfloat16)
    received = send_experts(sent_rows.reshape(expert_count, image_count * slot_limit, model_width))
    weights_in, weights_out = (
        lax.all_gather(expert_in, "seq", axis=2, tiled=True),
        lax.all_gather(expert_out, "seq", axis=1, tiled=True),
    )
    total_rows = received.shape[1]
    block_rows = pick_block(total_rows)
    block_count = total_rows // block_rows

    def expert_step(block_index, produced):
        row_piece = lax.dynamic_slice_in_dim(received, block_index * block_rows, block_rows, 1)
        hidden_pre = jnp.einsum(
            "erd,edf->erf", row_piece, weights_in, preferred_element_type=jnp.float32
        )
        activated = jax.nn.gelu(hidden_pre).astype(jnp.bfloat16)
        result = jnp.einsum(
            "erf,efd->erd", activated, weights_out, preferred_element_type=jnp.float32
        ).astype(jnp.bfloat16)
        return lax.dynamic_update_slice_in_dim(produced, result, block_index * block_rows, 1)

    produced = lax.fori_loop(
        0,
        block_count,
        expert_step,
        jnp.zeros((local_experts, total_rows, model_width), jnp.bfloat16),
    )
    returned = send_tokens(produced).reshape(expert_count, image_count, slot_limit, model_width)
    per_choice = jnp.einsum(
        "bskem,ebmd->bskd", dispatch, returned, preferred_element_type=jnp.float32
    ).reshape(row_count, 2, model_width)
    mixed_rows = (
        residual_two
        + gate_values[:, 0:1] * per_choice[:, 0]
        + gate_values[:, 1:2] * per_choice[:, 1]
    )
    target_rows = targets.reshape(row_count, model_width).astype(jnp.float32)
    grad_mixed = (mixed_rows - target_rows) * valid_rows[:, None].astype(jnp.float32)
    grad_gates = jnp.sum(grad_mixed[:, None, :] * per_choice, axis=-1)
    grad_choice = (
        (gate_values[:, :, None] * grad_mixed[:, None, :])
        .astype(jnp.bfloat16)
        .reshape(image_count, slot_count, 2, model_width)
    )
    grad_sent = jnp.einsum(
        "bskem,bskd->ebmd", dispatch, grad_choice, preferred_element_type=jnp.float32
    ).astype(jnp.bfloat16)
    grad_received = send_experts(
        grad_sent.reshape(expert_count, image_count * slot_limit, model_width)
    )
    back_in, back_out = (
        lax.all_gather(expert_in, "seq", axis=2, tiled=True),
        lax.all_gather(expert_out, "seq", axis=1, tiled=True),
    )

    def expert_back(block_index, loop_carry):
        grad_in_sum, grad_out_sum, grad_rows = loop_carry
        row_piece = lax.dynamic_slice_in_dim(received, block_index * block_rows, block_rows, 1)
        grad_piece = lax.dynamic_slice_in_dim(
            grad_received, block_index * block_rows, block_rows, 1
        )
        hidden_pre = jnp.einsum(
            "erd,edf->erf", row_piece, back_in, preferred_element_type=jnp.float32
        )
        activated, gelu_back = jax.vjp(jax.nn.gelu, hidden_pre)
        grad_act = jnp.einsum(
            "erd,efd->erf", grad_piece, back_out, preferred_element_type=jnp.float32
        )
        grad_pre = gelu_back(grad_act)[0].astype(jnp.bfloat16)
        grad_out_sum = grad_out_sum + jnp.einsum(
            "erf,erd->efd",
            activated.astype(jnp.bfloat16),
            grad_piece,
            preferred_element_type=jnp.float32,
        )
        grad_in_sum = grad_in_sum + jnp.einsum(
            "erd,erf->edf", row_piece, grad_pre, preferred_element_type=jnp.float32
        )
        rows_back = jnp.einsum(
            "erf,edf->erd", grad_pre, back_in, preferred_element_type=jnp.float32
        ).astype(jnp.bfloat16)
        grad_rows = lax.dynamic_update_slice_in_dim(
            grad_rows, rows_back, block_index * block_rows, 1
        )
        return (grad_in_sum, grad_out_sum, grad_rows)

    start_carry = (
        jnp.zeros(back_in.shape, jnp.float32),
        jnp.zeros(back_out.shape, jnp.float32),
        jnp.zeros((local_experts, total_rows, model_width), jnp.bfloat16),
    )
    grad_in_sum, grad_out_sum, grad_rows = lax.fori_loop(0, block_count, expert_back, start_carry)
    grad_returned = send_tokens(grad_rows).reshape(
        expert_count, image_count, slot_limit, model_width
    )
    grad_normed_two = jnp.einsum(
        "bskem,ebmd->bsd", dispatch, grad_returned, preferred_element_type=jnp.float32
    ).reshape(row_count, model_width)
    grad_logits = gate_back(grad_gates)[0].astype(jnp.bfloat16)
    grad_router = jnp.einsum(
        "rd,re->de", normed_two_b, grad_logits, preferred_element_type=jnp.float32
    )
    grad_normed_two = grad_normed_two + jnp.einsum(
        "re,de->rd", grad_logits, router_weight, preferred_element_type=jnp.float32
    )
    grad_res_two, grad_gain_two, grad_bias_two = norm_two_back(grad_normed_two)
    grad_residual = grad_mixed + grad_res_two
    grad_branch = grad_residual.astype(jnp.bfloat16)
    grad_out_weight = jnp.einsum(
        "rd,re->de", attended_rows, grad_branch, preferred_element_type=jnp.float32
    )
    grad_attended = jnp.einsum(
        "re,de->rd", grad_branch, out_weight, preferred_element_type=jnp.float32
    ).astype(jnp.bfloat16)
    grad_heads = regroup_heads(grad_attended.reshape(image_count, slot_count, 1, H, head_size))[
        :, :, 0
    ]
    grad_qkv_heads = attention_backward(
        queries, keys_in, values, log_total, grad_heads, key_valid
    ).astype(jnp.bfloat16)
    grad_qkv_rows = regroup_slots(grad_qkv_heads).reshape(row_count, 3 * model_width)
    grad_qkv_weight = jnp.einsum(
        "rd,rf->df", normed_one_b, grad_qkv_rows, preferred_element_type=jnp.float32
    )
    grad_normed_one = jnp.einsum(
        "rf,df->rd", grad_qkv_rows, qkv_weight, preferred_element_type=jnp.float32
    )
    grad_token_ln, grad_gain_one, grad_bias_one = norm_one_back(grad_normed_one)
    grad_tokens = grad_residual + grad_token_ln
    dense_grads = (
        grad_gain_one,
        grad_bias_one,
        grad_qkv_weight,
        grad_out_weight,
        grad_gain_two,
        grad_bias_two,
        grad_router,
    )
    dense_grads = (
        lax.psum(dense_grads[0].astype(jnp.bfloat16), "seq").astype(jnp.float32),
        lax.psum(dense_grads[1].astype(jnp.bfloat16), "seq").astype(jnp.float32),
        lax.psum(dense_grads[2].astype(jnp.bfloat16), "seq").astype(jnp.float32),
        lax.psum(dense_grads[3].astype(jnp.bfloat16), "seq").astype(jnp.float32),
        lax.psum(dense_grads[4].astype(jnp.bfloat16), "seq").astype(jnp.float32),
        lax.psum(dense_grads[5].astype(jnp.bfloat16), "seq").astype(jnp.float32),
        lax.psum(dense_grads[6].astype(jnp.bfloat16), "seq").astype(jnp.float32),
    )
    dense_grads = (
        lax.psum_scatter(
            dense_grads[0].astype(jnp.bfloat16), "dp", scatter_dimension=0, tiled=True
        ).astype(jnp.float32),
        lax.psum_scatter(
            dense_grads[1].astype(jnp.bfloat16), "dp", scatter_dimension=0, tiled=True
        ).astype(jnp.float32),
        lax.psum_scatter(
            dense_grads[2].astype(jnp.bfloat16), "dp", scatter_dimension=0, tiled=True
        ).astype(jnp.float32),
        lax.psum_scatter(
            dense_grads[3].astype(jnp.bfloat16), "dp", scatter_dimension=0, tiled=True
        ).astype(jnp.float32),
        lax.psum_scatter(
            dense_grads[4].astype(jnp.bfloat16), "dp", scatter_dimension=0, tiled=True
        ).astype(jnp.float32),
        lax.psum_scatter(
            dense_grads[5].astype(jnp.bfloat16), "dp", scatter_dimension=0, tiled=True
        ).astype(jnp.float32),
        lax.psum_scatter(
            dense_grads[6].astype(jnp.bfloat16), "dp", scatter_dimension=0, tiled=True
        ).astype(jnp.float32),
    )
    expert_in_grad, expert_out_grad = (
        lax.psum_scatter(
            grad_in_sum.astype(jnp.bfloat16), "seq", scatter_dimension=2, tiled=True
        ).astype(jnp.float32),
        lax.psum_scatter(
            grad_out_sum.astype(jnp.bfloat16), "seq", scatter_dimension=1, tiled=True
        ).astype(jnp.float32),
    )
    mixed = mixed_rows.astype(jnp.bfloat16).reshape(image_count, slot_count, model_width)
    return (
        mixed,
        grad_tokens.reshape(image_count, slot_count, model_width),
        dense_grads[0],
        dense_grads[1],
        dense_grads[2],
        dense_grads[3],
        dense_grads[4],
        dense_grads[5],
        dense_grads[6],
        expert_in_grad,
        expert_out_grad,
    )


BF = jnp.bfloat16
F32 = jnp.float32
MESH_ID = pl.DeviceIdType.MESH
NEG = -1e30
BP = 64
VMEM_LIMIT = 67000000
GELU_C = 0.7978845608028654
GELU_K = 0.044715


def nn(a, b):
    return lax.dot_general(a, b, (((1,), (0,)), ((), ())), preferred_element_type=F32)


def nt(a, b):
    return lax.dot_general(a, b, (((1,), (1,)), ((), ())), preferred_element_type=F32)


def tn(a, b):
    return lax.dot_general(a, b, (((0,), (0,)), ((), ())), preferred_element_type=F32)


def remote(src, dst, send_sem, recv_sem, dp, z):
    return pltpu.make_async_remote_copy(
        src_ref=src,
        dst_ref=dst,
        send_sem=send_sem,
        recv_sem=recv_sem,
        device_id=(dp, z),
        device_id_type=MESH_ID,
    )


def rows_of(index, size):
    return pl.ds(pl.multiple_of(index * size, size), size)


def norm_parts(x):
    centre = x - jnp.mean(x, axis=-1, keepdims=True)
    scale = lax.rsqrt(jnp.mean(centre * centre, axis=-1, keepdims=True) + 1e-06)
    return centre * scale, scale


def norm_back(grad_hat, hat, scale):
    return scale * (
        grad_hat
        - jnp.mean(grad_hat, axis=-1, keepdims=True)
        - hat * jnp.mean(grad_hat * hat, axis=-1, keepdims=True)
    )


def half_masks():
    lane = lax.broadcasted_iota(jnp.int32, (1, 128), 1)
    low = jnp.where(lane < 64, 1.0, 0.0).astype(BF)
    high = jnp.where(lane < 64, 0.0, 1.0).astype(BF)
    return (low, high)


def slot_ok(position, block):
    return (position % BP < block) & ((position // BP) * block + position % BP < VALID)


def block_kernel(
    dims,
    tok, tgt, rts, wq, wo, vec, win, wout,
    mixed, gtok, gqkv, gwo, gsmall, gin, gout,
    xin, rin, tin, vec_all, wq_all, wo_all, vsum, xpad, x2s, n2s, qkvs, outs, lses, gts, meta, metat,
    win_all, wout_all, recv, ret, acts, slopes, sbuf,
    mbuf, drows, dys, dlogs, dus, dret, dws, arrived,
    gacc, gvec, gbig, crecv, cvec, gsum, hrecv, hvec, zsend, zrecv, zall, zvec,
    loc_sem, tok_ss, tok_rs, rts_ss, rts_rs, tgt_ss, tgt_rs, den_ss, den_rs, fwd_ss, win_ss, win_rs, wout_ss, wout_rs,
    row_ss, row_rs, u_ss, u_rs, du_ss, du_rs, dn_ss, dn_rs, mix_ss, mix_rs, gt_ss, gt_rs,
    r_ss, r_rs, l_ss, l_rs, c_ss, c_rs, cv_ss, cv_rs, h_ss, h_rs, hv_ss, hv_rs, za_ss, za_rs, zb_ss, zb_rs, zv_ss, zv_rs,
):
    n_dp, n_z, im, block, cap, er = dims
    me, z = lax.axis_index("dp"), lax.axis_index("seq")
    sp = n_z * BP
    nr = n_dp * er
    two = 2 * er
    half = n_dp // 2
    last = n_z - 1
    core, chip = lax.rem(me, 2), me // 2
    partner = chip * 2 + 1 - core

    barrier = pltpu.get_barrier_semaphore()
    for k in range(1, n_dp):
        pl.semaphore_signal(barrier, inc=1, device_id=(lax.rem(me + k, n_dp), z), device_id_type=MESH_ID)
    for k in range(1, n_z):
        pl.semaphore_signal(barrier, inc=1, device_id=(me, lax.rem(z + k, n_z)), device_id_type=MESH_ID)
    own_copies = [
        pltpu.make_async_copy(tok.at[pl.ds(z * im, im)], xin.at[z], loc_sem.at[0]),
        pltpu.make_async_copy(rts.at[pl.ds(z * im, im)], rin.at[z], loc_sem.at[1]),
        pltpu.make_async_copy(tgt.at[pl.ds(z * im, im)], tin.at[z], loc_sem.at[2]),
        pltpu.make_async_copy(win, win_all.at[z], loc_sem.at[3]),
        pltpu.make_async_copy(wout, wout_all.at[z], loc_sem.at[4]),
        pltpu.make_async_copy(wq, wq_all.at[rows_of(me, 64)], loc_sem.at[5]),
        pltpu.make_async_copy(wo, wo_all.at[rows_of(me, 64)], loc_sem.at[6]),
        pltpu.make_async_copy(vec, vec_all.at[me], loc_sem.at[7]),
    ]
    for copy in own_copies:
        copy.start()
    xpad[...] = jnp.zeros_like(xpad)
    gacc[...] = jnp.zeros_like(gacc)
    gvec[...] = jnp.zeros_like(gvec)
    pl.semaphore_wait(barrier, n_dp + n_z - 2)

    def z_start(source, target, send_sem, recv_sem):
        for k in range(1, n_z):
            peer = lax.rem(z + k, n_z)
            remote(source(peer), target(z), send_sem.at[k], recv_sem.at[z], me, peer).start()

    def z_arrive(target, recv_sem):
        for k in range(1, n_z):
            origin = lax.rem(z + k, n_z)
            remote(target(origin), target(origin), loc_sem.at[8], recv_sem.at[origin], me, z).wait_recv()

    def z_sent(source, send_sem):
        for k in range(1, n_z):
            remote(source(0), source(0), send_sem.at[k], loc_sem.at[8], me, z).wait_send()

    tok_of = lambda peer: tok.at[pl.ds(peer * im, im)]
    rts_of = lambda peer: rts.at[pl.ds(peer * im, im)]
    tgt_of = lambda peer: tgt.at[pl.ds(peer * im, im)]
    z_start(tok_of, lambda i: xin.at[i], tok_ss, tok_rs)
    z_start(rts_of, lambda i: rin.at[i], rts_ss, rts_rs)

    def dense_slot(array, index):
        if array == 0:
            return wq_all.at[rows_of(index, 64)]
        if array == 1:
            return wo_all.at[rows_of(index, 64)]
        return vec_all.at[index]

    dense_in = (wq, wo, vec)
    for array in range(3):
        for k in range(1, half):
            peer = lax.rem(chip + k, half) * 2 + core
            remote(
                dense_in[array], dense_slot(array, me), den_ss.at[array, k], den_rs.at[array, me], peer, z
            ).start()
        remote(
            dense_in[array], dense_slot(array, me), den_ss.at[array, 0], den_rs.at[array, me], partner, z
        ).start()

    experts = ((win, win_all, win_ss, win_rs), (wout, wout_all, wout_ss, wout_rs))

    def gather_hop(array, step):
        source, full, send_sem, recv_sem = experts[array]
        for way, there, slot in ((0, z >= step, z - step), (1, z + step < n_z, z + step)):

            @pl.when(there)
            def _():
                at = full.at[slot]
                if step > 0:
                    remote(at, at, send_sem.at[way, step], recv_sem.at[slot], me, z).wait_recv()

                @pl.when((z < last) if way == 0 else (z > 0))
                def _():
                    remote(
                        at if step > 0 else source,
                        at,
                        send_sem.at[way, step],
                        recv_sem.at[slot],
                        me,
                        z + 1 if way == 0 else z - 1,
                    ).start()

    def gather_sent(array):
        source, full, send_sem, recv_sem = experts[array]
        for step in range(n_z):
            for way, there in ((0, (z >= step) & (z < last)), (1, (z + step < n_z) & (z > 0))):

                @pl.when(there)
                def _():
                    remote(
                        full.at[0], full.at[0], send_sem.at[way, step], recv_sem.at[0], me, z
                    ).wait_send()

    gather_hop(0, 0)
    gather_hop(1, 0)

    for k in range(1, half):
        origin = lax.rem(chip + k, half) * 2 + core
        for array in range(3):
            slot = dense_slot(array, origin)
            remote(slot, slot, den_ss.at[array, 0], den_rs.at[array, origin], me, z).wait_recv()
            remote(slot, slot, fwd_ss.at[array, k], den_rs.at[array, origin], partner, z).start()
    for k in range(half):
        origin = lax.rem(chip + k, half) * 2 + 1 - core
        for array in range(3):
            slot = dense_slot(array, origin)
            remote(slot, slot, den_ss.at[array, 0], den_rs.at[array, origin], me, z).wait_recv()
    for copy in own_copies:
        copy.wait()
    total = vec_all[0].astype(F32)
    for k in range(1, n_dp):
        total = total + vec_all[k].astype(F32)
    vsum[...] = total
    z_arrive(lambda i: xin.at[i], tok_rs)
    z_arrive(lambda i: rin.at[i], rts_rs)

    masks = half_masks()
    keys_ok = slot_ok(lax.broadcasted_iota(jnp.int32, (1, sp), 1), block)
    rows_ok = slot_ok(lax.broadcasted_iota(jnp.int32, (sp, 1), 0), block)
    gain_one, bias_one = vsum[0:1, :], vsum[1:2, :]
    gain_two, bias_two = vsum[2:3, :], vsum[3:4, :]
    router_t = vsum[8:16, :].astype(BF)
    lane_id = lax.broadcasted_iota(jnp.int32, (sp, 128), 1)
    lane_low = lane_id < 64

    def front(i, carry):
        before = lax.broadcasted_iota(jnp.int32, (sp, sp), 0)
        after = lax.broadcasted_iota(jnp.int32, (sp, sp), 1)
        prefix = jnp.where((before < after) & (before // BP == after // BP), 1.0, 0.0).astype(BF)
        expert_id = lax.broadcasted_iota(jnp.int32, (8, sp), 0)
        slot_lane = lax.broadcasted_iota(jnp.int32, (8, sp), 1)
        for b in range(n_z):
            xpad[i, b * BP : b * BP + block, :] = xin[b, i]
        x = xpad[i].astype(F32)
        hat, _ = norm_parts(x)
        normed = (hat * gain_one + bias_one).astype(BF)
        qkvs[i] = nn(normed, wq_all[...]).astype(BF)
        lse_all = jnp.zeros((sp, 128), F32)
        for pair in range(4):
            q2 = qkvs[i, :, pair * 128 : pair * 128 + 128]
            k2 = qkvs[i, :, 512 + pair * 128 : 512 + pair * 128 + 128]
            v2 = qkvs[i, :, 1024 + pair * 128 : 1024 + pair * 128 + 128]
            parts = []
            for side in range(2):
                scores = nt(q2 * masks[side], k2) * 0.125
                scores = jnp.where(keys_ok, scores, NEG)
                top = jnp.max(scores, axis=-1, keepdims=True)
                exponent = jnp.exp(scores - top)
                whole = jnp.sum(exponent, axis=-1, keepdims=True)
                lse_all = jnp.where(lane_id == pair * 2 + side, top + jnp.log(whole), lse_all)
                parts.append(nn((exponent / whole).astype(BF), v2))
            outs[i, :, pair * 128 : pair * 128 + 128] = jnp.where(lane_low, parts[0], parts[1]).astype(BF)
        lses[i] = lse_all
        x2 = x + nn(outs[i], wo_all[...])
        x2s[i] = x2
        hat2, _ = norm_parts(x2)
        n2 = (hat2 * gain_two + bias_two).astype(BF)
        n2s[i] = n2
        logits = nt(router_t, n2)
        raised = jnp.exp(logits - jnp.max(logits, axis=0, keepdims=True))
        share = raised / jnp.sum(raised, axis=0, keepdims=True)
        gts[i] = share
        wide = jnp.concatenate([rin[0, i] + rin[1, i], rin[2, i] + rin[3, i]], axis=1)
        hits = [(expert_id + 1) == wide[j : j + 1, :] for j in range(2)]
        any_hit = jnp.where(hits[0] | hits[1], 1.0, 0.0)
        place = nn(any_hit.astype(BF), prefix)
        base = place + (expert_id * er + (slot_lane // BP) * cap + i * (n_z * cap) + 1).astype(F32)
        lines = [jnp.sum(jnp.where(hit, base, 0.0), axis=0, keepdims=True) - 1.0 for hit in hits]
        lines += [jnp.sum(jnp.where(hit, share, 0.0), axis=0, keepdims=True) for hit in hits]
        table = jnp.concatenate(lines + [jnp.zeros((124, sp), F32)], axis=0)
        meta[i] = table[0:8]
        metat[i] = jnp.transpose(table)
        return carry

    lax.fori_loop(0, im, front, 0)

    row_id = lax.broadcasted_iota(jnp.int32, (er, sp), 0)

    def to_experts(product, target, send_sem, recv_sem):
        for j in (1, 2, 3, 0):
            for c in range(2):
                if j > 0:
                    peer = lax.rem(chip + j, half) * 2 + c
                else:
                    peer = me if c == 0 else partner
                out = product(peer).astype(BF)
                if j == 0 and c == 0:
                    target[rows_of(me, er)] = out
                else:
                    sbuf[2 * j + c] = out
                    remote(
                        sbuf.at[2 * j + c],
                        target.at[rows_of(me, er)],
                        send_sem.at[2 * j + c],
                        recv_sem.at[me],
                        peer,
                        z,
                    ).start()

    def to_tokens(product, target, send_sem, recv_sem):
        for j in (1, 2, 3, 0):
            part = lax.rem(chip + j, half)
            out = product(part).astype(BF)
            sbuf[2 * j] = out[0:er]
            sbuf[2 * j + 1] = out[er:two]
            if j > 0:
                for c in range(2):
                    remote(
                        sbuf.at[2 * j + c],
                        target.at[rows_of(me, er)],
                        send_sem.at[2 * j + c],
                        recv_sem.at[me],
                        part * 2 + c,
                        z,
                    ).start()
            else:
                target[rows_of(me, er)] = sbuf[core]
                remote(
                    sbuf.at[1 - core], target.at[rows_of(me, er)], send_sem.at[1], recv_sem.at[me], partner, z
                ).start()

    def dp_arrive(target, recv_sem):
        for k in range(1, n_dp):
            origin = lax.rem(me + k, n_dp)
            spot = target.at[rows_of(origin, er)]
            remote(spot, spot, loc_sem.at[8], recv_sem.at[origin], me, z).wait_recv()

    def dp_sent(send_sem):
        for k in range(1, n_dp):
            remote(sbuf.at[0], sbuf.at[0], send_sem.at[k], loc_sem.at[8], me, z).wait_send()

    def tokens_for(peer):
        want = (row_id + peer * er).astype(F32)
        total = jnp.zeros((er, 512), F32)
        for i in range(im):
            pick = (want == meta[i, 0:1, :]) | (want == meta[i, 1:2, :])
            total = total + nn(jnp.where(pick, 1.0, 0.0).astype(BF), n2s[i])
        return total

    to_experts(tokens_for, recv, row_ss, row_rs)

    def hidden(shard):
        def part_step(part, carry):
            at = rows_of(part, two)
            x = recv[at]
            for side in range(2):
                pre = nn(x, win_all[shard, :, side * 256 : side * 256 + 256])
                square = pre * pre
                tanh = jnp.tanh(pre * (GELU_C + (GELU_C * GELU_K) * square))
                gate = 0.5 + 0.5 * tanh
                acts[shard, at, side * 256 : side * 256 + 256] = (pre * gate).astype(BF)
                slope = gate + pre * (0.5 - 0.5 * tanh * tanh) * (GELU_C + (3.0 * GELU_C * GELU_K) * square)
                slopes[shard, at, side * 256 : side * 256 + 256] = slope.astype(BF)
            return carry

        lax.fori_loop(0, n_dp // 2, part_step, 0)

    def hidden_at(step):
        @pl.when(z >= step)
        def _():
            hidden(z - step)

        @pl.when(z + step < n_z)
        def _():
            hidden(z + step)

    gather_hop(0, 1)
    gather_hop(1, 1)
    dp_arrive(recv, row_rs)
    dp_sent(row_ss)
    hidden(z)
    gather_hop(0, 2)
    hidden_at(1)
    gather_hop(1, 2)
    z_start(tgt_of, lambda i: tin.at[i], tgt_ss, tgt_rs)
    hidden_at(2)
    gather_hop(0, 3)
    hidden_at(3)
    gather_hop(1, 3)

    def results_for(part):
        total = jnp.zeros((two, 512), F32)
        for shard in range(n_z):
            total = total + nn(acts[shard, rows_of(part, two)], wout_all[shard])
        return total

    to_tokens(results_for, ret, u_ss, u_rs)

    z_arrive(lambda i: tin.at[i], tgt_rs)
    for b in range(n_z):
        for i in range(im):
            dys[i, b * BP : b * BP + block, :] = tin[b, i].astype(F32)
    dp_arrive(ret, u_rs)

    def mix(i, carry):
        line = lax.broadcasted_iota(jnp.int32, (sp, nr), 1).astype(F32)
        cols = metat[i]
        picked = []
        for j in range(2):
            pick = jnp.where(line == cols[:, j : j + 1], 1.0, 0.0).astype(BF)
            picked.append(nn(pick, ret[...]))
        mix = x2s[i] + cols[:, 2:3] * picked[0] + cols[:, 3:4] * picked[1]
        mix_b = mix.astype(BF)
        for b in range(n_z):
            mbuf[b, i] = mix_b[b * BP : b * BP + block]
        dy = jnp.where(rows_ok, mix - dys[i], 0.0)
        dys[i] = dy
        dus[0, i] = (cols[:, 2:3] * dy).astype(BF)
        dus[1, i] = (cols[:, 3:4] * dy).astype(BF)
        dlogs[i] = jnp.where(
            lane_id == 0, jnp.sum(dy * picked[0], axis=-1, keepdims=True), 0.0
        ) + jnp.where(lane_id == 1, jnp.sum(dy * picked[1], axis=-1, keepdims=True), 0.0)
        return carry

    lax.fori_loop(0, im, mix, 0)
    dp_sent(u_ss)

    def gradients_for(peer):
        want = (row_id + peer * er).astype(F32)
        total = jnp.zeros((er, 512), F32)
        for i in range(im):
            for j in range(2):
                pick = jnp.where(want == meta[i, j : j + 1, :], 1.0, 0.0).astype(BF)
                total = total + nn(pick, dus[j, i])
        return total

    to_experts(gradients_for, drows, du_ss, du_rs)
    z_start(lambda peer: mbuf.at[peer], lambda i: mixed.at[pl.ds(i * im, im)], mix_ss, mix_rs)
    own_mixed = pltpu.make_async_copy(mbuf.at[z], mixed.at[pl.ds(z * im, im)], loc_sem.at[0])
    own_mixed.start()
    expert_row = lax.broadcasted_iota(jnp.int32, (8, sp), 0).astype(F32)
    for i in range(im):
        flat = jnp.transpose(dlogs[i])
        share = gts[i]
        grad = jnp.zeros((8, sp), F32)
        for j in range(2):
            at = meta[i, j : j + 1, :]
            inside = (at >= expert_row * er) & (at < expert_row * er + er)
            grad = grad + jnp.where(inside, flat[j : j + 1, :], 0.0)
        dlog = share * (grad - jnp.sum(share * grad, axis=0, keepdims=True))
        gts[i] = dlog
        gvec[8:16, :] += nn(dlog.astype(BF), n2s[i])
    dp_arrive(drows, du_rs)
    dp_sent(du_ss)

    def pass_on(right, target, piece, edge):
        send_sem, recv_sem = (r_ss, r_rs) if right else (l_ss, l_rs)
        concerned = (z < target) if right else (z > target)
        at_edge = (z == 0) if right else (z == last)
        slot = target
        if not right:
            slot = jnp.where(z - 1 == target, n_z, target)

        def send():
            remote(
                dws.at[target, piece],
                arrived.at[slot, piece],
                send_sem.at[target, piece],
                recv_sem.at[target, piece],
                me,
                z + 1 if right else z - 1,
            ).start()

        if edge:

            @pl.when(concerned & at_edge)
            def _():
                send()

        else:

            @pl.when(concerned & jnp.logical_not(at_edge))
            def _():
                here = arrived.at[target, piece]
                remote(here, here, send_sem.at[target, piece], recv_sem.at[target, piece], me, z).wait_recv()

                def add(c, carry):
                    at = rows_of(c, 128)
                    dws[target, piece, at] = (
                        dws[target, piece, at].astype(F32) + arrived[target, piece, at].astype(F32)
                    ).astype(BF)
                    return carry

                lax.fori_loop(0, 4, add, 0)
                send()

    order = (3, 0, 2, 1)
    for target in order:
        dws[target, 0] = tn(acts[target], drows[...]).astype(BF)
        pass_on(True, target, 0, True)
        pass_on(False, target, 0, True)

    def input_grads_for(part):
        at = rows_of(part, two)
        du = drows[at]
        total = jnp.zeros((two, 512), F32)
        for shard in range(n_z):
            dpre = (nt(du, wout_all[shard]) * slopes[shard, at].astype(F32)).astype(BF)
            slopes[shard, at] = dpre
            total = total + nt(dpre, win_all[shard])
        return total

    to_tokens(input_grads_for, dret, dn_ss, dn_rs)
    for target in order:
        dws[target, 1] = tn(recv[...], slopes[target]).astype(BF)
        pass_on(True, target, 1, True)
        pass_on(False, target, 1, True)

    def forward_first(piece):
        @pl.when(z == 1)
        def _():
            pass_on(True, last, piece, False)

        @pl.when(z == last - 1)
        def _():
            pass_on(False, 0, piece, False)

    def forward_second(piece):
        @pl.when(z == 1)
        def _():
            pass_on(True, last - 1, piece, False)
            pass_on(False, 0, piece, False)

        @pl.when(z == last - 1)
        def _():
            pass_on(False, 1, piece, False)
            pass_on(True, last, piece, False)

    forward_first(0)
    own_mixed.wait()
    z_sent(lambda peer: mbuf.at[peer], mix_ss)
    dp_arrive(dret, dn_rs)

    def back(i, carry):
        line = lax.broadcasted_iota(jnp.int32, (sp, nr), 1).astype(F32)
        cols = metat[i]
        pick = jnp.where((line == cols[:, 0:1]) | (line == cols[:, 1:2]), 1.0, 0.0).astype(BF)
        dn2 = nn(pick, dret[...]) + tn(gts[i].astype(BF), router_t)
        hat2, scale2 = norm_parts(x2s[i])
        gvec[2:3, :] += jnp.sum(dn2 * hat2, axis=0, keepdims=True)
        gvec[3:4, :] += jnp.sum(dn2, axis=0, keepdims=True)
        dx2 = dys[i] + norm_back(dn2 * gain_two, hat2, scale2)
        da = dx2.astype(BF)
        gacc[:, 1536:2048] += tn(outs[i], da)
        do = nt(da, wo_all[...]).astype(BF)
        hat1, scale1 = norm_parts(xpad[i].astype(F32))
        n1 = (hat1 * gain_one + bias_one).astype(BF)
        dn1 = jnp.zeros((sp, 512), F32)
        for pair in range(4):
            at = pair * 128
            q2 = qkvs[i, :, at : at + 128]
            k2 = qkvs[i, :, 512 + at : 512 + at + 128]
            v2 = qkvs[i, :, 1024 + at : 1024 + at + 128]
            do2 = do[:, at : at + 128]
            grads = ([], [], [])
            for side in range(2):
                head = pair * 2 + side
                scores = nt(q2 * masks[side], k2) * 0.125
                scores = jnp.where(keys_ok, scores, NEG)
                prob = jnp.exp(scores - lses[i, :, head : head + 1])
                dprob = nt(do2 * masks[side], v2)
                inner = jnp.sum(prob * dprob, axis=-1, keepdims=True)
                ds = (prob * (dprob - inner)).astype(BF)
                grads[0].append(nn(ds, k2))
                grads[1].append(tn(ds, q2))
                grads[2].append(tn(prob.astype(BF), do2))
            for part in range(3):
                grad = jnp.where(lane_low, grads[part][0], grads[part][1])
                if part < 2:
                    grad = grad * 0.125
                grad = grad.astype(BF)
                col = part * 512 + at
                gacc[:, col : col + 128] += tn(n1, grad)
                dn1 = dn1 + nt(grad, wq_all[:, col : col + 128])
        gvec[0:1, :] += jnp.sum(dn1 * hat1, axis=0, keepdims=True)
        gvec[1:2, :] += jnp.sum(dn1, axis=0, keepdims=True)
        dx = (dx2 + norm_back(dn1 * gain_one, hat1, scale1)).astype(BF)
        for b in range(n_z):
            mbuf[b, i] = dx[b * BP : b * BP + block]
        return carry

    back(0, 0)
    forward_second(0)
    lax.fori_loop(1, im, back, 0)
    z_start(lambda peer: mbuf.at[peer], lambda i: gtok.at[pl.ds(i * im, im)], gt_ss, gt_rs)
    own_gtok = pltpu.make_async_copy(mbuf.at[z], gtok.at[pl.ds(z * im, im)], loc_sem.at[1])
    own_gtok.start()

    gbig[...] = gacc[...].astype(BF)
    for q in range(half):
        remote(
            gbig.at[rows_of(2 * q + 1 - core, 64)], crecv.at[q], c_ss.at[q], c_rs.at[q], partner, z
        ).start()
    remote(gvec, cvec, cv_ss.at[0], cv_rs.at[0], partner, z).start()
    forward_first(1)
    for q in range(half):
        remote(crecv.at[q], crecv.at[q], c_ss.at[q], c_rs.at[q], me, z).wait_recv()
    for k in range(1, half):
        q = lax.rem(chip + k, half)
        gsum[q] = (gacc[rows_of(2 * q + core, 64)] + crecv[q].astype(F32)).astype(BF)
        remote(gsum.at[q], hrecv.at[chip], h_ss.at[k], h_rs.at[chip], q * 2 + core, z).start()
    remote(cvec, cvec, cv_ss.at[0], cv_rs.at[0], me, z).wait_recv()
    hvec[chip] = gvec[...] + cvec[...]
    for k in range(1, half):
        q = lax.rem(chip + k, half)
        remote(hvec.at[chip], hvec.at[chip], hv_ss.at[k], hv_rs.at[chip], q * 2 + core, z).start()
    forward_second(1)
    dense = gacc[rows_of(me, 64)] + crecv[chip].astype(F32)
    for k in range(1, half):
        q = lax.rem(chip + k, half)
        remote(hrecv.at[q], hrecv.at[q], h_ss.at[0], h_rs.at[q], me, z).wait_recv()
        dense = dense + hrecv[q].astype(F32)
    for peer in range(n_z):
        zsend[peer] = dense[peer * 16 : peer * 16 + 16].astype(BF)
    z_start(lambda peer: zsend.at[peer], lambda i: zrecv.at[i], za_ss, za_rs)
    for k in range(1, half):
        q = lax.rem(chip + k, half)
        remote(hvec.at[q], hvec.at[q], hv_ss.at[0], hv_rs.at[q], me, z).wait_recv()
    zvec[z] = hvec[0] + hvec[1] + hvec[2] + hvec[3]
    z_start(lambda peer: zvec.at[z], lambda i: zvec.at[i], zv_ss, zv_rs)
    zrecv[z] = zsend[z]
    z_arrive(lambda i: zrecv.at[i], za_rs)
    total = zrecv[0].astype(F32)
    for k in range(1, n_z):
        total = total + zrecv[k].astype(F32)
    zall[z] = total.astype(BF)
    z_start(lambda peer: zall.at[z], lambda i: zall.at[i], zb_ss, zb_rs)

    for piece, out in ((0, gout), (1, gin)):

        @pl.when(z > 0)
        def _():
            here = arrived.at[z, piece]
            remote(here, here, r_ss.at[0, piece], r_rs.at[z, piece], me, z).wait_recv()

        @pl.when(z < last)
        def _():
            here = arrived.at[n_z, piece]
            remote(here, here, l_ss.at[0, piece], l_rs.at[z, piece], me, z).wait_recv()

        def finish(c, carry):
            at = rows_of(c, 128)
            left = jnp.where(z > 0, arrived[z, piece, at].astype(F32), 0.0)
            right = jnp.where(z < last, arrived[n_z, piece, at].astype(F32), 0.0)
            out[at] = dws[z, piece, at].astype(F32) + left + right
            return carry

        lax.fori_loop(0, 4, finish, 0)
    z_arrive(lambda i: zvec.at[i], zv_rs)
    gsmall[...] = zvec[0] + zvec[1] + zvec[2] + zvec[3]
    z_arrive(lambda i: zall.at[i], zb_rs)
    for k in range(n_z):
        piece = zall[k].astype(F32)
        gqkv[k * 16 : k * 16 + 16] = piece[:, 0:1536]
        gwo[k * 16 : k * 16 + 16] = piece[:, 1536:2048]
    own_gtok.wait()
    z_arrive(lambda i: gtok.at[pl.ds(i * im, im)], gt_rs)
    z_arrive(lambda i: mixed.at[pl.ds(i * im, im)], mix_rs)

    z_sent(lambda peer: xin.at[peer], tok_ss)
    z_sent(lambda peer: rin.at[peer], rts_ss)
    z_sent(lambda peer: tin.at[peer], tgt_ss)
    z_sent(lambda peer: mbuf.at[peer], gt_ss)
    z_sent(lambda peer: zsend.at[peer], za_ss)
    z_sent(lambda peer: zvec.at[peer], zv_ss)
    z_sent(lambda peer: zall.at[peer], zb_ss)
    dp_sent(dn_ss)
    gather_sent(0)
    gather_sent(1)
    for array in range(3):
        slot = dense_slot(array, 0)
        for k in range(half):
            remote(slot, slot, den_ss.at[array, k], loc_sem.at[8], me, z).wait_send()
        for k in range(1, half):
            remote(slot, slot, fwd_ss.at[array, k], loc_sem.at[8], me, z).wait_send()
    for piece in range(2):
        for target in range(n_z):
            here = dws.at[0, 0]

            @pl.when(z < target)
            def _():
                remote(here, here, r_ss.at[target, piece], loc_sem.at[8], me, z).wait_send()

            @pl.when(z > target)
            def _():
                remote(here, here, l_ss.at[target, piece], loc_sem.at[8], me, z).wait_send()

    for q in range(half):
        remote(crecv.at[q], crecv.at[q], c_ss.at[q], loc_sem.at[8], me, z).wait_send()
    remote(cvec, cvec, cv_ss.at[0], loc_sem.at[8], me, z).wait_send()
    for k in range(1, half):
        remote(gsum.at[0], gsum.at[0], h_ss.at[k], loc_sem.at[8], me, z).wait_send()
        remote(cvec, cvec, hv_ss.at[k], loc_sem.at[8], me, z).wait_send()


def whole_images(
    tokens, ln1_gain, ln1_bias, w_qkv, w_out, ln2_gain, ln2_bias, w_router, expert_in, expert_out, routes, targets
):
    n_dp, n_z = lax.axis_size("dp"), lax.axis_size("seq")
    image_count, block, width = tokens.shape
    im = image_count // n_z
    cap = 2 * S // (n_z * w_router.shape[1]) + 2
    er = -(-(im * n_z * cap) // 16) * 16
    dims = (n_dp, n_z, im, block, cap, er)
    sp, nr, half = n_z * BP, n_dp * er, n_dp // 2
    me, z = lax.axis_index("dp"), lax.axis_index("seq")
    dma, vm = pltpu.SemaphoreType.DMA, pltpu.VMEM

    valid = z * block + jnp.arange(block) < VALID
    lines = jnp.where(valid[None, None, :], jnp.transpose(routes, (0, 2, 1)) + 1, 0)
    lines = jnp.pad(lines, ((0, 0), (0, 6), (0, BP - block)))
    odd = lax.rem(z, 2) == 1
    lines = jnp.concatenate([jnp.where(odd, 0, lines), jnp.where(odd, lines, 0)], axis=-1)
    vec = jnp.concatenate(
        [
            jnp.stack([ln1_gain, ln1_bias, ln2_gain, ln2_bias]),
            jnp.zeros((4, ln1_gain.shape[0]), BF),
            jnp.transpose(w_router),
        ],
        axis=0,
    )
    vec = lax.dynamic_update_slice(jnp.zeros((16, width), BF), vec, (0, me * ln1_gain.shape[0]))
    blocks = (n_z, im, block, width)
    in_any, in_vmem = pl.BlockSpec(memory_space=pl.ANY), pl.BlockSpec(memory_space=pltpu.VMEM)
    mixed, gtok, gqkv, gwo, gsmall, gin, gout = pl.pallas_call(
        functools.partial(block_kernel, dims),
        out_shape=[
            jax.ShapeDtypeStruct((image_count, block, width), BF),
            jax.ShapeDtypeStruct((image_count, block, width), BF),
            jax.ShapeDtypeStruct((64, 1536), F32),
            jax.ShapeDtypeStruct((64, width), F32),
            jax.ShapeDtypeStruct((16, width), F32),
            jax.ShapeDtypeStruct((512, 512), F32),
            jax.ShapeDtypeStruct((512, 512), F32),
        ],
        in_specs=[in_any, in_any, in_vmem, in_any, in_any, in_vmem, in_any, in_any],
        out_specs=[in_any, in_any] + [in_vmem] * 5,
        scratch_shapes=[
            vm(blocks, BF), vm((n_z, im, 8, 128), jnp.int32), vm(blocks, BF), vm((n_dp, 16, width), BF),
            vm((width, 1536), BF), vm((width, width), BF), vm((16, width), F32), vm((im, sp, width), BF),
            vm((im, sp, width), F32), vm((im, sp, width), BF), vm((im, sp, 1536), BF), vm((im, sp, width), BF),
            vm((im, sp, 128), F32), vm((im, 8, sp), F32), vm((im, 8, sp), F32), vm((im, sp, 128), F32),
            vm((n_z, 512, 512), BF), vm((n_z, 512, 512), BF), vm((nr, width), BF), vm((nr, width), BF),
            vm((n_z, nr, 512), BF), vm((n_z, nr, 512), BF), vm((n_dp, er, width), BF),
            vm(blocks, BF), vm((nr, width), BF), vm((im, sp, width), F32), vm((im, sp, 128), F32),
            vm((2, im, sp, width), BF), vm((nr, width), BF), vm((n_z, 2, 512, 512), BF), vm((n_z + 1, 2, 512, 512), BF),
            vm((width, 2048), F32), vm((16, width), F32), vm((width, 2048), BF), vm((half, 64, 2048), BF),
            vm((16, width), F32), vm((half, 64, 2048), BF), vm((half, 64, 2048), BF), vm((half, 16, width), F32),
            vm((n_z, 16, 2048), BF), vm((n_z, 16, 2048), BF), vm((n_z, 16, 2048), BF), vm((n_z, 16, width), F32),
            dma((9,)), dma((n_z,)), dma((n_z,)), dma((n_z,)), dma((n_z,)), dma((n_z,)), dma((n_z,)),
            dma((3, half)), dma((3, n_dp)), dma((3, half)), dma((2, n_z)), dma((n_z,)), dma((2, n_z)), dma((n_z,)),
            dma((n_dp,)), dma((n_dp,)), dma((n_dp,)), dma((n_dp,)), dma((n_dp,)), dma((n_dp,)), dma((n_dp,)), dma((n_dp,)),
            dma((n_z,)), dma((n_z,)), dma((n_z,)), dma((n_z,)),
            dma((n_z, 2)), dma((n_z, 2)), dma((n_z, 2)), dma((n_z, 2)), dma((half,)), dma((half,)), dma((1,)), dma((1,)),
            dma((half,)), dma((half,)), dma((half,)), dma((half,)), dma((n_z,)), dma((n_z,)), dma((n_z,)), dma((n_z,)),
            dma((n_z,)), dma((n_z,)),
        ],
        compiler_params=pltpu.CompilerParams(
            collective_id=1, has_side_effects=True, vmem_limit_bytes=VMEM_LIMIT
        ),
        name="block",
    )(tokens, targets, lines, w_qkv, w_out, vec, expert_in[0], expert_out[0])
    part = lax.dynamic_slice(gsmall, (0, me * ln1_gain.shape[0]), (16, ln1_gain.shape[0]))
    return (
        mixed,
        gtok.astype(F32),
        part[0],
        part[1],
        gqkv,
        gwo,
        part[2],
        part[3],
        jnp.transpose(part[8:16]),
        gin[None],
        gout[None],
    )


def fits(tokens, w_qkv, w_router, expert_in):
    n_dp, n_z = lax.axis_size("dp"), lax.axis_size("seq")
    return (
        n_dp == 8
        and n_z == 4
        and tokens.shape[0] % n_z == 0
        and tokens.shape[1] <= BP
        and tokens.shape[2] == 512
        and w_qkv.shape == (64, 1536)
        and w_router.shape[1] == n_dp
        and expert_in.shape == (1, 512, 512)
    )


def local(*args):
    if fits(args[0], args[3], args[7], args[8]):
        return whole_images(*args)
    return by_heads(*args)


def solution(mesh):
    placed = (
        P("dp", "seq", None),
        P("dp"),
        P("dp"),
        P("dp", None),
        P("dp", None),
        P("dp"),
        P("dp"),
        P("dp", None),
        P("dp", None, "seq"),
        P("dp", "seq", None),
        P("dp", "seq", None),
        P("dp", "seq", None),
    )
    return jax.shard_map(
        local,
        mesh=mesh,
        in_specs=placed,
        out_specs=(
            P("dp", "seq", None),
            P("dp", "seq", None),
            P("dp"),
            P("dp"),
            P("dp", None),
            P("dp", None),
            P("dp"),
            P("dp"),
            P("dp", None),
            P("dp", None, "seq"),
            P("dp", "seq", None),
        ),
        check_vma=False,
    )
```

```python
import functools

import jax
import jax.numpy as jnp
from jax import lax
from jax.experimental import pallas as pl
from jax.experimental.pallas import tpu as pltpu
from jax.sharding import PartitionSpec as P

H = 8
S = 200
VALID = 197


def layer_norm(values, gain_vec, bias_vec):
    centre = values - jnp.mean(values, axis=-1, keepdims=True)
    spread = jnp.mean(centre * centre, axis=-1, keepdims=True)
    return centre * lax.rsqrt(spread + 1e-06) * gain_vec + bias_vec


def regroup_heads(values):
    return lax.all_to_all(values, "seq", split_axis=3, concat_axis=1, tiled=True)


def regroup_slots(values):
    return lax.all_to_all(values, "seq", split_axis=1, concat_axis=3, tiled=True)


def send_experts(values):
    return lax.all_to_all(values, "dp", split_axis=0, concat_axis=1, tiled=True)


def send_tokens(values):
    return lax.all_to_all(values, "dp", split_axis=1, concat_axis=0, tiled=True)


def masked_scores(queries, keys_in, key_valid):
    scores = (
        jnp.einsum("bqhd,bkhd->bhqk", queries, keys_in, preferred_element_type=jnp.float32) * 0.125
    )
    return jnp.where(key_valid, scores, -1e30)


def attention_forward(queries, keys_in, values, key_valid):
    scores = masked_scores(queries, keys_in, key_valid)
    row_top = jnp.max(scores, axis=-1, keepdims=True)
    exponent = jnp.exp(scores - row_top)
    row_total = jnp.sum(exponent, axis=-1, keepdims=True)
    prob_rows = exponent / row_total
    log_total = row_top + jnp.log(row_total)
    attended = jnp.einsum(
        "bhqk,bkhd->bqhd",
        prob_rows.astype(jnp.bfloat16),
        values,
        preferred_element_type=jnp.float32,
    )
    return (attended.astype(jnp.bfloat16), log_total)


def attention_backward(queries, keys_in, values, log_total, grad_attended, key_valid):
    scores = masked_scores(queries, keys_in, key_valid)
    prob_rows = jnp.exp(scores - log_total)
    grad_values = jnp.einsum(
        "bhqk,bqhd->bkhd",
        prob_rows.astype(jnp.bfloat16),
        grad_attended,
        preferred_element_type=jnp.float32,
    )
    grad_probs = jnp.einsum(
        "bqhd,bkhd->bhqk", grad_attended, values, preferred_element_type=jnp.float32
    )
    inner_sum = jnp.sum(prob_rows * grad_probs, axis=-1, keepdims=True)
    grad_scores = (prob_rows * (grad_probs - inner_sum)).astype(jnp.bfloat16)
    grad_queries = (
        jnp.einsum("bhqk,bkhd->bqhd", grad_scores, keys_in, preferred_element_type=jnp.float32)
        * 0.125
    )
    grad_keys = (
        jnp.einsum("bhqk,bqhd->bkhd", grad_scores, queries, preferred_element_type=jnp.float32)
        * 0.125
    )
    return jnp.stack([grad_queries, grad_keys, grad_values], axis=2)


def pick_block(total_rows):
    for candidate in (1024, 768, 512, 384, 256):
        if total_rows % candidate == 0:
            return candidate
    return total_rows


def by_heads(
    tokens,
    ln1_gain,
    ln1_bias,
    w_qkv,
    w_out,
    ln2_gain,
    ln2_bias,
    w_router,
    expert_in,
    expert_out,
    routes,
    targets,
):
    image_count, slot_count, model_width = tokens.shape
    seq_devices = lax.axis_size("seq")
    row_count = image_count * slot_count
    expert_count = w_router.shape[1]
    local_experts = expert_in.shape[0]
    slot_limit = 2 * S // (seq_devices * expert_count) + 2
    head_size = model_width // H
    gathered = (
        lax.all_gather(ln1_gain, "dp", axis=0, tiled=True),
        lax.all_gather(ln1_bias, "dp", axis=0, tiled=True),
        lax.all_gather(w_qkv, "dp", axis=0, tiled=True),
        lax.all_gather(w_out, "dp", axis=0, tiled=True),
        lax.all_gather(ln2_gain, "dp", axis=0, tiled=True),
        lax.all_gather(ln2_bias, "dp", axis=0, tiled=True),
        lax.all_gather(w_router, "dp", axis=0, tiled=True),
    )
    gain_one = gathered[0].astype(jnp.float32)
    bias_one = gathered[1].astype(jnp.float32)
    qkv_weight = gathered[2]
    out_weight = gathered[3]
    gain_two = gathered[4].astype(jnp.float32)
    bias_two = gathered[5].astype(jnp.float32)
    router_weight = gathered[6]
    slot_start = lax.axis_index("seq") * slot_count
    valid_slot = slot_start + jnp.arange(slot_count) < VALID
    valid_rows = jnp.tile(valid_slot, image_count)
    key_valid = (jnp.arange(S) < VALID)[None, None, None, :]
    token_rows = tokens.reshape(row_count, model_width).astype(jnp.float32)
    normed_one, norm_one_back = jax.vjp(layer_norm, token_rows, gain_one, bias_one)
    normed_one_b = normed_one.astype(jnp.bfloat16)
    mixed_qkv = jnp.dot(normed_one_b, qkv_weight, preferred_element_type=jnp.float32).astype(
        jnp.bfloat16
    )
    qkv_heads = regroup_heads(mixed_qkv.reshape(image_count, slot_count, 3, H, head_size))
    queries = qkv_heads[:, :, 0]
    keys_in = qkv_heads[:, :, 1]
    values = qkv_heads[:, :, 2]
    attended, log_total = attention_forward(queries, keys_in, values, key_valid)
    attended_rows = regroup_slots(attended[:, :, None]).reshape(row_count, model_width)
    residual_two = token_rows + jnp.dot(
        attended_rows, out_weight, preferred_element_type=jnp.float32
    )
    normed_two, norm_two_back = jax.vjp(layer_norm, residual_two, gain_two, bias_two)
    normed_two_b = normed_two.astype(jnp.bfloat16)
    logits = jnp.dot(normed_two_b, router_weight, preferred_element_type=jnp.float32)
    route_rows = routes.reshape(row_count, 2)
    chosen = (route_rows[:, :, None] == jnp.arange(expert_count)[None, None, :]) & valid_rows[
        :, None, None
    ]
    chosen_f = chosen.astype(jnp.float32)

    def gate_pick(logit_rows):
        return jnp.sum(jax.nn.softmax(logit_rows, axis=-1)[:, None, :] * chosen_f, axis=-1)

    gate_values, gate_back = jax.vjp(gate_pick, logits)
    pick_count = chosen.astype(jnp.int32).reshape(image_count, slot_count * 2, expert_count)
    before = jnp.cumsum(pick_count, axis=1) - pick_count
    place_hit = (before[..., None] == jnp.arange(slot_limit)) & (pick_count[..., None] > 0)
    dispatch = place_hit.astype(jnp.bfloat16).reshape(
        image_count, slot_count, 2, expert_count, slot_limit
    )
    normed_img = normed_two_b.reshape(image_count, slot_count, model_width)
    sent_rows = jnp.einsum(
        "bskem,bsd->ebmd", dispatch, normed_img, preferred_element_type=jnp.float32
    ).astype(jnp.bfloat16)
    received = send_experts(sent_rows.reshape(expert_count, image_count * slot_limit, model_width))
    weights_in, weights_out = (
        lax.all_gather(expert_in, "seq", axis=2, tiled=True),
        lax.all_gather(expert_out, "seq", axis=1, tiled=True),
    )
    total_rows = received.shape[1]
    block_rows = pick_block(total_rows)
    block_count = total_rows // block_rows

    def expert_step(block_index, produced):
        row_piece = lax.dynamic_slice_in_dim(received, block_index * block_rows, block_rows, 1)
        hidden_pre = jnp.einsum(
            "erd,edf->erf", row_piece, weights_in, preferred_element_type=jnp.float32
        )
        activated = jax.nn.gelu(hidden_pre).astype(jnp.bfloat16)
        result = jnp.einsum(
            "erf,efd->erd", activated, weights_out, preferred_element_type=jnp.float32
        ).astype(jnp.bfloat16)
        return lax.dynamic_update_slice_in_dim(produced, result, block_index * block_rows, 1)

    produced = lax.fori_loop(
        0,
        block_count,
        expert_step,
        jnp.zeros((local_experts, total_rows, model_width), jnp.bfloat16),
    )
    returned = send_tokens(produced).reshape(expert_count, image_count, slot_limit, model_width)
    per_choice = jnp.einsum(
        "bskem,ebmd->bskd", dispatch, returned, preferred_element_type=jnp.float32
    ).reshape(row_count, 2, model_width)
    mixed_rows = (
        residual_two
        + gate_values[:, 0:1] * per_choice[:, 0]
        + gate_values[:, 1:2] * per_choice[:, 1]
    )
    target_rows = targets.reshape(row_count, model_width).astype(jnp.float32)
    grad_mixed = (mixed_rows - target_rows) * valid_rows[:, None].astype(jnp.float32)
    grad_gates = jnp.sum(grad_mixed[:, None, :] * per_choice, axis=-1)
    grad_choice = (
        (gate_values[:, :, None] * grad_mixed[:, None, :])
        .astype(jnp.bfloat16)
        .reshape(image_count, slot_count, 2, model_width)
    )
    grad_sent = jnp.einsum(
        "bskem,bskd->ebmd", dispatch, grad_choice, preferred_element_type=jnp.float32
    ).astype(jnp.bfloat16)
    grad_received = send_experts(
        grad_sent.reshape(expert_count, image_count * slot_limit, model_width)
    )
    back_in, back_out = (
        lax.all_gather(expert_in, "seq", axis=2, tiled=True),
        lax.all_gather(expert_out, "seq", axis=1, tiled=True),
    )

    def expert_back(block_index, loop_carry):
        grad_in_sum, grad_out_sum, grad_rows = loop_carry
        row_piece = lax.dynamic_slice_in_dim(received, block_index * block_rows, block_rows, 1)
        grad_piece = lax.dynamic_slice_in_dim(
            grad_received, block_index * block_rows, block_rows, 1
        )
        hidden_pre = jnp.einsum(
            "erd,edf->erf", row_piece, back_in, preferred_element_type=jnp.float32
        )
        activated, gelu_back = jax.vjp(jax.nn.gelu, hidden_pre)
        grad_act = jnp.einsum(
            "erd,efd->erf", grad_piece, back_out, preferred_element_type=jnp.float32
        )
        grad_pre = gelu_back(grad_act)[0].astype(jnp.bfloat16)
        grad_out_sum = grad_out_sum + jnp.einsum(
            "erf,erd->efd",
            activated.astype(jnp.bfloat16),
            grad_piece,
            preferred_element_type=jnp.float32,
        )
        grad_in_sum = grad_in_sum + jnp.einsum(
            "erd,erf->edf", row_piece, grad_pre, preferred_element_type=jnp.float32
        )
        rows_back = jnp.einsum(
            "erf,edf->erd", grad_pre, back_in, preferred_element_type=jnp.float32
        ).astype(jnp.bfloat16)
        grad_rows = lax.dynamic_update_slice_in_dim(
            grad_rows, rows_back, block_index * block_rows, 1
        )
        return (grad_in_sum, grad_out_sum, grad_rows)

    start_carry = (
        jnp.zeros(back_in.shape, jnp.float32),
        jnp.zeros(back_out.shape, jnp.float32),
        jnp.zeros((local_experts, total_rows, model_width), jnp.bfloat16),
    )
    grad_in_sum, grad_out_sum, grad_rows = lax.fori_loop(0, block_count, expert_back, start_carry)
    grad_returned = send_tokens(grad_rows).reshape(
        expert_count, image_count, slot_limit, model_width
    )
    grad_normed_two = jnp.einsum(
        "bskem,ebmd->bsd", dispatch, grad_returned, preferred_element_type=jnp.float32
    ).reshape(row_count, model_width)
    grad_logits = gate_back(grad_gates)[0].astype(jnp.bfloat16)
    grad_router = jnp.einsum(
        "rd,re->de", normed_two_b, grad_logits, preferred_element_type=jnp.float32
    )
    grad_normed_two = grad_normed_two + jnp.einsum(
        "re,de->rd", grad_logits, router_weight, preferred_element_type=jnp.float32
    )
    grad_res_two, grad_gain_two, grad_bias_two = norm_two_back(grad_normed_two)
    grad_residual = grad_mixed + grad_res_two
    grad_branch = grad_residual.astype(jnp.bfloat16)
    grad_out_weight = jnp.einsum(
        "rd,re->de", attended_rows, grad_branch, preferred_element_type=jnp.float32
    )
    grad_attended = jnp.einsum(
        "re,de->rd", grad_branch, out_weight, preferred_element_type=jnp.float32
    ).astype(jnp.bfloat16)
    grad_heads = regroup_heads(grad_attended.reshape(image_count, slot_count, 1, H, head_size))[
        :, :, 0
    ]
    grad_qkv_heads = attention_backward(
        queries, keys_in, values, log_total, grad_heads, key_valid
    ).astype(jnp.bfloat16)
    grad_qkv_rows = regroup_slots(grad_qkv_heads).reshape(row_count, 3 * model_width)
    grad_qkv_weight = jnp.einsum(
        "rd,rf->df", normed_one_b, grad_qkv_rows, preferred_element_type=jnp.float32
    )
    grad_normed_one = jnp.einsum(
        "rf,df->rd", grad_qkv_rows, qkv_weight, preferred_element_type=jnp.float32
    )
    grad_token_ln, grad_gain_one, grad_bias_one = norm_one_back(grad_normed_one)
    grad_tokens = grad_residual + grad_token_ln
    dense_grads = (
        grad_gain_one,
        grad_bias_one,
        grad_qkv_weight,
        grad_out_weight,
        grad_gain_two,
        grad_bias_two,
        grad_router,
    )
    dense_grads = (
        lax.psum(dense_grads[0].astype(jnp.bfloat16), "seq").astype(jnp.float32),
        lax.psum(dense_grads[1].astype(jnp.bfloat16), "seq").astype(jnp.float32),
        lax.psum(dense_grads[2].astype(jnp.bfloat16), "seq").astype(jnp.float32),
        lax.psum(dense_grads[3].astype(jnp.bfloat16), "seq").astype(jnp.float32),
        lax.psum(dense_grads[4].astype(jnp.bfloat16), "seq").astype(jnp.float32),
        lax.psum(dense_grads[5].astype(jnp.bfloat16), "seq").astype(jnp.float32),
        lax.psum(dense_grads[6].astype(jnp.bfloat16), "seq").astype(jnp.float32),
    )
    dense_grads = (
        lax.psum_scatter(
            dense_grads[0].astype(jnp.bfloat16), "dp", scatter_dimension=0, tiled=True
        ).astype(jnp.float32),
        lax.psum_scatter(
            dense_grads[1].astype(jnp.bfloat16), "dp", scatter_dimension=0, tiled=True
        ).astype(jnp.float32),
        lax.psum_scatter(
            dense_grads[2].astype(jnp.bfloat16), "dp", scatter_dimension=0, tiled=True
        ).astype(jnp.float32),
        lax.psum_scatter(
            dense_grads[3].astype(jnp.bfloat16), "dp", scatter_dimension=0, tiled=True
        ).astype(jnp.float32),
        lax.psum_scatter(
            dense_grads[4].astype(jnp.bfloat16), "dp", scatter_dimension=0, tiled=True
        ).astype(jnp.float32),
        lax.psum_scatter(
            dense_grads[5].astype(jnp.bfloat16), "dp", scatter_dimension=0, tiled=True
        ).astype(jnp.float32),
        lax.psum_scatter(
            dense_grads[6].astype(jnp.bfloat16), "dp", scatter_dimension=0, tiled=True
        ).astype(jnp.float32),
    )
    expert_in_grad, expert_out_grad = (
        lax.psum_scatter(
            grad_in_sum.astype(jnp.bfloat16), "seq", scatter_dimension=2, tiled=True
        ).astype(jnp.float32),
        lax.psum_scatter(
            grad_out_sum.astype(jnp.bfloat16), "seq", scatter_dimension=1, tiled=True
        ).astype(jnp.float32),
    )
    mixed = mixed_rows.astype(jnp.bfloat16).reshape(image_count, slot_count, model_width)
    return (
        mixed,
        grad_tokens.reshape(image_count, slot_count, model_width),
        dense_grads[0],
        dense_grads[1],
        dense_grads[2],
        dense_grads[3],
        dense_grads[4],
        dense_grads[5],
        dense_grads[6],
        expert_in_grad,
        expert_out_grad,
    )


BF = jnp.bfloat16
F32 = jnp.float32
MESH_ID = pl.DeviceIdType.MESH
NEG = -1e30
BP = 64
VMEM_LIMIT = 67000000
GELU_C = 0.7978845608028654
GELU_K = 0.044715


def nn(a, b):
    return lax.dot_general(a, b, (((1,), (0,)), ((), ())), preferred_element_type=F32)


def nt(a, b):
    return lax.dot_general(a, b, (((1,), (1,)), ((), ())), preferred_element_type=F32)


def tn(a, b):
    return lax.dot_general(a, b, (((0,), (0,)), ((), ())), preferred_element_type=F32)


def remote(src, dst, send_sem, recv_sem, dp, z):
    return pltpu.make_async_remote_copy(
        src_ref=src,
        dst_ref=dst,
        send_sem=send_sem,
        recv_sem=recv_sem,
        device_id=(dp, z),
        device_id_type=MESH_ID,
    )


def rows_of(index, size):
    return pl.ds(pl.multiple_of(index * size, size), size)


def norm_parts(x):
    centre = x - jnp.mean(x, axis=-1, keepdims=True)
    scale = lax.rsqrt(jnp.mean(centre * centre, axis=-1, keepdims=True) + 1e-06)
    return centre * scale, scale


def norm_back(grad_hat, hat, scale):
    return scale * (
        grad_hat
        - jnp.mean(grad_hat, axis=-1, keepdims=True)
        - hat * jnp.mean(grad_hat * hat, axis=-1, keepdims=True)
    )


def half_masks():
    lane = lax.broadcasted_iota(jnp.int32, (1, 128), 1)
    low = jnp.where(lane < 64, 1.0, 0.0).astype(BF)
    high = jnp.where(lane < 64, 0.0, 1.0).astype(BF)
    return (low, high)


def slot_ok(position, block):
    return (position % BP < block) & ((position // BP) * block + position % BP < VALID)


def block_kernel(
    dims,
    tok, tgt, rts, wq, wo, vec, win, wout,
    mixed, gtok, gqkv, gwo, gsmall, gin, gout,
    xin, rin, tin, vec_all, wq_all, wo_all, vsum, xpad, x2s, n2s, qkvs, outs, lses, gts, meta, metat,
    win_all, wout_all, recv, ret, acts, slopes, sbuf,
    mbuf, drows, dys, dlogs, dus, dret, dws, arrived,
    gacc, gvec, gbig, crecv, cvec, gsum, hrecv, hvec, zsend, zrecv, zall, zvec,
    loc_sem, tok_ss, tok_rs, rts_ss, rts_rs, tgt_ss, tgt_rs, den_ss, den_rs, fwd_ss, win_ss, win_rs, wout_ss, wout_rs,
    row_ss, row_rs, u_ss, u_rs, du_ss, du_rs, dn_ss, dn_rs, mix_ss, mix_rs, gt_ss, gt_rs,
    r_ss, r_rs, c_ss, c_rs, cv_ss, cv_rs, h_ss, h_rs, hv_ss, hv_rs, za_ss, za_rs, zb_ss, zb_rs, zv_ss, zv_rs,
):
    n_dp, n_z, im, block, cap, er = dims
    me, z = lax.axis_index("dp"), lax.axis_index("seq")
    sp = n_z * BP
    nr = n_dp * er
    two = 2 * er
    half = n_dp // 2
    last = n_z - 1
    core, chip = lax.rem(me, 2), me // 2
    partner = chip * 2 + 1 - core

    barrier = pltpu.get_barrier_semaphore()
    for k in range(1, n_dp):
        pl.semaphore_signal(barrier, inc=1, device_id=(lax.rem(me + k, n_dp), z), device_id_type=MESH_ID)
    for k in range(1, n_z):
        pl.semaphore_signal(barrier, inc=1, device_id=(me, lax.rem(z + k, n_z)), device_id_type=MESH_ID)
    own_copies = [
        pltpu.make_async_copy(tok.at[pl.ds(z * im, im)], xin.at[z], loc_sem.at[0]),
        pltpu.make_async_copy(rts.at[pl.ds(z * im, im)], rin.at[z], loc_sem.at[1]),
        pltpu.make_async_copy(tgt.at[pl.ds(z * im, im)], tin.at[z], loc_sem.at[2]),
        pltpu.make_async_copy(win, win_all.at[z], loc_sem.at[3]),
        pltpu.make_async_copy(wout, wout_all.at[z], loc_sem.at[4]),
        pltpu.make_async_copy(wq, wq_all.at[rows_of(me, 64)], loc_sem.at[5]),
        pltpu.make_async_copy(wo, wo_all.at[rows_of(me, 64)], loc_sem.at[6]),
        pltpu.make_async_copy(vec, vec_all.at[me], loc_sem.at[7]),
    ]
    for copy in own_copies:
        copy.start()
    xpad[...] = jnp.zeros_like(xpad)
    gacc[...] = jnp.zeros_like(gacc)
    gvec[...] = jnp.zeros_like(gvec)
    pl.semaphore_wait(barrier, n_dp + n_z - 2)

    def z_start(source, target, send_sem, recv_sem):
        for k in range(1, n_z):
            peer = lax.rem(z + k, n_z)
            remote(source(peer), target(z), send_sem.at[k], recv_sem.at[z], me, peer).start()

    def z_arrive(target, recv_sem):
        for k in range(1, n_z):
            origin = lax.rem(z + k, n_z)
            remote(target(origin), target(origin), loc_sem.at[8], recv_sem.at[origin], me, z).wait_recv()

    def z_sent(source, send_sem):
        for k in range(1, n_z):
            remote(source(0), source(0), send_sem.at[k], loc_sem.at[8], me, z).wait_send()

    tok_of = lambda peer: tok.at[pl.ds(peer * im, im)]
    rts_of = lambda peer: rts.at[pl.ds(peer * im, im)]
    tgt_of = lambda peer: tgt.at[pl.ds(peer * im, im)]
    z_start(tok_of, lambda i: xin.at[i], tok_ss, tok_rs)
    z_start(rts_of, lambda i: rin.at[i], rts_ss, rts_rs)

    def dense_slot(array, index):
        if array == 0:
            return wq_all.at[rows_of(index, 64)]
        if array == 1:
            return wo_all.at[rows_of(index, 64)]
        return vec_all.at[index]

    dense_in = (wq, wo, vec)
    for array in range(3):
        for k in range(1, half):
            peer = lax.rem(chip + k, half) * 2 + core
            remote(
                dense_in[array], dense_slot(array, me), den_ss.at[array, k], den_rs.at[array, me], peer, z
            ).start()
        remote(
            dense_in[array], dense_slot(array, me), den_ss.at[array, 0], den_rs.at[array, me], partner, z
        ).start()

    experts = ((win, win_all, win_ss, win_rs), (wout, wout_all, wout_ss, wout_rs))
    inner = (z == 1) | (z == last - 1)
    far_end = jnp.where(z == 1, last, 0)

    def weight_send(array, kind, there, peer):
        source, full, send_sem, recv_sem = experts[array]

        @pl.when(there)
        def _():
            remote(source, full.at[z], send_sem.at[kind], recv_sem.at[z], me, peer).start()

    for array in range(2):
        weight_send(array, 0, z >= 0, jnp.where(z < 2, z + 2, z - 2))
    for array in range(2):
        weight_send(array, 1, z < last, z + 1)
        weight_send(array, 2, z > 0, z - 1)

    def weight_wait(array, slot):
        source, full, send_sem, recv_sem = experts[array]
        at = full.at[slot]
        remote(at, at, send_sem.at[0], recv_sem.at[slot], me, z).wait_recv()

    def weight_forward(array):
        source, full, send_sem, recv_sem = experts[array]

        @pl.when(inner)
        def _():
            weight_wait(array, far_end)
            at = full.at[far_end]
            remote(at, at, send_sem.at[3], recv_sem.at[far_end], me, last - far_end).start()

    def weights_sent():
        for kind, there in ((0, z >= 0), (1, z < last), (2, z > 0), (3, inner)):

            @pl.when(there)
            def _():
                for source, full, send_sem, recv_sem in experts:
                    remote(full.at[0], full.at[0], send_sem.at[kind], recv_sem.at[0], me, z).wait_send()

    for k in range(1, half):
        origin = lax.rem(chip + k, half) * 2 + core
        for array in range(3):
            slot = dense_slot(array, origin)
            remote(slot, slot, den_ss.at[array, 0], den_rs.at[array, origin], me, z).wait_recv()
            remote(slot, slot, fwd_ss.at[array, k], den_rs.at[array, origin], partner, z).start()
    for k in range(half):
        origin = lax.rem(chip + k, half) * 2 + 1 - core
        for array in range(3):
            slot = dense_slot(array, origin)
            remote(slot, slot, den_ss.at[array, 0], den_rs.at[array, origin], me, z).wait_recv()
    for copy in own_copies:
        copy.wait()
    total = vec_all[0].astype(F32)
    for k in range(1, n_dp):
        total = total + vec_all[k].astype(F32)
    vsum[...] = total
    z_arrive(lambda i: xin.at[i], tok_rs)
    z_arrive(lambda i: rin.at[i], rts_rs)

    masks = half_masks()
    keys_ok = slot_ok(lax.broadcasted_iota(jnp.int32, (1, sp), 1), block)
    rows_ok = slot_ok(lax.broadcasted_iota(jnp.int32, (sp, 1), 0), block)
    gain_one, bias_one = vsum[0:1, :], vsum[1:2, :]
    gain_two, bias_two = vsum[2:3, :], vsum[3:4, :]
    router_t = vsum[8:16, :].astype(BF)
    lane_id = lax.broadcasted_iota(jnp.int32, (sp, 128), 1)
    lane_low = lane_id < 64

    def front(i, carry):
        before = lax.broadcasted_iota(jnp.int32, (sp, sp), 0)
        after = lax.broadcasted_iota(jnp.int32, (sp, sp), 1)
        prefix = jnp.where((before < after) & (before // BP == after // BP), 1.0, 0.0).astype(BF)
        expert_id = lax.broadcasted_iota(jnp.int32, (8, sp), 0)
        slot_lane = lax.broadcasted_iota(jnp.int32, (8, sp), 1)
        for b in range(n_z):
            xpad[i, b * BP : b * BP + block, :] = xin[b, i]
        x = xpad[i].astype(F32)
        hat, _ = norm_parts(x)
        normed = (hat * gain_one + bias_one).astype(BF)
        qkvs[i] = nn(normed, wq_all[...]).astype(BF)
        lse_all = jnp.zeros((sp, 128), F32)
        for pair in range(4):
            q2 = qkvs[i, :, pair * 128 : pair * 128 + 128]
            k2 = qkvs[i, :, 512 + pair * 128 : 512 + pair * 128 + 128]
            v2 = qkvs[i, :, 1024 + pair * 128 : 1024 + pair * 128 + 128]
            parts = []
            for side in range(2):
                scores = nt(q2 * masks[side], k2) * 0.125
                scores = jnp.where(keys_ok, scores, NEG)
                top = jnp.max(scores, axis=-1, keepdims=True)
                exponent = jnp.exp(scores - top)
                whole = jnp.sum(exponent, axis=-1, keepdims=True)
                lse_all = jnp.where(lane_id == pair * 2 + side, top + jnp.log(whole), lse_all)
                parts.append(nn((exponent / whole).astype(BF), v2))
            outs[i, :, pair * 128 : pair * 128 + 128] = jnp.where(lane_low, parts[0], parts[1]).astype(BF)
        lses[i] = lse_all
        x2 = x + nn(outs[i], wo_all[...])
        x2s[i] = x2
        hat2, _ = norm_parts(x2)
        n2 = (hat2 * gain_two + bias_two).astype(BF)
        n2s[i] = n2
        logits = nt(router_t, n2)
        raised = jnp.exp(logits - jnp.max(logits, axis=0, keepdims=True))
        share = raised / jnp.sum(raised, axis=0, keepdims=True)
        gts[i] = share
        wide = jnp.concatenate([rin[0, i] + rin[1, i], rin[2, i] + rin[3, i]], axis=1)
        hits = [(expert_id + 1) == wide[j : j + 1, :] for j in range(2)]
        any_hit = jnp.where(hits[0] | hits[1], 1.0, 0.0)
        place = nn(any_hit.astype(BF), prefix)
        base = place + (expert_id * er + (slot_lane // BP) * cap + i * (n_z * cap) + 1).astype(F32)
        lines = [jnp.sum(jnp.where(hit, base, 0.0), axis=0, keepdims=True) - 1.0 for hit in hits]
        lines += [jnp.sum(jnp.where(hit, share, 0.0), axis=0, keepdims=True) for hit in hits]
        table = jnp.concatenate(lines + [jnp.zeros((124, sp), F32)], axis=0)
        meta[i] = table[0:8]
        metat[i] = jnp.transpose(table)
        return carry

    lax.fori_loop(0, im, front, 0)

    row_id = lax.broadcasted_iota(jnp.int32, (er, sp), 0)

    def to_experts(product, target, send_sem, recv_sem):
        def step(s, carry):
            j, c = lax.rem(s // 2 + 1, half), lax.rem(s, 2)
            index = 2 * j + c
            peer = lax.rem(chip + j, half) * 2 + lax.rem(core + c, 2)
            sbuf[index] = product(peer).astype(BF)

            @pl.when(index > 0)
            def _():
                remote(
                    sbuf.at[index], target.at[rows_of(me, er)], send_sem.at[index], recv_sem.at[me], peer, z
                ).start()

            @pl.when(index == 0)
            def _():
                target[rows_of(me, er)] = sbuf[index]

            return carry

        lax.fori_loop(0, n_dp, step, 0)

    def to_tokens(product, target, send_sem, recv_sem):
        def step(s, carry):
            j = lax.rem(s + 1, half)
            part = lax.rem(chip + j, half)
            out = product(part).astype(BF)
            sbuf[2 * j] = out[0:er]
            sbuf[2 * j + 1] = out[er:two]

            @pl.when(j > 0)
            def _():
                for c in range(2):
                    remote(
                        sbuf.at[2 * j + c],
                        target.at[rows_of(me, er)],
                        send_sem.at[2 * j + c],
                        recv_sem.at[me],
                        part * 2 + c,
                        z,
                    ).start()

            @pl.when(j == 0)
            def _():
                target[rows_of(me, er)] = sbuf[core]
                remote(
                    sbuf.at[1 - core], target.at[rows_of(me, er)], send_sem.at[1], recv_sem.at[me], partner, z
                ).start()

            return carry

        lax.fori_loop(0, half, step, 0)

    def dp_arrive(target, recv_sem):
        for k in range(1, n_dp):
            origin = lax.rem(me + k, n_dp)
            spot = target.at[rows_of(origin, er)]
            remote(spot, spot, loc_sem.at[8], recv_sem.at[origin], me, z).wait_recv()

    def dp_sent(send_sem):
        for k in range(1, n_dp):
            remote(sbuf.at[0], sbuf.at[0], send_sem.at[k], loc_sem.at[8], me, z).wait_send()

    def tokens_for(peer):
        want = (row_id + peer * er).astype(F32)
        total = jnp.zeros((er, 512), F32)
        for i in range(im):
            pick = (want == meta[i, 0:1, :]) | (want == meta[i, 1:2, :])
            total = total + nn(jnp.where(pick, 1.0, 0.0).astype(BF), n2s[i])
        return total

    to_experts(tokens_for, recv, row_ss, row_rs)

    def hidden(shard):
        def part_step(part, carry):
            at = rows_of(part, two)
            x = recv[at]
            for side in range(2):
                pre = nn(x, win_all[shard, :, side * 256 : side * 256 + 256])
                square = pre * pre
                tanh = jnp.tanh(pre * (GELU_C + (GELU_C * GELU_K) * square))
                gate = 0.5 + 0.5 * tanh
                acts[shard, at, side * 256 : side * 256 + 256] = (pre * gate).astype(BF)
                slope = gate + pre * (0.5 - 0.5 * tanh * tanh) * (GELU_C + (3.0 * GELU_C * GELU_K) * square)
                slopes[shard, at, side * 256 : side * 256 + 256] = slope.astype(BF)
            return carry

        lax.fori_loop(0, n_dp // 2, part_step, 0)

    def hidden_step(s, carry):
        second = jnp.where(z == 0, 2, jnp.where(z == last, 1, last - far_end))
        shard = jnp.where(
            s == 0,
            z,
            jnp.where(
                s == 1,
                jnp.where(inner, far_end, jnp.where(z == 0, 1, last - 1)),
                jnp.where(s == 2, second, last - z),
            ),
        )

        @pl.when(inner & (s == 1))
        def _():
            weight_forward(1)

        @pl.when((s > 1) | ((s == 1) & jnp.logical_not(inner)))
        def _():
            weight_wait(0, shard)

        hidden(shard)
        return carry

    weight_forward(0)
    dp_arrive(recv, row_rs)
    dp_sent(row_ss)
    lax.fori_loop(0, n_z, hidden_step, 0)
    for slot in range(n_z):

        @pl.when((z != slot) & jnp.logical_not(inner & (far_end == slot)))
        def _():
            weight_wait(1, slot)

    z_start(tgt_of, lambda i: tin.at[i], tgt_ss, tgt_rs)

    def results_for(part):
        total = jnp.zeros((two, 512), F32)
        for shard in range(n_z):
            total = total + nn(acts[shard, rows_of(part, two)], wout_all[shard])
        return total

    to_tokens(results_for, ret, u_ss, u_rs)

    z_arrive(lambda i: tin.at[i], tgt_rs)
    for b in range(n_z):
        for i in range(im):
            dys[i, b * BP : b * BP + block, :] = tin[b, i].astype(F32)
    dp_arrive(ret, u_rs)

    def mix(i, carry):
        line = lax.broadcasted_iota(jnp.int32, (sp, nr), 1).astype(F32)
        cols = metat[i]
        picked = []
        for j in range(2):
            pick = jnp.where(line == cols[:, j : j + 1], 1.0, 0.0).astype(BF)
            picked.append(nn(pick, ret[...]))
        mix = x2s[i] + cols[:, 2:3] * picked[0] + cols[:, 3:4] * picked[1]
        mix_b = mix.astype(BF)
        for b in range(n_z):
            mbuf[b, i] = mix_b[b * BP : b * BP + block]
        dy = jnp.where(rows_ok, mix - dys[i], 0.0)
        dys[i] = dy
        dus[0, i] = (cols[:, 2:3] * dy).astype(BF)
        dus[1, i] = (cols[:, 3:4] * dy).astype(BF)
        dlogs[i] = jnp.where(
            lane_id == 0, jnp.sum(dy * picked[0], axis=-1, keepdims=True), 0.0
        ) + jnp.where(lane_id == 1, jnp.sum(dy * picked[1], axis=-1, keepdims=True), 0.0)
        return carry

    lax.fori_loop(0, im, mix, 0)
    dp_sent(u_ss)

    def gradients_for(peer):
        want = (row_id + peer * er).astype(F32)
        total = jnp.zeros((er, 512), F32)
        for i in range(im):
            for j in range(2):
                pick = jnp.where(want == meta[i, j : j + 1, :], 1.0, 0.0).astype(BF)
                total = total + nn(pick, dus[j, i])
        return total

    to_experts(gradients_for, drows, du_ss, du_rs)
    z_start(lambda peer: mbuf.at[peer], lambda i: mixed.at[pl.ds(i * im, im)], mix_ss, mix_rs)
    own_mixed = pltpu.make_async_copy(mbuf.at[z], mixed.at[pl.ds(z * im, im)], loc_sem.at[0])
    own_mixed.start()
    expert_row = lax.broadcasted_iota(jnp.int32, (8, sp), 0).astype(F32)
    for i in range(im):
        flat = jnp.transpose(dlogs[i])
        share = gts[i]
        grad = jnp.zeros((8, sp), F32)
        for j in range(2):
            at = meta[i, j : j + 1, :]
            inside = (at >= expert_row * er) & (at < expert_row * er + er)
            grad = grad + jnp.where(inside, flat[j : j + 1, :], 0.0)
        dlog = share * (grad - jnp.sum(share * grad, axis=0, keepdims=True))
        gts[i] = dlog
        gvec[8:16, :] += nn(dlog.astype(BF), n2s[i])
    dp_arrive(drows, du_rs)
    dp_sent(du_ss)

    def reduce_start(target, piece):
        held = inner & (target == far_end)
        via = ((z == 0) & (target == last)) | ((z == last) & (target == 0))
        peer = jnp.where(via, jnp.where(z == 0, 1, last - 1), target)

        @pl.when((target != z) & jnp.logical_not(held))
        def _():
            slot = jnp.where(via, peer, z)
            remote(
                dws.at[target, piece], arrived.at[slot, piece], r_ss.at[target, piece], r_rs.at[slot, piece], me, peer
            ).start()

    def reduce_forward(piece):
        @pl.when(inner)
        def _():
            here = arrived.at[z, piece]
            remote(here, here, r_ss.at[far_end, piece], r_rs.at[z, piece], me, z).wait_recv()

            def add(c, carry):
                at = rows_of(c, 128)
                dws[far_end, piece, at] = (
                    dws[far_end, piece, at].astype(F32) + arrived[z, piece, at].astype(F32)
                ).astype(BF)
                return carry

            lax.fori_loop(0, 4, add, 0)
            remote(
                dws.at[far_end, piece], here, r_ss.at[far_end, piece], r_rs.at[z, piece], me, far_end
            ).start()

    def owner(s):
        return jnp.where(z < n_z // 2, lax.rem(z + 2 * n_z - 1 - s, n_z), lax.rem(z + 1 + s, n_z))

    def out_grads(s, carry):
        target = owner(s)
        dws[target, 0] = tn(acts[target], drows[...]).astype(BF)
        reduce_start(target, 0)
        return carry

    def in_grads(s, carry):
        target = owner(s)
        dws[target, 1] = tn(recv[...], slopes[target]).astype(BF)
        reduce_start(target, 1)
        return carry

    lax.fori_loop(0, n_z, out_grads, 0)

    def input_grads_for(part):
        at = rows_of(part, two)
        du = drows[at]
        total = jnp.zeros((two, 512), F32)
        for shard in range(n_z):
            dpre = (nt(du, wout_all[shard]) * slopes[shard, at].astype(F32)).astype(BF)
            slopes[shard, at] = dpre
            total = total + nt(dpre, win_all[shard])
        return total

    to_tokens(input_grads_for, dret, dn_ss, dn_rs)
    lax.fori_loop(0, n_z, in_grads, 0)
    own_mixed.wait()
    z_sent(lambda peer: mbuf.at[peer], mix_ss)
    dp_arrive(dret, dn_rs)
    reduce_forward(0)

    def back(i, carry):
        line = lax.broadcasted_iota(jnp.int32, (sp, nr), 1).astype(F32)
        cols = metat[i]
        pick = jnp.where((line == cols[:, 0:1]) | (line == cols[:, 1:2]), 1.0, 0.0).astype(BF)
        dn2 = nn(pick, dret[...]) + tn(gts[i].astype(BF), router_t)
        hat2, scale2 = norm_parts(x2s[i])
        gvec[2:3, :] += jnp.sum(dn2 * hat2, axis=0, keepdims=True)
        gvec[3:4, :] += jnp.sum(dn2, axis=0, keepdims=True)
        dx2 = dys[i] + norm_back(dn2 * gain_two, hat2, scale2)
        da = dx2.astype(BF)
        gacc[:, 1536:2048] += tn(outs[i], da)
        do = nt(da, wo_all[...]).astype(BF)
        hat1, scale1 = norm_parts(xpad[i].astype(F32))
        n1 = (hat1 * gain_one + bias_one).astype(BF)
        dn1 = jnp.zeros((sp, 512), F32)
        for pair in range(4):
            at = pair * 128
            q2 = qkvs[i, :, at : at + 128]
            k2 = qkvs[i, :, 512 + at : 512 + at + 128]
            v2 = qkvs[i, :, 1024 + at : 1024 + at + 128]
            do2 = do[:, at : at + 128]
            grads = ([], [], [])
            for side in range(2):
                head = pair * 2 + side
                scores = nt(q2 * masks[side], k2) * 0.125
                scores = jnp.where(keys_ok, scores, NEG)
                prob = jnp.exp(scores - lses[i, :, head : head + 1])
                dprob = nt(do2 * masks[side], v2)
                inner = jnp.sum(prob * dprob, axis=-1, keepdims=True)
                ds = (prob * (dprob - inner)).astype(BF)
                grads[0].append(nn(ds, k2))
                grads[1].append(tn(ds, q2))
                grads[2].append(tn(prob.astype(BF), do2))
            for part in range(3):
                grad = jnp.where(lane_low, grads[part][0], grads[part][1])
                if part < 2:
                    grad = grad * 0.125
                grad = grad.astype(BF)
                col = part * 512 + at
                gacc[:, col : col + 128] += tn(n1, grad)
                dn1 = dn1 + nt(grad, wq_all[:, col : col + 128])
        gvec[0:1, :] += jnp.sum(dn1 * hat1, axis=0, keepdims=True)
        gvec[1:2, :] += jnp.sum(dn1, axis=0, keepdims=True)
        dx = (dx2 + norm_back(dn1 * gain_one, hat1, scale1)).astype(BF)
        for b in range(n_z):
            mbuf[b, i] = dx[b * BP : b * BP + block]
        return carry

    lax.fori_loop(0, im, back, 0)
    z_start(lambda peer: mbuf.at[peer], lambda i: gtok.at[pl.ds(i * im, im)], gt_ss, gt_rs)
    own_gtok = pltpu.make_async_copy(mbuf.at[z], gtok.at[pl.ds(z * im, im)], loc_sem.at[1])
    own_gtok.start()

    gbig[...] = gacc[...].astype(BF)
    for q in range(half):
        remote(
            gbig.at[rows_of(2 * q + 1 - core, 64)], crecv.at[q], c_ss.at[q], c_rs.at[q], partner, z
        ).start()
    remote(gvec, cvec, cv_ss.at[0], cv_rs.at[0], partner, z).start()
    for q in range(half):
        remote(crecv.at[q], crecv.at[q], c_ss.at[q], c_rs.at[q], me, z).wait_recv()
    for k in range(1, half):
        q = lax.rem(chip + k, half)
        gsum[q] = (gacc[rows_of(2 * q + core, 64)] + crecv[q].astype(F32)).astype(BF)
        remote(gsum.at[q], hrecv.at[chip], h_ss.at[k], h_rs.at[chip], q * 2 + core, z).start()
    remote(cvec, cvec, cv_ss.at[0], cv_rs.at[0], me, z).wait_recv()
    hvec[chip] = gvec[...] + cvec[...]
    for k in range(1, half):
        q = lax.rem(chip + k, half)
        remote(hvec.at[chip], hvec.at[chip], hv_ss.at[k], hv_rs.at[chip], q * 2 + core, z).start()
    reduce_forward(1)
    dense = gacc[rows_of(me, 64)] + crecv[chip].astype(F32)
    for k in range(1, half):
        q = lax.rem(chip + k, half)
        remote(hrecv.at[q], hrecv.at[q], h_ss.at[0], h_rs.at[q], me, z).wait_recv()
        dense = dense + hrecv[q].astype(F32)
    for peer in range(n_z):
        zsend[peer] = dense[peer * 16 : peer * 16 + 16].astype(BF)
    z_start(lambda peer: zsend.at[peer], lambda i: zrecv.at[i], za_ss, za_rs)
    for k in range(1, half):
        q = lax.rem(chip + k, half)
        remote(hvec.at[q], hvec.at[q], hv_ss.at[0], hv_rs.at[q], me, z).wait_recv()
    zvec[z] = hvec[0] + hvec[1] + hvec[2] + hvec[3]
    z_start(lambda peer: zvec.at[z], lambda i: zvec.at[i], zv_ss, zv_rs)
    zrecv[z] = zsend[z]
    z_arrive(lambda i: zrecv.at[i], za_rs)
    total = zrecv[0].astype(F32)
    for k in range(1, n_z):
        total = total + zrecv[k].astype(F32)
    zall[z] = total.astype(BF)
    z_start(lambda peer: zall.at[z], lambda i: zall.at[i], zb_ss, zb_rs)

    for piece, out in ((0, gout), (1, gin)):
        for source in range(n_z):
            merged = ((z == last) & (source == 0)) | ((z == 0) & (source == last))

            @pl.when((z != source) & jnp.logical_not(merged))
            def _():
                here = arrived.at[source, piece]
                remote(here, here, r_ss.at[0, piece], r_rs.at[source, piece], me, z).wait_recv()

        def finish(c, carry):
            at = rows_of(c, 128)
            total = dws[z, piece, at].astype(F32)
            for source in range(n_z):
                merged = ((z == last) & (source == 0)) | ((z == 0) & (source == last))
                counted = (z != source) & jnp.logical_not(merged)
                total = total + jnp.where(counted, arrived[source, piece, at].astype(F32), 0.0)
            out[at] = total
            return carry

        lax.fori_loop(0, 4, finish, 0)
    z_arrive(lambda i: zvec.at[i], zv_rs)
    gsmall[...] = zvec[0] + zvec[1] + zvec[2] + zvec[3]
    z_arrive(lambda i: zall.at[i], zb_rs)
    for k in range(n_z):
        piece = zall[k].astype(F32)
        gqkv[k * 16 : k * 16 + 16] = piece[:, 0:1536]
        gwo[k * 16 : k * 16 + 16] = piece[:, 1536:2048]
    own_gtok.wait()
    z_arrive(lambda i: gtok.at[pl.ds(i * im, im)], gt_rs)
    z_arrive(lambda i: mixed.at[pl.ds(i * im, im)], mix_rs)

    z_sent(lambda peer: xin.at[peer], tok_ss)
    z_sent(lambda peer: rin.at[peer], rts_ss)
    z_sent(lambda peer: tin.at[peer], tgt_ss)
    z_sent(lambda peer: mbuf.at[peer], gt_ss)
    z_sent(lambda peer: zsend.at[peer], za_ss)
    z_sent(lambda peer: zvec.at[peer], zv_ss)
    z_sent(lambda peer: zall.at[peer], zb_ss)
    dp_sent(dn_ss)
    weights_sent()
    for array in range(3):
        slot = dense_slot(array, 0)
        for k in range(half):
            remote(slot, slot, den_ss.at[array, k], loc_sem.at[8], me, z).wait_send()
        for k in range(1, half):
            remote(slot, slot, fwd_ss.at[array, k], loc_sem.at[8], me, z).wait_send()
    for piece in range(2):
        for target in range(n_z):
            here = dws.at[0, 0]

            @pl.when(z != target)
            def _():
                remote(here, here, r_ss.at[target, piece], loc_sem.at[8], me, z).wait_send()

    for q in range(half):
        remote(crecv.at[q], crecv.at[q], c_ss.at[q], loc_sem.at[8], me, z).wait_send()
    remote(cvec, cvec, cv_ss.at[0], loc_sem.at[8], me, z).wait_send()
    for k in range(1, half):
        remote(gsum.at[0], gsum.at[0], h_ss.at[k], loc_sem.at[8], me, z).wait_send()
        remote(cvec, cvec, hv_ss.at[k], loc_sem.at[8], me, z).wait_send()


def finish_kernel(mixed, gtok, gqkv, gwo, gsmall, gin, gout, *outs):
    me = lax.axis_index("dp")
    outs[0][...] = mixed[...]
    outs[1][...] = gtok[...].astype(F32)
    for source, target in ((gqkv, outs[2]), (gwo, outs[3]), (gin, outs[4]), (gout, outs[5])):
        target[...] = source[...]
    lanes = gsmall[:, pl.ds(pl.multiple_of((me // 2) * 128, 128), 128)]
    lanes = jnp.where(lax.rem(me, 2) == 1, pltpu.roll(lanes, 64, 1), lanes)
    outs[6][...] = lanes[:, 0:64]


def whole_images(
    tokens, ln1_gain, ln1_bias, w_qkv, w_out, ln2_gain, ln2_bias, w_router, expert_in, expert_out, routes, targets
):
    n_dp, n_z = lax.axis_size("dp"), lax.axis_size("seq")
    image_count, block, width = tokens.shape
    im = image_count // n_z
    cap = 2 * S // (n_z * w_router.shape[1]) + 2
    er = -(-(im * n_z * cap) // 16) * 16
    dims = (n_dp, n_z, im, block, cap, er)
    sp, nr, half = n_z * BP, n_dp * er, n_dp // 2
    me, z = lax.axis_index("dp"), lax.axis_index("seq")
    dma, vm = pltpu.SemaphoreType.DMA, pltpu.VMEM

    valid = z * block + jnp.arange(block) < VALID
    lines = jnp.where(valid[None, None, :], jnp.transpose(routes, (0, 2, 1)) + 1, 0)
    lines = jnp.pad(lines, ((0, 0), (0, 6), (0, BP - block)))
    odd = lax.rem(z, 2) == 1
    lines = jnp.concatenate([jnp.where(odd, 0, lines), jnp.where(odd, lines, 0)], axis=-1)
    vec = jnp.concatenate(
        [
            jnp.stack([ln1_gain, ln1_bias, ln2_gain, ln2_bias]),
            jnp.zeros((4, ln1_gain.shape[0]), BF),
            jnp.transpose(w_router),
        ],
        axis=0,
    )
    vec = lax.dynamic_update_slice(jnp.zeros((16, width), BF), vec, (0, me * ln1_gain.shape[0]))
    blocks = (n_z, im, block, width)
    in_any, in_vmem = pl.BlockSpec(memory_space=pl.ANY), pl.BlockSpec(memory_space=pltpu.VMEM)
    mixed, gtok, gqkv, gwo, gsmall, gin, gout = pl.pallas_call(
        functools.partial(block_kernel, dims),
        out_shape=[
            jax.ShapeDtypeStruct((image_count, block, width), BF),
            jax.ShapeDtypeStruct((image_count, block, width), BF),
            jax.ShapeDtypeStruct((64, 1536), F32),
            jax.ShapeDtypeStruct((64, width), F32),
            jax.ShapeDtypeStruct((16, width), F32),
            jax.ShapeDtypeStruct((512, 512), F32),
            jax.ShapeDtypeStruct((512, 512), F32),
        ],
        in_specs=[in_any, in_any, in_vmem, in_any, in_any, in_vmem, in_any, in_any],
        out_specs=[in_any, in_any] + [in_vmem] * 5,
        scratch_shapes=[
            vm(blocks, BF), vm((n_z, im, 8, 128), jnp.int32), vm(blocks, BF), vm((n_dp, 16, width), BF),
            vm((width, 1536), BF), vm((width, width), BF), vm((16, width), F32), vm((im, sp, width), BF),
            vm((im, sp, width), F32), vm((im, sp, width), BF), vm((im, sp, 1536), BF), vm((im, sp, width), BF),
            vm((im, sp, 128), F32), vm((im, 8, sp), F32), vm((im, 8, sp), F32), vm((im, sp, 128), F32),
            vm((n_z, 512, 512), BF), vm((n_z, 512, 512), BF), vm((nr, width), BF), vm((nr, width), BF),
            vm((n_z, nr, 512), BF), vm((n_z, nr, 512), BF), vm((n_dp, er, width), BF),
            vm(blocks, BF), vm((nr, width), BF), vm((im, sp, width), F32), vm((im, sp, 128), F32),
            vm((2, im, sp, width), BF), vm((nr, width), BF), vm((n_z, 2, 512, 512), BF), vm((n_z, 2, 512, 512), BF),
            vm((width, 2048), F32), vm((16, width), F32), vm((width, 2048), BF), vm((half, 64, 2048), BF),
            vm((16, width), F32), vm((half, 64, 2048), BF), vm((half, 64, 2048), BF), vm((half, 16, width), F32),
            vm((n_z, 16, 2048), BF), vm((n_z, 16, 2048), BF), vm((n_z, 16, 2048), BF), vm((n_z, 16, width), F32),
            dma((9,)), dma((n_z,)), dma((n_z,)), dma((n_z,)), dma((n_z,)), dma((n_z,)), dma((n_z,)),
            dma((3, half)), dma((3, n_dp)), dma((3, half)), dma((4,)), dma((n_z,)), dma((4,)), dma((n_z,)),
            dma((n_dp,)), dma((n_dp,)), dma((n_dp,)), dma((n_dp,)), dma((n_dp,)), dma((n_dp,)), dma((n_dp,)), dma((n_dp,)),
            dma((n_z,)), dma((n_z,)), dma((n_z,)), dma((n_z,)),
            dma((n_z, 2)), dma((n_z, 2)), dma((half,)), dma((half,)), dma((1,)), dma((1,)),
            dma((half,)), dma((half,)), dma((half,)), dma((half,)), dma((n_z,)), dma((n_z,)), dma((n_z,)), dma((n_z,)),
            dma((n_z,)), dma((n_z,)),
        ],
        compiler_params=pltpu.CompilerParams(
            collective_id=1, has_side_effects=True, vmem_limit_bytes=VMEM_LIMIT
        ),
        name="block",
    )(tokens, targets, lines, w_qkv, w_out, vec, expert_in[0], expert_out[0])
    whole = pl.BlockSpec(memory_space=pltpu.VMEM)
    mixed, gtok, gqkv, gwo, gin, gout, part = pl.pallas_call(
        finish_kernel,
        out_shape=[
            jax.ShapeDtypeStruct((image_count, block, width), BF),
            jax.ShapeDtypeStruct((image_count, block, width), F32),
            jax.ShapeDtypeStruct((64, 1536), F32),
            jax.ShapeDtypeStruct((64, width), F32),
            jax.ShapeDtypeStruct((512, 512), F32),
            jax.ShapeDtypeStruct((512, 512), F32),
            jax.ShapeDtypeStruct((16, 64), F32),
        ],
        in_specs=[whole] * 7,
        out_specs=[whole] * 7,
        name="finish",
    )(mixed, gtok, gqkv, gwo, gsmall, gin, gout)
    return (
        mixed,
        gtok,
        part[0],
        part[1],
        gqkv,
        gwo,
        part[2],
        part[3],
        jnp.transpose(part[8:16]),
        gin[None],
        gout[None],
    )


def fits(tokens, w_qkv, w_router, expert_in):
    n_dp, n_z = lax.axis_size("dp"), lax.axis_size("seq")
    return (
        n_dp == 8
        and n_z == 4
        and tokens.shape[0] % n_z == 0
        and tokens.shape[1] <= BP
        and tokens.shape[2] == 512
        and w_qkv.shape == (64, 1536)
        and w_router.shape[1] == n_dp
        and expert_in.shape == (1, 512, 512)
    )


def local(*args):
    if fits(args[0], args[3], args[7], args[8]):
        return whole_images(*args)
    return by_heads(*args)


def solution(mesh):
    placed = (
        P("dp", "seq", None),
        P("dp"),
        P("dp"),
        P("dp", None),
        P("dp", None),
        P("dp"),
        P("dp"),
        P("dp", None),
        P("dp", None, "seq"),
        P("dp", "seq", None),
        P("dp", "seq", None),
        P("dp", "seq", None),
    )
    return jax.shard_map(
        local,
        mesh=mesh,
        in_specs=placed,
        out_specs=(
            P("dp", "seq", None),
            P("dp", "seq", None),
            P("dp"),
            P("dp"),
            P("dp", None),
            P("dp", None),
            P("dp"),
            P("dp"),
            P("dp", None),
            P("dp", None, "seq"),
            P("dp", "seq", None),
        ),
        check_vma=False,
    )
```

```python
import functools

import jax
import jax.numpy as jnp
from jax import lax
from jax.experimental import pallas as pl
from jax.experimental.pallas import tpu as pltpu
from jax.sharding import PartitionSpec as P

H = 8
S = 200
VALID = 197


def layer_norm(values, gain_vec, bias_vec):
    centre = values - jnp.mean(values, axis=-1, keepdims=True)
    spread = jnp.mean(centre * centre, axis=-1, keepdims=True)
    return centre * lax.rsqrt(spread + 1e-06) * gain_vec + bias_vec


def regroup_heads(values):
    return lax.all_to_all(values, "seq", split_axis=3, concat_axis=1, tiled=True)


def regroup_slots(values):
    return lax.all_to_all(values, "seq", split_axis=1, concat_axis=3, tiled=True)


def send_experts(values):
    return lax.all_to_all(values, "dp", split_axis=0, concat_axis=1, tiled=True)


def send_tokens(values):
    return lax.all_to_all(values, "dp", split_axis=1, concat_axis=0, tiled=True)


def masked_scores(queries, keys_in, key_valid):
    scores = (
        jnp.einsum("bqhd,bkhd->bhqk", queries, keys_in, preferred_element_type=jnp.float32) * 0.125
    )
    return jnp.where(key_valid, scores, -1e30)


def attention_forward(queries, keys_in, values, key_valid):
    scores = masked_scores(queries, keys_in, key_valid)
    row_top = jnp.max(scores, axis=-1, keepdims=True)
    exponent = jnp.exp(scores - row_top)
    row_total = jnp.sum(exponent, axis=-1, keepdims=True)
    prob_rows = exponent / row_total
    log_total = row_top + jnp.log(row_total)
    attended = jnp.einsum(
        "bhqk,bkhd->bqhd",
        prob_rows.astype(jnp.bfloat16),
        values,
        preferred_element_type=jnp.float32,
    )
    return (attended.astype(jnp.bfloat16), log_total)


def attention_backward(queries, keys_in, values, log_total, grad_attended, key_valid):
    scores = masked_scores(queries, keys_in, key_valid)
    prob_rows = jnp.exp(scores - log_total)
    grad_values = jnp.einsum(
        "bhqk,bqhd->bkhd",
        prob_rows.astype(jnp.bfloat16),
        grad_attended,
        preferred_element_type=jnp.float32,
    )
    grad_probs = jnp.einsum(
        "bqhd,bkhd->bhqk", grad_attended, values, preferred_element_type=jnp.float32
    )
    inner_sum = jnp.sum(prob_rows * grad_probs, axis=-1, keepdims=True)
    grad_scores = (prob_rows * (grad_probs - inner_sum)).astype(jnp.bfloat16)
    grad_queries = (
        jnp.einsum("bhqk,bkhd->bqhd", grad_scores, keys_in, preferred_element_type=jnp.float32)
        * 0.125
    )
    grad_keys = (
        jnp.einsum("bhqk,bqhd->bkhd", grad_scores, queries, preferred_element_type=jnp.float32)
        * 0.125
    )
    return jnp.stack([grad_queries, grad_keys, grad_values], axis=2)


def pick_block(total_rows):
    for candidate in (1024, 768, 512, 384, 256):
        if total_rows % candidate == 0:
            return candidate
    return total_rows


def by_heads(
    tokens,
    ln1_gain,
    ln1_bias,
    w_qkv,
    w_out,
    ln2_gain,
    ln2_bias,
    w_router,
    expert_in,
    expert_out,
    routes,
    targets,
):
    image_count, slot_count, model_width = tokens.shape
    seq_devices = lax.axis_size("seq")
    row_count = image_count * slot_count
    expert_count = w_router.shape[1]
    local_experts = expert_in.shape[0]
    slot_limit = 2 * S // (seq_devices * expert_count) + 2
    head_size = model_width // H
    gathered = (
        lax.all_gather(ln1_gain, "dp", axis=0, tiled=True),
        lax.all_gather(ln1_bias, "dp", axis=0, tiled=True),
        lax.all_gather(w_qkv, "dp", axis=0, tiled=True),
        lax.all_gather(w_out, "dp", axis=0, tiled=True),
        lax.all_gather(ln2_gain, "dp", axis=0, tiled=True),
        lax.all_gather(ln2_bias, "dp", axis=0, tiled=True),
        lax.all_gather(w_router, "dp", axis=0, tiled=True),
    )
    gain_one = gathered[0].astype(jnp.float32)
    bias_one = gathered[1].astype(jnp.float32)
    qkv_weight = gathered[2]
    out_weight = gathered[3]
    gain_two = gathered[4].astype(jnp.float32)
    bias_two = gathered[5].astype(jnp.float32)
    router_weight = gathered[6]
    slot_start = lax.axis_index("seq") * slot_count
    valid_slot = slot_start + jnp.arange(slot_count) < VALID
    valid_rows = jnp.tile(valid_slot, image_count)
    key_valid = (jnp.arange(S) < VALID)[None, None, None, :]
    token_rows = tokens.reshape(row_count, model_width).astype(jnp.float32)
    normed_one, norm_one_back = jax.vjp(layer_norm, token_rows, gain_one, bias_one)
    normed_one_b = normed_one.astype(jnp.bfloat16)
    mixed_qkv = jnp.dot(normed_one_b, qkv_weight, preferred_element_type=jnp.float32).astype(
        jnp.bfloat16
    )
    qkv_heads = regroup_heads(mixed_qkv.reshape(image_count, slot_count, 3, H, head_size))
    queries = qkv_heads[:, :, 0]
    keys_in = qkv_heads[:, :, 1]
    values = qkv_heads[:, :, 2]
    attended, log_total = attention_forward(queries, keys_in, values, key_valid)
    attended_rows = regroup_slots(attended[:, :, None]).reshape(row_count, model_width)
    residual_two = token_rows + jnp.dot(
        attended_rows, out_weight, preferred_element_type=jnp.float32
    )
    normed_two, norm_two_back = jax.vjp(layer_norm, residual_two, gain_two, bias_two)
    normed_two_b = normed_two.astype(jnp.bfloat16)
    logits = jnp.dot(normed_two_b, router_weight, preferred_element_type=jnp.float32)
    route_rows = routes.reshape(row_count, 2)
    chosen = (route_rows[:, :, None] == jnp.arange(expert_count)[None, None, :]) & valid_rows[
        :, None, None
    ]
    chosen_f = chosen.astype(jnp.float32)

    def gate_pick(logit_rows):
        return jnp.sum(jax.nn.softmax(logit_rows, axis=-1)[:, None, :] * chosen_f, axis=-1)

    gate_values, gate_back = jax.vjp(gate_pick, logits)
    pick_count = chosen.astype(jnp.int32).reshape(image_count, slot_count * 2, expert_count)
    before = jnp.cumsum(pick_count, axis=1) - pick_count
    place_hit = (before[..., None] == jnp.arange(slot_limit)) & (pick_count[..., None] > 0)
    dispatch = place_hit.astype(jnp.bfloat16).reshape(
        image_count, slot_count, 2, expert_count, slot_limit
    )
    normed_img = normed_two_b.reshape(image_count, slot_count, model_width)
    sent_rows = jnp.einsum(
        "bskem,bsd->ebmd", dispatch, normed_img, preferred_element_type=jnp.float32
    ).astype(jnp.bfloat16)
    received = send_experts(sent_rows.reshape(expert_count, image_count * slot_limit, model_width))
    weights_in, weights_out = (
        lax.all_gather(expert_in, "seq", axis=2, tiled=True),
        lax.all_gather(expert_out, "seq", axis=1, tiled=True),
    )
    total_rows = received.shape[1]
    block_rows = pick_block(total_rows)
    block_count = total_rows // block_rows

    def expert_step(block_index, produced):
        row_piece = lax.dynamic_slice_in_dim(received, block_index * block_rows, block_rows, 1)
        hidden_pre = jnp.einsum(
            "erd,edf->erf", row_piece, weights_in, preferred_element_type=jnp.float32
        )
        activated = jax.nn.gelu(hidden_pre).astype(jnp.bfloat16)
        result = jnp.einsum(
            "erf,efd->erd", activated, weights_out, preferred_element_type=jnp.float32
        ).astype(jnp.bfloat16)
        return lax.dynamic_update_slice_in_dim(produced, result, block_index * block_rows, 1)

    produced = lax.fori_loop(
        0,
        block_count,
        expert_step,
        jnp.zeros((local_experts, total_rows, model_width), jnp.bfloat16),
    )
    returned = send_tokens(produced).reshape(expert_count, image_count, slot_limit, model_width)
    per_choice = jnp.einsum(
        "bskem,ebmd->bskd", dispatch, returned, preferred_element_type=jnp.float32
    ).reshape(row_count, 2, model_width)
    mixed_rows = (
        residual_two
        + gate_values[:, 0:1] * per_choice[:, 0]
        + gate_values[:, 1:2] * per_choice[:, 1]
    )
    target_rows = targets.reshape(row_count, model_width).astype(jnp.float32)
    grad_mixed = (mixed_rows - target_rows) * valid_rows[:, None].astype(jnp.float32)
    grad_gates = jnp.sum(grad_mixed[:, None, :] * per_choice, axis=-1)
    grad_choice = (
        (gate_values[:, :, None] * grad_mixed[:, None, :])
        .astype(jnp.bfloat16)
        .reshape(image_count, slot_count, 2, model_width)
    )
    grad_sent = jnp.einsum(
        "bskem,bskd->ebmd", dispatch, grad_choice, preferred_element_type=jnp.float32
    ).astype(jnp.bfloat16)
    grad_received = send_experts(
        grad_sent.reshape(expert_count, image_count * slot_limit, model_width)
    )
    back_in, back_out = (
        lax.all_gather(expert_in, "seq", axis=2, tiled=True),
        lax.all_gather(expert_out, "seq", axis=1, tiled=True),
    )

    def expert_back(block_index, loop_carry):
        grad_in_sum, grad_out_sum, grad_rows = loop_carry
        row_piece = lax.dynamic_slice_in_dim(received, block_index * block_rows, block_rows, 1)
        grad_piece = lax.dynamic_slice_in_dim(
            grad_received, block_index * block_rows, block_rows, 1
        )
        hidden_pre = jnp.einsum(
            "erd,edf->erf", row_piece, back_in, preferred_element_type=jnp.float32
        )
        activated, gelu_back = jax.vjp(jax.nn.gelu, hidden_pre)
        grad_act = jnp.einsum(
            "erd,efd->erf", grad_piece, back_out, preferred_element_type=jnp.float32
        )
        grad_pre = gelu_back(grad_act)[0].astype(jnp.bfloat16)
        grad_out_sum = grad_out_sum + jnp.einsum(
            "erf,erd->efd",
            activated.astype(jnp.bfloat16),
            grad_piece,
            preferred_element_type=jnp.float32,
        )
        grad_in_sum = grad_in_sum + jnp.einsum(
            "erd,erf->edf", row_piece, grad_pre, preferred_element_type=jnp.float32
        )
        rows_back = jnp.einsum(
            "erf,edf->erd", grad_pre, back_in, preferred_element_type=jnp.float32
        ).astype(jnp.bfloat16)
        grad_rows = lax.dynamic_update_slice_in_dim(
            grad_rows, rows_back, block_index * block_rows, 1
        )
        return (grad_in_sum, grad_out_sum, grad_rows)

    start_carry = (
        jnp.zeros(back_in.shape, jnp.float32),
        jnp.zeros(back_out.shape, jnp.float32),
        jnp.zeros((local_experts, total_rows, model_width), jnp.bfloat16),
    )
    grad_in_sum, grad_out_sum, grad_rows = lax.fori_loop(0, block_count, expert_back, start_carry)
    grad_returned = send_tokens(grad_rows).reshape(
        expert_count, image_count, slot_limit, model_width
    )
    grad_normed_two = jnp.einsum(
        "bskem,ebmd->bsd", dispatch, grad_returned, preferred_element_type=jnp.float32
    ).reshape(row_count, model_width)
    grad_logits = gate_back(grad_gates)[0].astype(jnp.bfloat16)
    grad_router = jnp.einsum(
        "rd,re->de", normed_two_b, grad_logits, preferred_element_type=jnp.float32
    )
    grad_normed_two = grad_normed_two + jnp.einsum(
        "re,de->rd", grad_logits, router_weight, preferred_element_type=jnp.float32
    )
    grad_res_two, grad_gain_two, grad_bias_two = norm_two_back(grad_normed_two)
    grad_residual = grad_mixed + grad_res_two
    grad_branch = grad_residual.astype(jnp.bfloat16)
    grad_out_weight = jnp.einsum(
        "rd,re->de", attended_rows, grad_branch, preferred_element_type=jnp.float32
    )
    grad_attended = jnp.einsum(
        "re,de->rd", grad_branch, out_weight, preferred_element_type=jnp.float32
    ).astype(jnp.bfloat16)
    grad_heads = regroup_heads(grad_attended.reshape(image_count, slot_count, 1, H, head_size))[
        :, :, 0
    ]
    grad_qkv_heads = attention_backward(
        queries, keys_in, values, log_total, grad_heads, key_valid
    ).astype(jnp.bfloat16)
    grad_qkv_rows = regroup_slots(grad_qkv_heads).reshape(row_count, 3 * model_width)
    grad_qkv_weight = jnp.einsum(
        "rd,rf->df", normed_one_b, grad_qkv_rows, preferred_element_type=jnp.float32
    )
    grad_normed_one = jnp.einsum(
        "rf,df->rd", grad_qkv_rows, qkv_weight, preferred_element_type=jnp.float32
    )
    grad_token_ln, grad_gain_one, grad_bias_one = norm_one_back(grad_normed_one)
    grad_tokens = grad_residual + grad_token_ln
    dense_grads = (
        grad_gain_one,
        grad_bias_one,
        grad_qkv_weight,
        grad_out_weight,
        grad_gain_two,
        grad_bias_two,
        grad_router,
    )
    dense_grads = (
        lax.psum(dense_grads[0].astype(jnp.bfloat16), "seq").astype(jnp.float32),
        lax.psum(dense_grads[1].astype(jnp.bfloat16), "seq").astype(jnp.float32),
        lax.psum(dense_grads[2].astype(jnp.bfloat16), "seq").astype(jnp.float32),
        lax.psum(dense_grads[3].astype(jnp.bfloat16), "seq").astype(jnp.float32),
        lax.psum(dense_grads[4].astype(jnp.bfloat16), "seq").astype(jnp.float32),
        lax.psum(dense_grads[5].astype(jnp.bfloat16), "seq").astype(jnp.float32),
        lax.psum(dense_grads[6].astype(jnp.bfloat16), "seq").astype(jnp.float32),
    )
    dense_grads = (
        lax.psum_scatter(
            dense_grads[0].astype(jnp.bfloat16), "dp", scatter_dimension=0, tiled=True
        ).astype(jnp.float32),
        lax.psum_scatter(
            dense_grads[1].astype(jnp.bfloat16), "dp", scatter_dimension=0, tiled=True
        ).astype(jnp.float32),
        lax.psum_scatter(
            dense_grads[2].astype(jnp.bfloat16), "dp", scatter_dimension=0, tiled=True
        ).astype(jnp.float32),
        lax.psum_scatter(
            dense_grads[3].astype(jnp.bfloat16), "dp", scatter_dimension=0, tiled=True
        ).astype(jnp.float32),
        lax.psum_scatter(
            dense_grads[4].astype(jnp.bfloat16), "dp", scatter_dimension=0, tiled=True
        ).astype(jnp.float32),
        lax.psum_scatter(
            dense_grads[5].astype(jnp.bfloat16), "dp", scatter_dimension=0, tiled=True
        ).astype(jnp.float32),
        lax.psum_scatter(
            dense_grads[6].astype(jnp.bfloat16), "dp", scatter_dimension=0, tiled=True
        ).astype(jnp.float32),
    )
    expert_in_grad, expert_out_grad = (
        lax.psum_scatter(
            grad_in_sum.astype(jnp.bfloat16), "seq", scatter_dimension=2, tiled=True
        ).astype(jnp.float32),
        lax.psum_scatter(
            grad_out_sum.astype(jnp.bfloat16), "seq", scatter_dimension=1, tiled=True
        ).astype(jnp.float32),
    )
    mixed = mixed_rows.astype(jnp.bfloat16).reshape(image_count, slot_count, model_width)
    return (
        mixed,
        grad_tokens.reshape(image_count, slot_count, model_width),
        dense_grads[0],
        dense_grads[1],
        dense_grads[2],
        dense_grads[3],
        dense_grads[4],
        dense_grads[5],
        dense_grads[6],
        expert_in_grad,
        expert_out_grad,
    )


BF = jnp.bfloat16
F32 = jnp.float32
MESH_ID = pl.DeviceIdType.MESH
NEG = -1e30
BP = 64
VMEM_LIMIT = 67000000
GELU_C = 0.7978845608028654
GELU_K = 0.044715


def nn(a, b):
    return lax.dot_general(a, b, (((1,), (0,)), ((), ())), preferred_element_type=F32)


def nt(a, b):
    return lax.dot_general(a, b, (((1,), (1,)), ((), ())), preferred_element_type=F32)


def tn(a, b):
    return lax.dot_general(a, b, (((0,), (0,)), ((), ())), preferred_element_type=F32)


def remote(src, dst, send_sem, recv_sem, dp, z):
    return pltpu.make_async_remote_copy(
        src_ref=src,
        dst_ref=dst,
        send_sem=send_sem,
        recv_sem=recv_sem,
        device_id=(dp, z),
        device_id_type=MESH_ID,
    )


def rows_of(index, size):
    return pl.ds(pl.multiple_of(index * size, size), size)


def norm_parts(x):
    centre = x - jnp.mean(x, axis=-1, keepdims=True)
    scale = lax.rsqrt(jnp.mean(centre * centre, axis=-1, keepdims=True) + 1e-06)
    return centre * scale, scale


def norm_back(grad_hat, hat, scale):
    return scale * (
        grad_hat
        - jnp.mean(grad_hat, axis=-1, keepdims=True)
        - hat * jnp.mean(grad_hat * hat, axis=-1, keepdims=True)
    )


def half_masks():
    lane = lax.broadcasted_iota(jnp.int32, (1, 128), 1)
    low = jnp.where(lane < 64, 1.0, 0.0).astype(BF)
    high = jnp.where(lane < 64, 0.0, 1.0).astype(BF)
    return (low, high)


def slot_ok(position, block):
    return (position % BP < block) & ((position // BP) * block + position % BP < VALID)


def block_kernel(
    dims,
    tok, tgt, rts, wq, wo, vec, win, wout,
    mixed, gtok, gqkv, gwo, gsmall, gin, gout,
    xin, rin, tin, vec_all, wq_all, wo_all, vsum, xpad, x2s, n2s, qkvs, outs, lses, gts, meta, metat,
    win_all, wout_all, recv, ret, acts, slopes, sbuf,
    mbuf, drows, dys, dlogs, dus, dret, dws, arrived,
    gacc, gvec, gbig, crecv, cvec, gsum, hrecv, hvec, zsend, zrecv, zall, zvec,
    loc_sem, tok_ss, tok_rs, rts_ss, rts_rs, tgt_ss, tgt_rs, den_ss, den_rs, fwd_ss, win_ss, win_rs, wout_ss, wout_rs,
    row_ss, row_rs, u_ss, u_rs, du_ss, du_rs, dn_ss, dn_rs, mix_ss, mix_rs, gt_ss, gt_rs,
    r_ss, r_rs, c_ss, c_rs, cv_ss, cv_rs, h_ss, h_rs, hv_ss, hv_rs, za_ss, za_rs, zb_ss, zb_rs, zv_ss, zv_rs,
):
    n_dp, n_z, im, block, cap, er = dims
    me, z = lax.axis_index("dp"), lax.axis_index("seq")
    sp = n_z * BP
    nr = n_dp * er
    two = 2 * er
    half = n_dp // 2
    last = n_z - 1
    core, chip = lax.rem(me, 2), me // 2
    partner = chip * 2 + 1 - core

    barrier = pltpu.get_barrier_semaphore()
    for k in range(1, n_dp):
        pl.semaphore_signal(barrier, inc=1, device_id=(lax.rem(me + k, n_dp), z), device_id_type=MESH_ID)
    for k in range(1, n_z):
        pl.semaphore_signal(barrier, inc=1, device_id=(me, lax.rem(z + k, n_z)), device_id_type=MESH_ID)
    own_copies = [
        pltpu.make_async_copy(tok.at[pl.ds(z * im, im)], xin.at[z], loc_sem.at[0]),
        pltpu.make_async_copy(rts.at[pl.ds(z * im, im)], rin.at[z], loc_sem.at[1]),
        pltpu.make_async_copy(tgt.at[pl.ds(z * im, im)], tin.at[z], loc_sem.at[2]),
        pltpu.make_async_copy(win, win_all.at[z], loc_sem.at[3]),
        pltpu.make_async_copy(wout, wout_all.at[z], loc_sem.at[4]),
        pltpu.make_async_copy(wq, wq_all.at[rows_of(me, 64)], loc_sem.at[5]),
        pltpu.make_async_copy(wo, wo_all.at[rows_of(me, 64)], loc_sem.at[6]),
        pltpu.make_async_copy(vec, vec_all.at[me], loc_sem.at[7]),
    ]
    for copy in own_copies:
        copy.start()
    xpad[...] = jnp.zeros_like(xpad)
    gacc[...] = jnp.zeros_like(gacc)
    gvec[...] = jnp.zeros_like(gvec)
    pl.semaphore_wait(barrier, n_dp + n_z - 2)

    def z_start(source, target, send_sem, recv_sem):
        for k in range(1, n_z):
            peer = lax.rem(z + k, n_z)
            remote(source(peer), target(z), send_sem.at[k], recv_sem.at[z], me, peer).start()

    def z_arrive(target, recv_sem):
        for k in range(1, n_z):
            origin = lax.rem(z + k, n_z)
            remote(target(origin), target(origin), loc_sem.at[8], recv_sem.at[origin], me, z).wait_recv()

    def z_sent(source, send_sem):
        for k in range(1, n_z):
            remote(source(0), source(0), send_sem.at[k], loc_sem.at[8], me, z).wait_send()

    tok_of = lambda peer: tok.at[pl.ds(peer * im, im)]
    rts_of = lambda peer: rts.at[pl.ds(peer * im, im)]
    tgt_of = lambda peer: tgt.at[pl.ds(peer * im, im)]
    z_start(tok_of, lambda i: xin.at[i], tok_ss, tok_rs)
    z_start(rts_of, lambda i: rin.at[i], rts_ss, rts_rs)

    def dense_slot(array, index):
        if array == 0:
            return wq_all.at[rows_of(index, 64)]
        if array == 1:
            return wo_all.at[rows_of(index, 64)]
        return vec_all.at[index]

    dense_in = (wq, wo, vec)
    for array in range(3):
        for k in range(1, half):
            peer = lax.rem(chip + k, half) * 2 + core
            remote(
                dense_in[array], dense_slot(array, me), den_ss.at[array, k], den_rs.at[array, me], peer, z
            ).start()
        remote(
            dense_in[array], dense_slot(array, me), den_ss.at[array, 0], den_rs.at[array, me], partner, z
        ).start()

    experts = ((win, win_all, win_ss, win_rs), (wout, wout_all, wout_ss, wout_rs))
    inner = (z == 1) | (z == last - 1)
    far_end = jnp.where(z < n_z // 2, last, 0)
    near_end = last - far_end
    middle = last - z

    def gather_hop(array, step):
        source, full, send_sem, recv_sem = experts[array]
        for way, there, slot in ((0, z >= step, z - step), (1, z + step < n_z, z + step)):

            @pl.when(there)
            def _():
                at = full.at[slot]
                if step > 0:
                    remote(at, at, send_sem.at[way, step], recv_sem.at[slot], me, z).wait_recv()

                @pl.when((z < last) if way == 0 else (z > 0))
                def _():
                    remote(
                        at if step > 0 else source,
                        at,
                        send_sem.at[way, step],
                        recv_sem.at[slot],
                        me,
                        z + 1 if way == 0 else z - 1,
                    ).start()

    def weights_sent():
        for step in range(n_z - 1):
            for way, there in ((0, (z >= step) & (z < last)), (1, (z + step < n_z) & (z > 0))):

                @pl.when(there)
                def _():
                    for source, full, send_sem, recv_sem in experts:
                        remote(
                            full.at[0], full.at[0], send_sem.at[way, step], recv_sem.at[0], me, z
                        ).wait_send()

    gather_hop(0, 0)
    gather_hop(1, 0)

    for k in range(1, half):
        origin = lax.rem(chip + k, half) * 2 + core
        for array in range(3):
            slot = dense_slot(array, origin)
            remote(slot, slot, den_ss.at[array, 0], den_rs.at[array, origin], me, z).wait_recv()
            remote(slot, slot, fwd_ss.at[array, k], den_rs.at[array, origin], partner, z).start()
    for k in range(half):
        origin = lax.rem(chip + k, half) * 2 + 1 - core
        for array in range(3):
            slot = dense_slot(array, origin)
            remote(slot, slot, den_ss.at[array, 0], den_rs.at[array, origin], me, z).wait_recv()
    for copy in own_copies:
        copy.wait()
    total = vec_all[0].astype(F32)
    for k in range(1, n_dp):
        total = total + vec_all[k].astype(F32)
    vsum[...] = total
    z_arrive(lambda i: xin.at[i], tok_rs)
    z_arrive(lambda i: rin.at[i], rts_rs)

    masks = half_masks()
    keys_ok = slot_ok(lax.broadcasted_iota(jnp.int32, (1, sp), 1), block)
    rows_ok = slot_ok(lax.broadcasted_iota(jnp.int32, (sp, 1), 0), block)
    gain_one, bias_one = vsum[0:1, :], vsum[1:2, :]
    gain_two, bias_two = vsum[2:3, :], vsum[3:4, :]
    router_t = vsum[8:16, :].astype(BF)
    lane_id = lax.broadcasted_iota(jnp.int32, (sp, 128), 1)
    lane_low = lane_id < 64

    def front(i, carry):
        before = lax.broadcasted_iota(jnp.int32, (sp, sp), 0)
        after = lax.broadcasted_iota(jnp.int32, (sp, sp), 1)
        prefix = jnp.where((before < after) & (before // BP == after // BP), 1.0, 0.0).astype(BF)
        expert_id = lax.broadcasted_iota(jnp.int32, (8, sp), 0)
        slot_lane = lax.broadcasted_iota(jnp.int32, (8, sp), 1)
        for b in range(n_z):
            xpad[i, b * BP : b * BP + block, :] = xin[b, i]
        x = xpad[i].astype(F32)
        hat, _ = norm_parts(x)
        normed = (hat * gain_one + bias_one).astype(BF)
        qkvs[i] = nn(normed, wq_all[...]).astype(BF)
        lse_all = jnp.zeros((sp, 128), F32)
        for pair in range(4):
            q2 = qkvs[i, :, pair * 128 : pair * 128 + 128]
            k2 = qkvs[i, :, 512 + pair * 128 : 512 + pair * 128 + 128]
            v2 = qkvs[i, :, 1024 + pair * 128 : 1024 + pair * 128 + 128]
            parts = []
            for side in range(2):
                scores = nt(q2 * masks[side], k2) * 0.125
                scores = jnp.where(keys_ok, scores, NEG)
                top = jnp.max(scores, axis=-1, keepdims=True)
                exponent = jnp.exp(scores - top)
                whole = jnp.sum(exponent, axis=-1, keepdims=True)
                lse_all = jnp.where(lane_id == pair * 2 + side, top + jnp.log(whole), lse_all)
                parts.append(nn((exponent / whole).astype(BF), v2))
            outs[i, :, pair * 128 : pair * 128 + 128] = jnp.where(lane_low, parts[0], parts[1]).astype(BF)
        lses[i] = lse_all
        x2 = x + nn(outs[i], wo_all[...])
        x2s[i] = x2
        hat2, _ = norm_parts(x2)
        n2 = (hat2 * gain_two + bias_two).astype(BF)
        n2s[i] = n2
        logits = nt(router_t, n2)
        raised = jnp.exp(logits - jnp.max(logits, axis=0, keepdims=True))
        share = raised / jnp.sum(raised, axis=0, keepdims=True)
        gts[i] = share
        wide = jnp.concatenate([rin[0, i] + rin[1, i], rin[2, i] + rin[3, i]], axis=1)
        hits = [(expert_id + 1) == wide[j : j + 1, :] for j in range(2)]
        any_hit = jnp.where(hits[0] | hits[1], 1.0, 0.0)
        place = nn(any_hit.astype(BF), prefix)
        base = place + (expert_id * er + (slot_lane // BP) * cap + i * (n_z * cap) + 1).astype(F32)
        lines = [jnp.sum(jnp.where(hit, base, 0.0), axis=0, keepdims=True) - 1.0 for hit in hits]
        lines += [jnp.sum(jnp.where(hit, share, 0.0), axis=0, keepdims=True) for hit in hits]
        table = jnp.concatenate(lines + [jnp.zeros((124, sp), F32)], axis=0)
        meta[i] = table[0:8]
        metat[i] = jnp.transpose(table)

        @pl.when(i == im - 2)
        def _():
            gather_hop(0, 1)

        return carry

    lax.fori_loop(0, im, front, 0)

    row_id = lax.broadcasted_iota(jnp.int32, (er, sp), 0)

    def to_experts(product, target, send_sem, recv_sem):
        def step(s, carry):
            j, c = lax.rem(s // 2 + 1, half), lax.rem(s, 2)
            index = 2 * j + c
            peer = lax.rem(chip + j, half) * 2 + lax.rem(core + c, 2)
            sbuf[index] = product(peer).astype(BF)

            @pl.when(index > 0)
            def _():
                remote(
                    sbuf.at[index], target.at[rows_of(me, er)], send_sem.at[index], recv_sem.at[me], peer, z
                ).start()

            @pl.when(index == 0)
            def _():
                target[rows_of(me, er)] = sbuf[index]

            return carry

        lax.fori_loop(0, n_dp, step, 0)

    def to_tokens(product, target, send_sem, recv_sem):
        def step(s, carry):
            j = lax.rem(s + 1, half)
            part = lax.rem(chip + j, half)
            out = product(part).astype(BF)
            sbuf[2 * j] = out[0:er]
            sbuf[2 * j + 1] = out[er:two]

            @pl.when(j > 0)
            def _():
                for c in range(2):
                    remote(
                        sbuf.at[2 * j + c],
                        target.at[rows_of(me, er)],
                        send_sem.at[2 * j + c],
                        recv_sem.at[me],
                        part * 2 + c,
                        z,
                    ).start()

            @pl.when(j == 0)
            def _():
                target[rows_of(me, er)] = sbuf[core]
                remote(
                    sbuf.at[1 - core], target.at[rows_of(me, er)], send_sem.at[1], recv_sem.at[me], partner, z
                ).start()

            return carry

        lax.fori_loop(0, half, step, 0)

    def dp_arrive(target, recv_sem):
        for k in range(1, n_dp):
            origin = lax.rem(me + k, n_dp)
            spot = target.at[rows_of(origin, er)]
            remote(spot, spot, loc_sem.at[8], recv_sem.at[origin], me, z).wait_recv()

    def dp_sent(send_sem):
        for k in range(1, n_dp):
            remote(sbuf.at[0], sbuf.at[0], send_sem.at[k], loc_sem.at[8], me, z).wait_send()

    def tokens_for(peer):
        want = (row_id + peer * er).astype(F32)
        total = jnp.zeros((er, 512), F32)
        for i in range(im):
            pick = (want == meta[i, 0:1, :]) | (want == meta[i, 1:2, :])
            total = total + nn(jnp.where(pick, 1.0, 0.0).astype(BF), n2s[i])
        return total

    to_experts(tokens_for, recv, row_ss, row_rs)

    def hidden(shard):
        def part_step(part, carry):
            at = rows_of(part, two)
            x = recv[at]
            for side in range(2):
                pre = nn(x, win_all[shard, :, side * 256 : side * 256 + 256])
                square = pre * pre
                tanh = jnp.tanh(pre * (GELU_C + (GELU_C * GELU_K) * square))
                gate = 0.5 + 0.5 * tanh
                acts[shard, at, side * 256 : side * 256 + 256] = (pre * gate).astype(BF)
                slope = gate + pre * (0.5 - 0.5 * tanh * tanh) * (GELU_C + (3.0 * GELU_C * GELU_K) * square)
                slopes[shard, at, side * 256 : side * 256 + 256] = slope.astype(BF)
            return carry

        lax.fori_loop(0, n_dp // 2, part_step, 0)

    def hidden_step(s, carry):
        for at_step, hop in ((1, 2), (3, 3)):

            @pl.when(s == at_step)
            def _():
                gather_hop(0, hop)

        for way in range(2):
            shard = z - s if way == 0 else z + s

            @pl.when((shard >= 0) & (shard < n_z) & ((s > 0) | (way == 0)))
            def _():
                hidden(shard)

        @pl.when(s == 1)
        def _():
            gather_hop(1, 2)

        return carry

    gather_hop(1, 1)
    dp_arrive(recv, row_rs)
    dp_sent(row_ss)
    lax.fori_loop(0, n_z, hidden_step, 0)
    gather_hop(1, 3)

    z_start(tgt_of, lambda i: tin.at[i], tgt_ss, tgt_rs)

    def results_for(part):
        total = jnp.zeros((two, 512), F32)
        for shard in range(n_z):
            total = total + nn(acts[shard, rows_of(part, two)], wout_all[shard])
        return total

    to_tokens(results_for, ret, u_ss, u_rs)

    z_arrive(lambda i: tin.at[i], tgt_rs)
    for b in range(n_z):
        for i in range(im):
            dys[i, b * BP : b * BP + block, :] = tin[b, i].astype(F32)
    dp_arrive(ret, u_rs)

    def mix(i, carry):
        line = lax.broadcasted_iota(jnp.int32, (sp, nr), 1).astype(F32)
        cols = metat[i]
        picked = []
        for j in range(2):
            pick = jnp.where(line == cols[:, j : j + 1], 1.0, 0.0).astype(BF)
            picked.append(nn(pick, ret[...]))
        mix = x2s[i] + cols[:, 2:3] * picked[0] + cols[:, 3:4] * picked[1]
        mix_b = mix.astype(BF)
        for b in range(n_z):
            mbuf[b, i] = mix_b[b * BP : b * BP + block]
        dy = jnp.where(rows_ok, mix - dys[i], 0.0)
        dys[i] = dy
        dus[0, i] = (cols[:, 2:3] * dy).astype(BF)
        dus[1, i] = (cols[:, 3:4] * dy).astype(BF)
        dlogs[i] = jnp.where(
            lane_id == 0, jnp.sum(dy * picked[0], axis=-1, keepdims=True), 0.0
        ) + jnp.where(lane_id == 1, jnp.sum(dy * picked[1], axis=-1, keepdims=True), 0.0)
        return carry

    lax.fori_loop(0, im, mix, 0)
    dp_sent(u_ss)

    def gradients_for(peer):
        want = (row_id + peer * er).astype(F32)
        total = jnp.zeros((er, 512), F32)
        for i in range(im):
            for j in range(2):
                pick = jnp.where(want == meta[i, j : j + 1, :], 1.0, 0.0).astype(BF)
                total = total + nn(pick, dus[j, i])
        return total

    to_experts(gradients_for, drows, du_ss, du_rs)
    z_start(lambda peer: mbuf.at[peer], lambda i: mixed.at[pl.ds(i * im, im)], mix_ss, mix_rs)
    own_mixed = pltpu.make_async_copy(mbuf.at[z], mixed.at[pl.ds(z * im, im)], loc_sem.at[0])
    own_mixed.start()
    expert_row = lax.broadcasted_iota(jnp.int32, (8, sp), 0).astype(F32)
    for i in range(im):
        flat = jnp.transpose(dlogs[i])
        share = gts[i]
        grad = jnp.zeros((8, sp), F32)
        for j in range(2):
            at = meta[i, j : j + 1, :]
            inside = (at >= expert_row * er) & (at < expert_row * er + er)
            grad = grad + jnp.where(inside, flat[j : j + 1, :], 0.0)
        dlog = share * (grad - jnp.sum(share * grad, axis=0, keepdims=True))
        gts[i] = dlog
        gvec[8:16, :] += nn(dlog.astype(BF), n2s[i])
    dp_arrive(drows, du_rs)
    dp_sent(du_ss)

    def reduce_start(target, piece):
        peer = jnp.where(z == 0, 1, last - 1)
        slot = jnp.where(target == peer, 0, jnp.where(target == far_end, 2, 1))
        remote(
            dws.at[target, piece], arrived.at[slot, piece], r_ss.at[target, piece], r_rs.at[slot, piece], me, peer
        ).start()

    def reduce_forward(piece, steps):
        @pl.when(inner)
        def _():
            for target, slot, peer, there in steps:
                here = arrived.at[slot, piece]
                remote(here, here, r_ss.at[target, piece], r_rs.at[slot, piece], me, z).wait_recv()

                def add(c, carry):
                    at = rows_of(c, 128)
                    dws[target, piece, at] = (
                        dws[target, piece, at].astype(F32) + arrived[slot, piece, at].astype(F32)
                    ).astype(BF)
                    return carry

                lax.fori_loop(0, 4, add, 0)
                remote(
                    dws.at[target, piece],
                    arrived.at[there, piece],
                    r_ss.at[target, piece],
                    r_rs.at[there, piece],
                    me,
                    peer,
                ).start()

    first_steps = ((far_end, 2, middle, 4),)
    second_steps = ((middle, 1, middle, 3), (near_end, 4, near_end, 0))

    def owner(s):
        return jnp.where(z < n_z // 2, lax.rem(z + 2 * n_z - 1 - s, n_z), lax.rem(z + 1 + s, n_z))

    def out_grads(s, carry):
        target = owner(s)
        dws[target, 0] = tn(acts[target], drows[...]).astype(BF)

        @pl.when(jnp.logical_not(inner) & (s < 2))
        def _():
            reduce_start(target, 0)

        return carry

    def in_grads(s, carry):
        target = owner(s)
        dws[target, 1] = tn(recv[...], slopes[target]).astype(BF)

        @pl.when(jnp.logical_not(inner) & (s < 2))
        def _():
            reduce_start(target, 1)

        return carry

    lax.fori_loop(0, n_z, out_grads, 0)

    def input_grads_for(part):
        at = rows_of(part, two)
        du = drows[at]
        total = jnp.zeros((two, 512), F32)
        for shard in range(n_z):
            dpre = (nt(du, wout_all[shard]) * slopes[shard, at].astype(F32)).astype(BF)
            slopes[shard, at] = dpre
            total = total + nt(dpre, win_all[shard])
        return total

    to_tokens(input_grads_for, dret, dn_ss, dn_rs)
    lax.fori_loop(0, n_z, in_grads, 0)

    @pl.when(jnp.logical_not(inner))
    def _():
        reduce_start(owner(2), 0)
        reduce_start(owner(2), 1)

    reduce_forward(0, first_steps)
    own_mixed.wait()
    z_sent(lambda peer: mbuf.at[peer], mix_ss)
    dp_arrive(dret, dn_rs)
    reduce_forward(0, second_steps)

    def back(i, carry):
        line = lax.broadcasted_iota(jnp.int32, (sp, nr), 1).astype(F32)
        cols = metat[i]
        pick = jnp.where((line == cols[:, 0:1]) | (line == cols[:, 1:2]), 1.0, 0.0).astype(BF)
        dn2 = nn(pick, dret[...]) + tn(gts[i].astype(BF), router_t)
        hat2, scale2 = norm_parts(x2s[i])
        gvec[2:3, :] += jnp.sum(dn2 * hat2, axis=0, keepdims=True)
        gvec[3:4, :] += jnp.sum(dn2, axis=0, keepdims=True)
        dx2 = dys[i] + norm_back(dn2 * gain_two, hat2, scale2)
        da = dx2.astype(BF)
        gacc[:, 1536:2048] += tn(outs[i], da)
        do = nt(da, wo_all[...]).astype(BF)
        hat1, scale1 = norm_parts(xpad[i].astype(F32))
        n1 = (hat1 * gain_one + bias_one).astype(BF)
        dn1 = jnp.zeros((sp, 512), F32)
        for pair in range(4):
            at = pair * 128
            q2 = qkvs[i, :, at : at + 128]
            k2 = qkvs[i, :, 512 + at : 512 + at + 128]
            v2 = qkvs[i, :, 1024 + at : 1024 + at + 128]
            do2 = do[:, at : at + 128]
            grads = ([], [], [])
            for side in range(2):
                head = pair * 2 + side
                scores = nt(q2 * masks[side], k2) * 0.125
                scores = jnp.where(keys_ok, scores, NEG)
                prob = jnp.exp(scores - lses[i, :, head : head + 1])
                dprob = nt(do2 * masks[side], v2)
                inner = jnp.sum(prob * dprob, axis=-1, keepdims=True)
                ds = (prob * (dprob - inner)).astype(BF)
                grads[0].append(nn(ds, k2))
                grads[1].append(tn(ds, q2))
                grads[2].append(tn(prob.astype(BF), do2))
            for part in range(3):
                grad = jnp.where(lane_low, grads[part][0], grads[part][1])
                if part < 2:
                    grad = grad * 0.125
                grad = grad.astype(BF)
                col = part * 512 + at
                gacc[:, col : col + 128] += tn(n1, grad)
                dn1 = dn1 + nt(grad, wq_all[:, col : col + 128])
        gvec[0:1, :] += jnp.sum(dn1 * hat1, axis=0, keepdims=True)
        gvec[1:2, :] += jnp.sum(dn1, axis=0, keepdims=True)
        dx = (dx2 + norm_back(dn1 * gain_one, hat1, scale1)).astype(BF)
        for b in range(n_z):
            mbuf[b, i] = dx[b * BP : b * BP + block]

        @pl.when(i == im - 2)
        def _():
            reduce_forward(1, first_steps)

        return carry

    lax.fori_loop(0, im, back, 0)

    gbig[...] = gacc[...].astype(BF)
    for q in range(half):
        remote(
            gbig.at[rows_of(2 * q + 1 - core, 64)], crecv.at[q], c_ss.at[q], c_rs.at[q], partner, z
        ).start()
    remote(gvec, cvec, cv_ss.at[0], cv_rs.at[0], partner, z).start()
    for q in range(half):
        remote(crecv.at[q], crecv.at[q], c_ss.at[q], c_rs.at[q], me, z).wait_recv()
    for k in range(1, half):
        q = lax.rem(chip + k, half)
        gsum[q] = (gacc[rows_of(2 * q + core, 64)] + crecv[q].astype(F32)).astype(BF)
        remote(gsum.at[q], hrecv.at[chip], h_ss.at[k], h_rs.at[chip], q * 2 + core, z).start()
    remote(cvec, cvec, cv_ss.at[0], cv_rs.at[0], me, z).wait_recv()
    hvec[chip] = gvec[...] + cvec[...]
    for k in range(1, half):
        q = lax.rem(chip + k, half)
        remote(hvec.at[chip], hvec.at[chip], hv_ss.at[k], hv_rs.at[chip], q * 2 + core, z).start()
    reduce_forward(1, second_steps)
    dense = gacc[rows_of(me, 64)] + crecv[chip].astype(F32)
    for k in range(1, half):
        q = lax.rem(chip + k, half)
        remote(hrecv.at[q], hrecv.at[q], h_ss.at[0], h_rs.at[q], me, z).wait_recv()
        dense = dense + hrecv[q].astype(F32)
    for h in range(2):
        zsend[h] = dense[h * 32 : h * 32 + 32].astype(BF)

        @pl.when(z == h + 1)
        def _():
            zrecv[z] = zsend[h]

        @pl.when(z != h + 1)
        def _():
            remote(zsend.at[h], zrecv.at[z], za_ss.at[h], za_rs.at[z], me, h + 1).start()

    for k in range(1, half):
        q = lax.rem(chip + k, half)
        remote(hvec.at[q], hvec.at[q], hv_ss.at[0], hv_rs.at[q], me, z).wait_recv()
    zvec[z] = hvec[0] + hvec[1] + hvec[2] + hvec[3]

    @pl.when(z != 1)
    def _():
        remote(zvec.at[z], zvec.at[z], zv_ss.at[0], zv_rs.at[z], me, 1).start()

    z_start(lambda peer: mbuf.at[peer], lambda i: gtok.at[pl.ds(i * im, im)], gt_ss, gt_rs)
    own_gtok = pltpu.make_async_copy(mbuf.at[z], gtok.at[pl.ds(z * im, im)], loc_sem.at[1])
    own_gtok.start()

    for piece, out in ((0, gout), (1, gin)):
        for slot, there in ((0, z >= 0), (3, inner)):

            @pl.when(there)
            def _():
                here = arrived.at[slot, piece]
                remote(here, here, r_ss.at[0, piece], r_rs.at[slot, piece], me, z).wait_recv()

        def finish(c, carry):
            at = rows_of(c, 128)
            out[at] = (
                dws[z, piece, at].astype(F32)
                + arrived[0, piece, at].astype(F32)
                + jnp.where(inner, arrived[3, piece, at].astype(F32), 0.0)
            )
            return carry

        lax.fori_loop(0, 4, finish, 0)
    for h in range(2):

        @pl.when(z == h + 1)
        def _():
            z_arrive(lambda i: zrecv.at[i], za_rs)
            total = zrecv[0].astype(F32)
            for k in range(1, n_z):
                total = total + zrecv[k].astype(F32)
            zall[h] = total.astype(BF)
            for k in range(1, n_z):
                peer = lax.rem(z + k, n_z)
                remote(zall.at[h], zall.at[h], zb_ss.at[k], zb_rs.at[h], me, peer).start()

    @pl.when(z == 1)
    def _():
        z_arrive(lambda i: zvec.at[i], zv_rs)
        gsmall[...] = zvec[0] + zvec[1] + zvec[2] + zvec[3]
        zvec[n_z] = gsmall[...]
        for k in range(1, n_z):
            peer = lax.rem(z + k, n_z)
            remote(zvec.at[n_z], zvec.at[n_z], zv_ss.at[k], zv_rs.at[n_z], me, peer).start()

    @pl.when(z != 1)
    def _():
        remote(zvec.at[n_z], zvec.at[n_z], zv_ss.at[0], zv_rs.at[n_z], me, z).wait_recv()
        gsmall[...] = zvec[n_z]

    for h in range(2):

        @pl.when(z != h + 1)
        def _():
            remote(zall.at[h], zall.at[h], zb_ss.at[0], zb_rs.at[h], me, z).wait_recv()

        piece = zall[h].astype(F32)
        gqkv[h * 32 : h * 32 + 32] = piece[:, 0:1536]
        gwo[h * 32 : h * 32 + 32] = piece[:, 1536:2048]
    own_gtok.wait()
    z_arrive(lambda i: gtok.at[pl.ds(i * im, im)], gt_rs)
    z_arrive(lambda i: mixed.at[pl.ds(i * im, im)], mix_rs)

    z_sent(lambda peer: xin.at[peer], tok_ss)
    z_sent(lambda peer: rin.at[peer], rts_ss)
    z_sent(lambda peer: tin.at[peer], tgt_ss)
    z_sent(lambda peer: mbuf.at[peer], gt_ss)
    for h in range(2):

        @pl.when(z != h + 1)
        def _():
            remote(zsend.at[h], zsend.at[h], za_ss.at[h], loc_sem.at[8], me, z).wait_send()

        @pl.when(z == h + 1)
        def _():
            z_sent(lambda peer: zall.at[0], zb_ss)

    @pl.when(z == 1)
    def _():
        z_sent(lambda peer: zvec.at[0], zv_ss)

    @pl.when(z != 1)
    def _():
        remote(zvec.at[0], zvec.at[0], zv_ss.at[0], loc_sem.at[8], me, z).wait_send()

    dp_sent(dn_ss)
    weights_sent()
    for array in range(3):
        slot = dense_slot(array, 0)
        for k in range(half):
            remote(slot, slot, den_ss.at[array, k], loc_sem.at[8], me, z).wait_send()
        for k in range(1, half):
            remote(slot, slot, fwd_ss.at[array, k], loc_sem.at[8], me, z).wait_send()
    for piece in range(2):
        for target in range(n_z):
            here = dws.at[0, 0]

            @pl.when(z != target)
            def _():
                remote(here, here, r_ss.at[target, piece], loc_sem.at[8], me, z).wait_send()

    for q in range(half):
        remote(crecv.at[q], crecv.at[q], c_ss.at[q], loc_sem.at[8], me, z).wait_send()
    remote(cvec, cvec, cv_ss.at[0], loc_sem.at[8], me, z).wait_send()
    for k in range(1, half):
        remote(gsum.at[0], gsum.at[0], h_ss.at[k], loc_sem.at[8], me, z).wait_send()
        remote(cvec, cvec, hv_ss.at[k], loc_sem.at[8], me, z).wait_send()


def finish_kernel(mixed, gtok, gqkv, gwo, gsmall, gin, gout, *outs):
    me = lax.axis_index("dp")
    outs[0][...] = mixed[...]
    outs[1][...] = gtok[...].astype(F32)
    for source, target in ((gqkv, outs[2]), (gwo, outs[3]), (gin, outs[4]), (gout, outs[5])):
        target[...] = source[...]
    lanes = gsmall[:, pl.ds(pl.multiple_of((me // 2) * 128, 128), 128)]
    lanes = jnp.where(lax.rem(me, 2) == 1, pltpu.roll(lanes, 64, 1), lanes)
    outs[6][...] = lanes[:, 0:64]


def whole_images(
    tokens, ln1_gain, ln1_bias, w_qkv, w_out, ln2_gain, ln2_bias, w_router, expert_in, expert_out, routes, targets
):
    n_dp, n_z = lax.axis_size("dp"), lax.axis_size("seq")
    image_count, block, width = tokens.shape
    im = image_count // n_z
    cap = 2 * S // (n_z * w_router.shape[1]) + 2
    er = -(-(im * n_z * cap) // 16) * 16
    dims = (n_dp, n_z, im, block, cap, er)
    sp, nr, half = n_z * BP, n_dp * er, n_dp // 2
    me, z = lax.axis_index("dp"), lax.axis_index("seq")
    dma, vm = pltpu.SemaphoreType.DMA, pltpu.VMEM

    valid = z * block + jnp.arange(block) < VALID
    lines = jnp.where(valid[None, None, :], jnp.transpose(routes, (0, 2, 1)) + 1, 0)
    lines = jnp.pad(lines, ((0, 0), (0, 6), (0, BP - block)))
    odd = lax.rem(z, 2) == 1
    lines = jnp.concatenate([jnp.where(odd, 0, lines), jnp.where(odd, lines, 0)], axis=-1)
    vec = jnp.concatenate(
        [
            jnp.stack([ln1_gain, ln1_bias, ln2_gain, ln2_bias]),
            jnp.zeros((4, ln1_gain.shape[0]), BF),
            jnp.transpose(w_router),
        ],
        axis=0,
    )
    vec = lax.dynamic_update_slice(jnp.zeros((16, width), BF), vec, (0, me * ln1_gain.shape[0]))
    blocks = (n_z, im, block, width)
    in_any, in_vmem = pl.BlockSpec(memory_space=pl.ANY), pl.BlockSpec(memory_space=pltpu.VMEM)
    mixed, gtok, gqkv, gwo, gsmall, gin, gout = pl.pallas_call(
        functools.partial(block_kernel, dims),
        out_shape=[
            jax.ShapeDtypeStruct((image_count, block, width), BF),
            jax.ShapeDtypeStruct((image_count, block, width), BF),
            jax.ShapeDtypeStruct((64, 1536), F32),
            jax.ShapeDtypeStruct((64, width), F32),
            jax.ShapeDtypeStruct((16, width), F32),
            jax.ShapeDtypeStruct((512, 512), F32),
            jax.ShapeDtypeStruct((512, 512), F32),
        ],
        in_specs=[in_any, in_any, in_vmem, in_any, in_any, in_vmem, in_any, in_any],
        out_specs=[in_any, in_any] + [in_vmem] * 5,
        scratch_shapes=[
            vm(blocks, BF), vm((n_z, im, 8, 128), jnp.int32), vm(blocks, BF), vm((n_dp, 16, width), BF),
            vm((width, 1536), BF), vm((width, width), BF), vm((16, width), F32), vm((im, sp, width), BF),
            vm((im, sp, width), F32), vm((im, sp, width), BF), vm((im, sp, 1536), BF), vm((im, sp, width), BF),
            vm((im, sp, 128), F32), vm((im, 8, sp), F32), vm((im, 8, sp), F32), vm((im, sp, 128), F32),
            vm((n_z, 512, 512), BF), vm((n_z, 512, 512), BF), vm((nr, width), BF), vm((nr, width), BF),
            vm((n_z, nr, 512), BF), vm((n_z, nr, 512), BF), vm((n_dp, er, width), BF),
            vm(blocks, BF), vm((nr, width), BF), vm((im, sp, width), F32), vm((im, sp, 128), F32),
            vm((2, im, sp, width), BF), vm((nr, width), BF), vm((n_z, 2, 512, 512), BF), vm((5, 2, 512, 512), BF),
            vm((width, 2048), F32), vm((16, width), F32), vm((width, 2048), BF), vm((half, 64, 2048), BF),
            vm((16, width), F32), vm((half, 64, 2048), BF), vm((half, 64, 2048), BF), vm((half, 16, width), F32),
            vm((2, 32, 2048), BF), vm((n_z, 32, 2048), BF), vm((2, 32, 2048), BF), vm((n_z + 1, 16, width), F32),
            dma((9,)), dma((n_z,)), dma((n_z,)), dma((n_z,)), dma((n_z,)), dma((n_z,)), dma((n_z,)),
            dma((3, half)), dma((3, n_dp)), dma((3, half)), dma((2, n_z)), dma((n_z,)), dma((2, n_z)), dma((n_z,)),
            dma((n_dp,)), dma((n_dp,)), dma((n_dp,)), dma((n_dp,)), dma((n_dp,)), dma((n_dp,)), dma((n_dp,)), dma((n_dp,)),
            dma((n_z,)), dma((n_z,)), dma((n_z,)), dma((n_z,)),
            dma((n_z, 2)), dma((5, 2)), dma((half,)), dma((half,)), dma((1,)), dma((1,)),
            dma((half,)), dma((half,)), dma((half,)), dma((half,)), dma((2,)), dma((n_z,)), dma((n_z,)), dma((2,)),
            dma((n_z,)), dma((n_z + 1,)),
        ],
        compiler_params=pltpu.CompilerParams(
            collective_id=1, has_side_effects=True, vmem_limit_bytes=VMEM_LIMIT
        ),
        name="block",
    )(tokens, targets, lines, w_qkv, w_out, vec, expert_in[0], expert_out[0])
    whole = pl.BlockSpec(memory_space=pltpu.VMEM)
    mixed, gtok, gqkv, gwo, gin, gout, part = pl.pallas_call(
        finish_kernel,
        out_shape=[
            jax.ShapeDtypeStruct((image_count, block, width), BF),
            jax.ShapeDtypeStruct((image_count, block, width), F32),
            jax.ShapeDtypeStruct((64, 1536), F32),
            jax.ShapeDtypeStruct((64, width), F32),
            jax.ShapeDtypeStruct((512, 512), F32),
            jax.ShapeDtypeStruct((512, 512), F32),
            jax.ShapeDtypeStruct((16, 64), F32),
        ],
        in_specs=[whole] * 7,
        out_specs=[whole] * 7,
        name="finish",
    )(mixed, gtok, gqkv, gwo, gsmall, gin, gout)
    return (
        mixed,
        gtok,
        part[0],
        part[1],
        gqkv,
        gwo,
        part[2],
        part[3],
        jnp.transpose(part[8:16]),
        gin[None],
        gout[None],
    )


def fits(tokens, w_qkv, w_router, expert_in):
    n_dp, n_z = lax.axis_size("dp"), lax.axis_size("seq")
    return (
        n_dp == 8
        and n_z == 4
        and tokens.shape[0] % n_z == 0
        and tokens.shape[1] <= BP
        and tokens.shape[2] == 512
        and w_qkv.shape == (64, 1536)
        and w_router.shape[1] == n_dp
        and expert_in.shape == (1, 512, 512)
    )


def local(*args):
    if fits(args[0], args[3], args[7], args[8]):
        return whole_images(*args)
    return by_heads(*args)


def solution(mesh):
    placed = (
        P("dp", "seq", None),
        P("dp"),
        P("dp"),
        P("dp", None),
        P("dp", None),
        P("dp"),
        P("dp"),
        P("dp", None),
        P("dp", None, "seq"),
        P("dp", "seq", None),
        P("dp", "seq", None),
        P("dp", "seq", None),
    )
    return jax.shard_map(
        local,
        mesh=mesh,
        in_specs=placed,
        out_specs=(
            P("dp", "seq", None),
            P("dp", "seq", None),
            P("dp"),
            P("dp"),
            P("dp", None),
            P("dp", None),
            P("dp"),
            P("dp"),
            P("dp", None),
            P("dp", None, "seq"),
            P("dp", "seq", None),
        ),
        check_vma=False,
    )
```

```python
import functools

import jax
import jax.numpy as jnp
from jax import lax
from jax.experimental import pallas as pl
from jax.experimental.pallas import tpu as pltpu
from jax.sharding import PartitionSpec as P

H = 8
S = 200
VALID = 197


def layer_norm(values, gain_vec, bias_vec):
    centre = values - jnp.mean(values, axis=-1, keepdims=True)
    spread = jnp.mean(centre * centre, axis=-1, keepdims=True)
    return centre * lax.rsqrt(spread + 1e-06) * gain_vec + bias_vec


def regroup_heads(values):
    return lax.all_to_all(values, "seq", split_axis=3, concat_axis=1, tiled=True)


def regroup_slots(values):
    return lax.all_to_all(values, "seq", split_axis=1, concat_axis=3, tiled=True)


def send_experts(values):
    return lax.all_to_all(values, "dp", split_axis=0, concat_axis=1, tiled=True)


def send_tokens(values):
    return lax.all_to_all(values, "dp", split_axis=1, concat_axis=0, tiled=True)


def masked_scores(queries, keys_in, key_valid):
    scores = (
        jnp.einsum("bqhd,bkhd->bhqk", queries, keys_in, preferred_element_type=jnp.float32) * 0.125
    )
    return jnp.where(key_valid, scores, -1e30)


def attention_forward(queries, keys_in, values, key_valid):
    scores = masked_scores(queries, keys_in, key_valid)
    row_top = jnp.max(scores, axis=-1, keepdims=True)
    exponent = jnp.exp(scores - row_top)
    row_total = jnp.sum(exponent, axis=-1, keepdims=True)
    prob_rows = exponent / row_total
    log_total = row_top + jnp.log(row_total)
    attended = jnp.einsum(
        "bhqk,bkhd->bqhd",
        prob_rows.astype(jnp.bfloat16),
        values,
        preferred_element_type=jnp.float32,
    )
    return (attended.astype(jnp.bfloat16), log_total)


def attention_backward(queries, keys_in, values, log_total, grad_attended, key_valid):
    scores = masked_scores(queries, keys_in, key_valid)
    prob_rows = jnp.exp(scores - log_total)
    grad_values = jnp.einsum(
        "bhqk,bqhd->bkhd",
        prob_rows.astype(jnp.bfloat16),
        grad_attended,
        preferred_element_type=jnp.float32,
    )
    grad_probs = jnp.einsum(
        "bqhd,bkhd->bhqk", grad_attended, values, preferred_element_type=jnp.float32
    )
    inner_sum = jnp.sum(prob_rows * grad_probs, axis=-1, keepdims=True)
    grad_scores = (prob_rows * (grad_probs - inner_sum)).astype(jnp.bfloat16)
    grad_queries = (
        jnp.einsum("bhqk,bkhd->bqhd", grad_scores, keys_in, preferred_element_type=jnp.float32)
        * 0.125
    )
    grad_keys = (
        jnp.einsum("bhqk,bqhd->bkhd", grad_scores, queries, preferred_element_type=jnp.float32)
        * 0.125
    )
    return jnp.stack([grad_queries, grad_keys, grad_values], axis=2)


def pick_block(total_rows):
    for candidate in (1024, 768, 512, 384, 256):
        if total_rows % candidate == 0:
            return candidate
    return total_rows


def by_heads(
    tokens,
    ln1_gain,
    ln1_bias,
    w_qkv,
    w_out,
    ln2_gain,
    ln2_bias,
    w_router,
    expert_in,
    expert_out,
    routes,
    targets,
):
    image_count, slot_count, model_width = tokens.shape
    seq_devices = lax.axis_size("seq")
    row_count = image_count * slot_count
    expert_count = w_router.shape[1]
    local_experts = expert_in.shape[0]
    slot_limit = 2 * S // (seq_devices * expert_count) + 2
    head_size = model_width // H
    gathered = (
        lax.all_gather(ln1_gain, "dp", axis=0, tiled=True),
        lax.all_gather(ln1_bias, "dp", axis=0, tiled=True),
        lax.all_gather(w_qkv, "dp", axis=0, tiled=True),
        lax.all_gather(w_out, "dp", axis=0, tiled=True),
        lax.all_gather(ln2_gain, "dp", axis=0, tiled=True),
        lax.all_gather(ln2_bias, "dp", axis=0, tiled=True),
        lax.all_gather(w_router, "dp", axis=0, tiled=True),
    )
    gain_one = gathered[0].astype(jnp.float32)
    bias_one = gathered[1].astype(jnp.float32)
    qkv_weight = gathered[2]
    out_weight = gathered[3]
    gain_two = gathered[4].astype(jnp.float32)
    bias_two = gathered[5].astype(jnp.float32)
    router_weight = gathered[6]
    slot_start = lax.axis_index("seq") * slot_count
    valid_slot = slot_start + jnp.arange(slot_count) < VALID
    valid_rows = jnp.tile(valid_slot, image_count)
    key_valid = (jnp.arange(S) < VALID)[None, None, None, :]
    token_rows = tokens.reshape(row_count, model_width).astype(jnp.float32)
    normed_one, norm_one_back = jax.vjp(layer_norm, token_rows, gain_one, bias_one)
    normed_one_b = normed_one.astype(jnp.bfloat16)
    mixed_qkv = jnp.dot(normed_one_b, qkv_weight, preferred_element_type=jnp.float32).astype(
        jnp.bfloat16
    )
    qkv_heads = regroup_heads(mixed_qkv.reshape(image_count, slot_count, 3, H, head_size))
    queries = qkv_heads[:, :, 0]
    keys_in = qkv_heads[:, :, 1]
    values = qkv_heads[:, :, 2]
    attended, log_total = attention_forward(queries, keys_in, values, key_valid)
    attended_rows = regroup_slots(attended[:, :, None]).reshape(row_count, model_width)
    residual_two = token_rows + jnp.dot(
        attended_rows, out_weight, preferred_element_type=jnp.float32
    )
    normed_two, norm_two_back = jax.vjp(layer_norm, residual_two, gain_two, bias_two)
    normed_two_b = normed_two.astype(jnp.bfloat16)
    logits = jnp.dot(normed_two_b, router_weight, preferred_element_type=jnp.float32)
    route_rows = routes.reshape(row_count, 2)
    chosen = (route_rows[:, :, None] == jnp.arange(expert_count)[None, None, :]) & valid_rows[
        :, None, None
    ]
    chosen_f = chosen.astype(jnp.float32)

    def gate_pick(logit_rows):
        return jnp.sum(jax.nn.softmax(logit_rows, axis=-1)[:, None, :] * chosen_f, axis=-1)

    gate_values, gate_back = jax.vjp(gate_pick, logits)
    pick_count = chosen.astype(jnp.int32).reshape(image_count, slot_count * 2, expert_count)
    before = jnp.cumsum(pick_count, axis=1) - pick_count
    place_hit = (before[..., None] == jnp.arange(slot_limit)) & (pick_count[..., None] > 0)
    dispatch = place_hit.astype(jnp.bfloat16).reshape(
        image_count, slot_count, 2, expert_count, slot_limit
    )
    normed_img = normed_two_b.reshape(image_count, slot_count, model_width)
    sent_rows = jnp.einsum(
        "bskem,bsd->ebmd", dispatch, normed_img, preferred_element_type=jnp.float32
    ).astype(jnp.bfloat16)
    received = send_experts(sent_rows.reshape(expert_count, image_count * slot_limit, model_width))
    weights_in, weights_out = (
        lax.all_gather(expert_in, "seq", axis=2, tiled=True),
        lax.all_gather(expert_out, "seq", axis=1, tiled=True),
    )
    total_rows = received.shape[1]
    block_rows = pick_block(total_rows)
    block_count = total_rows // block_rows

    def expert_step(block_index, produced):
        row_piece = lax.dynamic_slice_in_dim(received, block_index * block_rows, block_rows, 1)
        hidden_pre = jnp.einsum(
            "erd,edf->erf", row_piece, weights_in, preferred_element_type=jnp.float32
        )
        activated = jax.nn.gelu(hidden_pre).astype(jnp.bfloat16)
        result = jnp.einsum(
            "erf,efd->erd", activated, weights_out, preferred_element_type=jnp.float32
        ).astype(jnp.bfloat16)
        return lax.dynamic_update_slice_in_dim(produced, result, block_index * block_rows, 1)

    produced = lax.fori_loop(
        0,
        block_count,
        expert_step,
        jnp.zeros((local_experts, total_rows, model_width), jnp.bfloat16),
    )
    returned = send_tokens(produced).reshape(expert_count, image_count, slot_limit, model_width)
    per_choice = jnp.einsum(
        "bskem,ebmd->bskd", dispatch, returned, preferred_element_type=jnp.float32
    ).reshape(row_count, 2, model_width)
    mixed_rows = (
        residual_two
        + gate_values[:, 0:1] * per_choice[:, 0]
        + gate_values[:, 1:2] * per_choice[:, 1]
    )
    target_rows = targets.reshape(row_count, model_width).astype(jnp.float32)
    grad_mixed = (mixed_rows - target_rows) * valid_rows[:, None].astype(jnp.float32)
    grad_gates = jnp.sum(grad_mixed[:, None, :] * per_choice, axis=-1)
    grad_choice = (
        (gate_values[:, :, None] * grad_mixed[:, None, :])
        .astype(jnp.bfloat16)
        .reshape(image_count, slot_count, 2, model_width)
    )
    grad_sent = jnp.einsum(
        "bskem,bskd->ebmd", dispatch, grad_choice, preferred_element_type=jnp.float32
    ).astype(jnp.bfloat16)
    grad_received = send_experts(
        grad_sent.reshape(expert_count, image_count * slot_limit, model_width)
    )
    back_in, back_out = (
        lax.all_gather(expert_in, "seq", axis=2, tiled=True),
        lax.all_gather(expert_out, "seq", axis=1, tiled=True),
    )

    def expert_back(block_index, loop_carry):
        grad_in_sum, grad_out_sum, grad_rows = loop_carry
        row_piece = lax.dynamic_slice_in_dim(received, block_index * block_rows, block_rows, 1)
        grad_piece = lax.dynamic_slice_in_dim(
            grad_received, block_index * block_rows, block_rows, 1
        )
        hidden_pre = jnp.einsum(
            "erd,edf->erf", row_piece, back_in, preferred_element_type=jnp.float32
        )
        activated, gelu_back = jax.vjp(jax.nn.gelu, hidden_pre)
        grad_act = jnp.einsum(
            "erd,efd->erf", grad_piece, back_out, preferred_element_type=jnp.float32
        )
        grad_pre = gelu_back(grad_act)[0].astype(jnp.bfloat16)
        grad_out_sum = grad_out_sum + jnp.einsum(
            "erf,erd->efd",
            activated.astype(jnp.bfloat16),
            grad_piece,
            preferred_element_type=jnp.float32,
        )
        grad_in_sum = grad_in_sum + jnp.einsum(
            "erd,erf->edf", row_piece, grad_pre, preferred_element_type=jnp.float32
        )
        rows_back = jnp.einsum(
            "erf,edf->erd", grad_pre, back_in, preferred_element_type=jnp.float32
        ).astype(jnp.bfloat16)
        grad_rows = lax.dynamic_update_slice_in_dim(
            grad_rows, rows_back, block_index * block_rows, 1
        )
        return (grad_in_sum, grad_out_sum, grad_rows)

    start_carry = (
        jnp.zeros(back_in.shape, jnp.float32),
        jnp.zeros(back_out.shape, jnp.float32),
        jnp.zeros((local_experts, total_rows, model_width), jnp.bfloat16),
    )
    grad_in_sum, grad_out_sum, grad_rows = lax.fori_loop(0, block_count, expert_back, start_carry)
    grad_returned = send_tokens(grad_rows).reshape(
        expert_count, image_count, slot_limit, model_width
    )
    grad_normed_two = jnp.einsum(
        "bskem,ebmd->bsd", dispatch, grad_returned, preferred_element_type=jnp.float32
    ).reshape(row_count, model_width)
    grad_logits = gate_back(grad_gates)[0].astype(jnp.bfloat16)
    grad_router = jnp.einsum(
        "rd,re->de", normed_two_b, grad_logits, preferred_element_type=jnp.float32
    )
    grad_normed_two = grad_normed_two + jnp.einsum(
        "re,de->rd", grad_logits, router_weight, preferred_element_type=jnp.float32
    )
    grad_res_two, grad_gain_two, grad_bias_two = norm_two_back(grad_normed_two)
    grad_residual = grad_mixed + grad_res_two
    grad_branch = grad_residual.astype(jnp.bfloat16)
    grad_out_weight = jnp.einsum(
        "rd,re->de", attended_rows, grad_branch, preferred_element_type=jnp.float32
    )
    grad_attended = jnp.einsum(
        "re,de->rd", grad_branch, out_weight, preferred_element_type=jnp.float32
    ).astype(jnp.bfloat16)
    grad_heads = regroup_heads(grad_attended.reshape(image_count, slot_count, 1, H, head_size))[
        :, :, 0
    ]
    grad_qkv_heads = attention_backward(
        queries, keys_in, values, log_total, grad_heads, key_valid
    ).astype(jnp.bfloat16)
    grad_qkv_rows = regroup_slots(grad_qkv_heads).reshape(row_count, 3 * model_width)
    grad_qkv_weight = jnp.einsum(
        "rd,rf->df", normed_one_b, grad_qkv_rows, preferred_element_type=jnp.float32
    )
    grad_normed_one = jnp.einsum(
        "rf,df->rd", grad_qkv_rows, qkv_weight, preferred_element_type=jnp.float32
    )
    grad_token_ln, grad_gain_one, grad_bias_one = norm_one_back(grad_normed_one)
    grad_tokens = grad_residual + grad_token_ln
    dense_grads = (
        grad_gain_one,
        grad_bias_one,
        grad_qkv_weight,
        grad_out_weight,
        grad_gain_two,
        grad_bias_two,
        grad_router,
    )
    dense_grads = (
        lax.psum(dense_grads[0].astype(jnp.bfloat16), "seq").astype(jnp.float32),
        lax.psum(dense_grads[1].astype(jnp.bfloat16), "seq").astype(jnp.float32),
        lax.psum(dense_grads[2].astype(jnp.bfloat16), "seq").astype(jnp.float32),
        lax.psum(dense_grads[3].astype(jnp.bfloat16), "seq").astype(jnp.float32),
        lax.psum(dense_grads[4].astype(jnp.bfloat16), "seq").astype(jnp.float32),
        lax.psum(dense_grads[5].astype(jnp.bfloat16), "seq").astype(jnp.float32),
        lax.psum(dense_grads[6].astype(jnp.bfloat16), "seq").astype(jnp.float32),
    )
    dense_grads = (
        lax.psum_scatter(
            dense_grads[0].astype(jnp.bfloat16), "dp", scatter_dimension=0, tiled=True
        ).astype(jnp.float32),
        lax.psum_scatter(
            dense_grads[1].astype(jnp.bfloat16), "dp", scatter_dimension=0, tiled=True
        ).astype(jnp.float32),
        lax.psum_scatter(
            dense_grads[2].astype(jnp.bfloat16), "dp", scatter_dimension=0, tiled=True
        ).astype(jnp.float32),
        lax.psum_scatter(
            dense_grads[3].astype(jnp.bfloat16), "dp", scatter_dimension=0, tiled=True
        ).astype(jnp.float32),
        lax.psum_scatter(
            dense_grads[4].astype(jnp.bfloat16), "dp", scatter_dimension=0, tiled=True
        ).astype(jnp.float32),
        lax.psum_scatter(
            dense_grads[5].astype(jnp.bfloat16), "dp", scatter_dimension=0, tiled=True
        ).astype(jnp.float32),
        lax.psum_scatter(
            dense_grads[6].astype(jnp.bfloat16), "dp", scatter_dimension=0, tiled=True
        ).astype(jnp.float32),
    )
    expert_in_grad, expert_out_grad = (
        lax.psum_scatter(
            grad_in_sum.astype(jnp.bfloat16), "seq", scatter_dimension=2, tiled=True
        ).astype(jnp.float32),
        lax.psum_scatter(
            grad_out_sum.astype(jnp.bfloat16), "seq", scatter_dimension=1, tiled=True
        ).astype(jnp.float32),
    )
    mixed = mixed_rows.astype(jnp.bfloat16).reshape(image_count, slot_count, model_width)
    return (
        mixed,
        grad_tokens.reshape(image_count, slot_count, model_width),
        dense_grads[0],
        dense_grads[1],
        dense_grads[2],
        dense_grads[3],
        dense_grads[4],
        dense_grads[5],
        dense_grads[6],
        expert_in_grad,
        expert_out_grad,
    )


BF = jnp.bfloat16
F32 = jnp.float32
MESH_ID = pl.DeviceIdType.MESH
NEG = -1e30
BP = 64
VMEM_LIMIT = 67000000
GELU_C = 0.7978845608028654
GELU_K = 0.044715


def nn(a, b):
    return lax.dot_general(a, b, (((1,), (0,)), ((), ())), preferred_element_type=F32)


def nt(a, b):
    return lax.dot_general(a, b, (((1,), (1,)), ((), ())), preferred_element_type=F32)


def tn(a, b):
    return lax.dot_general(a, b, (((0,), (0,)), ((), ())), preferred_element_type=F32)


def remote(src, dst, send_sem, recv_sem, dp, z):
    return pltpu.make_async_remote_copy(
        src_ref=src,
        dst_ref=dst,
        send_sem=send_sem,
        recv_sem=recv_sem,
        device_id=(dp, z),
        device_id_type=MESH_ID,
    )


def rows_of(index, size):
    return pl.ds(pl.multiple_of(index * size, size), size)


def norm_parts(x):
    centre = x - jnp.mean(x, axis=-1, keepdims=True)
    scale = lax.rsqrt(jnp.mean(centre * centre, axis=-1, keepdims=True) + 1e-06)
    return centre * scale, scale


def norm_back(grad_hat, hat, scale):
    return scale * (
        grad_hat
        - jnp.mean(grad_hat, axis=-1, keepdims=True)
        - hat * jnp.mean(grad_hat * hat, axis=-1, keepdims=True)
    )


def half_masks():
    lane = lax.broadcasted_iota(jnp.int32, (1, 128), 1)
    low = jnp.where(lane < 64, 1.0, 0.0).astype(BF)
    high = jnp.where(lane < 64, 0.0, 1.0).astype(BF)
    return (low, high)


def slot_ok(position, block):
    return (position % BP < block) & ((position // BP) * block + position % BP < VALID)


def block_kernel(
    dims,
    tok, tgt, rts, wq, wo, vec, win, wout,
    mixed, gtok, gqkv, gwo, gsmall, gin, gout,
    xin, rin, tin, vec_all, wq_all, wo_all, vsum, xpad, n2s, qkvs, outs, cols, gts, meta,
    win_all, wout_all, recv, ret, acts, slopes, sbuf,
    drows, dys, dws, arrived,
    gacc, gvec, csend, crecv, cvec, hrecv, hvec, zsend, zrecv, zall, zvec,
    loc_sem, tok_ss, tok_rs, rts_ss, rts_rs, tgt_ss, tgt_rs, den_ss, den_rs, fwd_ss, win_ss, win_rs, wout_ss, wout_rs,
    row_ss, row_rs, u_ss, u_rs, du_ss, du_rs, dn_ss, dn_rs, mix_ss, mix_rs, gt_ss, gt_rs,
    r_ss, r_rs, c_ss, c_rs, cv_ss, cv_rs, h_ss, h_rs, hv_ss, hv_rs, za_ss, za_rs, zb_ss, zb_rs, zv_ss, zv_rs,
):
    n_dp, n_z, counts, block, cap = dims
    firsts = tuple(sum(counts[:h]) for h in range(n_z))
    me, z = lax.axis_index("dp"), lax.axis_index("seq")
    sp = n_z * BP
    half = n_dp // 2
    last = n_z - 1
    core, chip = lax.rem(me, 2), me // 2
    partner = chip * 2 + 1 - core
    inner = (z == 1) | (z == last - 1)
    ends = jnp.logical_not(inner)
    far_end = jnp.where(z < n_z // 2, last, 0)
    near_end = last - far_end
    middle = last - z
    im = jnp.where(inner, counts[1], counts[0])
    sizes = ((counts[1], inner), (counts[0], ends))
    first = jnp.where(z == 0, firsts[0], jnp.where(z == 1, firsts[1], jnp.where(z == 2, firsts[2], firsts[3])))

    barrier = pltpu.get_barrier_semaphore()
    for k in range(1, n_dp):
        pl.semaphore_signal(barrier, inc=1, device_id=(lax.rem(me + k, n_dp), z), device_id_type=MESH_ID)
    for k in range(1, n_z):
        pl.semaphore_signal(barrier, inc=1, device_id=(me, lax.rem(z + k, n_z)), device_id_type=MESH_ID)

    def hosts_own(source, target, sem):
        for h in range(n_z):

            @pl.when(z == h)
            def _():
                pltpu.make_async_copy(
                    source.at[pl.ds(firsts[h], counts[h])], target.at[z, pl.ds(0, counts[h])], sem
                ).start()

    def hosts_own_wait(source, target, sem):
        for h in range(n_z):

            @pl.when(z == h)
            def _():
                pltpu.make_async_copy(
                    source.at[pl.ds(firsts[h], counts[h])], target.at[z, pl.ds(0, counts[h])], sem
                ).wait()

    def hosts_start(source, target, send_sem, recv_sem, hosts, who):
        for h in hosts:

            @pl.when((z != h) & who)
            def _():
                remote(
                    source.at[pl.ds(firsts[h], counts[h])],
                    target.at[z, pl.ds(0, counts[h])],
                    send_sem.at[h],
                    recv_sem.at[z],
                    me,
                    h,
                ).start()

    def hosts_arrive(target, recv_sem):
        for size, there in sizes:

            @pl.when(there)
            def _():
                for k in range(1, n_z):
                    origin = lax.rem(z + k, n_z)
                    spot = target.at[origin, pl.ds(0, size)]
                    remote(spot, spot, loc_sem.at[8], recv_sem.at[origin], me, z).wait_recv()

    def hosts_sent(target, send_sem):
        for h in range(n_z):

            @pl.when(z != h)
            def _():
                spot = target.at[0, pl.ds(0, counts[h])]
                remote(spot, spot, send_sem.at[h], loc_sem.at[8], me, z).wait_send()

    def home_own(source, target, sem):
        return [
            (there, pltpu.make_async_copy(source.at[z, pl.ds(0, size)], target.at[pl.ds(first, size)], sem))
            for size, there in sizes
        ]

    def home_start(source, target, send_sem, recv_sem, who):
        for size, there in who:

            @pl.when(there)
            def _():
                for k in range(1, n_z):
                    peer = lax.rem(z + k, n_z)
                    remote(
                        source.at[peer, pl.ds(0, size)],
                        target.at[pl.ds(first, size)],
                        send_sem.at[k],
                        recv_sem.at[z],
                        me,
                        peer,
                    ).start()

    def home_arrive(target, recv_sem):
        for h in range(n_z):

            @pl.when(z != h)
            def _():
                spot = target.at[pl.ds(firsts[h], counts[h])]
                remote(spot, spot, loc_sem.at[8], recv_sem.at[h], me, z).wait_recv()

    def home_sent(source, send_sem):
        for size, there in sizes:

            @pl.when(there)
            def _():
                for k in range(1, n_z):
                    spot = source.at[0, pl.ds(0, size)]
                    remote(spot, spot, send_sem.at[k], loc_sem.at[8], me, z).wait_send()

    def each(pairs, act):
        for there, copy in pairs:

            @pl.when(there)
            def _():
                getattr(copy, act)()

    def z_arrive(target, recv_sem):
        for k in range(1, n_z):
            origin = lax.rem(z + k, n_z)
            remote(target(origin), target(origin), loc_sem.at[8], recv_sem.at[origin], me, z).wait_recv()

    def z_sent(source, send_sem):
        for k in range(1, n_z):
            remote(source(0), source(0), send_sem.at[k], loc_sem.at[8], me, z).wait_send()

    own_copies = [
        pltpu.make_async_copy(win, win_all.at[z], loc_sem.at[3]),
        pltpu.make_async_copy(wout, wout_all.at[z], loc_sem.at[4]),
        pltpu.make_async_copy(wq, wq_all.at[rows_of(me, 64)], loc_sem.at[5]),
        pltpu.make_async_copy(wo, wo_all.at[rows_of(me, 64)], loc_sem.at[6]),
        pltpu.make_async_copy(vec, vec_all.at[me], loc_sem.at[7]),
    ]
    for copy in own_copies:
        copy.start()
    hosts_own(tok, xin, loc_sem.at[0])
    hosts_own(rts, rin, loc_sem.at[1])
    hosts_own(tgt, tin, loc_sem.at[2])
    for buffer in (xpad, gacc, gvec, recv, ret, drows):
        buffer[...] = jnp.zeros_like(buffer)
    pl.semaphore_wait(barrier, n_dp + n_z - 2)
    hosts_start(tok, xin, tok_ss, tok_rs, range(n_z), z >= 0)
    hosts_start(rts, rin, rts_ss, rts_rs, range(n_z), z >= 0)

    def dense_slot(array, index):
        if array == 0:
            return wq_all.at[rows_of(index, 64)]
        if array == 1:
            return wo_all.at[rows_of(index, 64)]
        return vec_all.at[index]

    dense_in = (wq, wo, vec)
    for array in range(3):
        for k in range(1, half):
            peer = lax.rem(chip + k, half) * 2 + core
            remote(
                dense_in[array], dense_slot(array, me), den_ss.at[array, k], den_rs.at[array, me], peer, z
            ).start()
        remote(
            dense_in[array], dense_slot(array, me), den_ss.at[array, 0], den_rs.at[array, me], partner, z
        ).start()

    experts = ((win, win_all, win_ss, win_rs), (wout, wout_all, wout_ss, wout_rs))

    def gather_hop(array, step):
        source, full, send_sem, recv_sem = experts[array]
        for way, there, slot in ((0, z >= step, z - step), (1, z + step < n_z, z + step)):

            @pl.when(there)
            def _():
                at = full.at[slot]
                if step > 0:
                    remote(at, at, send_sem.at[way, step], recv_sem.at[slot], me, z).wait_recv()

                @pl.when((z < last) if way == 0 else (z > 0))
                def _():
                    remote(
                        at if step > 0 else source,
                        at,
                        send_sem.at[way, step],
                        recv_sem.at[slot],
                        me,
                        z + 1 if way == 0 else z - 1,
                    ).start()

    def weights_sent():
        for step in range(n_z - 1):
            for way, there in ((0, (z >= step) & (z < last)), (1, (z + step < n_z) & (z > 0))):

                @pl.when(there)
                def _():
                    for source, full, send_sem, recv_sem in experts:
                        remote(
                            full.at[0], full.at[0], send_sem.at[way, step], recv_sem.at[0], me, z
                        ).wait_send()

    gather_hop(0, 0)
    gather_hop(1, 0)

    for k in range(1, half):
        origin = lax.rem(chip + k, half) * 2 + core
        for array in range(3):
            slot = dense_slot(array, origin)
            remote(slot, slot, den_ss.at[array, 0], den_rs.at[array, origin], me, z).wait_recv()
            remote(slot, slot, fwd_ss.at[array, k], den_rs.at[array, origin], partner, z).start()
    for k in range(half):
        origin = lax.rem(chip + k, half) * 2 + 1 - core
        for array in range(3):
            slot = dense_slot(array, origin)
            remote(slot, slot, den_ss.at[array, 0], den_rs.at[array, origin], me, z).wait_recv()
    for copy in own_copies:
        copy.wait()
    hosts_own_wait(tok, xin, loc_sem.at[0])
    hosts_own_wait(rts, rin, loc_sem.at[1])
    hosts_own_wait(tgt, tin, loc_sem.at[2])
    total = vec_all[0].astype(F32)
    for k in range(1, n_dp):
        total = total + vec_all[k].astype(F32)
    vsum[...] = total
    hosts_arrive(xin, tok_rs)
    hosts_arrive(rin, rts_rs)

    masks = half_masks()
    keys_ok = slot_ok(lax.broadcasted_iota(jnp.int32, (1, sp), 1), block)
    rows_ok = slot_ok(lax.broadcasted_iota(jnp.int32, (sp, 1), 0), block)
    gain_one, bias_one = vsum[0:1, :], vsum[1:2, :]
    gain_two, bias_two = vsum[2:3, :], vsum[3:4, :]
    router_t = vsum[8:16, :].astype(BF)
    lane_id = lax.broadcasted_iota(jnp.int32, (sp, 128), 1)
    lane_low = lane_id < 64
    row_id = lax.broadcasted_iota(jnp.int32, (512, sp), 0).astype(F32)

    def rows_at(index):
        return pl.ds(pl.multiple_of(index * 64, 64), n_z * cap)

    def send_rows(i, target, send_sem, recv_sem):
        def step(s, carry):
            j, c = lax.rem(s // 2 + 1, half), lax.rem(s, 2)
            index = 2 * j + c
            peer = lax.rem(chip + j, half) * 2 + lax.rem(core + c, 2)

            @pl.when(index > 0)
            def _():
                remote(
                    sbuf.at[i, rows_at(peer)],
                    target.at[i, rows_at(me)],
                    send_sem.at[i, index],
                    recv_sem.at[i, me],
                    peer,
                    z,
                ).start()

            return carry

        lax.fori_loop(0, n_dp, step, 0)
        target[i, rows_of(me, 64)] = sbuf[i, rows_of(me, 64)]

    def arrive(i, target, recv_sem):
        def step(k, carry):
            origin = lax.rem(me + k, n_dp)
            spot = target.at[i, rows_at(origin)]
            remote(spot, spot, loc_sem.at[8], recv_sem.at[i, origin], me, z).wait_recv()
            return carry

        lax.fori_loop(1, n_dp, step, 0)

    def sent(i, send_sem):
        def step(index, carry):
            spot = sbuf.at[i, rows_at(0)]
            remote(spot, spot, send_sem.at[i, index], loc_sem.at[8], me, z).wait_send()
            return carry

        lax.fori_loop(1, n_dp, step, 0)

    def front(i, carry):
        before = lax.broadcasted_iota(jnp.int32, (sp, sp), 0)
        after = lax.broadcasted_iota(jnp.int32, (sp, sp), 1)
        prefix = jnp.where((before < after) & (before // BP == after // BP), 1.0, 0.0).astype(BF)
        expert_id = lax.broadcasted_iota(jnp.int32, (8, sp), 0)
        slot_lane = lax.broadcasted_iota(jnp.int32, (8, sp), 1)
        for b in range(n_z):
            xpad[i, b * BP : b * BP + block, :] = xin[b, i]
        x = xpad[i].astype(F32)
        hat, _ = norm_parts(x)
        normed = (hat * gain_one + bias_one).astype(BF)
        qkvs[i] = nn(normed, wq_all[...]).astype(BF)
        lse_all = jnp.zeros((sp, 128), F32)
        for pair in range(4):
            q2 = qkvs[i, :, pair * 128 : pair * 128 + 128]
            k2 = qkvs[i, :, 512 + pair * 128 : 512 + pair * 128 + 128]
            v2 = qkvs[i, :, 1024 + pair * 128 : 1024 + pair * 128 + 128]
            parts = []
            for side in range(2):
                scores = nt(q2 * masks[side], k2) * 0.125
                scores = jnp.where(keys_ok, scores, NEG)
                top = jnp.max(scores, axis=-1, keepdims=True)
                exponent = jnp.exp(scores - top)
                whole = jnp.sum(exponent, axis=-1, keepdims=True)
                lse_all = jnp.where(lane_id == pair * 2 + side, top + jnp.log(whole), lse_all)
                parts.append(nn((exponent / whole).astype(BF), v2))
            outs[i, :, pair * 128 : pair * 128 + 128] = jnp.where(lane_low, parts[0], parts[1]).astype(BF)
        x2 = x + nn(outs[i], wo_all[...])
        hat2, _ = norm_parts(x2)
        n2 = (hat2 * gain_two + bias_two).astype(BF)
        n2s[i] = n2
        logits = nt(router_t, n2)
        raised = jnp.exp(logits - jnp.max(logits, axis=0, keepdims=True))
        share = raised / jnp.sum(raised, axis=0, keepdims=True)
        gts[i] = share
        wide = jnp.concatenate([rin[0, i] + rin[1, i], rin[2, i] + rin[3, i]], axis=1)
        hits = [(expert_id + 1) == wide[j : j + 1, :] for j in range(2)]
        any_hit = jnp.where(hits[0] | hits[1], 1.0, 0.0)
        place = nn(any_hit.astype(BF), prefix)
        base = place + (expert_id * 64 + (slot_lane // BP) * cap + 1).astype(F32)
        lines = [jnp.sum(jnp.where(hit, base, 0.0), axis=0, keepdims=True) - 1.0 for hit in hits]
        lines += [jnp.sum(jnp.where(hit, share, 0.0), axis=0, keepdims=True) for hit in hits]
        lines = jnp.concatenate(lines + [jnp.zeros((4, sp), F32)], axis=0)
        meta[i] = lines
        table = jnp.concatenate([jnp.zeros((8, sp), F32), lines, jnp.zeros((112, sp), F32)], axis=0)
        cols[i] = jnp.transpose(table) + lse_all
        pick = (row_id == lines[0:1, :]) | (row_id == lines[1:2, :])
        sbuf[i] = nn(jnp.where(pick, 1.0, 0.0).astype(BF), n2).astype(BF)
        send_rows(i, recv, row_ss, row_rs)

        @pl.when(i == 1)
        def _():
            gather_hop(0, 1)

        return carry

    lax.fori_loop(0, im, front, 0)

    hosts_start(tgt, tin, tgt_ss, tgt_rs, (1, 2), z >= 0)

    def hidden(shard):
        def image(i, carry):
            x = recv[i]
            for side in range(2):
                pre = nn(x, win_all[shard, :, side * 256 : side * 256 + 256])
                square = pre * pre
                tanh = jnp.tanh(pre * (GELU_C + (GELU_C * GELU_K) * square))
                gate = 0.5 + 0.5 * tanh
                acts[shard, i, :, side * 256 : side * 256 + 256] = (pre * gate).astype(BF)
                slope = gate + pre * (0.5 - 0.5 * tanh * tanh) * (GELU_C + (3.0 * GELU_C * GELU_K) * square)
                slopes[shard, i, :, side * 256 : side * 256 + 256] = slope.astype(BF)
            return carry

        lax.fori_loop(0, im, image, 0)

    def hidden_step(s, carry):
        for at_step, hop in ((1, 2), (3, 3)):

            @pl.when(s == at_step)
            def _():
                gather_hop(0, hop)

        for way in range(2):
            shard = z - s if way == 0 else z + s

            @pl.when((shard >= 0) & (shard < n_z) & ((s > 0) | (way == 0)))
            def _():
                hidden(shard)

        @pl.when(s == 2)
        def _():
            gather_hop(1, 2)

        return carry

    gather_hop(1, 1)

    def rows_here(i, carry):
        arrive(i, recv, row_rs)
        return carry

    lax.fori_loop(0, im, rows_here, 0)
    lax.fori_loop(0, n_z, hidden_step, 0)
    gather_hop(1, 3)

    hosts_start(tgt, tin, tgt_ss, tgt_rs, (0, last), ends)

    def results(i, carry):
        total = nn(acts[0, i], wout_all[0])
        for shard in range(1, n_z):
            total = total + nn(acts[shard, i], wout_all[shard])
        sent(i, row_ss)
        sbuf[i] = total.astype(BF)
        send_rows(i, ret, u_ss, u_rs)
        return carry

    lax.fori_loop(0, im, results, 0)

    def mix(i, carry):
        @pl.when(i == 1)
        def _():
            hosts_start(tgt, tin, tgt_ss, tgt_rs, (0, last), inner)

        arrive(i, ret, u_rs)

        @pl.when(i == 0)
        def _():
            hosts_arrive(tin, tgt_rs)

        line = lax.broadcasted_iota(jnp.int32, (sp, 512), 1).astype(F32)
        here = cols[i]
        picked = []
        for j in range(2):
            pick = jnp.where(line == here[:, 8 + j : 9 + j], 1.0, 0.0).astype(BF)
            picked.append(nn(pick, ret[i]))
        x2 = xpad[i].astype(F32) + nn(outs[i], wo_all[...])
        mix = x2 + here[:, 10:11] * picked[0] + here[:, 11:12] * picked[1]
        mix_b = mix.astype(BF)
        for b in range(n_z):
            xin[b, i] = mix_b[b * BP : b * BP + block]
            dys[i, b * BP : b * BP + block, :] = tin[b, i].astype(F32)
        dy = jnp.where(rows_ok, mix - dys[i], 0.0)
        dys[i] = dy
        total = jnp.zeros((512, 512), F32)
        for j in range(2):
            pick = jnp.where(row_id == meta[i, j : j + 1, :], 1.0, 0.0).astype(BF)
            total = total + nn(pick, (here[:, 10 + j : 11 + j] * dy).astype(BF))
        sent(i, u_ss)
        sbuf[i] = total.astype(BF)
        send_rows(i, drows, du_ss, du_rs)
        for j in range(2):
            here = jnp.where(lane_id == 12 + j, jnp.sum(dy * picked[j], axis=-1, keepdims=True), here)
        cols[i] = here
        return carry

    lax.fori_loop(0, im, mix, 0)
    home_start(xin, mixed, mix_ss, mix_rs, sizes)
    own_mixed = home_own(xin, mixed, loc_sem.at[0])
    each(own_mixed, "start")
    expert_row = lax.broadcasted_iota(jnp.int32, (8, sp), 0).astype(F32)

    def gates_back(i, carry):
        flat = jnp.transpose(cols[i])
        share = gts[i]
        grad = jnp.zeros((8, sp), F32)
        for j in range(2):
            at = meta[i, j : j + 1, :]
            inside = (at >= expert_row * 64) & (at < expert_row * 64 + 64)
            grad = grad + jnp.where(inside, flat[12 + j : 13 + j, :], 0.0)
        dlog = share * (grad - jnp.sum(share * grad, axis=0, keepdims=True))
        gts[i] = dlog
        gvec[8:16, :] += nn(dlog.astype(BF), n2s[i])
        return carry

    lax.fori_loop(0, im, gates_back, 0)

    def reduce_start(target, piece):
        peer = jnp.where(z == 0, 1, last - 1)
        slot = jnp.where(target == peer, 0, jnp.where(target == far_end, 2, 1))
        remote(
            dws.at[target, piece], arrived.at[slot, piece], r_ss.at[target, piece], r_rs.at[slot, piece], me, peer
        ).start()

    def reduce_forward(piece, steps):
        @pl.when(inner)
        def _():
            for target, slot, peer, there in steps:
                here = arrived.at[slot, piece]
                remote(here, here, r_ss.at[target, piece], r_rs.at[slot, piece], me, z).wait_recv()

                def add(c, carry):
                    at = rows_of(c, 128)
                    dws[target, piece, at] = (
                        dws[target, piece, at].astype(F32) + arrived[slot, piece, at].astype(F32)
                    ).astype(BF)
                    return carry

                lax.fori_loop(0, 4, add, 0)
                remote(
                    dws.at[target, piece],
                    arrived.at[there, piece],
                    r_ss.at[target, piece],
                    r_rs.at[there, piece],
                    me,
                    peer,
                ).start()

    first_steps = ((far_end, 2, middle, 4),)
    second_steps = ((middle, 1, middle, 3), (near_end, 4, near_end, 0))

    def owner(s):
        return jnp.where(z < n_z // 2, lax.rem(z + 2 * n_z - 1 - s, n_z), lax.rem(z + 1 + s, n_z))

    def lanes_of(target):
        return pl.ds(pl.multiple_of(target * 512, 512), 512)

    def out_ready(s, carry):
        target = owner(s)
        dws[target, 0] = gacc[:, lanes_of(target)].astype(BF)

        @pl.when(ends & (s < 2))
        def _():
            reduce_start(target, 0)

        return carry

    def experts_back(i, carry):
        arrive(i, drows, du_rs)
        du = drows[i]
        for target in range(n_z):
            gacc[:, target * 512 : target * 512 + 512] += tn(acts[target, i], du)

        @pl.when(i == im - 1)
        def _():
            lax.fori_loop(0, n_z, out_ready, 0)

        total = jnp.zeros((512, 512), F32)
        for shard in range(n_z):
            dpre = (nt(du, wout_all[shard]) * slopes[shard, i].astype(F32)).astype(BF)
            slopes[shard, i] = dpre
            total = total + nt(dpre, win_all[shard])
        sent(i, du_ss)
        sbuf[i] = total.astype(BF)
        send_rows(i, ret, dn_ss, dn_rs)
        return carry

    lax.fori_loop(0, im, experts_back, 0)
    reduce_forward(0, first_steps)

    def in_grads(s, carry):
        target = owner(s)
        gacc[:, 0:512] = tn(recv[0], slopes[target, 0])

        def more(i, carry):
            gacc[:, 0:512] += tn(recv[i], slopes[target, i])
            return carry

        lax.fori_loop(1, im, more, 0)
        dws[target, 1] = gacc[:, 0:512].astype(BF)

        @pl.when(ends & (s < 2))
        def _():
            reduce_start(target, 1)

        return carry

    lax.fori_loop(0, n_z, in_grads, 0)

    gacc[...] = jnp.zeros_like(gacc)
    each(own_mixed, "wait")
    home_sent(xin, mix_ss)
    reduce_forward(0, second_steps)

    def back(i, carry):
        arrive(i, ret, dn_rs)
        line = lax.broadcasted_iota(jnp.int32, (sp, 512), 1).astype(F32)
        here = cols[i]
        pick = jnp.where((line == here[:, 8:9]) | (line == here[:, 9:10]), 1.0, 0.0).astype(BF)
        dn2 = nn(pick, ret[i]) + tn(gts[i].astype(BF), router_t)
        hat2, scale2 = norm_parts(xpad[i].astype(F32) + nn(outs[i], wo_all[...]))
        gvec[2:3, :] += jnp.sum(dn2 * hat2, axis=0, keepdims=True)
        gvec[3:4, :] += jnp.sum(dn2, axis=0, keepdims=True)
        dx2 = dys[i] + norm_back(dn2 * gain_two, hat2, scale2)
        da = dx2.astype(BF)
        gacc[:, 1536:2048] += tn(outs[i], da)
        do = nt(da, wo_all[...]).astype(BF)
        hat1, scale1 = norm_parts(xpad[i].astype(F32))
        n1 = (hat1 * gain_one + bias_one).astype(BF)
        for pair in range(4):
            at = pair * 128
            q2 = qkvs[i, :, at : at + 128]
            k2 = qkvs[i, :, 512 + at : 512 + at + 128]
            v2 = qkvs[i, :, 1024 + at : 1024 + at + 128]
            do2 = do[:, at : at + 128]
            grads = ([], [], [])
            for side in range(2):
                head = pair * 2 + side
                scores = nt(q2 * masks[side], k2) * 0.125
                scores = jnp.where(keys_ok, scores, NEG)
                prob = jnp.exp(scores - here[:, head : head + 1])
                dprob = nt(do2 * masks[side], v2)
                inner = jnp.sum(prob * dprob, axis=-1, keepdims=True)
                ds = (prob * (dprob - inner)).astype(BF)
                grads[0].append(nn(ds, k2))
                grads[1].append(tn(ds, q2))
                grads[2].append(tn(prob.astype(BF), do2))
            for part in range(3):
                grad = jnp.where(lane_low, grads[part][0], grads[part][1])
                if part < 2:
                    grad = grad * 0.125
                qkvs[i, :, part * 512 + at : part * 512 + at + 128] = grad.astype(BF)
        dqkv = qkvs[i]
        gacc[:, 0:1536] += tn(n1, dqkv)
        dn1 = nt(dqkv, wq_all[...])
        gvec[0:1, :] += jnp.sum(dn1 * hat1, axis=0, keepdims=True)
        gvec[1:2, :] += jnp.sum(dn1, axis=0, keepdims=True)
        dx = (dx2 + norm_back(dn1 * gain_one, hat1, scale1)).astype(BF)
        for b in range(n_z):
            xin[b, i] = dx[b * BP : b * BP + block]

        @pl.when(i == 0)
        def _():
            reduce_forward(1, first_steps)

        @pl.when(i == 1)
        def _():
            reduce_forward(1, second_steps)

        return carry

    lax.fori_loop(0, im, back, 0)
    home_start(xin, gtok, gt_ss, gt_rs, sizes[:1])
    own_gtok = home_own(xin, gtok, loc_sem.at[1])
    each(own_gtok, "start")

    for q in range(half):
        csend[q] = gacc[rows_of(2 * q + 1 - core, 64)].astype(BF)
        remote(csend.at[q], crecv.at[q], c_ss.at[q], c_rs.at[q], partner, z).start()
    remote(gvec, cvec, cv_ss.at[0], cv_rs.at[0], partner, z).start()
    for q in range(half):
        remote(crecv.at[q], crecv.at[q], c_ss.at[q], c_rs.at[q], me, z).wait_recv()
    for k in range(1, half):
        q = lax.rem(chip + k, half)
        crecv[q] = (gacc[rows_of(2 * q + core, 64)] + crecv[q].astype(F32)).astype(BF)
        remote(crecv.at[q], hrecv.at[chip], h_ss.at[k], h_rs.at[chip], q * 2 + core, z).start()
    remote(cvec, cvec, cv_ss.at[0], cv_rs.at[0], me, z).wait_recv()
    hvec[chip] = gvec[...] + cvec[...]
    for k in range(1, half):
        q = lax.rem(chip + k, half)
        remote(hvec.at[chip], hvec.at[chip], hv_ss.at[k], hv_rs.at[chip], q * 2 + core, z).start()
    dense = gacc[rows_of(me, 64)] + crecv[chip].astype(F32)
    for k in range(1, half):
        q = lax.rem(chip + k, half)
        remote(hrecv.at[q], hrecv.at[q], h_ss.at[0], h_rs.at[q], me, z).wait_recv()
        dense = dense + hrecv[q].astype(F32)
    for h in range(2):
        zsend[h] = dense[h * 32 : h * 32 + 32].astype(BF)

        @pl.when(z == h + 1)
        def _():
            zrecv[z] = zsend[h]

        @pl.when(z != h + 1)
        def _():
            remote(zsend.at[h], zrecv.at[z], za_ss.at[h], za_rs.at[z], me, h + 1).start()

    for k in range(1, half):
        q = lax.rem(chip + k, half)
        remote(hvec.at[q], hvec.at[q], hv_ss.at[0], hv_rs.at[q], me, z).wait_recv()
    zvec[z] = hvec[0] + hvec[1] + hvec[2] + hvec[3]

    @pl.when(z != 1)
    def _():
        remote(zvec.at[z], zvec.at[z], zv_ss.at[0], zv_rs.at[z], me, 1).start()

    @pl.when(ends)
    def _():
        reduce_start(owner(2), 0)
        reduce_start(owner(2), 1)

    home_start(xin, gtok, gt_ss, gt_rs, sizes[1:])

    final_copies = [
        pltpu.make_async_copy(gacc.at[:, pl.ds(piece * 512, 512)], out, loc_sem.at[2 + piece])
        for piece, out in ((0, gout), (1, gin))
    ]
    for piece in range(2):
        for slot, there in ((0, z >= 0), (3, inner)):

            @pl.when(there)
            def _():
                here = arrived.at[slot, piece]
                remote(here, here, r_ss.at[0, piece], r_rs.at[slot, piece], me, z).wait_recv()

        def finish(c, carry):
            at = rows_of(c, 128)
            gacc[at, piece * 512 : piece * 512 + 512] = (
                dws[z, piece, at].astype(F32)
                + arrived[0, piece, at].astype(F32)
                + jnp.where(inner, arrived[3, piece, at].astype(F32), 0.0)
            )
            return carry

        lax.fori_loop(0, 4, finish, 0)
        final_copies[piece].start()
    for h in range(2):

        @pl.when(z == h + 1)
        def _():
            z_arrive(lambda i: zrecv.at[i], za_rs)
            total = zrecv[0].astype(F32)
            for k in range(1, n_z):
                total = total + zrecv[k].astype(F32)
            zall[h] = total.astype(BF)
            for k in range(1, n_z):
                peer = lax.rem(z + k, n_z)
                remote(zall.at[h], zall.at[h], zb_ss.at[k], zb_rs.at[h], me, peer).start()

    @pl.when(z == 1)
    def _():
        z_arrive(lambda i: zvec.at[i], zv_rs)
        gsmall[...] = zvec[0] + zvec[1] + zvec[2] + zvec[3]
        zvec[n_z] = gsmall[...]
        for k in range(1, n_z):
            peer = lax.rem(z + k, n_z)
            remote(zvec.at[n_z], zvec.at[n_z], zv_ss.at[k], zv_rs.at[n_z], me, peer).start()

    @pl.when(z != 1)
    def _():
        remote(zvec.at[n_z], zvec.at[n_z], zv_ss.at[0], zv_rs.at[n_z], me, z).wait_recv()
        gsmall[...] = zvec[n_z]

    for h in range(2):

        @pl.when(z != h + 1)
        def _():
            remote(zall.at[h], zall.at[h], zb_ss.at[0], zb_rs.at[h], me, z).wait_recv()

        piece = zall[h].astype(F32)
        gqkv[h * 32 : h * 32 + 32] = piece[:, 0:1536]
        gwo[h * 32 : h * 32 + 32] = piece[:, 1536:2048]
    each(own_gtok, "wait")
    home_arrive(gtok, gt_rs)
    home_arrive(mixed, mix_rs)
    for copy in final_copies:
        copy.wait()

    hosts_sent(xin, tok_ss)
    hosts_sent(rin, rts_ss)
    hosts_sent(tin, tgt_ss)
    home_sent(xin, gt_ss)
    for h in range(2):

        @pl.when(z != h + 1)
        def _():
            remote(zsend.at[h], zsend.at[h], za_ss.at[h], loc_sem.at[8], me, z).wait_send()

        @pl.when(z == h + 1)
        def _():
            z_sent(lambda peer: zall.at[0], zb_ss)

    @pl.when(z == 1)
    def _():
        z_sent(lambda peer: zvec.at[0], zv_ss)

    @pl.when(z != 1)
    def _():
        remote(zvec.at[0], zvec.at[0], zv_ss.at[0], loc_sem.at[8], me, z).wait_send()


    def rows_sent(i, carry):
        sent(i, dn_ss)
        return carry

    lax.fori_loop(0, im, rows_sent, 0)
    weights_sent()
    for array in range(3):
        slot = dense_slot(array, 0)
        for k in range(half):
            remote(slot, slot, den_ss.at[array, k], loc_sem.at[8], me, z).wait_send()
        for k in range(1, half):
            remote(slot, slot, fwd_ss.at[array, k], loc_sem.at[8], me, z).wait_send()
    for piece in range(2):
        for target in range(n_z):
            here = dws.at[0, 0]

            @pl.when(z != target)
            def _():
                remote(here, here, r_ss.at[target, piece], loc_sem.at[8], me, z).wait_send()

    for q in range(half):
        remote(crecv.at[q], crecv.at[q], c_ss.at[q], loc_sem.at[8], me, z).wait_send()
    remote(cvec, cvec, cv_ss.at[0], loc_sem.at[8], me, z).wait_send()
    for k in range(1, half):
        remote(crecv.at[0], crecv.at[0], h_ss.at[k], loc_sem.at[8], me, z).wait_send()
        remote(cvec, cvec, hv_ss.at[k], loc_sem.at[8], me, z).wait_send()


def finish_kernel(mixed, gtok, gqkv, gwo, gsmall, gin, gout, *outs):
    me = lax.axis_index("dp")
    outs[0][...] = mixed[...]
    outs[1][...] = gtok[...].astype(F32)
    for source, target in ((gqkv, outs[2]), (gwo, outs[3]), (gin, outs[4]), (gout, outs[5])):
        target[...] = source[...]
    lanes = gsmall[:, pl.ds(pl.multiple_of((me // 2) * 128, 128), 128)]
    lanes = jnp.where(lax.rem(me, 2) == 1, pltpu.roll(lanes, 64, 1), lanes)
    outs[6][...] = lanes[:, 0:64]


def whole_images(
    tokens, ln1_gain, ln1_bias, w_qkv, w_out, ln2_gain, ln2_bias, w_router, expert_in, expert_out, routes, targets
):
    n_dp, n_z = lax.axis_size("dp"), lax.axis_size("seq")
    image_count, block, width = tokens.shape
    im = image_count // 3
    cap = 2 * S // (n_z * w_router.shape[1]) + 2
    dims = (n_dp, n_z, (image_count // 6, im, im, image_count // 6), block, cap)
    sp, half = n_z * BP, n_dp // 2
    me, z = lax.axis_index("dp"), lax.axis_index("seq")
    dma, vm = pltpu.SemaphoreType.DMA, pltpu.VMEM

    valid = z * block + jnp.arange(block) < VALID
    lines = jnp.where(valid[None, None, :], jnp.transpose(routes, (0, 2, 1)) + 1, 0)
    lines = jnp.pad(lines, ((0, 0), (0, 6), (0, BP - block)))
    odd = lax.rem(z, 2) == 1
    lines = jnp.concatenate([jnp.where(odd, 0, lines), jnp.where(odd, lines, 0)], axis=-1)
    vec = jnp.concatenate(
        [
            jnp.stack([ln1_gain, ln1_bias, ln2_gain, ln2_bias]),
            jnp.zeros((4, ln1_gain.shape[0]), BF),
            jnp.transpose(w_router),
        ],
        axis=0,
    )
    vec = lax.dynamic_update_slice(jnp.zeros((16, width), BF), vec, (0, me * ln1_gain.shape[0]))
    blocks = (n_z, im, block, width)
    in_any, in_vmem = pl.BlockSpec(memory_space=pl.ANY), pl.BlockSpec(memory_space=pltpu.VMEM)
    mixed, gtok, gqkv, gwo, gsmall, gin, gout = pl.pallas_call(
        functools.partial(block_kernel, dims),
        out_shape=[
            jax.ShapeDtypeStruct((image_count, block, width), BF),
            jax.ShapeDtypeStruct((image_count, block, width), BF),
            jax.ShapeDtypeStruct((64, 1536), F32),
            jax.ShapeDtypeStruct((64, width), F32),
            jax.ShapeDtypeStruct((16, width), F32),
            jax.ShapeDtypeStruct((512, 512), F32),
            jax.ShapeDtypeStruct((512, 512), F32),
        ],
        in_specs=[in_any, in_any, in_vmem, in_any, in_any, in_vmem, in_any, in_any],
        out_specs=[in_any, in_any] + [in_vmem] * 3 + [in_any] * 2,
        scratch_shapes=[
            vm(blocks, BF), vm((n_z, im, 8, 128), jnp.int32), vm(blocks, BF), vm((n_dp, 16, width), BF),
            vm((width, 1536), BF), vm((width, width), BF), vm((16, width), F32), vm((im, sp, width), BF),
            vm((im, sp, width), BF), vm((im, sp, 1536), BF), vm((im, sp, width), BF),
            vm((im, sp, 128), F32), vm((im, 8, sp), F32), vm((im, 8, sp), F32),
            vm((n_z, 512, 512), BF), vm((n_z, 512, 512), BF), vm((im, 512, 512), BF), vm((im, 512, 512), BF),
            vm((n_z, im, 512, 512), BF), vm((n_z, im, 512, 512), BF), vm((im, 512, 512), BF),
            vm((im, 512, 512), BF), vm((im, sp, width), F32), vm((n_z, 2, 512, 512), BF), vm((5, 2, 512, 512), BF),
            vm((width, 2048), F32), vm((16, width), F32), vm((half, 64, 2048), BF), vm((half, 64, 2048), BF),
            vm((16, width), F32), vm((half, 64, 2048), BF), vm((half, 16, width), F32),
            vm((2, 32, 2048), BF), vm((n_z, 32, 2048), BF), vm((2, 32, 2048), BF), vm((n_z + 1, 16, width), F32),
            dma((9,)), dma((n_z,)), dma((n_z,)), dma((n_z,)), dma((n_z,)), dma((n_z,)), dma((n_z,)),
            dma((3, half)), dma((3, n_dp)), dma((3, half)), dma((2, n_z)), dma((n_z,)), dma((2, n_z)), dma((n_z,)),
            dma((im, n_dp)), dma((im, n_dp)), dma((im, n_dp)), dma((im, n_dp)), dma((im, n_dp)), dma((im, n_dp)),
            dma((im, n_dp)), dma((im, n_dp)),
            dma((n_z,)), dma((n_z,)), dma((n_z,)), dma((n_z,)),
            dma((n_z, 2)), dma((5, 2)), dma((half,)), dma((half,)), dma((1,)), dma((1,)),
            dma((half,)), dma((half,)), dma((half,)), dma((half,)), dma((2,)), dma((n_z,)), dma((n_z,)), dma((2,)),
            dma((n_z,)), dma((n_z + 1,)),
        ],
        compiler_params=pltpu.CompilerParams(
            collective_id=1, has_side_effects=True, vmem_limit_bytes=VMEM_LIMIT
        ),
        name="block",
    )(tokens, targets, lines, w_qkv, w_out, vec, expert_in[0], expert_out[0])
    whole = pl.BlockSpec(memory_space=pltpu.VMEM)
    mixed, gtok, gqkv, gwo, gin, gout, part = pl.pallas_call(
        finish_kernel,
        out_shape=[
            jax.ShapeDtypeStruct((image_count, block, width), BF),
            jax.ShapeDtypeStruct((image_count, block, width), F32),
            jax.ShapeDtypeStruct((64, 1536), F32),
            jax.ShapeDtypeStruct((64, width), F32),
            jax.ShapeDtypeStruct((512, 512), F32),
            jax.ShapeDtypeStruct((512, 512), F32),
            jax.ShapeDtypeStruct((16, 64), F32),
        ],
        in_specs=[whole] * 7,
        out_specs=[whole] * 7,
        name="finish",
    )(mixed, gtok, gqkv, gwo, gsmall, gin, gout)
    return (
        mixed,
        gtok,
        part[0],
        part[1],
        gqkv,
        gwo,
        part[2],
        part[3],
        jnp.transpose(part[8:16]),
        gin[None],
        gout[None],
    )


def fits(tokens, w_qkv, w_router, expert_in):
    n_dp, n_z = lax.axis_size("dp"), lax.axis_size("seq")
    return (
        n_dp == 8
        and n_z == 4
        and tokens.shape[0] % 6 == 0
        and tokens.shape[1] <= BP
        and tokens.shape[2] == 512
        and w_qkv.shape == (64, 1536)
        and w_router.shape[1] == n_dp
        and expert_in.shape == (1, 512, 512)
    )


def local(*args):
    if fits(args[0], args[3], args[7], args[8]):
        return whole_images(*args)
    return by_heads(*args)


def solution(mesh):
    placed = (
        P("dp", "seq", None),
        P("dp"),
        P("dp"),
        P("dp", None),
        P("dp", None),
        P("dp"),
        P("dp"),
        P("dp", None),
        P("dp", None, "seq"),
        P("dp", "seq", None),
        P("dp", "seq", None),
        P("dp", "seq", None),
    )
    return jax.shard_map(
        local,
        mesh=mesh,
        in_specs=placed,
        out_specs=(
            P("dp", "seq", None),
            P("dp", "seq", None),
            P("dp"),
            P("dp"),
            P("dp", None),
            P("dp", None),
            P("dp"),
            P("dp"),
            P("dp", None),
            P("dp", None, "seq"),
            P("dp", "seq", None),
        ),
        check_vma=False,
    )
```

```python
import functools

import jax
import jax.numpy as jnp
from jax import lax
from jax.experimental import pallas as pl
from jax.experimental.pallas import tpu as pltpu
from jax.sharding import PartitionSpec as P

H = 8
S = 200
VALID = 197


def layer_norm(values, gain_vec, bias_vec):
    centre = values - jnp.mean(values, axis=-1, keepdims=True)
    spread = jnp.mean(centre * centre, axis=-1, keepdims=True)
    return centre * lax.rsqrt(spread + 1e-06) * gain_vec + bias_vec


def regroup_heads(values):
    return lax.all_to_all(values, "seq", split_axis=3, concat_axis=1, tiled=True)


def regroup_slots(values):
    return lax.all_to_all(values, "seq", split_axis=1, concat_axis=3, tiled=True)


def send_experts(values):
    return lax.all_to_all(values, "dp", split_axis=0, concat_axis=1, tiled=True)


def send_tokens(values):
    return lax.all_to_all(values, "dp", split_axis=1, concat_axis=0, tiled=True)


def masked_scores(queries, keys_in, key_valid):
    scores = (
        jnp.einsum("bqhd,bkhd->bhqk", queries, keys_in, preferred_element_type=jnp.float32) * 0.125
    )
    return jnp.where(key_valid, scores, -1e30)


def attention_forward(queries, keys_in, values, key_valid):
    scores = masked_scores(queries, keys_in, key_valid)
    row_top = jnp.max(scores, axis=-1, keepdims=True)
    exponent = jnp.exp(scores - row_top)
    row_total = jnp.sum(exponent, axis=-1, keepdims=True)
    prob_rows = exponent / row_total
    log_total = row_top + jnp.log(row_total)
    attended = jnp.einsum(
        "bhqk,bkhd->bqhd",
        prob_rows.astype(jnp.bfloat16),
        values,
        preferred_element_type=jnp.float32,
    )
    return (attended.astype(jnp.bfloat16), log_total)


def attention_backward(queries, keys_in, values, log_total, grad_attended, key_valid):
    scores = masked_scores(queries, keys_in, key_valid)
    prob_rows = jnp.exp(scores - log_total)
    grad_values = jnp.einsum(
        "bhqk,bqhd->bkhd",
        prob_rows.astype(jnp.bfloat16),
        grad_attended,
        preferred_element_type=jnp.float32,
    )
    grad_probs = jnp.einsum(
        "bqhd,bkhd->bhqk", grad_attended, values, preferred_element_type=jnp.float32
    )
    inner_sum = jnp.sum(prob_rows * grad_probs, axis=-1, keepdims=True)
    grad_scores = (prob_rows * (grad_probs - inner_sum)).astype(jnp.bfloat16)
    grad_queries = (
        jnp.einsum("bhqk,bkhd->bqhd", grad_scores, keys_in, preferred_element_type=jnp.float32)
        * 0.125
    )
    grad_keys = (
        jnp.einsum("bhqk,bqhd->bkhd", grad_scores, queries, preferred_element_type=jnp.float32)
        * 0.125
    )
    return jnp.stack([grad_queries, grad_keys, grad_values], axis=2)


def pick_block(total_rows):
    for candidate in (1024, 768, 512, 384, 256):
        if total_rows % candidate == 0:
            return candidate
    return total_rows


def by_heads(
    tokens,
    ln1_gain,
    ln1_bias,
    w_qkv,
    w_out,
    ln2_gain,
    ln2_bias,
    w_router,
    expert_in,
    expert_out,
    routes,
    targets,
):
    image_count, slot_count, model_width = tokens.shape
    seq_devices = lax.axis_size("seq")
    row_count = image_count * slot_count
    expert_count = w_router.shape[1]
    local_experts = expert_in.shape[0]
    slot_limit = 2 * S // (seq_devices * expert_count) + 2
    head_size = model_width // H
    gathered = (
        lax.all_gather(ln1_gain, "dp", axis=0, tiled=True),
        lax.all_gather(ln1_bias, "dp", axis=0, tiled=True),
        lax.all_gather(w_qkv, "dp", axis=0, tiled=True),
        lax.all_gather(w_out, "dp", axis=0, tiled=True),
        lax.all_gather(ln2_gain, "dp", axis=0, tiled=True),
        lax.all_gather(ln2_bias, "dp", axis=0, tiled=True),
        lax.all_gather(w_router, "dp", axis=0, tiled=True),
    )
    gain_one = gathered[0].astype(jnp.float32)
    bias_one = gathered[1].astype(jnp.float32)
    qkv_weight = gathered[2]
    out_weight = gathered[3]
    gain_two = gathered[4].astype(jnp.float32)
    bias_two = gathered[5].astype(jnp.float32)
    router_weight = gathered[6]
    slot_start = lax.axis_index("seq") * slot_count
    valid_slot = slot_start + jnp.arange(slot_count) < VALID
    valid_rows = jnp.tile(valid_slot, image_count)
    key_valid = (jnp.arange(S) < VALID)[None, None, None, :]
    token_rows = tokens.reshape(row_count, model_width).astype(jnp.float32)
    normed_one, norm_one_back = jax.vjp(layer_norm, token_rows, gain_one, bias_one)
    normed_one_b = normed_one.astype(jnp.bfloat16)
    mixed_qkv = jnp.dot(normed_one_b, qkv_weight, preferred_element_type=jnp.float32).astype(
        jnp.bfloat16
    )
    qkv_heads = regroup_heads(mixed_qkv.reshape(image_count, slot_count, 3, H, head_size))
    queries = qkv_heads[:, :, 0]
    keys_in = qkv_heads[:, :, 1]
    values = qkv_heads[:, :, 2]
    attended, log_total = attention_forward(queries, keys_in, values, key_valid)
    attended_rows = regroup_slots(attended[:, :, None]).reshape(row_count, model_width)
    residual_two = token_rows + jnp.dot(
        attended_rows, out_weight, preferred_element_type=jnp.float32
    )
    normed_two, norm_two_back = jax.vjp(layer_norm, residual_two, gain_two, bias_two)
    normed_two_b = normed_two.astype(jnp.bfloat16)
    logits = jnp.dot(normed_two_b, router_weight, preferred_element_type=jnp.float32)
    route_rows = routes.reshape(row_count, 2)
    chosen = (route_rows[:, :, None] == jnp.arange(expert_count)[None, None, :]) & valid_rows[
        :, None, None
    ]
    chosen_f = chosen.astype(jnp.float32)

    def gate_pick(logit_rows):
        return jnp.sum(jax.nn.softmax(logit_rows, axis=-1)[:, None, :] * chosen_f, axis=-1)

    gate_values, gate_back = jax.vjp(gate_pick, logits)
    pick_count = chosen.astype(jnp.int32).reshape(image_count, slot_count * 2, expert_count)
    before = jnp.cumsum(pick_count, axis=1) - pick_count
    place_hit = (before[..., None] == jnp.arange(slot_limit)) & (pick_count[..., None] > 0)
    dispatch = place_hit.astype(jnp.bfloat16).reshape(
        image_count, slot_count, 2, expert_count, slot_limit
    )
    normed_img = normed_two_b.reshape(image_count, slot_count, model_width)
    sent_rows = jnp.einsum(
        "bskem,bsd->ebmd", dispatch, normed_img, preferred_element_type=jnp.float32
    ).astype(jnp.bfloat16)
    received = send_experts(sent_rows.reshape(expert_count, image_count * slot_limit, model_width))
    weights_in, weights_out = (
        lax.all_gather(expert_in, "seq", axis=2, tiled=True),
        lax.all_gather(expert_out, "seq", axis=1, tiled=True),
    )
    total_rows = received.shape[1]
    block_rows = pick_block(total_rows)
    block_count = total_rows // block_rows

    def expert_step(block_index, produced):
        row_piece = lax.dynamic_slice_in_dim(received, block_index * block_rows, block_rows, 1)
        hidden_pre = jnp.einsum(
            "erd,edf->erf", row_piece, weights_in, preferred_element_type=jnp.float32
        )
        activated = jax.nn.gelu(hidden_pre).astype(jnp.bfloat16)
        result = jnp.einsum(
            "erf,efd->erd", activated, weights_out, preferred_element_type=jnp.float32
        ).astype(jnp.bfloat16)
        return lax.dynamic_update_slice_in_dim(produced, result, block_index * block_rows, 1)

    produced = lax.fori_loop(
        0,
        block_count,
        expert_step,
        jnp.zeros((local_experts, total_rows, model_width), jnp.bfloat16),
    )
    returned = send_tokens(produced).reshape(expert_count, image_count, slot_limit, model_width)
    per_choice = jnp.einsum(
        "bskem,ebmd->bskd", dispatch, returned, preferred_element_type=jnp.float32
    ).reshape(row_count, 2, model_width)
    mixed_rows = (
        residual_two
        + gate_values[:, 0:1] * per_choice[:, 0]
        + gate_values[:, 1:2] * per_choice[:, 1]
    )
    target_rows = targets.reshape(row_count, model_width).astype(jnp.float32)
    grad_mixed = (mixed_rows - target_rows) * valid_rows[:, None].astype(jnp.float32)
    grad_gates = jnp.sum(grad_mixed[:, None, :] * per_choice, axis=-1)
    grad_choice = (
        (gate_values[:, :, None] * grad_mixed[:, None, :])
        .astype(jnp.bfloat16)
        .reshape(image_count, slot_count, 2, model_width)
    )
    grad_sent = jnp.einsum(
        "bskem,bskd->ebmd", dispatch, grad_choice, preferred_element_type=jnp.float32
    ).astype(jnp.bfloat16)
    grad_received = send_experts(
        grad_sent.reshape(expert_count, image_count * slot_limit, model_width)
    )
    back_in, back_out = (
        lax.all_gather(expert_in, "seq", axis=2, tiled=True),
        lax.all_gather(expert_out, "seq", axis=1, tiled=True),
    )

    def expert_back(block_index, loop_carry):
        grad_in_sum, grad_out_sum, grad_rows = loop_carry
        row_piece = lax.dynamic_slice_in_dim(received, block_index * block_rows, block_rows, 1)
        grad_piece = lax.dynamic_slice_in_dim(
            grad_received, block_index * block_rows, block_rows, 1
        )
        hidden_pre = jnp.einsum(
            "erd,edf->erf", row_piece, back_in, preferred_element_type=jnp.float32
        )
        activated, gelu_back = jax.vjp(jax.nn.gelu, hidden_pre)
        grad_act = jnp.einsum(
            "erd,efd->erf", grad_piece, back_out, preferred_element_type=jnp.float32
        )
        grad_pre = gelu_back(grad_act)[0].astype(jnp.bfloat16)
        grad_out_sum = grad_out_sum + jnp.einsum(
            "erf,erd->efd",
            activated.astype(jnp.bfloat16),
            grad_piece,
            preferred_element_type=jnp.float32,
        )
        grad_in_sum = grad_in_sum + jnp.einsum(
            "erd,erf->edf", row_piece, grad_pre, preferred_element_type=jnp.float32
        )
        rows_back = jnp.einsum(
            "erf,edf->erd", grad_pre, back_in, preferred_element_type=jnp.float32
        ).astype(jnp.bfloat16)
        grad_rows = lax.dynamic_update_slice_in_dim(
            grad_rows, rows_back, block_index * block_rows, 1
        )
        return (grad_in_sum, grad_out_sum, grad_rows)

    start_carry = (
        jnp.zeros(back_in.shape, jnp.float32),
        jnp.zeros(back_out.shape, jnp.float32),
        jnp.zeros((local_experts, total_rows, model_width), jnp.bfloat16),
    )
    grad_in_sum, grad_out_sum, grad_rows = lax.fori_loop(0, block_count, expert_back, start_carry)
    grad_returned = send_tokens(grad_rows).reshape(
        expert_count, image_count, slot_limit, model_width
    )
    grad_normed_two = jnp.einsum(
        "bskem,ebmd->bsd", dispatch, grad_returned, preferred_element_type=jnp.float32
    ).reshape(row_count, model_width)
    grad_logits = gate_back(grad_gates)[0].astype(jnp.bfloat16)
    grad_router = jnp.einsum(
        "rd,re->de", normed_two_b, grad_logits, preferred_element_type=jnp.float32
    )
    grad_normed_two = grad_normed_two + jnp.einsum(
        "re,de->rd", grad_logits, router_weight, preferred_element_type=jnp.float32
    )
    grad_res_two, grad_gain_two, grad_bias_two = norm_two_back(grad_normed_two)
    grad_residual = grad_mixed + grad_res_two
    grad_branch = grad_residual.astype(jnp.bfloat16)
    grad_out_weight = jnp.einsum(
        "rd,re->de", attended_rows, grad_branch, preferred_element_type=jnp.float32
    )
    grad_attended = jnp.einsum(
        "re,de->rd", grad_branch, out_weight, preferred_element_type=jnp.float32
    ).astype(jnp.bfloat16)
    grad_heads = regroup_heads(grad_attended.reshape(image_count, slot_count, 1, H, head_size))[
        :, :, 0
    ]
    grad_qkv_heads = attention_backward(
        queries, keys_in, values, log_total, grad_heads, key_valid
    ).astype(jnp.bfloat16)
    grad_qkv_rows = regroup_slots(grad_qkv_heads).reshape(row_count, 3 * model_width)
    grad_qkv_weight = jnp.einsum(
        "rd,rf->df", normed_one_b, grad_qkv_rows, preferred_element_type=jnp.float32
    )
    grad_normed_one = jnp.einsum(
        "rf,df->rd", grad_qkv_rows, qkv_weight, preferred_element_type=jnp.float32
    )
    grad_token_ln, grad_gain_one, grad_bias_one = norm_one_back(grad_normed_one)
    grad_tokens = grad_residual + grad_token_ln
    dense_grads = (
        grad_gain_one,
        grad_bias_one,
        grad_qkv_weight,
        grad_out_weight,
        grad_gain_two,
        grad_bias_two,
        grad_router,
    )
    dense_grads = (
        lax.psum(dense_grads[0].astype(jnp.bfloat16), "seq").astype(jnp.float32),
        lax.psum(dense_grads[1].astype(jnp.bfloat16), "seq").astype(jnp.float32),
        lax.psum(dense_grads[2].astype(jnp.bfloat16), "seq").astype(jnp.float32),
        lax.psum(dense_grads[3].astype(jnp.bfloat16), "seq").astype(jnp.float32),
        lax.psum(dense_grads[4].astype(jnp.bfloat16), "seq").astype(jnp.float32),
        lax.psum(dense_grads[5].astype(jnp.bfloat16), "seq").astype(jnp.float32),
        lax.psum(dense_grads[6].astype(jnp.bfloat16), "seq").astype(jnp.float32),
    )
    dense_grads = (
        lax.psum_scatter(
            dense_grads[0].astype(jnp.bfloat16), "dp", scatter_dimension=0, tiled=True
        ).astype(jnp.float32),
        lax.psum_scatter(
            dense_grads[1].astype(jnp.bfloat16), "dp", scatter_dimension=0, tiled=True
        ).astype(jnp.float32),
        lax.psum_scatter(
            dense_grads[2].astype(jnp.bfloat16), "dp", scatter_dimension=0, tiled=True
        ).astype(jnp.float32),
        lax.psum_scatter(
            dense_grads[3].astype(jnp.bfloat16), "dp", scatter_dimension=0, tiled=True
        ).astype(jnp.float32),
        lax.psum_scatter(
            dense_grads[4].astype(jnp.bfloat16), "dp", scatter_dimension=0, tiled=True
        ).astype(jnp.float32),
        lax.psum_scatter(
            dense_grads[5].astype(jnp.bfloat16), "dp", scatter_dimension=0, tiled=True
        ).astype(jnp.float32),
        lax.psum_scatter(
            dense_grads[6].astype(jnp.bfloat16), "dp", scatter_dimension=0, tiled=True
        ).astype(jnp.float32),
    )
    expert_in_grad, expert_out_grad = (
        lax.psum_scatter(
            grad_in_sum.astype(jnp.bfloat16), "seq", scatter_dimension=2, tiled=True
        ).astype(jnp.float32),
        lax.psum_scatter(
            grad_out_sum.astype(jnp.bfloat16), "seq", scatter_dimension=1, tiled=True
        ).astype(jnp.float32),
    )
    mixed = mixed_rows.astype(jnp.bfloat16).reshape(image_count, slot_count, model_width)
    return (
        mixed,
        grad_tokens.reshape(image_count, slot_count, model_width),
        dense_grads[0],
        dense_grads[1],
        dense_grads[2],
        dense_grads[3],
        dense_grads[4],
        dense_grads[5],
        dense_grads[6],
        expert_in_grad,
        expert_out_grad,
    )


BF = jnp.bfloat16
F32 = jnp.float32
MESH_ID = pl.DeviceIdType.MESH
NEG = -1e30
BP = 64
VMEM_LIMIT = 67000000
GELU_C = 0.7978845608028654
GELU_K = 0.044715


def nn(a, b):
    return lax.dot_general(a, b, (((1,), (0,)), ((), ())), preferred_element_type=F32)


def nt(a, b):
    return lax.dot_general(a, b, (((1,), (1,)), ((), ())), preferred_element_type=F32)


def tn(a, b):
    return lax.dot_general(a, b, (((0,), (0,)), ((), ())), preferred_element_type=F32)


def remote(src, dst, send_sem, recv_sem, dp, z):
    return pltpu.make_async_remote_copy(
        src_ref=src,
        dst_ref=dst,
        send_sem=send_sem,
        recv_sem=recv_sem,
        device_id=(dp, z),
        device_id_type=MESH_ID,
    )


def rows_of(index, size):
    return pl.ds(pl.multiple_of(index * size, size), size)


def norm_parts(x):
    centre = x - jnp.mean(x, axis=-1, keepdims=True)
    scale = lax.rsqrt(jnp.mean(centre * centre, axis=-1, keepdims=True) + 1e-06)
    return centre * scale, scale


def norm_back(grad_hat, hat, scale):
    return scale * (
        grad_hat
        - jnp.mean(grad_hat, axis=-1, keepdims=True)
        - hat * jnp.mean(grad_hat * hat, axis=-1, keepdims=True)
    )


def half_masks():
    lane = lax.broadcasted_iota(jnp.int32, (1, 128), 1)
    low = jnp.where(lane < 64, 1.0, 0.0)
    return (low.astype(BF), (1.0 - low).astype(BF))


def slot_ok(position, block):
    return (position % BP < block) & ((position // BP) * block + position % BP < VALID)


def block_kernel(
    dims,
    tok, tgt, rts, wq, wo, vec, win, wout,
    mixed, gtok, gqkv, gwo, gsmall, gin, gout,
    xin, rin, tin, vec_all, wq_all, wo_all, vsum, xpad, n2s, qkvs, outs, cols, gts, meta,
    win_all, wout_all, recv, ret, acts, slopes, sbuf,
    drows, dys, dws, arrived,
    gacc, accf, gvec, csend, crecv, cvec, hrecv, hvec, zsend, zrecv, zall, zvec,
    loc_sem, tok_ss, tok_rs, rts_ss, rts_rs, tgt_ss, tgt_rs, den_ss, den_rs, fwd_ss, win_ss, win_rs, wout_ss, wout_rs,
    row_ss, row_rs, u_ss, u_rs, du_ss, du_rs, dn_ss, dn_rs, mix_ss, mix_rs, gt_ss, gt_rs,
    r_ss, r_rs, c_ss, c_rs, cv_ss, cv_rs, h_ss, h_rs, hv_ss, hv_rs, za_ss, za_rs, zb_ss, zb_rs, zv_ss, zv_rs,
):
    n_dp, n_z, counts, block, cap = dims
    firsts = tuple(sum(counts[:h]) for h in range(n_z))
    me, z = lax.axis_index("dp"), lax.axis_index("seq")
    sp = n_z * BP
    half = n_dp // 2
    last = n_z - 1
    core, chip = lax.rem(me, 2), me // 2
    partner = chip * 2 + 1 - core
    inner = (z == 1) | (z == last - 1)
    ends = jnp.logical_not(inner)
    far_end = jnp.where(z < n_z // 2, last, 0)
    near_end = last - far_end
    middle = last - z
    im = jnp.where(inner, counts[1], counts[0])
    sizes = ((counts[1], inner), (counts[0], ends))
    first = jnp.where(z == 0, firsts[0], jnp.where(z == 1, firsts[1], jnp.where(z == 2, firsts[2], firsts[3])))

    barrier = pltpu.get_barrier_semaphore()
    for k in range(1, n_dp):
        pl.semaphore_signal(barrier, inc=1, device_id=(lax.rem(me + k, n_dp), z), device_id_type=MESH_ID)
    for k in range(1, n_z):
        pl.semaphore_signal(barrier, inc=1, device_id=(me, lax.rem(z + k, n_z)), device_id_type=MESH_ID)

    def hosts_own(source, target, sem):
        for h in range(n_z):

            @pl.when(z == h)
            def _():
                pltpu.make_async_copy(
                    source.at[pl.ds(firsts[h], counts[h])], target.at[z, pl.ds(0, counts[h])], sem
                ).start()

    def hosts_own_wait(source, target, sem):
        for h in range(n_z):

            @pl.when(z == h)
            def _():
                pltpu.make_async_copy(
                    source.at[pl.ds(firsts[h], counts[h])], target.at[z, pl.ds(0, counts[h])], sem
                ).wait()

    def hosts_start(source, target, send_sem, recv_sem, hosts, who):
        for h in hosts:

            @pl.when((z != h) & who)
            def _():
                remote(
                    source.at[pl.ds(firsts[h], counts[h])],
                    target.at[z, pl.ds(0, counts[h])],
                    send_sem.at[h],
                    recv_sem.at[z],
                    me,
                    h,
                ).start()

    def hosts_arrive(target, recv_sem):
        for size, there in sizes:

            @pl.when(there)
            def _():
                for k in range(1, n_z):
                    origin = lax.rem(z + k, n_z)
                    spot = target.at[origin, pl.ds(0, size)]
                    remote(spot, spot, loc_sem.at[8], recv_sem.at[origin], me, z).wait_recv()

    def hosts_sent(target, send_sem):
        for h in range(n_z):

            @pl.when(z != h)
            def _():
                spot = target.at[0, pl.ds(0, counts[h])]
                remote(spot, spot, send_sem.at[h], loc_sem.at[8], me, z).wait_send()

    def home_own(source, target, sem):
        return [
            (there, pltpu.make_async_copy(source.at[z, pl.ds(0, size)], target.at[pl.ds(first, size)], sem))
            for size, there in sizes
        ]

    def home_start(source, target, send_sem, recv_sem, who):
        for size, there in who:

            @pl.when(there)
            def _():
                for k in range(1, n_z):
                    peer = lax.rem(z + k, n_z)
                    remote(
                        source.at[peer, pl.ds(0, size)],
                        target.at[pl.ds(first, size)],
                        send_sem.at[k],
                        recv_sem.at[z],
                        me,
                        peer,
                    ).start()

    def home_arrive(target, recv_sem):
        for h in range(n_z):

            @pl.when(z != h)
            def _():
                spot = target.at[pl.ds(firsts[h], counts[h])]
                remote(spot, spot, loc_sem.at[8], recv_sem.at[h], me, z).wait_recv()

    def home_sent(source, send_sem):
        for size, there in sizes:

            @pl.when(there)
            def _():
                for k in range(1, n_z):
                    spot = source.at[0, pl.ds(0, size)]
                    remote(spot, spot, send_sem.at[k], loc_sem.at[8], me, z).wait_send()

    def each(pairs, act):
        for there, copy in pairs:

            @pl.when(there)
            def _():
                getattr(copy, act)()

    own_copies = [
        pltpu.make_async_copy(win, win_all.at[z], loc_sem.at[3]),
        pltpu.make_async_copy(wout, wout_all.at[z], loc_sem.at[4]),
        pltpu.make_async_copy(wq, wq_all.at[rows_of(me, 64)], loc_sem.at[5]),
        pltpu.make_async_copy(wo, wo_all.at[rows_of(me, 64)], loc_sem.at[6]),
        pltpu.make_async_copy(vec, vec_all.at[me], loc_sem.at[7]),
    ]
    for copy in own_copies:
        copy.start()
    hosts_own(tok, xin, loc_sem.at[0])
    hosts_own(rts, rin, loc_sem.at[1])
    hosts_own(tgt, tin, loc_sem.at[2])
    for buffer in (xpad, gvec, recv, ret, drows):
        buffer[...] = jnp.zeros_like(buffer)
    pl.semaphore_wait(barrier, n_dp + n_z - 2)
    hosts_start(tok, xin, tok_ss, tok_rs, range(n_z), z >= 0)
    hosts_start(rts, rin, rts_ss, rts_rs, range(n_z), z >= 0)

    def dense_slot(array, index):
        if array == 0:
            return wq_all.at[rows_of(index, 64)]
        if array == 1:
            return wo_all.at[rows_of(index, 64)]
        return vec_all.at[index]

    dense_in = (wq, wo, vec)
    for array in range(3):
        for k in range(1, half):
            peer = lax.rem(chip + k, half) * 2 + core
            remote(
                dense_in[array], dense_slot(array, me), den_ss.at[array, k], den_rs.at[array, me], peer, z
            ).start()
        remote(
            dense_in[array], dense_slot(array, me), den_ss.at[array, 0], den_rs.at[array, me], partner, z
        ).start()

    experts = ((win, win_all, win_ss, win_rs), (wout, wout_all, wout_ss, wout_rs))

    def gather_hop(array, step):
        source, full, send_sem, recv_sem = experts[array]
        for way, there, slot in ((0, z >= step, z - step), (1, z + step < n_z, z + step)):

            @pl.when(there)
            def _():
                at = full.at[slot]
                if step > 0:
                    remote(at, at, send_sem.at[way, step], recv_sem.at[slot], me, z).wait_recv()

                @pl.when((z < last) if way == 0 else (z > 0))
                def _():
                    remote(
                        at if step > 0 else source,
                        at,
                        send_sem.at[way, step],
                        recv_sem.at[slot],
                        me,
                        z + 1 if way == 0 else z - 1,
                    ).start()

    def weights_sent():
        for step in range(n_z - 1):
            for way, there in ((0, (z >= step) & (z < last)), (1, (z + step < n_z) & (z > 0))):

                @pl.when(there)
                def _():
                    for source, full, send_sem, recv_sem in experts:
                        remote(
                            full.at[0], full.at[0], send_sem.at[way, step], recv_sem.at[0], me, z
                        ).wait_send()

    gather_hop(0, 0)
    gather_hop(1, 0)

    for k in range(1, half):
        origin = lax.rem(chip + k, half) * 2 + core
        for array in range(3):
            slot = dense_slot(array, origin)
            remote(slot, slot, den_ss.at[array, 0], den_rs.at[array, origin], me, z).wait_recv()
            remote(slot, slot, fwd_ss.at[array, k], den_rs.at[array, origin], partner, z).start()
    for k in range(half):
        origin = lax.rem(chip + k, half) * 2 + 1 - core
        for array in range(3):
            slot = dense_slot(array, origin)
            remote(slot, slot, den_ss.at[array, 0], den_rs.at[array, origin], me, z).wait_recv()
    for copy in own_copies:
        copy.wait()
    hosts_own_wait(tok, xin, loc_sem.at[0])
    hosts_own_wait(rts, rin, loc_sem.at[1])
    hosts_own_wait(tgt, tin, loc_sem.at[2])
    total = vec_all[0].astype(F32)
    for k in range(1, n_dp):
        total = total + vec_all[k].astype(F32)
    vsum[...] = total
    hosts_arrive(xin, tok_rs)
    hosts_arrive(rin, rts_rs)

    masks = half_masks()
    eighths = [mask * 0.125 for mask in masks]
    keys_ok = slot_ok(lax.broadcasted_iota(jnp.int32, (1, sp), 1), block)
    rows_ok = slot_ok(lax.broadcasted_iota(jnp.int32, (sp, 1), 0), block)
    gain_one, bias_one = vsum[0:1, :], vsum[1:2, :]
    gain_two, bias_two = vsum[2:3, :], vsum[3:4, :]
    router_t = vsum[8:16, :].astype(BF)
    lane_id = lax.broadcasted_iota(jnp.int32, (sp, 128), 1)
    lane_low = lane_id < 64
    row_id = lax.broadcasted_iota(jnp.int32, (512, sp), 0).astype(F32)

    def lanes_of(target):
        return pl.ds(pl.multiple_of(target * 512, 512), 512)

    def rows_at(index):
        return pl.ds(pl.multiple_of(index * 64, 64), n_z * cap)

    def send_rows(i, target, send_sem, recv_sem):
        def step(s, carry):
            j, c = lax.rem(s // 2 + 1, half), lax.rem(s, 2)
            index = 2 * j + c
            peer = lax.rem(chip + j, half) * 2 + lax.rem(core + c, 2)

            @pl.when(index > 0)
            def _():
                remote(
                    sbuf.at[i, rows_at(peer)],
                    target.at[i, rows_at(me)],
                    send_sem.at[i, index],
                    recv_sem.at[i, me],
                    peer,
                    z,
                ).start()

            return carry

        lax.fori_loop(0, n_dp, step, 0)
        target[i, rows_of(me, 64)] = sbuf[i, rows_of(me, 64)]

    def arrive(i, target, recv_sem):
        def step(k, carry):
            origin = lax.rem(me + k, n_dp)
            spot = target.at[i, rows_at(origin)]
            remote(spot, spot, loc_sem.at[8], recv_sem.at[i, origin], me, z).wait_recv()
            return carry

        lax.fori_loop(1, n_dp, step, 0)

    def sent(i, send_sem):
        def step(index, carry):
            spot = sbuf.at[i, rows_at(0)]
            remote(spot, spot, send_sem.at[i, index], loc_sem.at[8], me, z).wait_send()
            return carry

        lax.fori_loop(1, n_dp, step, 0)

    def front(i, carry):
        before = lax.broadcasted_iota(jnp.int32, (sp, sp), 0)
        after = lax.broadcasted_iota(jnp.int32, (sp, sp), 1)
        prefix = jnp.where((before < after) & (before // BP == after // BP), 1.0, 0.0).astype(BF)
        expert_id = lax.broadcasted_iota(jnp.int32, (8, sp), 0)
        slot_lane = lax.broadcasted_iota(jnp.int32, (8, sp), 1)
        for b in range(n_z):
            xpad[i, b * BP : b * BP + block, :] = xin[b, i]
        x = xpad[i].astype(F32)
        hat, _ = norm_parts(x)
        normed = (hat * gain_one + bias_one).astype(BF)
        qkvs[i] = nn(normed, wq_all[...]).astype(BF)
        lse_all = jnp.zeros((sp, 128), F32)
        for pair in range(4):
            q2 = qkvs[i, :, pair * 128 : pair * 128 + 128]
            k2 = qkvs[i, :, 512 + pair * 128 : 512 + pair * 128 + 128]
            v2 = qkvs[i, :, 1024 + pair * 128 : 1024 + pair * 128 + 128]
            parts = []
            for side in range(2):
                scores = nt(q2 * eighths[side], k2)
                scores = jnp.where(keys_ok, scores, NEG)
                top = jnp.max(scores, axis=-1, keepdims=True)
                exponent = jnp.exp(scores - top)
                whole = jnp.sum(exponent, axis=-1, keepdims=True)
                lse_all = jnp.where(lane_id == pair * 2 + side, top + jnp.log(whole), lse_all)
                parts.append(nn((exponent / whole).astype(BF), v2))
            outs[i, :, pair * 128 : pair * 128 + 128] = jnp.where(lane_low, parts[0], parts[1]).astype(BF)
        x2 = x + nn(outs[i], wo_all[...])
        hat2, _ = norm_parts(x2)
        n2 = (hat2 * gain_two + bias_two).astype(BF)
        n2s[i] = n2
        logits = nt(router_t, n2)
        raised = jnp.exp(logits - jnp.max(logits, axis=0, keepdims=True))
        share = raised / jnp.sum(raised, axis=0, keepdims=True)
        gts[i] = share
        wide = jnp.concatenate([rin[0, i] + rin[1, i], rin[2, i] + rin[3, i]], axis=1)
        hits = [(expert_id + 1) == wide[j : j + 1, :] for j in range(2)]
        any_hit = jnp.where(hits[0] | hits[1], 1.0, 0.0)
        place = nn(any_hit.astype(BF), prefix)
        base = place + (expert_id * 64 + (slot_lane // BP) * cap + 1).astype(F32)
        lines = [jnp.sum(jnp.where(hit, base, 0.0), axis=0, keepdims=True) - 1.0 for hit in hits]
        lines += [jnp.sum(jnp.where(hit, share, 0.0), axis=0, keepdims=True) for hit in hits]
        lines = jnp.concatenate(lines + [jnp.zeros((4, sp), F32)], axis=0)
        meta[i] = lines
        table = jnp.concatenate([jnp.zeros((8, sp), F32), lines, jnp.zeros((112, sp), F32)], axis=0)
        cols[i] = jnp.transpose(table) + lse_all
        pick = (row_id == lines[0:1, :]) | (row_id == lines[1:2, :])
        sbuf[i] = nn(jnp.where(pick, 1.0, 0.0).astype(BF), n2).astype(BF)
        send_rows(i, recv, row_ss, row_rs)

        @pl.when(i == 1)
        def _():
            gather_hop(0, 1)

        return carry

    lax.fori_loop(0, im, front, 0)


    def hidden(shard):
        def image(i, carry):
            x = recv[i]
            for side in range(2):
                pre = nn(x, win_all[shard, :, side * 256 : side * 256 + 256])
                square = pre * pre
                tanh = jnp.tanh(pre * (GELU_C + (GELU_C * GELU_K) * square))
                gate = 0.5 + 0.5 * tanh
                acts[shard, i, :, side * 256 : side * 256 + 256] = (pre * gate).astype(BF)
                slope = gate + pre * (0.5 - 0.5 * tanh * tanh) * (GELU_C + (3.0 * GELU_C * GELU_K) * square)
                slopes[shard, i, :, side * 256 : side * 256 + 256] = slope.astype(BF)
            return carry

        lax.fori_loop(0, im, image, 0)

    def hidden_step(s, carry):
        for at_step, hop in ((1, 2), (3, 3)):

            @pl.when(s == at_step)
            def _():
                gather_hop(0, hop)

        for way in range(2):
            shard = z - s if way == 0 else z + s

            @pl.when((shard >= 0) & (shard < n_z) & ((s > 0) | (way == 0)))
            def _():
                hidden(shard)

        @pl.when(s == 2)
        def _():
            gather_hop(1, 2)
            hosts_start(tgt, tin, tgt_ss, tgt_rs, (1, 2), z >= 0)

        return carry

    gather_hop(1, 1)

    def rows_here(i, carry):
        arrive(i, recv, row_rs)
        return carry

    lax.fori_loop(0, im, rows_here, 0)
    lax.fori_loop(0, n_z, hidden_step, 0)

    def early_results(i, carry):
        for k in range(1, n_z):
            shard = lax.rem(far_end + k, n_z)
            part = nn(acts[shard, i], wout_all[shard])
            if k == 1:
                gacc[:, lanes_of(i)] = part
            else:
                gacc[:, lanes_of(i)] += part
        return carry

    lax.fori_loop(0, im, early_results, 0)
    gather_hop(1, 3)
    hosts_start(tgt, tin, tgt_ss, tgt_rs, (0, last), ends)

    def results(i, carry):
        sent(i, row_ss)
        sbuf[i] = (gacc[:, lanes_of(i)] + nn(acts[far_end, i], wout_all[far_end])).astype(BF)
        send_rows(i, ret, u_ss, u_rs)
        return carry

    lax.fori_loop(0, im, results, 0)
    gacc[...] = jnp.zeros_like(gacc)

    def mix(i, carry):
        @pl.when(i == 1)
        def _():
            hosts_start(tgt, tin, tgt_ss, tgt_rs, (0, last), inner)

        arrive(i, ret, u_rs)

        @pl.when(i == 0)
        def _():
            hosts_arrive(tin, tgt_rs)

        line = lax.broadcasted_iota(jnp.int32, (sp, 512), 1).astype(F32)
        here = cols[i]
        picked = []
        for j in range(2):
            pick = jnp.where(line == here[:, 8 + j : 9 + j], 1.0, 0.0).astype(BF)
            picked.append(nn(pick, ret[i]))
        x2 = xpad[i].astype(F32) + nn(outs[i], wo_all[...])
        mix = x2 + here[:, 10:11] * picked[0] + here[:, 11:12] * picked[1]
        mix_b = mix.astype(BF)
        for b in range(n_z):
            xin[b, i] = mix_b[b * BP : b * BP + block]
            dys[i, b * BP : b * BP + block, :] = tin[b, i].astype(F32)
        dy = jnp.where(rows_ok, mix - dys[i], 0.0)
        dys[i] = dy
        total = jnp.zeros((512, 512), F32)
        for j in range(2):
            pick = jnp.where(row_id == meta[i, j : j + 1, :], 1.0, 0.0).astype(BF)
            total = total + nn(pick, (here[:, 10 + j : 11 + j] * dy).astype(BF))
        sent(i, u_ss)
        sbuf[i] = total.astype(BF)
        send_rows(i, drows, du_ss, du_rs)
        for j in range(2):
            here = jnp.where(lane_id == 12 + j, jnp.sum(dy * picked[j], axis=-1, keepdims=True), here)
        cols[i] = here
        return carry

    lax.fori_loop(0, im, mix, 0)
    home_start(xin, mixed, mix_ss, mix_rs, sizes)
    own_mixed = home_own(xin, mixed, loc_sem.at[0])
    each(own_mixed, "start")
    expert_row = lax.broadcasted_iota(jnp.int32, (8, sp), 0).astype(F32)

    def gates_back(i, carry):
        flat = jnp.transpose(cols[i])
        share = gts[i]
        grad = jnp.zeros((8, sp), F32)
        for j in range(2):
            at = meta[i, j : j + 1, :]
            inside = (at >= expert_row * 64) & (at < expert_row * 64 + 64)
            grad = grad + jnp.where(inside, flat[12 + j : 13 + j, :], 0.0)
        dlog = share * (grad - jnp.sum(share * grad, axis=0, keepdims=True))
        gts[i] = dlog
        gvec[8:16, :] += nn(dlog.astype(BF), n2s[i])
        return carry

    lax.fori_loop(0, im, gates_back, 0)

    def reduce_start(target, piece):
        peer = jnp.where(z == 0, 1, last - 1)
        slot = jnp.where(target == peer, 0, jnp.where(target == far_end, 2, 1))
        remote(
            dws.at[target, piece], arrived.at[slot, piece], r_ss.at[target, piece], r_rs.at[slot, piece], me, peer
        ).start()

    def reduce_forward(piece, steps):
        @pl.when(inner)
        def _():
            for target, slot, peer, there in steps:
                here = arrived.at[slot, piece]
                remote(here, here, r_ss.at[target, piece], r_rs.at[slot, piece], me, z).wait_recv()

                def add(c, carry):
                    at = rows_of(c, 128)
                    dws[target, piece, at] = (
                        dws[target, piece, at].astype(F32) + arrived[slot, piece, at].astype(F32)
                    ).astype(BF)
                    return carry

                lax.fori_loop(0, 4, add, 0)
                remote(
                    dws.at[target, piece],
                    arrived.at[there, piece],
                    r_ss.at[target, piece],
                    r_rs.at[there, piece],
                    me,
                    peer,
                ).start()

    first_steps = ((far_end, 2, middle, 4),)
    second_steps = ((middle, 1, middle, 3), (near_end, 4, near_end, 0))

    def owner(s):
        return jnp.where(z < n_z // 2, lax.rem(z + 2 * n_z - 1 - s, n_z), lax.rem(z + 1 + s, n_z))

    def out_ready(s, carry):
        target = owner(s)
        dws[target, 0] = gacc[:, lanes_of(target)].astype(BF)

        @pl.when(ends & (s < 2))
        def _():
            reduce_start(target, 0)

        return carry

    def experts_back(i, carry):
        arrive(i, drows, du_rs)
        du = drows[i]
        for target in range(n_z):
            gacc[:, target * 512 : target * 512 + 512] += tn(acts[target, i], du)

        @pl.when(i == im - 1)
        def _():
            lax.fori_loop(0, n_z, out_ready, 0)

        total = jnp.zeros((512, 512), F32)
        for shard in range(n_z):
            dpre = (nt(du, wout_all[shard]) * slopes[shard, i].astype(F32)).astype(BF)
            slopes[shard, i] = dpre
            total = total + nt(dpre, win_all[shard])
        sent(i, du_ss)
        sbuf[i] = total.astype(BF)
        send_rows(i, ret, dn_ss, dn_rs)
        return carry

    lax.fori_loop(0, im, experts_back, 0)

    def in_grads(target):
        accf[...] = tn(recv[0], slopes[target, 0])

        def more(i, carry):
            accf[...] += tn(recv[i], slopes[target, i])
            return carry

        lax.fori_loop(1, im, more, 0)
        dws[target, 1] = accf[...].astype(BF)

    def end_in_grads(s, carry):
        target = owner(s)
        in_grads(target)

        @pl.when(s < 2)
        def _():
            reduce_start(target, 1)

        return carry

    def inner_in_grads(s, carry):
        in_grads(jnp.where(s == 0, far_end, jnp.where(s == 1, middle, jnp.where(s == 2, near_end, z))))
        return carry

    @pl.when(ends)
    def _():
        lax.fori_loop(0, n_z, end_in_grads, 0)

    gacc[...] = jnp.zeros_like(gacc)
    each(own_mixed, "wait")
    home_sent(xin, mix_ss)

    def back(i, carry):
        arrive(i, ret, dn_rs)
        line = lax.broadcasted_iota(jnp.int32, (sp, 512), 1).astype(F32)
        here = cols[i]
        pick = jnp.where((line == here[:, 8:9]) | (line == here[:, 9:10]), 1.0, 0.0).astype(BF)
        dn2 = nn(pick, ret[i]) + tn(gts[i].astype(BF), router_t)
        hat2, scale2 = norm_parts(xpad[i].astype(F32) + nn(outs[i], wo_all[...]))
        gvec[2:3, :] += jnp.sum(dn2 * hat2, axis=0, keepdims=True)
        gvec[3:4, :] += jnp.sum(dn2, axis=0, keepdims=True)
        dx2 = dys[i] + norm_back(dn2 * gain_two, hat2, scale2)
        da = dx2.astype(BF)
        gacc[:, 1536:2048] += tn(outs[i], da)
        do = nt(da, wo_all[...]).astype(BF)
        hat1, scale1 = norm_parts(xpad[i].astype(F32))
        n1 = (hat1 * gain_one + bias_one).astype(BF)
        for pair in range(4):
            at = pair * 128
            q2 = qkvs[i, :, at : at + 128]
            k2 = qkvs[i, :, 512 + at : 512 + at + 128]
            v2 = qkvs[i, :, 1024 + at : 1024 + at + 128]
            do2 = do[:, at : at + 128]
            grads = ([], [], [])
            for side in range(2):
                head = pair * 2 + side
                scores = nt(q2 * eighths[side], k2)
                scores = jnp.where(keys_ok, scores, NEG)
                prob = jnp.exp(scores - here[:, head : head + 1])
                dprob = nt(do2 * masks[side], v2)
                weighted = jnp.sum(prob * dprob, axis=-1, keepdims=True)
                ds = (prob * (dprob - weighted)).astype(BF)
                grads[0].append(nn(ds, k2))
                grads[1].append(tn(ds, q2))
                grads[2].append(tn(prob.astype(BF), do2))
            for part in range(3):
                grad = jnp.where(lane_low, grads[part][0], grads[part][1])
                if part < 2:
                    grad = grad * 0.125
                qkvs[i, :, part * 512 + at : part * 512 + at + 128] = grad.astype(BF)
        dqkv = qkvs[i]
        gacc[:, 0:1536] += tn(n1, dqkv)
        dn1 = nt(dqkv, wq_all[...])
        gvec[0:1, :] += jnp.sum(dn1 * hat1, axis=0, keepdims=True)
        gvec[1:2, :] += jnp.sum(dn1, axis=0, keepdims=True)
        dx = (dx2 + norm_back(dn1 * gain_one, hat1, scale1)).astype(BF)
        for b in range(n_z):
            xin[b, i] = dx[b * BP : b * BP + block]

        @pl.when(i == 0)
        def _():
            reduce_forward(0, first_steps)

        @pl.when(i == 2)
        def _():
            reduce_forward(0, second_steps)

            @pl.when(inner)
            def _():
                lax.fori_loop(0, 1, inner_in_grads, 0)

            reduce_forward(1, first_steps)

        return carry

    lax.fori_loop(0, im, back, 0)
    own_gtok = home_own(xin, gtok, loc_sem.at[1])
    each(own_gtok, "start")

    for q in range(half):
        csend[q] = gacc[rows_of(2 * q + 1 - core, 64)].astype(BF)
        remote(csend.at[q], crecv.at[q], c_ss.at[q], c_rs.at[q], partner, z).start()
    remote(gvec, cvec, cv_ss.at[0], cv_rs.at[0], partner, z).start()

    @pl.when(inner)
    def _():
        lax.fori_loop(1, 3, inner_in_grads, 0)

    for q in range(half):
        remote(crecv.at[q], crecv.at[q], c_ss.at[q], c_rs.at[q], me, z).wait_recv()
    for k in range(1, half):
        q = lax.rem(chip + k, half)
        crecv[q] = (gacc[rows_of(2 * q + core, 64)] + crecv[q].astype(F32)).astype(BF)
        remote(crecv.at[q], hrecv.at[chip], h_ss.at[k], h_rs.at[chip], q * 2 + core, z).start()
    remote(cvec, cvec, cv_ss.at[0], cv_rs.at[0], me, z).wait_recv()
    hvec[chip] = gvec[...] + cvec[...]
    for k in range(1, half):
        q = lax.rem(chip + k, half)
        remote(hvec.at[chip], hvec.at[chip], hv_ss.at[k], hv_rs.at[chip], q * 2 + core, z).start()
    reduce_forward(1, second_steps)

    @pl.when(inner)
    def _():
        lax.fori_loop(3, n_z, inner_in_grads, 0)

    dense = gacc[rows_of(me, 64)] + crecv[chip].astype(F32)
    for k in range(1, half):
        q = lax.rem(chip + k, half)
        remote(hrecv.at[q], hrecv.at[q], h_ss.at[0], h_rs.at[q], me, z).wait_recv()
        dense = dense + hrecv[q].astype(F32)
    gacc[0:64] = dense
    for k in range(1, half):
        q = lax.rem(chip + k, half)
        remote(hvec.at[q], hvec.at[q], hv_ss.at[0], hv_rs.at[q], me, z).wait_recv()
    zvec[0] = hvec[0] + hvec[1] + hvec[2] + hvec[3]

    @pl.when(ends)
    def _():
        zsend[...] = gacc[0:64].astype(BF)
        peer = jnp.where(z == 0, 1, last - 1)
        remote(zsend, zrecv.at[0], za_ss.at[0], za_rs.at[0], me, peer).start()
        remote(zvec.at[0], zvec.at[1], zv_ss.at[0], zv_rs.at[1], me, peer).start()

    @pl.when(ends)
    def _():
        reduce_start(owner(2), 0)
        reduce_start(owner(2), 1)

    home_start(xin, gtok, gt_ss, gt_rs, sizes[1:])

    @pl.when(inner)
    def _():
        remote(zrecv.at[0], zrecv.at[0], za_ss.at[0], za_rs.at[0], me, z).wait_recv()
        zsend[...] = (gacc[0:64] + zrecv[0].astype(F32)).astype(BF)
        remote(zsend, zrecv.at[1], za_ss.at[1], za_rs.at[1], me, middle).start()
        home_start(xin, gtok, gt_ss, gt_rs, sizes[:1])
        remote(zvec.at[1], zvec.at[1], zv_ss.at[0], zv_rs.at[1], me, z).wait_recv()
        zvec[2] = zvec[0] + zvec[1]
        remote(zvec.at[2], zvec.at[3], zv_ss.at[1], zv_rs.at[3], me, middle).start()
        remote(zrecv.at[1], zrecv.at[1], za_ss.at[0], za_rs.at[1], me, z).wait_recv()
        zall[...] = (zsend[...].astype(F32) + zrecv[1].astype(F32)).astype(BF)
        remote(zall, zall, zb_ss.at[0], zb_rs.at[0], me, near_end).start()
        remote(zvec.at[3], zvec.at[3], zv_ss.at[0], zv_rs.at[3], me, z).wait_recv()
        zvec[4] = zvec[2] + zvec[3]
        remote(zvec.at[4], zvec.at[4], zv_ss.at[2], zv_rs.at[4], me, near_end).start()

    final_copies = [
        pltpu.make_async_copy(gacc.at[:, pl.ds(piece * 512, 512)], out, loc_sem.at[2 + piece])
        for piece, out in ((0, gout), (1, gin))
    ]
    for piece in range(2):
        for slot, there in ((0, z >= 0), (3, inner)):

            @pl.when(there)
            def _():
                here = arrived.at[slot, piece]
                remote(here, here, r_ss.at[0, piece], r_rs.at[slot, piece], me, z).wait_recv()

        def finish(c, carry):
            at = rows_of(c, 128)
            gacc[at, piece * 512 : piece * 512 + 512] = (
                dws[z, piece, at].astype(F32)
                + arrived[0, piece, at].astype(F32)
                + jnp.where(inner, arrived[3, piece, at].astype(F32), 0.0)
            )
            return carry

        lax.fori_loop(0, 4, finish, 0)
        final_copies[piece].start()
    @pl.when(ends)
    def _():
        remote(zvec.at[4], zvec.at[4], zv_ss.at[0], zv_rs.at[4], me, z).wait_recv()
        remote(zall, zall, zb_ss.at[0], zb_rs.at[0], me, z).wait_recv()

    gsmall[...] = zvec[4]
    gqkv[...] = zall[:, 0:1536].astype(F32)
    gwo[...] = zall[:, 1536:2048].astype(F32)
    each(own_gtok, "wait")
    home_arrive(gtok, gt_rs)
    home_arrive(mixed, mix_rs)
    for copy in final_copies:
        copy.wait()

    hosts_sent(xin, tok_ss)
    hosts_sent(rin, rts_ss)
    hosts_sent(tin, tgt_ss)
    home_sent(xin, gt_ss)
    @pl.when(ends)
    def _():
        remote(zsend, zsend, za_ss.at[0], loc_sem.at[8], me, z).wait_send()
        remote(zvec.at[0], zvec.at[0], zv_ss.at[0], loc_sem.at[8], me, z).wait_send()

    @pl.when(inner)
    def _():
        remote(zsend, zsend, za_ss.at[1], loc_sem.at[8], me, z).wait_send()
        remote(zall, zall, zb_ss.at[0], loc_sem.at[8], me, z).wait_send()
        for k in (1, 2):
            remote(zvec.at[0], zvec.at[0], zv_ss.at[k], loc_sem.at[8], me, z).wait_send()


    def rows_sent(i, carry):
        sent(i, dn_ss)
        return carry

    lax.fori_loop(0, im, rows_sent, 0)
    weights_sent()
    for array in range(3):
        slot = dense_slot(array, 0)
        for k in range(half):
            remote(slot, slot, den_ss.at[array, k], loc_sem.at[8], me, z).wait_send()
        for k in range(1, half):
            remote(slot, slot, fwd_ss.at[array, k], loc_sem.at[8], me, z).wait_send()
    for piece in range(2):
        for target in range(n_z):
            here = dws.at[0, 0]

            @pl.when(z != target)
            def _():
                remote(here, here, r_ss.at[target, piece], loc_sem.at[8], me, z).wait_send()

    for q in range(half):
        remote(crecv.at[q], crecv.at[q], c_ss.at[q], loc_sem.at[8], me, z).wait_send()
    remote(cvec, cvec, cv_ss.at[0], loc_sem.at[8], me, z).wait_send()
    for k in range(1, half):
        remote(crecv.at[0], crecv.at[0], h_ss.at[k], loc_sem.at[8], me, z).wait_send()
        remote(cvec, cvec, hv_ss.at[k], loc_sem.at[8], me, z).wait_send()


def finish_kernel(mixed, gtok, gqkv, gwo, gsmall, gin, gout, *outs):
    me = lax.axis_index("dp")
    outs[0][...] = mixed[...]
    outs[1][...] = gtok[...].astype(F32)
    for source, target in ((gqkv, outs[2]), (gwo, outs[3]), (gin, outs[4]), (gout, outs[5])):
        target[...] = source[...]

    lanes = gsmall[:, pl.ds(pl.multiple_of((me // 2) * 128, 128), 128)]
    lanes = jnp.where(lax.rem(me, 2) == 1, pltpu.roll(lanes, 64, 1), lanes)
    for row in range(4):
        outs[6 + row][...] = lanes[row, 0:64]
    outs[10][...] = lanes[8:16, 0:64]


def whole_images(
    tokens, ln1_gain, ln1_bias, w_qkv, w_out, ln2_gain, ln2_bias, w_router, expert_in, expert_out, routes, targets
):
    n_dp, n_z = lax.axis_size("dp"), lax.axis_size("seq")
    image_count, block, width = tokens.shape
    im = image_count // 3
    cap = 2 * S // (n_z * w_router.shape[1]) + 2
    dims = (n_dp, n_z, (image_count // 6, im, im, image_count // 6), block, cap)
    sp, half = n_z * BP, n_dp // 2
    me, z = lax.axis_index("dp"), lax.axis_index("seq")
    dma, vm = pltpu.SemaphoreType.DMA, pltpu.VMEM

    valid = z * block + jnp.arange(block) < VALID
    lines = jnp.where(valid[None, None, :], jnp.transpose(routes, (0, 2, 1)) + 1, 0)
    lines = jnp.pad(lines, ((0, 0), (0, 6), (0, BP - block)))
    odd = lax.rem(z, 2) == 1
    lines = jnp.concatenate([jnp.where(odd, 0, lines), jnp.where(odd, lines, 0)], axis=-1)
    vec = jnp.concatenate(
        [
            jnp.stack([ln1_gain, ln1_bias, ln2_gain, ln2_bias]),
            jnp.zeros((4, ln1_gain.shape[0]), BF),
            jnp.transpose(w_router),
        ],
        axis=0,
    )
    vec = lax.dynamic_update_slice(jnp.zeros((16, width), BF), vec, (0, me * ln1_gain.shape[0]))
    blocks = (n_z, im, block, width)
    in_any, in_vmem = pl.BlockSpec(memory_space=pl.ANY), pl.BlockSpec(memory_space=pltpu.VMEM)
    mixed, gtok, gqkv, gwo, gsmall, gin, gout = pl.pallas_call(
        functools.partial(block_kernel, dims),
        out_shape=[
            jax.ShapeDtypeStruct((image_count, block, width), BF),
            jax.ShapeDtypeStruct((image_count, block, width), BF),
            jax.ShapeDtypeStruct((64, 1536), F32),
            jax.ShapeDtypeStruct((64, width), F32),
            jax.ShapeDtypeStruct((16, width), F32),
            jax.ShapeDtypeStruct((512, 512), F32),
            jax.ShapeDtypeStruct((512, 512), F32),
        ],
        in_specs=[in_any, in_any, in_vmem, in_any, in_any, in_vmem, in_any, in_any],
        out_specs=[in_any, in_any] + [in_vmem] * 3 + [in_any] * 2,
        scratch_shapes=[
            vm(blocks, BF), vm((n_z, im, 8, 128), jnp.int32), vm(blocks, BF), vm((n_dp, 16, width), BF),
            vm((width, 1536), BF), vm((width, width), BF), vm((16, width), F32), vm((im, sp, width), BF),
            vm((im, sp, width), BF), vm((im, sp, 1536), BF), vm((im, sp, width), BF),
            vm((im, sp, 128), F32), vm((im, 8, sp), F32), vm((im, 8, sp), F32),
            vm((n_z, 512, 512), BF), vm((n_z, 512, 512), BF), vm((im, 512, 512), BF), vm((im, 512, 512), BF),
            vm((n_z, im, 512, 512), BF), vm((n_z, im, 512, 512), BF), vm((im, 512, 512), BF),
            vm((im, 512, 512), BF), vm((im, sp, width), F32), vm((n_z, 2, 512, 512), BF), vm((5, 2, 512, 512), BF),
            vm((width, 2048), F32), vm((512, 512), F32), vm((16, width), F32), vm((half, 64, 2048), BF), vm((half, 64, 2048), BF),
            vm((16, width), F32), vm((half, 64, 2048), BF), vm((half, 16, width), F32),
            vm((64, 2048), BF), vm((2, 64, 2048), BF), vm((64, 2048), BF), vm((5, 16, width), F32),
            dma((9,)), dma((n_z,)), dma((n_z,)), dma((n_z,)), dma((n_z,)), dma((n_z,)), dma((n_z,)),
            dma((3, half)), dma((3, n_dp)), dma((3, half)), dma((2, n_z)), dma((n_z,)), dma((2, n_z)), dma((n_z,)),
            dma((im, n_dp)), dma((im, n_dp)), dma((im, n_dp)), dma((im, n_dp)), dma((im, n_dp)), dma((im, n_dp)),
            dma((im, n_dp)), dma((im, n_dp)),
            dma((n_z,)), dma((n_z,)), dma((n_z,)), dma((n_z,)),
            dma((n_z, 2)), dma((5, 2)), dma((half,)), dma((half,)), dma((1,)), dma((1,)),
            dma((half,)), dma((half,)), dma((half,)), dma((half,)), dma((2,)), dma((2,)), dma((1,)), dma((1,)),
            dma((3,)), dma((5,)),
        ],
        compiler_params=pltpu.CompilerParams(
            collective_id=1, has_side_effects=True, vmem_limit_bytes=VMEM_LIMIT
        ),
        name="block",
    )(tokens, targets, lines, w_qkv, w_out, vec, expert_in[0], expert_out[0])
    whole = pl.BlockSpec(memory_space=pltpu.VMEM)
    mixed, gtok, gqkv, gwo, gin, gout, g1, b1, g2, b2, grouter = pl.pallas_call(
        finish_kernel,
        out_shape=[
            jax.ShapeDtypeStruct((image_count, block, width), BF),
            jax.ShapeDtypeStruct((image_count, block, width), F32),
            jax.ShapeDtypeStruct((64, 1536), F32),
            jax.ShapeDtypeStruct((64, width), F32),
            jax.ShapeDtypeStruct((512, 512), F32),
            jax.ShapeDtypeStruct((512, 512), F32),
        ]
        + [jax.ShapeDtypeStruct((64,), F32)] * 4
        + [jax.ShapeDtypeStruct((8, 64), F32)],
        in_specs=[whole] * 7,
        out_specs=[whole] * 11,
        name="finish",
    )(mixed, gtok, gqkv, gwo, gsmall, gin, gout)
    return (mixed, gtok, g1, b1, gqkv, gwo, g2, b2, jnp.transpose(grouter), gin[None], gout[None])


def fits(tokens, w_qkv, w_router, expert_in):
    n_dp, n_z = lax.axis_size("dp"), lax.axis_size("seq")
    return (
        n_dp == 8
        and n_z == 4
        and tokens.shape[0] % 6 == 0
        and tokens.shape[1] <= BP
        and tokens.shape[2] == 512
        and w_qkv.shape == (64, 1536)
        and w_router.shape[1] == n_dp
        and expert_in.shape == (1, 512, 512)
    )


def local(*args):
    if fits(args[0], args[3], args[7], args[8]):
        return whole_images(*args)
    return by_heads(*args)


def solution(mesh):
    placed = (
        P("dp", "seq", None),
        P("dp"),
        P("dp"),
        P("dp", None),
        P("dp", None),
        P("dp"),
        P("dp"),
        P("dp", None),
        P("dp", None, "seq"),
        P("dp", "seq", None),
        P("dp", "seq", None),
        P("dp", "seq", None),
    )
    return jax.shard_map(
        local,
        mesh=mesh,
        in_specs=placed,
        out_specs=(
            P("dp", "seq", None),
            P("dp", "seq", None),
            P("dp"),
            P("dp"),
            P("dp", None),
            P("dp", None),
            P("dp"),
            P("dp"),
            P("dp", None),
            P("dp", None, "seq"),
            P("dp", "seq", None),
        ),
        check_vma=False,
    )
```

```python
import functools

import jax
import jax.numpy as jnp
from jax import lax
from jax.experimental import pallas as pl
from jax.experimental.pallas import tpu as pltpu
from jax.sharding import PartitionSpec as P

H = 8
S = 200
VALID = 197


def layer_norm(values, gain_vec, bias_vec):
    centre = values - jnp.mean(values, axis=-1, keepdims=True)
    spread = jnp.mean(centre * centre, axis=-1, keepdims=True)
    return centre * lax.rsqrt(spread + 1e-06) * gain_vec + bias_vec


def regroup_heads(values):
    return lax.all_to_all(values, "seq", split_axis=3, concat_axis=1, tiled=True)


def regroup_slots(values):
    return lax.all_to_all(values, "seq", split_axis=1, concat_axis=3, tiled=True)


def send_experts(values):
    return lax.all_to_all(values, "dp", split_axis=0, concat_axis=1, tiled=True)


def send_tokens(values):
    return lax.all_to_all(values, "dp", split_axis=1, concat_axis=0, tiled=True)


def masked_scores(queries, keys_in, key_valid):
    scores = (
        jnp.einsum("bqhd,bkhd->bhqk", queries, keys_in, preferred_element_type=jnp.float32) * 0.125
    )
    return jnp.where(key_valid, scores, -1e30)


def attention_forward(queries, keys_in, values, key_valid):
    scores = masked_scores(queries, keys_in, key_valid)
    row_top = jnp.max(scores, axis=-1, keepdims=True)
    exponent = jnp.exp(scores - row_top)
    row_total = jnp.sum(exponent, axis=-1, keepdims=True)
    prob_rows = exponent / row_total
    log_total = row_top + jnp.log(row_total)
    attended = jnp.einsum(
        "bhqk,bkhd->bqhd",
        prob_rows.astype(jnp.bfloat16),
        values,
        preferred_element_type=jnp.float32,
    )
    return (attended.astype(jnp.bfloat16), log_total)


def attention_backward(queries, keys_in, values, log_total, grad_attended, key_valid):
    scores = masked_scores(queries, keys_in, key_valid)
    prob_rows = jnp.exp(scores - log_total)
    grad_values = jnp.einsum(
        "bhqk,bqhd->bkhd",
        prob_rows.astype(jnp.bfloat16),
        grad_attended,
        preferred_element_type=jnp.float32,
    )
    grad_probs = jnp.einsum(
        "bqhd,bkhd->bhqk", grad_attended, values, preferred_element_type=jnp.float32
    )
    inner_sum = jnp.sum(prob_rows * grad_probs, axis=-1, keepdims=True)
    grad_scores = (prob_rows * (grad_probs - inner_sum)).astype(jnp.bfloat16)
    grad_queries = (
        jnp.einsum("bhqk,bkhd->bqhd", grad_scores, keys_in, preferred_element_type=jnp.float32)
        * 0.125
    )
    grad_keys = (
        jnp.einsum("bhqk,bqhd->bkhd", grad_scores, queries, preferred_element_type=jnp.float32)
        * 0.125
    )
    return jnp.stack([grad_queries, grad_keys, grad_values], axis=2)


def pick_block(total_rows):
    for candidate in (1024, 768, 512, 384, 256):
        if total_rows % candidate == 0:
            return candidate
    return total_rows


def by_heads(
    tokens,
    ln1_gain,
    ln1_bias,
    w_qkv,
    w_out,
    ln2_gain,
    ln2_bias,
    w_router,
    expert_in,
    expert_out,
    routes,
    targets,
):
    image_count, slot_count, model_width = tokens.shape
    seq_devices = lax.axis_size("seq")
    row_count = image_count * slot_count
    expert_count = w_router.shape[1]
    local_experts = expert_in.shape[0]
    slot_limit = 2 * S // (seq_devices * expert_count) + 2
    head_size = model_width // H
    gathered = (
        lax.all_gather(ln1_gain, "dp", axis=0, tiled=True),
        lax.all_gather(ln1_bias, "dp", axis=0, tiled=True),
        lax.all_gather(w_qkv, "dp", axis=0, tiled=True),
        lax.all_gather(w_out, "dp", axis=0, tiled=True),
        lax.all_gather(ln2_gain, "dp", axis=0, tiled=True),
        lax.all_gather(ln2_bias, "dp", axis=0, tiled=True),
        lax.all_gather(w_router, "dp", axis=0, tiled=True),
    )
    gain_one = gathered[0].astype(jnp.float32)
    bias_one = gathered[1].astype(jnp.float32)
    qkv_weight = gathered[2]
    out_weight = gathered[3]
    gain_two = gathered[4].astype(jnp.float32)
    bias_two = gathered[5].astype(jnp.float32)
    router_weight = gathered[6]
    slot_start = lax.axis_index("seq") * slot_count
    valid_slot = slot_start + jnp.arange(slot_count) < VALID
    valid_rows = jnp.tile(valid_slot, image_count)
    key_valid = (jnp.arange(S) < VALID)[None, None, None, :]
    token_rows = tokens.reshape(row_count, model_width).astype(jnp.float32)
    normed_one, norm_one_back = jax.vjp(layer_norm, token_rows, gain_one, bias_one)
    normed_one_b = normed_one.astype(jnp.bfloat16)
    mixed_qkv = jnp.dot(normed_one_b, qkv_weight, preferred_element_type=jnp.float32).astype(
        jnp.bfloat16
    )
    qkv_heads = regroup_heads(mixed_qkv.reshape(image_count, slot_count, 3, H, head_size))
    queries = qkv_heads[:, :, 0]
    keys_in = qkv_heads[:, :, 1]
    values = qkv_heads[:, :, 2]
    attended, log_total = attention_forward(queries, keys_in, values, key_valid)
    attended_rows = regroup_slots(attended[:, :, None]).reshape(row_count, model_width)
    residual_two = token_rows + jnp.dot(
        attended_rows, out_weight, preferred_element_type=jnp.float32
    )
    normed_two, norm_two_back = jax.vjp(layer_norm, residual_two, gain_two, bias_two)
    normed_two_b = normed_two.astype(jnp.bfloat16)
    logits = jnp.dot(normed_two_b, router_weight, preferred_element_type=jnp.float32)
    route_rows = routes.reshape(row_count, 2)
    chosen = (route_rows[:, :, None] == jnp.arange(expert_count)[None, None, :]) & valid_rows[
        :, None, None
    ]
    chosen_f = chosen.astype(jnp.float32)

    def gate_pick(logit_rows):
        return jnp.sum(jax.nn.softmax(logit_rows, axis=-1)[:, None, :] * chosen_f, axis=-1)

    gate_values, gate_back = jax.vjp(gate_pick, logits)
    pick_count = chosen.astype(jnp.int32).reshape(image_count, slot_count * 2, expert_count)
    before = jnp.cumsum(pick_count, axis=1) - pick_count
    place_hit = (before[..., None] == jnp.arange(slot_limit)) & (pick_count[..., None] > 0)
    dispatch = place_hit.astype(jnp.bfloat16).reshape(
        image_count, slot_count, 2, expert_count, slot_limit
    )
    normed_img = normed_two_b.reshape(image_count, slot_count, model_width)
    sent_rows = jnp.einsum(
        "bskem,bsd->ebmd", dispatch, normed_img, preferred_element_type=jnp.float32
    ).astype(jnp.bfloat16)
    received = send_experts(sent_rows.reshape(expert_count, image_count * slot_limit, model_width))
    weights_in, weights_out = (
        lax.all_gather(expert_in, "seq", axis=2, tiled=True),
        lax.all_gather(expert_out, "seq", axis=1, tiled=True),
    )
    total_rows = received.shape[1]
    block_rows = pick_block(total_rows)
    block_count = total_rows // block_rows

    def expert_step(block_index, produced):
        row_piece = lax.dynamic_slice_in_dim(received, block_index * block_rows, block_rows, 1)
        hidden_pre = jnp.einsum(
            "erd,edf->erf", row_piece, weights_in, preferred_element_type=jnp.float32
        )
        activated = jax.nn.gelu(hidden_pre).astype(jnp.bfloat16)
        result = jnp.einsum(
            "erf,efd->erd", activated, weights_out, preferred_element_type=jnp.float32
        ).astype(jnp.bfloat16)
        return lax.dynamic_update_slice_in_dim(produced, result, block_index * block_rows, 1)

    produced = lax.fori_loop(
        0,
        block_count,
        expert_step,
        jnp.zeros((local_experts, total_rows, model_width), jnp.bfloat16),
    )
    returned = send_tokens(produced).reshape(expert_count, image_count, slot_limit, model_width)
    per_choice = jnp.einsum(
        "bskem,ebmd->bskd", dispatch, returned, preferred_element_type=jnp.float32
    ).reshape(row_count, 2, model_width)
    mixed_rows = (
        residual_two
        + gate_values[:, 0:1] * per_choice[:, 0]
        + gate_values[:, 1:2] * per_choice[:, 1]
    )
    target_rows = targets.reshape(row_count, model_width).astype(jnp.float32)
    grad_mixed = (mixed_rows - target_rows) * valid_rows[:, None].astype(jnp.float32)
    grad_gates = jnp.sum(grad_mixed[:, None, :] * per_choice, axis=-1)
    grad_choice = (
        (gate_values[:, :, None] * grad_mixed[:, None, :])
        .astype(jnp.bfloat16)
        .reshape(image_count, slot_count, 2, model_width)
    )
    grad_sent = jnp.einsum(
        "bskem,bskd->ebmd", dispatch, grad_choice, preferred_element_type=jnp.float32
    ).astype(jnp.bfloat16)
    grad_received = send_experts(
        grad_sent.reshape(expert_count, image_count * slot_limit, model_width)
    )
    back_in, back_out = (
        lax.all_gather(expert_in, "seq", axis=2, tiled=True),
        lax.all_gather(expert_out, "seq", axis=1, tiled=True),
    )

    def expert_back(block_index, loop_carry):
        grad_in_sum, grad_out_sum, grad_rows = loop_carry
        row_piece = lax.dynamic_slice_in_dim(received, block_index * block_rows, block_rows, 1)
        grad_piece = lax.dynamic_slice_in_dim(
            grad_received, block_index * block_rows, block_rows, 1
        )
        hidden_pre = jnp.einsum(
            "erd,edf->erf", row_piece, back_in, preferred_element_type=jnp.float32
        )
        activated, gelu_back = jax.vjp(jax.nn.gelu, hidden_pre)
        grad_act = jnp.einsum(
            "erd,efd->erf", grad_piece, back_out, preferred_element_type=jnp.float32
        )
        grad_pre = gelu_back(grad_act)[0].astype(jnp.bfloat16)
        grad_out_sum = grad_out_sum + jnp.einsum(
            "erf,erd->efd",
            activated.astype(jnp.bfloat16),
            grad_piece,
            preferred_element_type=jnp.float32,
        )
        grad_in_sum = grad_in_sum + jnp.einsum(
            "erd,erf->edf", row_piece, grad_pre, preferred_element_type=jnp.float32
        )
        rows_back = jnp.einsum(
            "erf,edf->erd", grad_pre, back_in, preferred_element_type=jnp.float32
        ).astype(jnp.bfloat16)
        grad_rows = lax.dynamic_update_slice_in_dim(
            grad_rows, rows_back, block_index * block_rows, 1
        )
        return (grad_in_sum, grad_out_sum, grad_rows)

    start_carry = (
        jnp.zeros(back_in.shape, jnp.float32),
        jnp.zeros(back_out.shape, jnp.float32),
        jnp.zeros((local_experts, total_rows, model_width), jnp.bfloat16),
    )
    grad_in_sum, grad_out_sum, grad_rows = lax.fori_loop(0, block_count, expert_back, start_carry)
    grad_returned = send_tokens(grad_rows).reshape(
        expert_count, image_count, slot_limit, model_width
    )
    grad_normed_two = jnp.einsum(
        "bskem,ebmd->bsd", dispatch, grad_returned, preferred_element_type=jnp.float32
    ).reshape(row_count, model_width)
    grad_logits = gate_back(grad_gates)[0].astype(jnp.bfloat16)
    grad_router = jnp.einsum(
        "rd,re->de", normed_two_b, grad_logits, preferred_element_type=jnp.float32
    )
    grad_normed_two = grad_normed_two + jnp.einsum(
        "re,de->rd", grad_logits, router_weight, preferred_element_type=jnp.float32
    )
    grad_res_two, grad_gain_two, grad_bias_two = norm_two_back(grad_normed_two)
    grad_residual = grad_mixed + grad_res_two
    grad_branch = grad_residual.astype(jnp.bfloat16)
    grad_out_weight = jnp.einsum(
        "rd,re->de", attended_rows, grad_branch, preferred_element_type=jnp.float32
    )
    grad_attended = jnp.einsum(
        "re,de->rd", grad_branch, out_weight, preferred_element_type=jnp.float32
    ).astype(jnp.bfloat16)
    grad_heads = regroup_heads(grad_attended.reshape(image_count, slot_count, 1, H, head_size))[
        :, :, 0
    ]
    grad_qkv_heads = attention_backward(
        queries, keys_in, values, log_total, grad_heads, key_valid
    ).astype(jnp.bfloat16)
    grad_qkv_rows = regroup_slots(grad_qkv_heads).reshape(row_count, 3 * model_width)
    grad_qkv_weight = jnp.einsum(
        "rd,rf->df", normed_one_b, grad_qkv_rows, preferred_element_type=jnp.float32
    )
    grad_normed_one = jnp.einsum(
        "rf,df->rd", grad_qkv_rows, qkv_weight, preferred_element_type=jnp.float32
    )
    grad_token_ln, grad_gain_one, grad_bias_one = norm_one_back(grad_normed_one)
    grad_tokens = grad_residual + grad_token_ln
    dense_grads = (
        grad_gain_one,
        grad_bias_one,
        grad_qkv_weight,
        grad_out_weight,
        grad_gain_two,
        grad_bias_two,
        grad_router,
    )
    dense_grads = (
        lax.psum(dense_grads[0].astype(jnp.bfloat16), "seq").astype(jnp.float32),
        lax.psum(dense_grads[1].astype(jnp.bfloat16), "seq").astype(jnp.float32),
        lax.psum(dense_grads[2].astype(jnp.bfloat16), "seq").astype(jnp.float32),
        lax.psum(dense_grads[3].astype(jnp.bfloat16), "seq").astype(jnp.float32),
        lax.psum(dense_grads[4].astype(jnp.bfloat16), "seq").astype(jnp.float32),
        lax.psum(dense_grads[5].astype(jnp.bfloat16), "seq").astype(jnp.float32),
        lax.psum(dense_grads[6].astype(jnp.bfloat16), "seq").astype(jnp.float32),
    )
    dense_grads = (
        lax.psum_scatter(
            dense_grads[0].astype(jnp.bfloat16), "dp", scatter_dimension=0, tiled=True
        ).astype(jnp.float32),
        lax.psum_scatter(
            dense_grads[1].astype(jnp.bfloat16), "dp", scatter_dimension=0, tiled=True
        ).astype(jnp.float32),
        lax.psum_scatter(
            dense_grads[2].astype(jnp.bfloat16), "dp", scatter_dimension=0, tiled=True
        ).astype(jnp.float32),
        lax.psum_scatter(
            dense_grads[3].astype(jnp.bfloat16), "dp", scatter_dimension=0, tiled=True
        ).astype(jnp.float32),
        lax.psum_scatter(
            dense_grads[4].astype(jnp.bfloat16), "dp", scatter_dimension=0, tiled=True
        ).astype(jnp.float32),
        lax.psum_scatter(
            dense_grads[5].astype(jnp.bfloat16), "dp", scatter_dimension=0, tiled=True
        ).astype(jnp.float32),
        lax.psum_scatter(
            dense_grads[6].astype(jnp.bfloat16), "dp", scatter_dimension=0, tiled=True
        ).astype(jnp.float32),
    )
    expert_in_grad, expert_out_grad = (
        lax.psum_scatter(
            grad_in_sum.astype(jnp.bfloat16), "seq", scatter_dimension=2, tiled=True
        ).astype(jnp.float32),
        lax.psum_scatter(
            grad_out_sum.astype(jnp.bfloat16), "seq", scatter_dimension=1, tiled=True
        ).astype(jnp.float32),
    )
    mixed = mixed_rows.astype(jnp.bfloat16).reshape(image_count, slot_count, model_width)
    return (
        mixed,
        grad_tokens.reshape(image_count, slot_count, model_width),
        dense_grads[0],
        dense_grads[1],
        dense_grads[2],
        dense_grads[3],
        dense_grads[4],
        dense_grads[5],
        dense_grads[6],
        expert_in_grad,
        expert_out_grad,
    )


BF = jnp.bfloat16
F32 = jnp.float32
MESH_ID = pl.DeviceIdType.MESH
NEG = -1e30
BP = 64
VMEM_LIMIT = 67000000
GELU_C = 0.7978845608028654
GELU_K = 0.044715


def nn(a, b):
    return lax.dot_general(a, b, (((1,), (0,)), ((), ())), preferred_element_type=F32)


def nt(a, b):
    return lax.dot_general(a, b, (((1,), (1,)), ((), ())), preferred_element_type=F32)


def tn(a, b):
    return lax.dot_general(a, b, (((0,), (0,)), ((), ())), preferred_element_type=F32)


def remote(src, dst, send_sem, recv_sem, dp, z):
    return pltpu.make_async_remote_copy(
        src_ref=src,
        dst_ref=dst,
        send_sem=send_sem,
        recv_sem=recv_sem,
        device_id=(dp, z),
        device_id_type=MESH_ID,
    )


def rows_of(index, size):
    return pl.ds(pl.multiple_of(index * size, size), size)


def norm_parts(x):
    centre = x - jnp.mean(x, axis=-1, keepdims=True)
    scale = lax.rsqrt(jnp.mean(centre * centre, axis=-1, keepdims=True) + 1e-06)
    return centre * scale, scale


def norm_back(grad_hat, hat, scale):
    return scale * (
        grad_hat
        - jnp.mean(grad_hat, axis=-1, keepdims=True)
        - hat * jnp.mean(grad_hat * hat, axis=-1, keepdims=True)
    )


def half_masks():
    lane = lax.broadcasted_iota(jnp.int32, (1, 128), 1)
    low = jnp.where(lane < 64, 1.0, 0.0)
    return (low.astype(BF), (1.0 - low).astype(BF))


def slot_ok(position, block):
    return (position % BP < block) & ((position // BP) * block + position % BP < VALID)


def block_kernel(
    dims,
    tok, tgt, rts, wq, wo, vec, win, wout,
    mixed, gtok, gqkv, gwo, gsmall, gin, gout,
    xin, rin, tin, vec_all, wq_all, wo_all, vsum, xpad, n2s, qkvs, outs, cols, gts, meta,
    win_all, wout_all, recv, ret, acts, slopes, sbuf,
    drows, dys, dws, arrived,
    gacc, accf, gvec, csend, crecv, cvec, hrecv, hvec, zsend, zrecv, zall, zvec,
    loc_sem, tok_ss, tok_rs, rts_ss, rts_rs, tgt_ss, tgt_rs, den_ss, den_rs, fwd_ss, win_ss, win_rs, wout_ss, wout_rs,
    row_ss, row_rs, u_ss, u_rs, du_ss, du_rs, dn_ss, dn_rs, mix_ss, mix_rs, gt_ss, gt_rs,
    r_ss, r_rs, c_ss, c_rs, cv_ss, cv_rs, h_ss, h_rs, hv_ss, hv_rs, za_ss, za_rs, zb_ss, zb_rs, zv_ss, zv_rs,
):
    n_dp, n_z, counts, block, cap = dims
    firsts = tuple(sum(counts[:h]) for h in range(n_z))
    me, z = lax.axis_index("dp"), lax.axis_index("seq")
    sp = n_z * BP
    half = n_dp // 2
    last = n_z - 1
    core, chip = lax.rem(me, 2), me // 2
    partner = chip * 2 + 1 - core
    inner = (z == 1) | (z == last - 1)
    ends = jnp.logical_not(inner)
    far_end = jnp.where(z < n_z // 2, last, 0)
    near_end = last - far_end
    middle = last - z
    im = jnp.where(inner, counts[1], counts[0])
    sizes = ((counts[1], inner), (counts[0], ends))
    first = jnp.where(z == 0, firsts[0], jnp.where(z == 1, firsts[1], jnp.where(z == 2, firsts[2], firsts[3])))

    barrier = pltpu.get_barrier_semaphore()
    for k in range(1, n_dp):
        pl.semaphore_signal(barrier, inc=1, device_id=(lax.rem(me + k, n_dp), z), device_id_type=MESH_ID)
    for k in range(1, n_z):
        pl.semaphore_signal(barrier, inc=1, device_id=(me, lax.rem(z + k, n_z)), device_id_type=MESH_ID)

    def hosts_own(source, target, sem):
        for h in range(n_z):

            @pl.when(z == h)
            def _():
                pltpu.make_async_copy(
                    source.at[pl.ds(firsts[h], counts[h])], target.at[z, pl.ds(0, counts[h])], sem
                ).start()

    def hosts_own_wait(source, target, sem):
        for h in range(n_z):

            @pl.when(z == h)
            def _():
                pltpu.make_async_copy(
                    source.at[pl.ds(firsts[h], counts[h])], target.at[z, pl.ds(0, counts[h])], sem
                ).wait()

    def hosts_start(source, target, send_sem, recv_sem, hosts, who):
        for h in hosts:

            @pl.when((z != h) & who)
            def _():
                remote(
                    source.at[pl.ds(firsts[h], counts[h])],
                    target.at[z, pl.ds(0, counts[h])],
                    send_sem.at[h],
                    recv_sem.at[z],
                    me,
                    h,
                ).start()

    def hosts_arrive(target, recv_sem):
        for size, there in sizes:

            @pl.when(there)
            def _():
                for k in range(1, n_z):
                    origin = lax.rem(z + k, n_z)
                    spot = target.at[origin, pl.ds(0, size)]
                    remote(spot, spot, loc_sem.at[8], recv_sem.at[origin], me, z).wait_recv()

    def hosts_sent(target, send_sem):
        for h in range(n_z):

            @pl.when(z != h)
            def _():
                spot = target.at[0, pl.ds(0, counts[h])]
                remote(spot, spot, send_sem.at[h], loc_sem.at[8], me, z).wait_send()

    def home_own(source, target, sem):
        return [
            (there, pltpu.make_async_copy(source.at[z, pl.ds(0, size)], target.at[pl.ds(first, size)], sem))
            for size, there in sizes
        ]

    def home_start(source, target, send_sem, recv_sem, who):
        for size, there in who:

            @pl.when(there)
            def _():
                for k in range(1, n_z):
                    peer = lax.rem(z + k, n_z)
                    remote(
                        source.at[peer, pl.ds(0, size)],
                        target.at[pl.ds(first, size)],
                        send_sem.at[k],
                        recv_sem.at[z],
                        me,
                        peer,
                    ).start()

    def home_arrive(target, recv_sem):
        for h in range(n_z):

            @pl.when(z != h)
            def _():
                spot = target.at[pl.ds(firsts[h], counts[h])]
                remote(spot, spot, loc_sem.at[8], recv_sem.at[h], me, z).wait_recv()

    def home_sent(source, send_sem):
        for size, there in sizes:

            @pl.when(there)
            def _():
                for k in range(1, n_z):
                    spot = source.at[0, pl.ds(0, size)]
                    remote(spot, spot, send_sem.at[k], loc_sem.at[8], me, z).wait_send()

    def each(pairs, act):
        for there, copy in pairs:

            @pl.when(there)
            def _():
                getattr(copy, act)()

    own_copies = [
        pltpu.make_async_copy(win, win_all.at[z], loc_sem.at[3]),
        pltpu.make_async_copy(wout, wout_all.at[z], loc_sem.at[4]),
        pltpu.make_async_copy(wq, wq_all.at[rows_of(me, 64)], loc_sem.at[5]),
        pltpu.make_async_copy(wo, wo_all.at[rows_of(me, 64)], loc_sem.at[6]),
        pltpu.make_async_copy(vec, vec_all.at[me], loc_sem.at[7]),
    ]
    for copy in own_copies:
        copy.start()
    hosts_own(tok, xin, loc_sem.at[0])
    hosts_own(rts, rin, loc_sem.at[1])
    hosts_own(tgt, tin, loc_sem.at[2])
    for buffer in (xpad, gvec, recv, ret, drows):
        buffer[...] = jnp.zeros_like(buffer)
    pl.semaphore_wait(barrier, n_dp + n_z - 2)
    hosts_start(tok, xin, tok_ss, tok_rs, range(n_z), z >= 0)
    hosts_start(rts, rin, rts_ss, rts_rs, range(n_z), z >= 0)

    def dense_slot(array, index):
        if array == 0:
            return wq_all.at[rows_of(index, 64)]
        if array == 1:
            return wo_all.at[rows_of(index, 64)]
        return vec_all.at[index]

    dense_in = (wq, wo, vec)
    for array in range(3):
        for k in range(1, half):
            peer = lax.rem(chip + k, half) * 2 + core
            remote(
                dense_in[array], dense_slot(array, me), den_ss.at[array, k], den_rs.at[array, me], peer, z
            ).start()
        remote(
            dense_in[array], dense_slot(array, me), den_ss.at[array, 0], den_rs.at[array, me], partner, z
        ).start()

    experts = ((win, win_all, win_ss, win_rs), (wout, wout_all, wout_ss, wout_rs))

    def gather_hop(array, step):
        source, full, send_sem, recv_sem = experts[array]
        for way, there, slot in ((0, z >= step, z - step), (1, z + step < n_z, z + step)):

            @pl.when(there)
            def _():
                at = full.at[slot]
                if step > 0:
                    remote(at, at, send_sem.at[way, step], recv_sem.at[slot], me, z).wait_recv()

                @pl.when((z < last) if way == 0 else (z > 0))
                def _():
                    remote(
                        at if step > 0 else source,
                        at,
                        send_sem.at[way, step],
                        recv_sem.at[slot],
                        me,
                        z + 1 if way == 0 else z - 1,
                    ).start()

    def weights_sent():
        for step in range(n_z - 1):
            for way, there in ((0, (z >= step) & (z < last)), (1, (z + step < n_z) & (z > 0))):

                @pl.when(there)
                def _():
                    for source, full, send_sem, recv_sem in experts:
                        remote(
                            full.at[0], full.at[0], send_sem.at[way, step], recv_sem.at[0], me, z
                        ).wait_send()

    gather_hop(0, 0)
    gather_hop(1, 0)

    for k in range(1, half):
        origin = lax.rem(chip + k, half) * 2 + core
        for array in range(3):
            slot = dense_slot(array, origin)
            remote(slot, slot, den_ss.at[array, 0], den_rs.at[array, origin], me, z).wait_recv()
            remote(slot, slot, fwd_ss.at[array, k], den_rs.at[array, origin], partner, z).start()
    for k in range(half):
        origin = lax.rem(chip + k, half) * 2 + 1 - core
        for array in range(3):
            slot = dense_slot(array, origin)
            remote(slot, slot, den_ss.at[array, 0], den_rs.at[array, origin], me, z).wait_recv()
    for copy in own_copies:
        copy.wait()
    hosts_own_wait(tok, xin, loc_sem.at[0])
    hosts_own_wait(rts, rin, loc_sem.at[1])
    hosts_own_wait(tgt, tin, loc_sem.at[2])
    total = vec_all[0].astype(F32)
    for k in range(1, n_dp):
        total = total + vec_all[k].astype(F32)
    vsum[...] = total
    hosts_arrive(xin, tok_rs)
    hosts_arrive(rin, rts_rs)

    masks = half_masks()
    eighths = [mask * 0.125 for mask in masks]
    keys_ok = slot_ok(lax.broadcasted_iota(jnp.int32, (1, sp), 1), block)
    rows_ok = slot_ok(lax.broadcasted_iota(jnp.int32, (sp, 1), 0), block)
    gain_one, bias_one = vsum[0:1, :], vsum[1:2, :]
    gain_two, bias_two = vsum[2:3, :], vsum[3:4, :]
    router_t = vsum[8:16, :].astype(BF)
    lane_id = lax.broadcasted_iota(jnp.int32, (sp, 128), 1)
    lane_low = lane_id < 64
    row_id = lax.broadcasted_iota(jnp.int32, (512, sp), 0).astype(F32)

    def lanes_of(target):
        return pl.ds(pl.multiple_of(target * 512, 512), 512)

    def rows_at(index):
        return pl.ds(pl.multiple_of(index * 64, 64), n_z * cap)

    def send_rows(i, target, send_sem, recv_sem):
        def step(s, carry):
            j, c = lax.rem(s // 2 + 1, half), lax.rem(s, 2)
            index = 2 * j + c
            peer = lax.rem(chip + j, half) * 2 + lax.rem(core + c, 2)

            @pl.when(index > 0)
            def _():
                remote(
                    sbuf.at[i, rows_at(peer)],
                    target.at[i, rows_at(me)],
                    send_sem.at[i, index],
                    recv_sem.at[i, me],
                    peer,
                    z,
                ).start()

            return carry

        lax.fori_loop(0, n_dp, step, 0)
        target[i, rows_of(me, 64)] = sbuf[i, rows_of(me, 64)]

    def arrive(i, target, recv_sem):
        def step(k, carry):
            origin = lax.rem(me + k, n_dp)
            spot = target.at[i, rows_at(origin)]
            remote(spot, spot, loc_sem.at[8], recv_sem.at[i, origin], me, z).wait_recv()
            return carry

        lax.fori_loop(1, n_dp, step, 0)

    def sent(i, send_sem):
        def step(index, carry):
            spot = sbuf.at[i, rows_at(0)]
            remote(spot, spot, send_sem.at[i, index], loc_sem.at[8], me, z).wait_send()
            return carry

        lax.fori_loop(1, n_dp, step, 0)

    def front(i, carry):
        before = lax.broadcasted_iota(jnp.int32, (sp, sp), 0)
        after = lax.broadcasted_iota(jnp.int32, (sp, sp), 1)
        prefix = jnp.where((before < after) & (before // BP == after // BP), 1.0, 0.0).astype(BF)
        expert_id = lax.broadcasted_iota(jnp.int32, (8, sp), 0)
        slot_lane = lax.broadcasted_iota(jnp.int32, (8, sp), 1)
        for b in range(n_z):
            xpad[i, b * BP : b * BP + block, :] = xin[b, i]
        x = xpad[i].astype(F32)
        hat, _ = norm_parts(x)
        normed = (hat * gain_one + bias_one).astype(BF)
        qkvs[i] = nn(normed, wq_all[...]).astype(BF)
        lse_all = jnp.zeros((sp, 128), F32)
        for pair in range(4):
            q2 = qkvs[i, :, pair * 128 : pair * 128 + 128]
            k2 = qkvs[i, :, 512 + pair * 128 : 512 + pair * 128 + 128]
            v2 = qkvs[i, :, 1024 + pair * 128 : 1024 + pair * 128 + 128]
            parts = []
            for side in range(2):
                scores = nt(q2 * eighths[side], k2)
                scores = jnp.where(keys_ok, scores, NEG)
                top = jnp.max(scores, axis=-1, keepdims=True)
                exponent = jnp.exp(scores - top)
                whole = jnp.sum(exponent, axis=-1, keepdims=True)
                lse_all = jnp.where(lane_id == pair * 2 + side, top + jnp.log(whole), lse_all)
                parts.append(nn((exponent / whole).astype(BF), v2))
            outs[i, :, pair * 128 : pair * 128 + 128] = jnp.where(lane_low, parts[0], parts[1]).astype(BF)
        x2 = x + nn(outs[i], wo_all[...])
        hat2, _ = norm_parts(x2)
        n2 = (hat2 * gain_two + bias_two).astype(BF)
        n2s[i] = n2
        logits = nt(router_t, n2)
        raised = jnp.exp(logits - jnp.max(logits, axis=0, keepdims=True))
        share = raised / jnp.sum(raised, axis=0, keepdims=True)
        gts[i] = share
        wide = jnp.concatenate([rin[0, i] + rin[1, i], rin[2, i] + rin[3, i]], axis=1)
        hits = [(expert_id + 1) == wide[j : j + 1, :] for j in range(2)]
        any_hit = jnp.where(hits[0] | hits[1], 1.0, 0.0)
        place = nn(any_hit.astype(BF), prefix)
        base = place + (expert_id * 64 + (slot_lane // BP) * cap + 1).astype(F32)
        lines = [jnp.sum(jnp.where(hit, base, 0.0), axis=0, keepdims=True) - 1.0 for hit in hits]
        lines += [jnp.sum(jnp.where(hit, share, 0.0), axis=0, keepdims=True) for hit in hits]
        lines = jnp.concatenate(lines + [jnp.zeros((4, sp), F32)], axis=0)
        meta[i] = lines
        table = jnp.concatenate([jnp.zeros((8, sp), F32), lines, jnp.zeros((112, sp), F32)], axis=0)
        cols[i] = jnp.transpose(table) + lse_all
        pick = (row_id == lines[0:1, :]) | (row_id == lines[1:2, :])
        sbuf[i] = nn(jnp.where(pick, 1.0, 0.0).astype(BF), n2).astype(BF)
        send_rows(i, recv, row_ss, row_rs)

        @pl.when(i == 1)
        def _():
            gather_hop(0, 1)

        return carry

    lax.fori_loop(0, im, front, 0)


    def hidden(shard):
        def image(i, carry):
            x = recv[i]
            for side in range(2):
                pre = nn(x, win_all[shard, :, side * 256 : side * 256 + 256])
                square = pre * pre
                tanh = jnp.tanh(pre * (GELU_C + (GELU_C * GELU_K) * square))
                gate = 0.5 + 0.5 * tanh
                acts[shard, i, :, side * 256 : side * 256 + 256] = (pre * gate).astype(BF)
                slope = gate + pre * (0.5 - 0.5 * tanh * tanh) * (GELU_C + (3.0 * GELU_C * GELU_K) * square)
                slopes[shard, i, :, side * 256 : side * 256 + 256] = slope.astype(BF)
            return carry

        lax.fori_loop(0, im, image, 0)

    def hidden_step(s, carry):
        for at_step, hop in ((1, 2), (3, 3)):

            @pl.when(s == at_step)
            def _():
                gather_hop(0, hop)

        for way in range(2):
            shard = z - s if way == 0 else z + s

            @pl.when((shard >= 0) & (shard < n_z) & ((s > 0) | (way == 0)))
            def _():
                hidden(shard)

        @pl.when(s == 2)
        def _():
            gather_hop(1, 2)
            hosts_start(tgt, tin, tgt_ss, tgt_rs, (1, 2), z >= 0)

        return carry

    gather_hop(1, 1)

    def rows_here(i, carry):
        arrive(i, recv, row_rs)
        return carry

    lax.fori_loop(0, im, rows_here, 0)
    lax.fori_loop(0, n_z, hidden_step, 0)

    def early_results(i, carry):
        for k in range(1, n_z):
            shard = lax.rem(far_end + k, n_z)
            part = nn(acts[shard, i], wout_all[shard])
            if k == 1:
                gacc[:, lanes_of(i)] = part
            else:
                gacc[:, lanes_of(i)] += part
        return carry

    lax.fori_loop(0, im, early_results, 0)
    gather_hop(1, 3)
    hosts_start(tgt, tin, tgt_ss, tgt_rs, (0, last), ends)

    def results(i, carry):
        sent(i, row_ss)
        sbuf[i] = (gacc[:, lanes_of(i)] + nn(acts[far_end, i], wout_all[far_end])).astype(BF)
        send_rows(i, ret, u_ss, u_rs)
        return carry

    lax.fori_loop(0, im, results, 0)
    gacc[...] = jnp.zeros_like(gacc)

    def mix(i, carry):
        @pl.when(i == 1)
        def _():
            hosts_start(tgt, tin, tgt_ss, tgt_rs, (0, last), inner)

        arrive(i, ret, u_rs)

        @pl.when(i == 0)
        def _():
            hosts_arrive(tin, tgt_rs)

        line = lax.broadcasted_iota(jnp.int32, (sp, 512), 1).astype(F32)
        here = cols[i]
        picked = []
        for j in range(2):
            pick = jnp.where(line == here[:, 8 + j : 9 + j], 1.0, 0.0).astype(BF)
            picked.append(nn(pick, ret[i]))
        x2 = xpad[i].astype(F32) + nn(outs[i], wo_all[...])
        mix = x2 + here[:, 10:11] * picked[0] + here[:, 11:12] * picked[1]
        mix_b = mix.astype(BF)
        for b in range(n_z):
            xin[b, i] = mix_b[b * BP : b * BP + block]
            dys[i, b * BP : b * BP + block, :] = tin[b, i].astype(F32)
        dy = jnp.where(rows_ok, mix - dys[i], 0.0)
        dys[i] = dy
        total = jnp.zeros((512, 512), F32)
        for j in range(2):
            pick = jnp.where(row_id == meta[i, j : j + 1, :], 1.0, 0.0).astype(BF)
            total = total + nn(pick, (here[:, 10 + j : 11 + j] * dy).astype(BF))
        sent(i, u_ss)
        sbuf[i] = total.astype(BF)
        send_rows(i, drows, du_ss, du_rs)
        for j in range(2):
            here = jnp.where(lane_id == 12 + j, jnp.sum(dy * picked[j], axis=-1, keepdims=True), here)
        cols[i] = here
        return carry

    lax.fori_loop(0, im, mix, 0)
    home_start(xin, mixed, mix_ss, mix_rs, sizes)
    own_mixed = home_own(xin, mixed, loc_sem.at[0])
    each(own_mixed, "start")
    expert_row = lax.broadcasted_iota(jnp.int32, (8, sp), 0).astype(F32)

    def gates_back(i, carry):
        flat = jnp.transpose(cols[i])
        share = gts[i]
        grad = jnp.zeros((8, sp), F32)
        for j in range(2):
            at = meta[i, j : j + 1, :]
            inside = (at >= expert_row * 64) & (at < expert_row * 64 + 64)
            grad = grad + jnp.where(inside, flat[12 + j : 13 + j, :], 0.0)
        dlog = share * (grad - jnp.sum(share * grad, axis=0, keepdims=True))
        gts[i] = dlog
        gvec[8:16, :] += nn(dlog.astype(BF), n2s[i])
        return carry

    lax.fori_loop(0, im, gates_back, 0)

    def turn(i, carry):
        recv[i] = jnp.transpose(recv[i])
        for shard in range(n_z):
            acts[shard, i] = jnp.transpose(acts[shard, i])
        return carry

    lax.fori_loop(0, im, turn, 0)

    def reduce_start(target, piece):
        peer = jnp.where(z == 0, 1, last - 1)
        slot = jnp.where(target == peer, 0, jnp.where(target == far_end, 2, 1))
        remote(
            dws.at[target, piece], arrived.at[slot, piece], r_ss.at[target, piece], r_rs.at[slot, piece], me, peer
        ).start()

    def reduce_forward(piece, steps):
        @pl.when(inner)
        def _():
            for target, slot, peer, there in steps:
                here = arrived.at[slot, piece]
                remote(here, here, r_ss.at[target, piece], r_rs.at[slot, piece], me, z).wait_recv()

                def add(c, carry):
                    at = rows_of(c, 128)
                    dws[target, piece, at] = (
                        dws[target, piece, at].astype(F32) + arrived[slot, piece, at].astype(F32)
                    ).astype(BF)
                    return carry

                lax.fori_loop(0, 4, add, 0)
                remote(
                    dws.at[target, piece],
                    arrived.at[there, piece],
                    r_ss.at[target, piece],
                    r_rs.at[there, piece],
                    me,
                    peer,
                ).start()

    first_steps = ((far_end, 2, middle, 4),)
    second_steps = ((middle, 1, middle, 3), (near_end, 4, near_end, 0))

    def owner(s):
        return jnp.where(z < n_z // 2, lax.rem(z + 2 * n_z - 1 - s, n_z), lax.rem(z + 1 + s, n_z))

    def out_ready(s, carry):
        target = owner(s)
        dws[target, 0] = gacc[:, lanes_of(target)].astype(BF)

        @pl.when(ends & (s < 2))
        def _():
            reduce_start(target, 0)

        return carry

    def experts_back(i, carry):
        arrive(i, drows, du_rs)
        du = drows[i]
        for target in range(n_z):
            gacc[:, target * 512 : target * 512 + 512] += nn(acts[target, i], du)

        @pl.when(i == im - 1)
        def _():
            lax.fori_loop(0, n_z, out_ready, 0)

        total = jnp.zeros((512, 512), F32)
        for shard in range(n_z):
            dpre = (nt(du, wout_all[shard]) * slopes[shard, i].astype(F32)).astype(BF)
            slopes[shard, i] = dpre
            total = total + nt(dpre, win_all[shard])
        sent(i, du_ss)
        sbuf[i] = total.astype(BF)
        send_rows(i, ret, dn_ss, dn_rs)
        return carry

    lax.fori_loop(0, im, experts_back, 0)

    def in_grads(target):
        accf[...] = nn(recv[0], slopes[target, 0])

        def more(i, carry):
            accf[...] += nn(recv[i], slopes[target, i])
            return carry

        lax.fori_loop(1, im, more, 0)
        dws[target, 1] = accf[...].astype(BF)

    def end_in_grads(s, carry):
        target = owner(s)
        in_grads(target)

        @pl.when(s < 2)
        def _():
            reduce_start(target, 1)

        return carry

    def inner_in_grads(s, carry):
        in_grads(jnp.where(s == 0, far_end, jnp.where(s == 1, middle, jnp.where(s == 2, near_end, z))))
        return carry

    @pl.when(ends)
    def _():
        lax.fori_loop(0, n_z, end_in_grads, 0)

    gacc[...] = jnp.zeros_like(gacc)
    each(own_mixed, "wait")
    home_sent(xin, mix_ss)

    reduce_forward(0, first_steps)

    def back(i, carry):
        arrive(i, ret, dn_rs)
        line = lax.broadcasted_iota(jnp.int32, (sp, 512), 1).astype(F32)
        here = cols[i]
        pick = jnp.where((line == here[:, 8:9]) | (line == here[:, 9:10]), 1.0, 0.0).astype(BF)
        dn2 = nn(pick, ret[i]) + tn(gts[i].astype(BF), router_t)
        hat2, scale2 = norm_parts(xpad[i].astype(F32) + nn(outs[i], wo_all[...]))
        gvec[2:3, :] += jnp.sum(dn2 * hat2, axis=0, keepdims=True)
        gvec[3:4, :] += jnp.sum(dn2, axis=0, keepdims=True)
        dx2 = dys[i] + norm_back(dn2 * gain_two, hat2, scale2)
        da = dx2.astype(BF)
        gacc[:, 1536:2048] += tn(outs[i], da)
        do = nt(da, wo_all[...]).astype(BF)
        hat1, scale1 = norm_parts(xpad[i].astype(F32))
        n1 = (hat1 * gain_one + bias_one).astype(BF)
        for pair in range(4):
            at = pair * 128
            q2 = qkvs[i, :, at : at + 128]
            k2 = qkvs[i, :, 512 + at : 512 + at + 128]
            v2 = qkvs[i, :, 1024 + at : 1024 + at + 128]
            do2 = do[:, at : at + 128]
            grads = ([], [], [])
            for side in range(2):
                head = pair * 2 + side
                scores = nt(q2 * eighths[side], k2)
                scores = jnp.where(keys_ok, scores, NEG)
                prob = jnp.exp(scores - here[:, head : head + 1])
                dprob = nt(do2 * masks[side], v2)
                weighted = jnp.sum(prob * dprob, axis=-1, keepdims=True)
                ds = (prob * (dprob - weighted)).astype(BF)
                grads[0].append(nn(ds, k2))
                grads[1].append(tn(ds, q2))
                grads[2].append(tn(prob.astype(BF), do2))
            for part in range(3):
                grad = jnp.where(lane_low, grads[part][0], grads[part][1])
                if part < 2:
                    grad = grad * 0.125
                qkvs[i, :, part * 512 + at : part * 512 + at + 128] = grad.astype(BF)
        dqkv = qkvs[i]
        gacc[:, 0:1536] += tn(n1, dqkv)
        dn1 = nt(dqkv, wq_all[...])
        gvec[0:1, :] += jnp.sum(dn1 * hat1, axis=0, keepdims=True)
        gvec[1:2, :] += jnp.sum(dn1, axis=0, keepdims=True)
        dx = (dx2 + norm_back(dn1 * gain_one, hat1, scale1)).astype(BF)
        for b in range(n_z):
            xin[b, i] = dx[b * BP : b * BP + block]

        @pl.when(i == 1)
        def _():
            reduce_forward(0, second_steps)

        @pl.when(i == 2)
        def _():

            @pl.when(inner)
            def _():
                lax.fori_loop(0, 1, inner_in_grads, 0)

            reduce_forward(1, first_steps)

        return carry

    lax.fori_loop(0, im, back, 0)
    own_gtok = home_own(xin, gtok, loc_sem.at[1])
    each(own_gtok, "start")

    for q in range(half):
        csend[q] = gacc[rows_of(2 * q + 1 - core, 64)].astype(BF)
        remote(csend.at[q], crecv.at[q], c_ss.at[q], c_rs.at[q], partner, z).start()
    remote(gvec, cvec, cv_ss.at[0], cv_rs.at[0], partner, z).start()

    @pl.when(inner)
    def _():
        lax.fori_loop(1, 3, inner_in_grads, 0)

    for q in range(half):
        remote(crecv.at[q], crecv.at[q], c_ss.at[q], c_rs.at[q], me, z).wait_recv()
    for k in range(1, half):
        q = lax.rem(chip + k, half)
        crecv[q] = (gacc[rows_of(2 * q + core, 64)] + crecv[q].astype(F32)).astype(BF)
        remote(crecv.at[q], hrecv.at[chip], h_ss.at[k], h_rs.at[chip], q * 2 + core, z).start()
    remote(cvec, cvec, cv_ss.at[0], cv_rs.at[0], me, z).wait_recv()
    hvec[chip] = gvec[...] + cvec[...]
    for k in range(1, half):
        q = lax.rem(chip + k, half)
        remote(hvec.at[chip], hvec.at[chip], hv_ss.at[k], hv_rs.at[chip], q * 2 + core, z).start()
    reduce_forward(1, second_steps)

    @pl.when(inner)
    def _():
        lax.fori_loop(3, n_z, inner_in_grads, 0)

    dense = gacc[rows_of(me, 64)] + crecv[chip].astype(F32)
    for k in range(1, half):
        q = lax.rem(chip + k, half)
        remote(hrecv.at[q], hrecv.at[q], h_ss.at[0], h_rs.at[q], me, z).wait_recv()
        dense = dense + hrecv[q].astype(F32)
    gacc[0:64] = dense
    for k in range(1, half):
        q = lax.rem(chip + k, half)
        remote(hvec.at[q], hvec.at[q], hv_ss.at[0], hv_rs.at[q], me, z).wait_recv()
    zvec[0] = hvec[0] + hvec[1] + hvec[2] + hvec[3]

    @pl.when(ends)
    def _():
        zsend[...] = gacc[0:64].astype(BF)
        peer = jnp.where(z == 0, 1, last - 1)
        remote(zsend, zrecv.at[0], za_ss.at[0], za_rs.at[0], me, peer).start()
        remote(zvec.at[0], zvec.at[1], zv_ss.at[0], zv_rs.at[1], me, peer).start()

    @pl.when(ends)
    def _():
        reduce_start(owner(2), 0)
        reduce_start(owner(2), 1)

    home_start(xin, gtok, gt_ss, gt_rs, sizes[1:])

    @pl.when(inner)
    def _():
        remote(zrecv.at[0], zrecv.at[0], za_ss.at[0], za_rs.at[0], me, z).wait_recv()
        zsend[...] = (gacc[0:64] + zrecv[0].astype(F32)).astype(BF)
        remote(zsend, zrecv.at[1], za_ss.at[1], za_rs.at[1], me, middle).start()
        home_start(xin, gtok, gt_ss, gt_rs, sizes[:1])
        remote(zvec.at[1], zvec.at[1], zv_ss.at[0], zv_rs.at[1], me, z).wait_recv()
        zvec[2] = zvec[0] + zvec[1]
        remote(zvec.at[2], zvec.at[3], zv_ss.at[1], zv_rs.at[3], me, middle).start()
        remote(zrecv.at[1], zrecv.at[1], za_ss.at[0], za_rs.at[1], me, z).wait_recv()
        zall[...] = (zsend[...].astype(F32) + zrecv[1].astype(F32)).astype(BF)
        remote(zall, zall, zb_ss.at[0], zb_rs.at[0], me, near_end).start()
        remote(zvec.at[3], zvec.at[3], zv_ss.at[0], zv_rs.at[3], me, z).wait_recv()
        zvec[4] = zvec[2] + zvec[3]
        remote(zvec.at[4], zvec.at[4], zv_ss.at[2], zv_rs.at[4], me, near_end).start()

    final_copies = [
        pltpu.make_async_copy(gacc.at[:, pl.ds(piece * 512, 512)], out, loc_sem.at[2 + piece])
        for piece, out in ((0, gout), (1, gin))
    ]
    for piece in range(2):
        for slot, there in ((0, z >= 0), (3, inner)):

            @pl.when(there)
            def _():
                here = arrived.at[slot, piece]
                remote(here, here, r_ss.at[0, piece], r_rs.at[slot, piece], me, z).wait_recv()

        def finish(c, carry):
            at = rows_of(c, 128)
            gacc[at, piece * 512 : piece * 512 + 512] = (
                dws[z, piece, at].astype(F32)
                + arrived[0, piece, at].astype(F32)
                + jnp.where(inner, arrived[3, piece, at].astype(F32), 0.0)
            )
            return carry

        lax.fori_loop(0, 4, finish, 0)
        final_copies[piece].start()
    @pl.when(ends)
    def _():
        remote(zvec.at[4], zvec.at[4], zv_ss.at[0], zv_rs.at[4], me, z).wait_recv()
        remote(zall, zall, zb_ss.at[0], zb_rs.at[0], me, z).wait_recv()

    gsmall[...] = zvec[4]
    gqkv[...] = zall[:, 0:1536].astype(F32)
    gwo[...] = zall[:, 1536:2048].astype(F32)
    each(own_gtok, "wait")
    home_arrive(gtok, gt_rs)
    home_arrive(mixed, mix_rs)
    for copy in final_copies:
        copy.wait()

    hosts_sent(xin, tok_ss)
    hosts_sent(rin, rts_ss)
    hosts_sent(tin, tgt_ss)
    home_sent(xin, gt_ss)
    @pl.when(ends)
    def _():
        remote(zsend, zsend, za_ss.at[0], loc_sem.at[8], me, z).wait_send()
        remote(zvec.at[0], zvec.at[0], zv_ss.at[0], loc_sem.at[8], me, z).wait_send()

    @pl.when(inner)
    def _():
        remote(zsend, zsend, za_ss.at[1], loc_sem.at[8], me, z).wait_send()
        remote(zall, zall, zb_ss.at[0], loc_sem.at[8], me, z).wait_send()
        for k in (1, 2):
            remote(zvec.at[0], zvec.at[0], zv_ss.at[k], loc_sem.at[8], me, z).wait_send()


    def rows_sent(i, carry):
        sent(i, dn_ss)
        return carry

    lax.fori_loop(0, im, rows_sent, 0)
    weights_sent()
    for array in range(3):
        slot = dense_slot(array, 0)
        for k in range(half):
            remote(slot, slot, den_ss.at[array, k], loc_sem.at[8], me, z).wait_send()
        for k in range(1, half):
            remote(slot, slot, fwd_ss.at[array, k], loc_sem.at[8], me, z).wait_send()
    for piece in range(2):
        for target in range(n_z):
            here = dws.at[0, 0]

            @pl.when(z != target)
            def _():
                remote(here, here, r_ss.at[target, piece], loc_sem.at[8], me, z).wait_send()

    for q in range(half):
        remote(crecv.at[q], crecv.at[q], c_ss.at[q], loc_sem.at[8], me, z).wait_send()
    remote(cvec, cvec, cv_ss.at[0], loc_sem.at[8], me, z).wait_send()
    for k in range(1, half):
        remote(crecv.at[0], crecv.at[0], h_ss.at[k], loc_sem.at[8], me, z).wait_send()
        remote(cvec, cvec, hv_ss.at[k], loc_sem.at[8], me, z).wait_send()


def finish_kernel(mixed, gtok, gqkv, gwo, gsmall, gin, gout, *outs):
    me = lax.axis_index("dp")
    outs[0][...] = mixed[...]
    outs[1][...] = gtok[...].astype(F32)
    for source, target in ((gqkv, outs[2]), (gwo, outs[3]), (gin, outs[4]), (gout, outs[5])):
        target[...] = source[...]

    lanes = gsmall[:, pl.ds(pl.multiple_of((me // 2) * 128, 128), 128)]
    lanes = jnp.where(lax.rem(me, 2) == 1, pltpu.roll(lanes, 64, 1), lanes)
    for row in range(4):
        outs[6 + row][...] = lanes[row, 0:64]
    outs[10][...] = lanes[8:16, 0:64]


def whole_images(
    tokens, ln1_gain, ln1_bias, w_qkv, w_out, ln2_gain, ln2_bias, w_router, expert_in, expert_out, routes, targets
):
    n_dp, n_z = lax.axis_size("dp"), lax.axis_size("seq")
    image_count, block, width = tokens.shape
    im = image_count // 3
    cap = 2 * S // (n_z * w_router.shape[1]) + 2
    dims = (n_dp, n_z, (image_count // 6, im, im, image_count // 6), block, cap)
    sp, half = n_z * BP, n_dp // 2
    me, z = lax.axis_index("dp"), lax.axis_index("seq")
    dma, vm = pltpu.SemaphoreType.DMA, pltpu.VMEM

    valid = z * block + jnp.arange(block) < VALID
    lines = jnp.where(valid[None, None, :], jnp.transpose(routes, (0, 2, 1)) + 1, 0)
    lines = jnp.pad(lines, ((0, 0), (0, 6), (0, BP - block)))
    odd = lax.rem(z, 2) == 1
    lines = jnp.concatenate([jnp.where(odd, 0, lines), jnp.where(odd, lines, 0)], axis=-1)
    vec = jnp.concatenate(
        [
            jnp.stack([ln1_gain, ln1_bias, ln2_gain, ln2_bias]),
            jnp.zeros((4, ln1_gain.shape[0]), BF),
            jnp.transpose(w_router),
        ],
        axis=0,
    )
    vec = lax.dynamic_update_slice(jnp.zeros((16, width), BF), vec, (0, me * ln1_gain.shape[0]))
    blocks = (n_z, im, block, width)
    in_any, in_vmem = pl.BlockSpec(memory_space=pl.ANY), pl.BlockSpec(memory_space=pltpu.VMEM)
    mixed, gtok, gqkv, gwo, gsmall, gin, gout = pl.pallas_call(
        functools.partial(block_kernel, dims),
        out_shape=[
            jax.ShapeDtypeStruct((image_count, block, width), BF),
            jax.ShapeDtypeStruct((image_count, block, width), BF),
            jax.ShapeDtypeStruct((64, 1536), F32),
            jax.ShapeDtypeStruct((64, width), F32),
            jax.ShapeDtypeStruct((16, width), F32),
            jax.ShapeDtypeStruct((512, 512), F32),
            jax.ShapeDtypeStruct((512, 512), F32),
        ],
        in_specs=[in_any, in_any, in_vmem, in_any, in_any, in_vmem, in_any, in_any],
        out_specs=[in_any, in_any] + [in_vmem] * 3 + [in_any] * 2,
        scratch_shapes=[
            vm(blocks, BF), vm((n_z, im, 8, 128), jnp.int32), vm(blocks, BF), vm((n_dp, 16, width), BF),
            vm((width, 1536), BF), vm((width, width), BF), vm((16, width), F32), vm((im, sp, width), BF),
            vm((im, sp, width), BF), vm((im, sp, 1536), BF), vm((im, sp, width), BF),
            vm((im, sp, 128), F32), vm((im, 8, sp), F32), vm((im, 8, sp), F32),
            vm((n_z, 512, 512), BF), vm((n_z, 512, 512), BF), vm((im, 512, 512), BF), vm((im, 512, 512), BF),
            vm((n_z, im, 512, 512), BF), vm((n_z, im, 512, 512), BF), vm((im, 512, 512), BF),
            vm((im, 512, 512), BF), vm((im, sp, width), F32), vm((n_z, 2, 512, 512), BF), vm((5, 2, 512, 512), BF),
            vm((width, 2048), F32), vm((512, 512), F32), vm((16, width), F32), vm((half, 64, 2048), BF), vm((half, 64, 2048), BF),
            vm((16, width), F32), vm((half, 64, 2048), BF), vm((half, 16, width), F32),
            vm((64, 2048), BF), vm((2, 64, 2048), BF), vm((64, 2048), BF), vm((5, 16, width), F32),
            dma((9,)), dma((n_z,)), dma((n_z,)), dma((n_z,)), dma((n_z,)), dma((n_z,)), dma((n_z,)),
            dma((3, half)), dma((3, n_dp)), dma((3, half)), dma((2, n_z)), dma((n_z,)), dma((2, n_z)), dma((n_z,)),
            dma((im, n_dp)), dma((im, n_dp)), dma((im, n_dp)), dma((im, n_dp)), dma((im, n_dp)), dma((im, n_dp)),
            dma((im, n_dp)), dma((im, n_dp)),
            dma((n_z,)), dma((n_z,)), dma((n_z,)), dma((n_z,)),
            dma((n_z, 2)), dma((5, 2)), dma((half,)), dma((half,)), dma((1,)), dma((1,)),
            dma((half,)), dma((half,)), dma((half,)), dma((half,)), dma((2,)), dma((2,)), dma((1,)), dma((1,)),
            dma((3,)), dma((5,)),
        ],
        compiler_params=pltpu.CompilerParams(
            collective_id=1, has_side_effects=True, vmem_limit_bytes=VMEM_LIMIT
        ),
        name="block",
    )(tokens, targets, lines, w_qkv, w_out, vec, expert_in[0], expert_out[0])
    whole = pl.BlockSpec(memory_space=pltpu.VMEM)
    mixed, gtok, gqkv, gwo, gin, gout, g1, b1, g2, b2, grouter = pl.pallas_call(
        finish_kernel,
        out_shape=[
            jax.ShapeDtypeStruct((image_count, block, width), BF),
            jax.ShapeDtypeStruct((image_count, block, width), F32),
            jax.ShapeDtypeStruct((64, 1536), F32),
            jax.ShapeDtypeStruct((64, width), F32),
            jax.ShapeDtypeStruct((512, 512), F32),
            jax.ShapeDtypeStruct((512, 512), F32),
        ]
        + [jax.ShapeDtypeStruct((64,), F32)] * 4
        + [jax.ShapeDtypeStruct((8, 64), F32)],
        in_specs=[whole] * 7,
        out_specs=[whole] * 11,
        name="finish",
    )(mixed, gtok, gqkv, gwo, gsmall, gin, gout)
    return (mixed, gtok, g1, b1, gqkv, gwo, g2, b2, jnp.transpose(grouter), gin[None], gout[None])


def fits(tokens, w_qkv, w_router, expert_in):
    n_dp, n_z = lax.axis_size("dp"), lax.axis_size("seq")
    return (
        n_dp == 8
        and n_z == 4
        and tokens.shape[0] % 6 == 0
        and tokens.shape[1] <= BP
        and tokens.shape[2] == 512
        and w_qkv.shape == (64, 1536)
        and w_router.shape[1] == n_dp
        and expert_in.shape == (1, 512, 512)
    )


def local(*args):
    if fits(args[0], args[3], args[7], args[8]):
        return whole_images(*args)
    return by_heads(*args)


def solution(mesh):
    placed = (
        P("dp", "seq", None),
        P("dp"),
        P("dp"),
        P("dp", None),
        P("dp", None),
        P("dp"),
        P("dp"),
        P("dp", None),
        P("dp", None, "seq"),
        P("dp", "seq", None),
        P("dp", "seq", None),
        P("dp", "seq", None),
    )
    return jax.shard_map(
        local,
        mesh=mesh,
        in_specs=placed,
        out_specs=(
            P("dp", "seq", None),
            P("dp", "seq", None),
            P("dp"),
            P("dp"),
            P("dp", None),
            P("dp", None),
            P("dp"),
            P("dp"),
            P("dp", None),
            P("dp", None, "seq"),
            P("dp", "seq", None),
        ),
        check_vma=False,
    )
```

```python
import functools

import jax
import jax.numpy as jnp
from jax import lax
from jax.experimental import pallas as pl
from jax.experimental.pallas import tpu as pltpu
from jax.sharding import PartitionSpec as P

H = 8
S = 200
VALID = 197


def layer_norm(values, gain_vec, bias_vec):
    centre = values - jnp.mean(values, axis=-1, keepdims=True)
    spread = jnp.mean(centre * centre, axis=-1, keepdims=True)
    return centre * lax.rsqrt(spread + 1e-06) * gain_vec + bias_vec


def regroup_heads(values):
    return lax.all_to_all(values, "seq", split_axis=3, concat_axis=1, tiled=True)


def regroup_slots(values):
    return lax.all_to_all(values, "seq", split_axis=1, concat_axis=3, tiled=True)


def send_experts(values):
    return lax.all_to_all(values, "dp", split_axis=0, concat_axis=1, tiled=True)


def send_tokens(values):
    return lax.all_to_all(values, "dp", split_axis=1, concat_axis=0, tiled=True)


def masked_scores(queries, keys_in, key_valid):
    scores = (
        jnp.einsum("bqhd,bkhd->bhqk", queries, keys_in, preferred_element_type=jnp.float32) * 0.125
    )
    return jnp.where(key_valid, scores, -1e30)


def attention_forward(queries, keys_in, values, key_valid):
    scores = masked_scores(queries, keys_in, key_valid)
    row_top = jnp.max(scores, axis=-1, keepdims=True)
    exponent = jnp.exp(scores - row_top)
    row_total = jnp.sum(exponent, axis=-1, keepdims=True)
    prob_rows = exponent / row_total
    log_total = row_top + jnp.log(row_total)
    attended = jnp.einsum(
        "bhqk,bkhd->bqhd",
        prob_rows.astype(jnp.bfloat16),
        values,
        preferred_element_type=jnp.float32,
    )
    return (attended.astype(jnp.bfloat16), log_total)


def attention_backward(queries, keys_in, values, log_total, grad_attended, key_valid):
    scores = masked_scores(queries, keys_in, key_valid)
    prob_rows = jnp.exp(scores - log_total)
    grad_values = jnp.einsum(
        "bhqk,bqhd->bkhd",
        prob_rows.astype(jnp.bfloat16),
        grad_attended,
        preferred_element_type=jnp.float32,
    )
    grad_probs = jnp.einsum(
        "bqhd,bkhd->bhqk", grad_attended, values, preferred_element_type=jnp.float32
    )
    inner_sum = jnp.sum(prob_rows * grad_probs, axis=-1, keepdims=True)
    grad_scores = (prob_rows * (grad_probs - inner_sum)).astype(jnp.bfloat16)
    grad_queries = (
        jnp.einsum("bhqk,bkhd->bqhd", grad_scores, keys_in, preferred_element_type=jnp.float32)
        * 0.125
    )
    grad_keys = (
        jnp.einsum("bhqk,bqhd->bkhd", grad_scores, queries, preferred_element_type=jnp.float32)
        * 0.125
    )
    return jnp.stack([grad_queries, grad_keys, grad_values], axis=2)


def pick_block(total_rows):
    for candidate in (1024, 768, 512, 384, 256):
        if total_rows % candidate == 0:
            return candidate
    return total_rows


def by_heads(
    tokens,
    ln1_gain,
    ln1_bias,
    w_qkv,
    w_out,
    ln2_gain,
    ln2_bias,
    w_router,
    expert_in,
    expert_out,
    routes,
    targets,
):
    image_count, slot_count, model_width = tokens.shape
    seq_devices = lax.axis_size("seq")
    row_count = image_count * slot_count
    expert_count = w_router.shape[1]
    local_experts = expert_in.shape[0]
    slot_limit = 2 * S // (seq_devices * expert_count) + 2
    head_size = model_width // H
    gathered = (
        lax.all_gather(ln1_gain, "dp", axis=0, tiled=True),
        lax.all_gather(ln1_bias, "dp", axis=0, tiled=True),
        lax.all_gather(w_qkv, "dp", axis=0, tiled=True),
        lax.all_gather(w_out, "dp", axis=0, tiled=True),
        lax.all_gather(ln2_gain, "dp", axis=0, tiled=True),
        lax.all_gather(ln2_bias, "dp", axis=0, tiled=True),
        lax.all_gather(w_router, "dp", axis=0, tiled=True),
    )
    gain_one = gathered[0].astype(jnp.float32)
    bias_one = gathered[1].astype(jnp.float32)
    qkv_weight = gathered[2]
    out_weight = gathered[3]
    gain_two = gathered[4].astype(jnp.float32)
    bias_two = gathered[5].astype(jnp.float32)
    router_weight = gathered[6]
    slot_start = lax.axis_index("seq") * slot_count
    valid_slot = slot_start + jnp.arange(slot_count) < VALID
    valid_rows = jnp.tile(valid_slot, image_count)
    key_valid = (jnp.arange(S) < VALID)[None, None, None, :]
    token_rows = tokens.reshape(row_count, model_width).astype(jnp.float32)
    normed_one, norm_one_back = jax.vjp(layer_norm, token_rows, gain_one, bias_one)
    normed_one_b = normed_one.astype(jnp.bfloat16)
    mixed_qkv = jnp.dot(normed_one_b, qkv_weight, preferred_element_type=jnp.float32).astype(
        jnp.bfloat16
    )
    qkv_heads = regroup_heads(mixed_qkv.reshape(image_count, slot_count, 3, H, head_size))
    queries = qkv_heads[:, :, 0]
    keys_in = qkv_heads[:, :, 1]
    values = qkv_heads[:, :, 2]
    attended, log_total = attention_forward(queries, keys_in, values, key_valid)
    attended_rows = regroup_slots(attended[:, :, None]).reshape(row_count, model_width)
    residual_two = token_rows + jnp.dot(
        attended_rows, out_weight, preferred_element_type=jnp.float32
    )
    normed_two, norm_two_back = jax.vjp(layer_norm, residual_two, gain_two, bias_two)
    normed_two_b = normed_two.astype(jnp.bfloat16)
    logits = jnp.dot(normed_two_b, router_weight, preferred_element_type=jnp.float32)
    route_rows = routes.reshape(row_count, 2)
    chosen = (route_rows[:, :, None] == jnp.arange(expert_count)[None, None, :]) & valid_rows[
        :, None, None
    ]
    chosen_f = chosen.astype(jnp.float32)

    def gate_pick(logit_rows):
        return jnp.sum(jax.nn.softmax(logit_rows, axis=-1)[:, None, :] * chosen_f, axis=-1)

    gate_values, gate_back = jax.vjp(gate_pick, logits)
    pick_count = chosen.astype(jnp.int32).reshape(image_count, slot_count * 2, expert_count)
    before = jnp.cumsum(pick_count, axis=1) - pick_count
    place_hit = (before[..., None] == jnp.arange(slot_limit)) & (pick_count[..., None] > 0)
    dispatch = place_hit.astype(jnp.bfloat16).reshape(
        image_count, slot_count, 2, expert_count, slot_limit
    )
    normed_img = normed_two_b.reshape(image_count, slot_count, model_width)
    sent_rows = jnp.einsum(
        "bskem,bsd->ebmd", dispatch, normed_img, preferred_element_type=jnp.float32
    ).astype(jnp.bfloat16)
    received = send_experts(sent_rows.reshape(expert_count, image_count * slot_limit, model_width))
    weights_in, weights_out = (
        lax.all_gather(expert_in, "seq", axis=2, tiled=True),
        lax.all_gather(expert_out, "seq", axis=1, tiled=True),
    )
    total_rows = received.shape[1]
    block_rows = pick_block(total_rows)
    block_count = total_rows // block_rows

    def expert_step(block_index, produced):
        row_piece = lax.dynamic_slice_in_dim(received, block_index * block_rows, block_rows, 1)
        hidden_pre = jnp.einsum(
            "erd,edf->erf", row_piece, weights_in, preferred_element_type=jnp.float32
        )
        activated = jax.nn.gelu(hidden_pre).astype(jnp.bfloat16)
        result = jnp.einsum(
            "erf,efd->erd", activated, weights_out, preferred_element_type=jnp.float32
        ).astype(jnp.bfloat16)
        return lax.dynamic_update_slice_in_dim(produced, result, block_index * block_rows, 1)

    produced = lax.fori_loop(
        0,
        block_count,
        expert_step,
        jnp.zeros((local_experts, total_rows, model_width), jnp.bfloat16),
    )
    returned = send_tokens(produced).reshape(expert_count, image_count, slot_limit, model_width)
    per_choice = jnp.einsum(
        "bskem,ebmd->bskd", dispatch, returned, preferred_element_type=jnp.float32
    ).reshape(row_count, 2, model_width)
    mixed_rows = (
        residual_two
        + gate_values[:, 0:1] * per_choice[:, 0]
        + gate_values[:, 1:2] * per_choice[:, 1]
    )
    target_rows = targets.reshape(row_count, model_width).astype(jnp.float32)
    grad_mixed = (mixed_rows - target_rows) * valid_rows[:, None].astype(jnp.float32)
    grad_gates = jnp.sum(grad_mixed[:, None, :] * per_choice, axis=-1)
    grad_choice = (
        (gate_values[:, :, None] * grad_mixed[:, None, :])
        .astype(jnp.bfloat16)
        .reshape(image_count, slot_count, 2, model_width)
    )
    grad_sent = jnp.einsum(
        "bskem,bskd->ebmd", dispatch, grad_choice, preferred_element_type=jnp.float32
    ).astype(jnp.bfloat16)
    grad_received = send_experts(
        grad_sent.reshape(expert_count, image_count * slot_limit, model_width)
    )
    back_in, back_out = (
        lax.all_gather(expert_in, "seq", axis=2, tiled=True),
        lax.all_gather(expert_out, "seq", axis=1, tiled=True),
    )

    def expert_back(block_index, loop_carry):
        grad_in_sum, grad_out_sum, grad_rows = loop_carry
        row_piece = lax.dynamic_slice_in_dim(received, block_index * block_rows, block_rows, 1)
        grad_piece = lax.dynamic_slice_in_dim(
            grad_received, block_index * block_rows, block_rows, 1
        )
        hidden_pre = jnp.einsum(
            "erd,edf->erf", row_piece, back_in, preferred_element_type=jnp.float32
        )
        activated, gelu_back = jax.vjp(jax.nn.gelu, hidden_pre)
        grad_act = jnp.einsum(
            "erd,efd->erf", grad_piece, back_out, preferred_element_type=jnp.float32
        )
        grad_pre = gelu_back(grad_act)[0].astype(jnp.bfloat16)
        grad_out_sum = grad_out_sum + jnp.einsum(
            "erf,erd->efd",
            activated.astype(jnp.bfloat16),
            grad_piece,
            preferred_element_type=jnp.float32,
        )
        grad_in_sum = grad_in_sum + jnp.einsum(
            "erd,erf->edf", row_piece, grad_pre, preferred_element_type=jnp.float32
        )
        rows_back = jnp.einsum(
            "erf,edf->erd", grad_pre, back_in, preferred_element_type=jnp.float32
        ).astype(jnp.bfloat16)
        grad_rows = lax.dynamic_update_slice_in_dim(
            grad_rows, rows_back, block_index * block_rows, 1
        )
        return (grad_in_sum, grad_out_sum, grad_rows)

    start_carry = (
        jnp.zeros(back_in.shape, jnp.float32),
        jnp.zeros(back_out.shape, jnp.float32),
        jnp.zeros((local_experts, total_rows, model_width), jnp.bfloat16),
    )
    grad_in_sum, grad_out_sum, grad_rows = lax.fori_loop(0, block_count, expert_back, start_carry)
    grad_returned = send_tokens(grad_rows).reshape(
        expert_count, image_count, slot_limit, model_width
    )
    grad_normed_two = jnp.einsum(
        "bskem,ebmd->bsd", dispatch, grad_returned, preferred_element_type=jnp.float32
    ).reshape(row_count, model_width)
    grad_logits = gate_back(grad_gates)[0].astype(jnp.bfloat16)
    grad_router = jnp.einsum(
        "rd,re->de", normed_two_b, grad_logits, preferred_element_type=jnp.float32
    )
    grad_normed_two = grad_normed_two + jnp.einsum(
        "re,de->rd", grad_logits, router_weight, preferred_element_type=jnp.float32
    )
    grad_res_two, grad_gain_two, grad_bias_two = norm_two_back(grad_normed_two)
    grad_residual = grad_mixed + grad_res_two
    grad_branch = grad_residual.astype(jnp.bfloat16)
    grad_out_weight = jnp.einsum(
        "rd,re->de", attended_rows, grad_branch, preferred_element_type=jnp.float32
    )
    grad_attended = jnp.einsum(
        "re,de->rd", grad_branch, out_weight, preferred_element_type=jnp.float32
    ).astype(jnp.bfloat16)
    grad_heads = regroup_heads(grad_attended.reshape(image_count, slot_count, 1, H, head_size))[
        :, :, 0
    ]
    grad_qkv_heads = attention_backward(
        queries, keys_in, values, log_total, grad_heads, key_valid
    ).astype(jnp.bfloat16)
    grad_qkv_rows = regroup_slots(grad_qkv_heads).reshape(row_count, 3 * model_width)
    grad_qkv_weight = jnp.einsum(
        "rd,rf->df", normed_one_b, grad_qkv_rows, preferred_element_type=jnp.float32
    )
    grad_normed_one = jnp.einsum(
        "rf,df->rd", grad_qkv_rows, qkv_weight, preferred_element_type=jnp.float32
    )
    grad_token_ln, grad_gain_one, grad_bias_one = norm_one_back(grad_normed_one)
    grad_tokens = grad_residual + grad_token_ln
    dense_grads = (
        grad_gain_one,
        grad_bias_one,
        grad_qkv_weight,
        grad_out_weight,
        grad_gain_two,
        grad_bias_two,
        grad_router,
    )
    dense_grads = (
        lax.psum(dense_grads[0].astype(jnp.bfloat16), "seq").astype(jnp.float32),
        lax.psum(dense_grads[1].astype(jnp.bfloat16), "seq").astype(jnp.float32),
        lax.psum(dense_grads[2].astype(jnp.bfloat16), "seq").astype(jnp.float32),
        lax.psum(dense_grads[3].astype(jnp.bfloat16), "seq").astype(jnp.float32),
        lax.psum(dense_grads[4].astype(jnp.bfloat16), "seq").astype(jnp.float32),
        lax.psum(dense_grads[5].astype(jnp.bfloat16), "seq").astype(jnp.float32),
        lax.psum(dense_grads[6].astype(jnp.bfloat16), "seq").astype(jnp.float32),
    )
    dense_grads = (
        lax.psum_scatter(
            dense_grads[0].astype(jnp.bfloat16), "dp", scatter_dimension=0, tiled=True
        ).astype(jnp.float32),
        lax.psum_scatter(
            dense_grads[1].astype(jnp.bfloat16), "dp", scatter_dimension=0, tiled=True
        ).astype(jnp.float32),
        lax.psum_scatter(
            dense_grads[2].astype(jnp.bfloat16), "dp", scatter_dimension=0, tiled=True
        ).astype(jnp.float32),
        lax.psum_scatter(
            dense_grads[3].astype(jnp.bfloat16), "dp", scatter_dimension=0, tiled=True
        ).astype(jnp.float32),
        lax.psum_scatter(
            dense_grads[4].astype(jnp.bfloat16), "dp", scatter_dimension=0, tiled=True
        ).astype(jnp.float32),
        lax.psum_scatter(
            dense_grads[5].astype(jnp.bfloat16), "dp", scatter_dimension=0, tiled=True
        ).astype(jnp.float32),
        lax.psum_scatter(
            dense_grads[6].astype(jnp.bfloat16), "dp", scatter_dimension=0, tiled=True
        ).astype(jnp.float32),
    )
    expert_in_grad, expert_out_grad = (
        lax.psum_scatter(
            grad_in_sum.astype(jnp.bfloat16), "seq", scatter_dimension=2, tiled=True
        ).astype(jnp.float32),
        lax.psum_scatter(
            grad_out_sum.astype(jnp.bfloat16), "seq", scatter_dimension=1, tiled=True
        ).astype(jnp.float32),
    )
    mixed = mixed_rows.astype(jnp.bfloat16).reshape(image_count, slot_count, model_width)
    return (
        mixed,
        grad_tokens.reshape(image_count, slot_count, model_width),
        dense_grads[0],
        dense_grads[1],
        dense_grads[2],
        dense_grads[3],
        dense_grads[4],
        dense_grads[5],
        dense_grads[6],
        expert_in_grad,
        expert_out_grad,
    )


BF = jnp.bfloat16
F32 = jnp.float32
MESH_ID = pl.DeviceIdType.MESH
NEG = -1e30
BP = 64
VMEM_LIMIT = 67000000
GELU_C = 0.7978845608028654
GELU_K = 0.044715


def nn(a, b):
    return lax.dot_general(a, b, (((1,), (0,)), ((), ())), preferred_element_type=F32)


def nt(a, b):
    return lax.dot_general(a, b, (((1,), (1,)), ((), ())), preferred_element_type=F32)


def tn(a, b):
    return lax.dot_general(a, b, (((0,), (0,)), ((), ())), preferred_element_type=F32)


def remote(src, dst, send_sem, recv_sem, dp, z):
    return pltpu.make_async_remote_copy(
        src_ref=src,
        dst_ref=dst,
        send_sem=send_sem,
        recv_sem=recv_sem,
        device_id=(dp, z),
        device_id_type=MESH_ID,
    )


def rows_of(index, size):
    return pl.ds(pl.multiple_of(index * size, size), size)


def norm_parts(x):
    centre = x - jnp.mean(x, axis=-1, keepdims=True)
    scale = lax.rsqrt(jnp.mean(centre * centre, axis=-1, keepdims=True) + 1e-06)
    return centre * scale, scale


def norm_back(grad_hat, hat, scale):
    return scale * (
        grad_hat
        - jnp.mean(grad_hat, axis=-1, keepdims=True)
        - hat * jnp.mean(grad_hat * hat, axis=-1, keepdims=True)
    )


def half_masks():
    lane = lax.broadcasted_iota(jnp.int32, (1, 128), 1)
    low = jnp.where(lane < 64, 1.0, 0.0)
    return (low.astype(BF), (1.0 - low).astype(BF))


def slot_ok(position, block):
    return (position % BP < block) & ((position // BP) * block + position % BP < VALID)


def block_kernel(
    dims,
    tok, tgt, rts, wq, wo, vec, win, wout,
    mixed, gtok, gqkv, gwo, gsmall, gin, gout,
    xin, rin, tin, vec_all, wq_all, wo_all, vsum, xpad, n2s, qkvs, outs, cols, gts, meta,
    win_all, wout_all, recv, ret, acts, slopes, sbuf,
    drows, dys, dws, arrived,
    gacc, accf, gvec, csend, crecv, cvec, hrecv, hvec, zsend, zrecv, zall, zvec,
    loc_sem, tok_ss, tok_rs, rts_ss, rts_rs, tgt_ss, tgt_rs, den_ss, den_rs, fwd_ss, win_ss, win_rs, wout_ss, wout_rs,
    row_ss, row_rs, u_ss, u_rs, du_ss, du_rs, dn_ss, dn_rs, mix_ss, mix_rs, gt_ss, gt_rs,
    r_ss, r_rs, c_ss, c_rs, cv_ss, cv_rs, h_ss, h_rs, hv_ss, hv_rs, za_ss, za_rs, zb_ss, zb_rs, zv_ss, zv_rs,
):
    n_dp, n_z, counts, block, cap = dims
    firsts = tuple(sum(counts[:h]) for h in range(n_z))
    me, z = lax.axis_index("dp"), lax.axis_index("seq")
    sp = n_z * BP
    half = n_dp // 2
    last = n_z - 1
    core, chip = lax.rem(me, 2), me // 2
    partner = chip * 2 + 1 - core
    inner = (z == 1) | (z == last - 1)
    ends = jnp.logical_not(inner)
    far_end = jnp.where(z < n_z // 2, last, 0)
    near_end = last - far_end
    middle = last - z
    im = jnp.where(inner, counts[1], counts[0])
    sizes = ((counts[1], inner), (counts[0], ends))
    first = jnp.where(z == 0, firsts[0], jnp.where(z == 1, firsts[1], jnp.where(z == 2, firsts[2], firsts[3])))

    barrier = pltpu.get_barrier_semaphore()
    for k in range(1, n_dp):
        pl.semaphore_signal(barrier, inc=1, device_id=(lax.rem(me + k, n_dp), z), device_id_type=MESH_ID)
    for k in range(1, n_z):
        pl.semaphore_signal(barrier, inc=1, device_id=(me, lax.rem(z + k, n_z)), device_id_type=MESH_ID)

    def hosts_own(source, target, sem):
        for h in range(n_z):

            @pl.when(z == h)
            def _():
                pltpu.make_async_copy(
                    source.at[pl.ds(firsts[h], counts[h])], target.at[z, pl.ds(0, counts[h])], sem
                ).start()

    def hosts_own_wait(source, target, sem):
        for h in range(n_z):

            @pl.when(z == h)
            def _():
                pltpu.make_async_copy(
                    source.at[pl.ds(firsts[h], counts[h])], target.at[z, pl.ds(0, counts[h])], sem
                ).wait()

    def hosts_start(source, target, send_sem, recv_sem, hosts, who):
        for h in hosts:

            @pl.when((z != h) & who)
            def _():
                remote(
                    source.at[pl.ds(firsts[h], counts[h])],
                    target.at[z, pl.ds(0, counts[h])],
                    send_sem.at[h],
                    recv_sem.at[z],
                    me,
                    h,
                ).start()

    def hosts_arrive(target, recv_sem):
        for size, there in sizes:

            @pl.when(there)
            def _():
                for k in range(1, n_z):
                    origin = lax.rem(z + k, n_z)
                    spot = target.at[origin, pl.ds(0, size)]
                    remote(spot, spot, loc_sem.at[8], recv_sem.at[origin], me, z).wait_recv()

    def hosts_sent(target, send_sem):
        for h in range(n_z):

            @pl.when(z != h)
            def _():
                spot = target.at[0, pl.ds(0, counts[h])]
                remote(spot, spot, send_sem.at[h], loc_sem.at[8], me, z).wait_send()

    def home_own(source, target, sem):
        return [
            (there, pltpu.make_async_copy(source.at[z, pl.ds(0, size)], target.at[pl.ds(first, size)], sem))
            for size, there in sizes
        ]

    def home_start(source, target, send_sem, recv_sem, who):
        for size, there in who:

            @pl.when(there)
            def _():
                for k in range(1, n_z):
                    peer = lax.rem(z + k, n_z)
                    remote(
                        source.at[peer, pl.ds(0, size)],
                        target.at[pl.ds(first, size)],
                        send_sem.at[k],
                        recv_sem.at[z],
                        me,
                        peer,
                    ).start()

    def home_arrive(target, recv_sem):
        for h in range(n_z):

            @pl.when(z != h)
            def _():
                spot = target.at[pl.ds(firsts[h], counts[h])]
                remote(spot, spot, loc_sem.at[8], recv_sem.at[h], me, z).wait_recv()

    def home_sent(source, send_sem):
        for size, there in sizes:

            @pl.when(there)
            def _():
                for k in range(1, n_z):
                    spot = source.at[0, pl.ds(0, size)]
                    remote(spot, spot, send_sem.at[k], loc_sem.at[8], me, z).wait_send()

    def each(pairs, act):
        for there, copy in pairs:

            @pl.when(there)
            def _():
                getattr(copy, act)()

    own_copies = [
        pltpu.make_async_copy(win, win_all.at[z], loc_sem.at[3]),
        pltpu.make_async_copy(wout, wout_all.at[z], loc_sem.at[4]),
        pltpu.make_async_copy(wq, wq_all.at[rows_of(me, 64)], loc_sem.at[5]),
        pltpu.make_async_copy(wo, wo_all.at[rows_of(me, 64)], loc_sem.at[6]),
        pltpu.make_async_copy(vec, vec_all.at[me], loc_sem.at[7]),
    ]
    for copy in own_copies:
        copy.start()
    hosts_own(tok, xin, loc_sem.at[0])
    hosts_own(rts, rin, loc_sem.at[1])
    hosts_own(tgt, tin, loc_sem.at[2])
    for buffer in (xpad, gvec, recv, ret, drows):
        buffer[...] = jnp.zeros_like(buffer)
    pl.semaphore_wait(barrier, n_dp + n_z - 2)
    hosts_start(tok, xin, tok_ss, tok_rs, range(n_z), z >= 0)
    hosts_start(rts, rin, rts_ss, rts_rs, range(n_z), z >= 0)

    def dense_slot(array, index):
        if array == 0:
            return wq_all.at[rows_of(index, 64)]
        if array == 1:
            return wo_all.at[rows_of(index, 64)]
        return vec_all.at[index]

    dense_in = (wq, wo, vec)
    for array in range(3):
        for k in range(1, half):
            peer = lax.rem(chip + k, half) * 2 + core
            remote(
                dense_in[array], dense_slot(array, me), den_ss.at[array, k], den_rs.at[array, me], peer, z
            ).start()
        remote(
            dense_in[array], dense_slot(array, me), den_ss.at[array, 0], den_rs.at[array, me], partner, z
        ).start()

    experts = ((win, win_all, win_ss, win_rs), (wout, wout_all, wout_ss, wout_rs))

    def gather_hop(array, step):
        source, full, send_sem, recv_sem = experts[array]
        for way, there, slot in ((0, z >= step, z - step), (1, z + step < n_z, z + step)):

            @pl.when(there)
            def _():
                at = full.at[slot]
                if step > 0:
                    remote(at, at, send_sem.at[way, step], recv_sem.at[slot], me, z).wait_recv()

                @pl.when((z < last) if way == 0 else (z > 0))
                def _():
                    remote(
                        at if step > 0 else source,
                        at,
                        send_sem.at[way, step],
                        recv_sem.at[slot],
                        me,
                        z + 1 if way == 0 else z - 1,
                    ).start()

    def weights_sent():
        for step in range(n_z - 1):
            for way, there in ((0, (z >= step) & (z < last)), (1, (z + step < n_z) & (z > 0))):

                @pl.when(there)
                def _():
                    for source, full, send_sem, recv_sem in experts:
                        remote(
                            full.at[0], full.at[0], send_sem.at[way, step], recv_sem.at[0], me, z
                        ).wait_send()

    gather_hop(0, 0)
    gather_hop(1, 0)

    for k in range(1, half):
        origin = lax.rem(chip + k, half) * 2 + core
        for array in range(3):
            slot = dense_slot(array, origin)
            remote(slot, slot, den_ss.at[array, 0], den_rs.at[array, origin], me, z).wait_recv()
            remote(slot, slot, fwd_ss.at[array, k], den_rs.at[array, origin], partner, z).start()
    for k in range(half):
        origin = lax.rem(chip + k, half) * 2 + 1 - core
        for array in range(3):
            slot = dense_slot(array, origin)
            remote(slot, slot, den_ss.at[array, 0], den_rs.at[array, origin], me, z).wait_recv()
    for copy in own_copies:
        copy.wait()
    hosts_own_wait(tok, xin, loc_sem.at[0])
    hosts_own_wait(rts, rin, loc_sem.at[1])
    hosts_own_wait(tgt, tin, loc_sem.at[2])
    total = vec_all[0].astype(F32)
    for k in range(1, n_dp):
        total = total + vec_all[k].astype(F32)
    vsum[...] = total
    hosts_arrive(xin, tok_rs)
    hosts_arrive(rin, rts_rs)

    masks = half_masks()
    eighths = [mask * 0.125 for mask in masks]
    keys_ok = slot_ok(lax.broadcasted_iota(jnp.int32, (1, sp), 1), block)
    rows_ok = slot_ok(lax.broadcasted_iota(jnp.int32, (sp, 1), 0), block)
    gain_one, bias_one = vsum[0:1, :], vsum[1:2, :]
    gain_two, bias_two = vsum[2:3, :], vsum[3:4, :]
    router_t = vsum[8:16, :].astype(BF)
    lane_id = lax.broadcasted_iota(jnp.int32, (sp, 128), 1)
    lane_low = lane_id < 64
    row_id = lax.broadcasted_iota(jnp.int32, (512, sp), 0).astype(F32)

    def lanes_of(target):
        return pl.ds(pl.multiple_of(target * 512, 512), 512)

    def rows_at(index):
        return pl.ds(pl.multiple_of(index * 64, 64), n_z * cap)

    def send_rows(i, target, send_sem, recv_sem):
        def step(s, carry):
            j, c = lax.rem(s // 2 + 1, half), lax.rem(s, 2)
            index = 2 * j + c
            peer = lax.rem(chip + j, half) * 2 + lax.rem(core + c, 2)

            @pl.when(index > 0)
            def _():
                remote(
                    sbuf.at[i, rows_at(peer)],
                    target.at[i, rows_at(me)],
                    send_sem.at[i, index],
                    recv_sem.at[i, me],
                    peer,
                    z,
                ).start()

            return carry

        lax.fori_loop(0, n_dp, step, 0)
        target[i, rows_of(me, 64)] = sbuf[i, rows_of(me, 64)]

    def arrive(i, target, recv_sem):
        def step(k, carry):
            origin = lax.rem(me + k, n_dp)
            spot = target.at[i, rows_at(origin)]
            remote(spot, spot, loc_sem.at[8], recv_sem.at[i, origin], me, z).wait_recv()
            return carry

        lax.fori_loop(1, n_dp, step, 0)

    def sent(i, send_sem):
        def step(index, carry):
            spot = sbuf.at[i, rows_at(0)]
            remote(spot, spot, send_sem.at[i, index], loc_sem.at[8], me, z).wait_send()
            return carry

        lax.fori_loop(1, n_dp, step, 0)

    def front(i, carry):
        before = lax.broadcasted_iota(jnp.int32, (sp, sp), 0)
        after = lax.broadcasted_iota(jnp.int32, (sp, sp), 1)
        prefix = jnp.where((before < after) & (before // BP == after // BP), 1.0, 0.0).astype(BF)
        expert_id = lax.broadcasted_iota(jnp.int32, (8, sp), 0)
        slot_lane = lax.broadcasted_iota(jnp.int32, (8, sp), 1)
        for b in range(n_z):
            xpad[i, b * BP : b * BP + block, :] = xin[b, i]
        x = xpad[i].astype(F32)
        hat, _ = norm_parts(x)
        normed = (hat * gain_one + bias_one).astype(BF)
        qkvs[i] = nn(normed, wq_all[...]).astype(BF)
        lse_all = jnp.zeros((sp, 128), F32)
        for pair in range(4):
            q2 = qkvs[i, :, pair * 128 : pair * 128 + 128]
            k2 = qkvs[i, :, 512 + pair * 128 : 512 + pair * 128 + 128]
            v2 = qkvs[i, :, 1024 + pair * 128 : 1024 + pair * 128 + 128]
            parts = []
            for side in range(2):
                scores = nt(q2 * eighths[side], k2)
                scores = jnp.where(keys_ok, scores, NEG)
                top = jnp.max(scores, axis=-1, keepdims=True)
                exponent = jnp.exp(scores - top)
                whole = jnp.sum(exponent, axis=-1, keepdims=True)
                lse_all = jnp.where(lane_id == pair * 2 + side, top + jnp.log(whole), lse_all)
                parts.append(nn((exponent / whole).astype(BF), v2))
            outs[i, :, pair * 128 : pair * 128 + 128] = jnp.where(lane_low, parts[0], parts[1]).astype(BF)
        x2 = x + nn(outs[i], wo_all[...])
        hat2, _ = norm_parts(x2)
        n2 = (hat2 * gain_two + bias_two).astype(BF)
        n2s[i] = n2
        logits = nt(router_t, n2)
        raised = jnp.exp(logits - jnp.max(logits, axis=0, keepdims=True))
        share = raised / jnp.sum(raised, axis=0, keepdims=True)
        gts[i] = share
        wide = jnp.concatenate([rin[0, i] + rin[1, i], rin[2, i] + rin[3, i]], axis=1)
        hits = [(expert_id + 1) == wide[j : j + 1, :] for j in range(2)]
        any_hit = jnp.where(hits[0] | hits[1], 1.0, 0.0)
        place = nn(any_hit.astype(BF), prefix)
        base = place + (expert_id * 64 + (slot_lane // BP) * cap + 1).astype(F32)
        lines = [jnp.sum(jnp.where(hit, base, 0.0), axis=0, keepdims=True) - 1.0 for hit in hits]
        lines += [jnp.sum(jnp.where(hit, share, 0.0), axis=0, keepdims=True) for hit in hits]
        lines = jnp.concatenate(lines + [jnp.zeros((4, sp), F32)], axis=0)
        meta[i] = lines
        table = jnp.concatenate([jnp.zeros((8, sp), F32), lines, jnp.zeros((112, sp), F32)], axis=0)
        cols[i] = jnp.transpose(table) + lse_all
        pick = (row_id == lines[0:1, :]) | (row_id == lines[1:2, :])
        sbuf[i] = nn(jnp.where(pick, 1.0, 0.0).astype(BF), n2).astype(BF)
        send_rows(i, recv, row_ss, row_rs)

        @pl.when(i == 1)
        def _():
            gather_hop(0, 1)

        return carry

    lax.fori_loop(0, im, front, 0)


    def hidden(shard):
        def image(i, carry):
            x = recv[i]
            for side in range(2):
                pre = nn(x, win_all[shard, :, side * 256 : side * 256 + 256])
                square = pre * pre
                tanh = jnp.tanh(pre * (GELU_C + (GELU_C * GELU_K) * square))
                gate = 0.5 + 0.5 * tanh
                acts[shard, i, :, side * 256 : side * 256 + 256] = (pre * gate).astype(BF)
                slope = gate + pre * (0.5 - 0.5 * tanh * tanh) * (GELU_C + (3.0 * GELU_C * GELU_K) * square)
                slopes[shard, i, :, side * 256 : side * 256 + 256] = slope.astype(BF)
            return carry

        lax.fori_loop(0, im, image, 0)

    def hidden_step(s, carry):
        for at_step, hop in ((1, 2), (3, 3)):

            @pl.when(s == at_step)
            def _():
                gather_hop(0, hop)

        for way in range(2):
            shard = z - s if way == 0 else z + s

            @pl.when((shard >= 0) & (shard < n_z) & ((s > 0) | (way == 0)))
            def _():
                hidden(shard)

        @pl.when(s == 2)
        def _():
            gather_hop(1, 2)
            hosts_start(tgt, tin, tgt_ss, tgt_rs, (1, 2), z >= 0)

        return carry

    gather_hop(1, 1)

    def rows_here(i, carry):
        arrive(i, recv, row_rs)
        return carry

    lax.fori_loop(0, im, rows_here, 0)
    lax.fori_loop(0, n_z, hidden_step, 0)

    def early_results(i, carry):
        for k in range(1, n_z):
            shard = lax.rem(far_end + k, n_z)
            part = nn(acts[shard, i], wout_all[shard])
            if k == 1:
                gacc[:, lanes_of(i)] = part
            else:
                gacc[:, lanes_of(i)] += part
        return carry

    lax.fori_loop(0, im, early_results, 0)
    gather_hop(1, 3)
    hosts_start(tgt, tin, tgt_ss, tgt_rs, (0, last), ends)

    def results(i, carry):
        sent(i, row_ss)
        sbuf[i] = (gacc[:, lanes_of(i)] + nn(acts[far_end, i], wout_all[far_end])).astype(BF)
        send_rows(i, ret, u_ss, u_rs)
        return carry

    lax.fori_loop(0, im, results, 0)
    gacc[...] = jnp.zeros_like(gacc)

    def mix(i, carry):
        @pl.when(i == 1)
        def _():
            hosts_start(tgt, tin, tgt_ss, tgt_rs, (0, last), inner)

        arrive(i, ret, u_rs)

        @pl.when(i == 0)
        def _():
            hosts_arrive(tin, tgt_rs)

        line = lax.broadcasted_iota(jnp.int32, (sp, 512), 1).astype(F32)
        here = cols[i]
        picked = []
        for j in range(2):
            pick = jnp.where(line == here[:, 8 + j : 9 + j], 1.0, 0.0).astype(BF)
            picked.append(nn(pick, ret[i]))
        x2 = xpad[i].astype(F32) + nn(outs[i], wo_all[...])
        mix = x2 + here[:, 10:11] * picked[0] + here[:, 11:12] * picked[1]
        mix_b = mix.astype(BF)
        for b in range(n_z):
            xin[b, i] = mix_b[b * BP : b * BP + block]
            dys[i, b * BP : b * BP + block, :] = tin[b, i].astype(F32)
        dy = jnp.where(rows_ok, mix - dys[i], 0.0)
        dys[i] = dy
        total = jnp.zeros((512, 512), F32)
        for j in range(2):
            pick = jnp.where(row_id == meta[i, j : j + 1, :], 1.0, 0.0).astype(BF)
            total = total + nn(pick, (here[:, 10 + j : 11 + j] * dy).astype(BF))
        sent(i, u_ss)
        sbuf[i] = total.astype(BF)
        send_rows(i, drows, du_ss, du_rs)
        for j in range(2):
            here = jnp.where(lane_id == 12 + j, jnp.sum(dy * picked[j], axis=-1, keepdims=True), here)
        cols[i] = here
        return carry

    lax.fori_loop(0, im, mix, 0)
    home_start(xin, mixed, mix_ss, mix_rs, sizes)
    own_mixed = home_own(xin, mixed, loc_sem.at[0])
    each(own_mixed, "start")
    expert_row = lax.broadcasted_iota(jnp.int32, (8, sp), 0).astype(F32)

    def gates_back(i, carry):
        flat = jnp.transpose(cols[i])
        share = gts[i]
        grad = jnp.zeros((8, sp), F32)
        for j in range(2):
            at = meta[i, j : j + 1, :]
            inside = (at >= expert_row * 64) & (at < expert_row * 64 + 64)
            grad = grad + jnp.where(inside, flat[12 + j : 13 + j, :], 0.0)
        dlog = share * (grad - jnp.sum(share * grad, axis=0, keepdims=True))
        gts[i] = dlog
        gvec[8:16, :] += nn(dlog.astype(BF), n2s[i])
        return carry

    lax.fori_loop(0, im, gates_back, 0)

    def turn(i, carry):
        recv[i] = jnp.transpose(recv[i])
        for shard in range(n_z):
            acts[shard, i] = jnp.transpose(acts[shard, i])
        return carry

    lax.fori_loop(0, im, turn, 0)

    def reduce_start(target, piece):
        peer = jnp.where(z == 0, 1, last - 1)
        slot = jnp.where(target == peer, 0, jnp.where(target == far_end, 2, 1))
        remote(
            dws.at[target, piece], arrived.at[slot, piece], r_ss.at[target, piece], r_rs.at[slot, piece], me, peer
        ).start()

    def reduce_forward(piece, steps):
        @pl.when(inner)
        def _():
            for target, slot, peer, there in steps:
                here = arrived.at[slot, piece]
                remote(here, here, r_ss.at[target, piece], r_rs.at[slot, piece], me, z).wait_recv()

                def add(c, carry):
                    at = rows_of(c, 128)
                    dws[target, piece, at] = (
                        dws[target, piece, at].astype(F32) + arrived[slot, piece, at].astype(F32)
                    ).astype(BF)
                    return carry

                lax.fori_loop(0, 4, add, 0)
                remote(
                    dws.at[target, piece],
                    arrived.at[there, piece],
                    r_ss.at[target, piece],
                    r_rs.at[there, piece],
                    me,
                    peer,
                ).start()

    first_steps = ((far_end, 2, middle, 4),)
    second_steps = ((middle, 1, middle, 3), (near_end, 4, near_end, 0))

    def owner(s):
        return jnp.where(z < n_z // 2, lax.rem(z + 2 * n_z - 1 - s, n_z), lax.rem(z + 1 + s, n_z))

    def out_ready(s, carry):
        target = owner(s)
        dws[target, 0] = gacc[:, lanes_of(target)].astype(BF)

        @pl.when(ends & (s < 2))
        def _():
            reduce_start(target, 0)

        return carry

    def experts_back(i, carry):
        arrive(i, drows, du_rs)
        du = drows[i]
        for target in range(n_z):
            gacc[:, target * 512 : target * 512 + 512] += nn(acts[target, i], du)

        @pl.when(i == im - 1)
        def _():
            lax.fori_loop(0, n_z, out_ready, 0)

        total = jnp.zeros((512, 512), F32)
        for shard in range(n_z):
            dpre = (nt(du, wout_all[shard]) * slopes[shard, i].astype(F32)).astype(BF)
            slopes[shard, i] = dpre
            total = total + nt(dpre, win_all[shard])
        sent(i, du_ss)
        sbuf[i] = total.astype(BF)
        send_rows(i, ret, dn_ss, dn_rs)
        return carry

    lax.fori_loop(0, im, experts_back, 0)

    def in_grads(target):
        accf[...] = nn(recv[0], slopes[target, 0])

        def more(i, carry):
            accf[...] += nn(recv[i], slopes[target, i])
            return carry

        lax.fori_loop(1, im, more, 0)
        dws[target, 1] = accf[...].astype(BF)

    def end_in_grads(s, carry):
        target = owner(s)
        in_grads(target)

        @pl.when(s < 2)
        def _():
            reduce_start(target, 1)

        return carry

    def inner_in_grads(s, carry):
        in_grads(jnp.where(s == 0, far_end, jnp.where(s == 1, middle, jnp.where(s == 2, near_end, z))))
        return carry

    @pl.when(ends)
    def _():
        lax.fori_loop(0, n_z, end_in_grads, 0)

    gacc[...] = jnp.zeros_like(gacc)
    each(own_mixed, "wait")
    home_sent(xin, mix_ss)

    reduce_forward(0, first_steps)

    def back(i, carry):
        arrive(i, ret, dn_rs)
        line = lax.broadcasted_iota(jnp.int32, (sp, 512), 1).astype(F32)
        here = cols[i]
        pick = jnp.where((line == here[:, 8:9]) | (line == here[:, 9:10]), 1.0, 0.0).astype(BF)
        dn2 = nn(pick, ret[i]) + tn(gts[i].astype(BF), router_t)
        hat2, scale2 = norm_parts(xpad[i].astype(F32) + nn(outs[i], wo_all[...]))
        gvec[2:3, :] += jnp.sum(dn2 * hat2, axis=0, keepdims=True)
        gvec[3:4, :] += jnp.sum(dn2, axis=0, keepdims=True)
        dx2 = dys[i] + norm_back(dn2 * gain_two, hat2, scale2)
        da = dx2.astype(BF)
        gacc[:, 1536:2048] += tn(outs[i], da)
        do = nt(da, wo_all[...]).astype(BF)
        hat1, scale1 = norm_parts(xpad[i].astype(F32))
        n1 = (hat1 * gain_one + bias_one).astype(BF)
        for pair in range(4):
            at = pair * 128
            q2 = qkvs[i, :, at : at + 128]
            k2 = qkvs[i, :, 512 + at : 512 + at + 128]
            v2 = qkvs[i, :, 1024 + at : 1024 + at + 128]
            do2 = do[:, at : at + 128]
            grads = ([], [], [])
            for side in range(2):
                head = pair * 2 + side
                scores = nt(q2 * eighths[side], k2)
                scores = jnp.where(keys_ok, scores, NEG)
                prob = jnp.exp(scores - here[:, head : head + 1])
                dprob = nt(do2 * masks[side], v2)
                weighted = jnp.sum(prob * dprob, axis=-1, keepdims=True)
                ds = (prob * (dprob - weighted)).astype(BF)
                grads[0].append(nn(ds, k2))
                grads[1].append(tn(ds, q2))
                grads[2].append(tn(prob.astype(BF), do2))
            for part in range(3):
                grad = jnp.where(lane_low, grads[part][0], grads[part][1])
                if part < 2:
                    grad = grad * 0.125
                qkvs[i, :, part * 512 + at : part * 512 + at + 128] = grad.astype(BF)
        dqkv = qkvs[i]
        gacc[:, 0:1536] += tn(n1, dqkv)
        dn1 = nt(dqkv, wq_all[...])
        gvec[0:1, :] += jnp.sum(dn1 * hat1, axis=0, keepdims=True)
        gvec[1:2, :] += jnp.sum(dn1, axis=0, keepdims=True)
        dx = (dx2 + norm_back(dn1 * gain_one, hat1, scale1)).astype(BF)
        for b in range(n_z):
            xin[b, i] = dx[b * BP : b * BP + block]

        @pl.when(i == 1)
        def _():
            reduce_forward(0, second_steps)

        @pl.when(i == 2)
        def _():

            @pl.when(inner)
            def _():
                lax.fori_loop(0, 1, inner_in_grads, 0)

            reduce_forward(1, first_steps)

        return carry

    lax.fori_loop(0, im, back, 0)

    def inner_tokens(near):
        @pl.when(inner)
        def _():
            for k in range(1, n_z):
                peer = lax.rem(z + k, n_z)

                @pl.when((peer == near_end) if near else (peer != near_end))
                def _():
                    remote(
                        xin.at[peer, pl.ds(0, counts[1])],
                        gtok.at[pl.ds(first, counts[1])],
                        gt_ss.at[k],
                        gt_rs.at[z],
                        me,
                        peer,
                    ).start()

    inner_tokens(True)
    own_gtok = home_own(xin, gtok, loc_sem.at[1])
    each(own_gtok, "start")

    for q in range(half):
        csend[q] = gacc[rows_of(2 * q + 1 - core, 64)].astype(BF)
        remote(csend.at[q], crecv.at[q], c_ss.at[q], c_rs.at[q], partner, z).start()
    remote(gvec, cvec, cv_ss.at[0], cv_rs.at[0], partner, z).start()

    @pl.when(inner)
    def _():
        lax.fori_loop(1, 3, inner_in_grads, 0)

    for q in range(half):
        remote(crecv.at[q], crecv.at[q], c_ss.at[q], c_rs.at[q], me, z).wait_recv()
    for k in range(1, half):
        q = lax.rem(chip + k, half)
        crecv[q] = (gacc[rows_of(2 * q + core, 64)] + crecv[q].astype(F32)).astype(BF)
        remote(crecv.at[q], hrecv.at[chip], h_ss.at[k], h_rs.at[chip], q * 2 + core, z).start()
    remote(cvec, cvec, cv_ss.at[0], cv_rs.at[0], me, z).wait_recv()
    hvec[chip] = gvec[...] + cvec[...]
    for k in range(1, half):
        q = lax.rem(chip + k, half)
        remote(hvec.at[chip], hvec.at[chip], hv_ss.at[k], hv_rs.at[chip], q * 2 + core, z).start()
    reduce_forward(1, second_steps)

    @pl.when(inner)
    def _():
        lax.fori_loop(3, n_z, inner_in_grads, 0)

    dense = gacc[rows_of(me, 64)] + crecv[chip].astype(F32)
    for k in range(1, half):
        q = lax.rem(chip + k, half)
        remote(hrecv.at[q], hrecv.at[q], h_ss.at[0], h_rs.at[q], me, z).wait_recv()
        dense = dense + hrecv[q].astype(F32)
    gacc[0:64] = dense
    for k in range(1, half):
        q = lax.rem(chip + k, half)
        remote(hvec.at[q], hvec.at[q], hv_ss.at[0], hv_rs.at[q], me, z).wait_recv()
    zvec[0] = hvec[0] + hvec[1] + hvec[2] + hvec[3]

    @pl.when(ends)
    def _():
        zsend[...] = gacc[0:64].astype(BF)
        peer = jnp.where(z == 0, 1, last - 1)
        remote(zsend, zrecv.at[0], za_ss.at[0], za_rs.at[0], me, peer).start()
        remote(zvec.at[0], zvec.at[1], zv_ss.at[0], zv_rs.at[1], me, peer).start()

    @pl.when(ends)
    def _():
        reduce_start(owner(2), 0)
        reduce_start(owner(2), 1)

    home_start(xin, gtok, gt_ss, gt_rs, sizes[1:])

    @pl.when(inner)
    def _():
        remote(zrecv.at[0], zrecv.at[0], za_ss.at[0], za_rs.at[0], me, z).wait_recv()
        zsend[...] = (gacc[0:64] + zrecv[0].astype(F32)).astype(BF)
        remote(zsend, zrecv.at[1], za_ss.at[1], za_rs.at[1], me, middle).start()
        remote(zvec.at[1], zvec.at[1], zv_ss.at[0], zv_rs.at[1], me, z).wait_recv()
        zvec[2] = zvec[0] + zvec[1]
        remote(zvec.at[2], zvec.at[3], zv_ss.at[1], zv_rs.at[3], me, middle).start()
        remote(zrecv.at[1], zrecv.at[1], za_ss.at[0], za_rs.at[1], me, z).wait_recv()
        zall[...] = (zsend[...].astype(F32) + zrecv[1].astype(F32)).astype(BF)
        remote(zall, zall, zb_ss.at[0], zb_rs.at[0], me, near_end).start()
        remote(zvec.at[3], zvec.at[3], zv_ss.at[0], zv_rs.at[3], me, z).wait_recv()
        zvec[4] = zvec[2] + zvec[3]
        remote(zvec.at[4], zvec.at[4], zv_ss.at[2], zv_rs.at[4], me, near_end).start()
        inner_tokens(False)

    final_copies = [
        pltpu.make_async_copy(gacc.at[:, pl.ds(piece * 512, 512)], out, loc_sem.at[2 + piece])
        for piece, out in ((0, gout), (1, gin))
    ]
    for piece in range(2):
        for slot, there in ((0, z >= 0), (3, inner)):

            @pl.when(there)
            def _():
                here = arrived.at[slot, piece]
                remote(here, here, r_ss.at[0, piece], r_rs.at[slot, piece], me, z).wait_recv()

        def finish(c, carry):
            at = rows_of(c, 128)
            gacc[at, piece * 512 : piece * 512 + 512] = (
                dws[z, piece, at].astype(F32)
                + arrived[0, piece, at].astype(F32)
                + jnp.where(inner, arrived[3, piece, at].astype(F32), 0.0)
            )
            return carry

        lax.fori_loop(0, 4, finish, 0)
        final_copies[piece].start()
    @pl.when(ends)
    def _():
        remote(zvec.at[4], zvec.at[4], zv_ss.at[0], zv_rs.at[4], me, z).wait_recv()
        remote(zall, zall, zb_ss.at[0], zb_rs.at[0], me, z).wait_recv()

    gsmall[...] = zvec[4]
    gqkv[...] = zall[:, 0:1536].astype(F32)
    gwo[...] = zall[:, 1536:2048].astype(F32)
    each(own_gtok, "wait")
    home_arrive(gtok, gt_rs)
    home_arrive(mixed, mix_rs)
    for copy in final_copies:
        copy.wait()

    hosts_sent(xin, tok_ss)
    hosts_sent(rin, rts_ss)
    hosts_sent(tin, tgt_ss)
    home_sent(xin, gt_ss)
    @pl.when(ends)
    def _():
        remote(zsend, zsend, za_ss.at[0], loc_sem.at[8], me, z).wait_send()
        remote(zvec.at[0], zvec.at[0], zv_ss.at[0], loc_sem.at[8], me, z).wait_send()

    @pl.when(inner)
    def _():
        remote(zsend, zsend, za_ss.at[1], loc_sem.at[8], me, z).wait_send()
        remote(zall, zall, zb_ss.at[0], loc_sem.at[8], me, z).wait_send()
        for k in (1, 2):
            remote(zvec.at[0], zvec.at[0], zv_ss.at[k], loc_sem.at[8], me, z).wait_send()


    def rows_sent(i, carry):
        sent(i, dn_ss)
        return carry

    lax.fori_loop(0, im, rows_sent, 0)
    weights_sent()
    for array in range(3):
        slot = dense_slot(array, 0)
        for k in range(half):
            remote(slot, slot, den_ss.at[array, k], loc_sem.at[8], me, z).wait_send()
        for k in range(1, half):
            remote(slot, slot, fwd_ss.at[array, k], loc_sem.at[8], me, z).wait_send()
    for piece in range(2):
        for target in range(n_z):
            here = dws.at[0, 0]

            @pl.when(z != target)
            def _():
                remote(here, here, r_ss.at[target, piece], loc_sem.at[8], me, z).wait_send()

    for q in range(half):
        remote(crecv.at[q], crecv.at[q], c_ss.at[q], loc_sem.at[8], me, z).wait_send()
    remote(cvec, cvec, cv_ss.at[0], loc_sem.at[8], me, z).wait_send()
    for k in range(1, half):
        remote(crecv.at[0], crecv.at[0], h_ss.at[k], loc_sem.at[8], me, z).wait_send()
        remote(cvec, cvec, hv_ss.at[k], loc_sem.at[8], me, z).wait_send()


def finish_kernel(mixed, gtok, gqkv, gwo, gsmall, gin, gout, *outs):
    me = lax.axis_index("dp")
    outs[0][...] = mixed[...]
    outs[1][...] = gtok[...].astype(F32)
    for source, target in ((gqkv, outs[2]), (gwo, outs[3]), (gin, outs[4]), (gout, outs[5])):
        target[...] = source[...]

    lanes = gsmall[:, pl.ds(pl.multiple_of((me // 2) * 128, 128), 128)]
    lanes = jnp.where(lax.rem(me, 2) == 1, pltpu.roll(lanes, 64, 1), lanes)
    for row in range(4):
        outs[6 + row][...] = lanes[row, 0:64]
    outs[10][...] = lanes[8:16, 0:64]


def whole_images(
    tokens, ln1_gain, ln1_bias, w_qkv, w_out, ln2_gain, ln2_bias, w_router, expert_in, expert_out, routes, targets
):
    n_dp, n_z = lax.axis_size("dp"), lax.axis_size("seq")
    image_count, block, width = tokens.shape
    im = image_count // 3
    cap = 2 * S // (n_z * w_router.shape[1]) + 2
    dims = (n_dp, n_z, (image_count // 6, im, im, image_count // 6), block, cap)
    sp, half = n_z * BP, n_dp // 2
    me, z = lax.axis_index("dp"), lax.axis_index("seq")
    dma, vm = pltpu.SemaphoreType.DMA, pltpu.VMEM

    valid = z * block + jnp.arange(block) < VALID
    lines = jnp.where(valid[None, None, :], jnp.transpose(routes, (0, 2, 1)) + 1, 0)
    lines = jnp.pad(lines, ((0, 0), (0, 6), (0, BP - block)))
    odd = lax.rem(z, 2) == 1
    lines = jnp.concatenate([jnp.where(odd, 0, lines), jnp.where(odd, lines, 0)], axis=-1)
    vec = jnp.concatenate(
        [
            jnp.stack([ln1_gain, ln1_bias, ln2_gain, ln2_bias]),
            jnp.zeros((4, ln1_gain.shape[0]), BF),
            jnp.transpose(w_router),
        ],
        axis=0,
    )
    vec = lax.dynamic_update_slice(jnp.zeros((16, width), BF), vec, (0, me * ln1_gain.shape[0]))
    blocks = (n_z, im, block, width)
    in_any, in_vmem = pl.BlockSpec(memory_space=pl.ANY), pl.BlockSpec(memory_space=pltpu.VMEM)
    mixed, gtok, gqkv, gwo, gsmall, gin, gout = pl.pallas_call(
        functools.partial(block_kernel, dims),
        out_shape=[
            jax.ShapeDtypeStruct((image_count, block, width), BF),
            jax.ShapeDtypeStruct((image_count, block, width), BF),
            jax.ShapeDtypeStruct((64, 1536), F32),
            jax.ShapeDtypeStruct((64, width), F32),
            jax.ShapeDtypeStruct((16, width), F32),
            jax.ShapeDtypeStruct((512, 512), F32),
            jax.ShapeDtypeStruct((512, 512), F32),
        ],
        in_specs=[in_any, in_any, in_vmem, in_any, in_any, in_vmem, in_any, in_any],
        out_specs=[in_any, in_any] + [in_vmem] * 3 + [in_any] * 2,
        scratch_shapes=[
            vm(blocks, BF), vm((n_z, im, 8, 128), jnp.int32), vm(blocks, BF), vm((n_dp, 16, width), BF),
            vm((width, 1536), BF), vm((width, width), BF), vm((16, width), F32), vm((im, sp, width), BF),
            vm((im, sp, width), BF), vm((im, sp, 1536), BF), vm((im, sp, width), BF),
            vm((im, sp, 128), F32), vm((im, 8, sp), F32), vm((im, 8, sp), F32),
            vm((n_z, 512, 512), BF), vm((n_z, 512, 512), BF), vm((im, 512, 512), BF), vm((im, 512, 512), BF),
            vm((n_z, im, 512, 512), BF), vm((n_z, im, 512, 512), BF), vm((im, 512, 512), BF),
            vm((im, 512, 512), BF), vm((im, sp, width), F32), vm((n_z, 2, 512, 512), BF), vm((5, 2, 512, 512), BF),
            vm((width, 2048), F32), vm((512, 512), F32), vm((16, width), F32), vm((half, 64, 2048), BF), vm((half, 64, 2048), BF),
            vm((16, width), F32), vm((half, 64, 2048), BF), vm((half, 16, width), F32),
            vm((64, 2048), BF), vm((2, 64, 2048), BF), vm((64, 2048), BF), vm((5, 16, width), F32),
            dma((9,)), dma((n_z,)), dma((n_z,)), dma((n_z,)), dma((n_z,)), dma((n_z,)), dma((n_z,)),
            dma((3, half)), dma((3, n_dp)), dma((3, half)), dma((2, n_z)), dma((n_z,)), dma((2, n_z)), dma((n_z,)),
            dma((im, n_dp)), dma((im, n_dp)), dma((im, n_dp)), dma((im, n_dp)), dma((im, n_dp)), dma((im, n_dp)),
            dma((im, n_dp)), dma((im, n_dp)),
            dma((n_z,)), dma((n_z,)), dma((n_z,)), dma((n_z,)),
            dma((n_z, 2)), dma((5, 2)), dma((half,)), dma((half,)), dma((1,)), dma((1,)),
            dma((half,)), dma((half,)), dma((half,)), dma((half,)), dma((2,)), dma((2,)), dma((1,)), dma((1,)),
            dma((3,)), dma((5,)),
        ],
        compiler_params=pltpu.CompilerParams(
            collective_id=1, has_side_effects=True, vmem_limit_bytes=VMEM_LIMIT
        ),
        name="block",
    )(tokens, targets, lines, w_qkv, w_out, vec, expert_in[0], expert_out[0])
    whole = pl.BlockSpec(memory_space=pltpu.VMEM)
    mixed, gtok, gqkv, gwo, gin, gout, g1, b1, g2, b2, grouter = pl.pallas_call(
        finish_kernel,
        out_shape=[
            jax.ShapeDtypeStruct((image_count, block, width), BF),
            jax.ShapeDtypeStruct((image_count, block, width), F32),
            jax.ShapeDtypeStruct((64, 1536), F32),
            jax.ShapeDtypeStruct((64, width), F32),
            jax.ShapeDtypeStruct((512, 512), F32),
            jax.ShapeDtypeStruct((512, 512), F32),
        ]
        + [jax.ShapeDtypeStruct((64,), F32)] * 4
        + [jax.ShapeDtypeStruct((8, 64), F32)],
        in_specs=[whole] * 7,
        out_specs=[whole] * 11,
        name="finish",
    )(mixed, gtok, gqkv, gwo, gsmall, gin, gout)
    return (mixed, gtok, g1, b1, gqkv, gwo, g2, b2, jnp.transpose(grouter), gin[None], gout[None])


def fits(tokens, w_qkv, w_router, expert_in):
    n_dp, n_z = lax.axis_size("dp"), lax.axis_size("seq")
    return (
        n_dp == 8
        and n_z == 4
        and tokens.shape[0] % 6 == 0
        and tokens.shape[1] <= BP
        and tokens.shape[2] == 512
        and w_qkv.shape == (64, 1536)
        and w_router.shape[1] == n_dp
        and expert_in.shape == (1, 512, 512)
    )


def local(*args):
    if fits(args[0], args[3], args[7], args[8]):
        return whole_images(*args)
    return by_heads(*args)


def solution(mesh):
    placed = (
        P("dp", "seq", None),
        P("dp"),
        P("dp"),
        P("dp", None),
        P("dp", None),
        P("dp"),
        P("dp"),
        P("dp", None),
        P("dp", None, "seq"),
        P("dp", "seq", None),
        P("dp", "seq", None),
        P("dp", "seq", None),
    )
    return jax.shard_map(
        local,
        mesh=mesh,
        in_specs=placed,
        out_specs=(
            P("dp", "seq", None),
            P("dp", "seq", None),
            P("dp"),
            P("dp"),
            P("dp", None),
            P("dp", None),
            P("dp"),
            P("dp"),
            P("dp", None),
            P("dp", None, "seq"),
            P("dp", "seq", None),
        ),
        check_vma=False,
    )
```

```python
import functools

import jax
import jax.numpy as jnp
from jax import lax
from jax.experimental import pallas as pl
from jax.experimental.pallas import tpu as pltpu
from jax.sharding import PartitionSpec as P

H = 8
S = 200
VALID = 197


def layer_norm(values, gain_vec, bias_vec):
    centre = values - jnp.mean(values, axis=-1, keepdims=True)
    spread = jnp.mean(centre * centre, axis=-1, keepdims=True)
    return centre * lax.rsqrt(spread + 1e-06) * gain_vec + bias_vec


def regroup_heads(values):
    return lax.all_to_all(values, "seq", split_axis=3, concat_axis=1, tiled=True)


def regroup_slots(values):
    return lax.all_to_all(values, "seq", split_axis=1, concat_axis=3, tiled=True)


def send_experts(values):
    return lax.all_to_all(values, "dp", split_axis=0, concat_axis=1, tiled=True)


def send_tokens(values):
    return lax.all_to_all(values, "dp", split_axis=1, concat_axis=0, tiled=True)


def masked_scores(queries, keys_in, key_valid):
    scores = (
        jnp.einsum("bqhd,bkhd->bhqk", queries, keys_in, preferred_element_type=jnp.float32) * 0.125
    )
    return jnp.where(key_valid, scores, -1e30)


def attention_forward(queries, keys_in, values, key_valid):
    scores = masked_scores(queries, keys_in, key_valid)
    row_top = jnp.max(scores, axis=-1, keepdims=True)
    exponent = jnp.exp(scores - row_top)
    row_total = jnp.sum(exponent, axis=-1, keepdims=True)
    prob_rows = exponent / row_total
    log_total = row_top + jnp.log(row_total)
    attended = jnp.einsum(
        "bhqk,bkhd->bqhd",
        prob_rows.astype(jnp.bfloat16),
        values,
        preferred_element_type=jnp.float32,
    )
    return (attended.astype(jnp.bfloat16), log_total)


def attention_backward(queries, keys_in, values, log_total, grad_attended, key_valid):
    scores = masked_scores(queries, keys_in, key_valid)
    prob_rows = jnp.exp(scores - log_total)
    grad_values = jnp.einsum(
        "bhqk,bqhd->bkhd",
        prob_rows.astype(jnp.bfloat16),
        grad_attended,
        preferred_element_type=jnp.float32,
    )
    grad_probs = jnp.einsum(
        "bqhd,bkhd->bhqk", grad_attended, values, preferred_element_type=jnp.float32
    )
    inner_sum = jnp.sum(prob_rows * grad_probs, axis=-1, keepdims=True)
    grad_scores = (prob_rows * (grad_probs - inner_sum)).astype(jnp.bfloat16)
    grad_queries = (
        jnp.einsum("bhqk,bkhd->bqhd", grad_scores, keys_in, preferred_element_type=jnp.float32)
        * 0.125
    )
    grad_keys = (
        jnp.einsum("bhqk,bqhd->bkhd", grad_scores, queries, preferred_element_type=jnp.float32)
        * 0.125
    )
    return jnp.stack([grad_queries, grad_keys, grad_values], axis=2)


def pick_block(total_rows):
    for candidate in (1024, 768, 512, 384, 256):
        if total_rows % candidate == 0:
            return candidate
    return total_rows


def by_heads(
    tokens,
    ln1_gain,
    ln1_bias,
    w_qkv,
    w_out,
    ln2_gain,
    ln2_bias,
    w_router,
    expert_in,
    expert_out,
    routes,
    targets,
):
    image_count, slot_count, model_width = tokens.shape
    seq_devices = lax.axis_size("seq")
    row_count = image_count * slot_count
    expert_count = w_router.shape[1]
    local_experts = expert_in.shape[0]
    slot_limit = 2 * S // (seq_devices * expert_count) + 2
    head_size = model_width // H
    gathered = (
        lax.all_gather(ln1_gain, "dp", axis=0, tiled=True),
        lax.all_gather(ln1_bias, "dp", axis=0, tiled=True),
        lax.all_gather(w_qkv, "dp", axis=0, tiled=True),
        lax.all_gather(w_out, "dp", axis=0, tiled=True),
        lax.all_gather(ln2_gain, "dp", axis=0, tiled=True),
        lax.all_gather(ln2_bias, "dp", axis=0, tiled=True),
        lax.all_gather(w_router, "dp", axis=0, tiled=True),
    )
    gain_one = gathered[0].astype(jnp.float32)
    bias_one = gathered[1].astype(jnp.float32)
    qkv_weight = gathered[2]
    out_weight = gathered[3]
    gain_two = gathered[4].astype(jnp.float32)
    bias_two = gathered[5].astype(jnp.float32)
    router_weight = gathered[6]
    slot_start = lax.axis_index("seq") * slot_count
    valid_slot = slot_start + jnp.arange(slot_count) < VALID
    valid_rows = jnp.tile(valid_slot, image_count)
    key_valid = (jnp.arange(S) < VALID)[None, None, None, :]
    token_rows = tokens.reshape(row_count, model_width).astype(jnp.float32)
    normed_one, norm_one_back = jax.vjp(layer_norm, token_rows, gain_one, bias_one)
    normed_one_b = normed_one.astype(jnp.bfloat16)
    mixed_qkv = jnp.dot(normed_one_b, qkv_weight, preferred_element_type=jnp.float32).astype(
        jnp.bfloat16
    )
    qkv_heads = regroup_heads(mixed_qkv.reshape(image_count, slot_count, 3, H, head_size))
    queries = qkv_heads[:, :, 0]
    keys_in = qkv_heads[:, :, 1]
    values = qkv_heads[:, :, 2]
    attended, log_total = attention_forward(queries, keys_in, values, key_valid)
    attended_rows = regroup_slots(attended[:, :, None]).reshape(row_count, model_width)
    residual_two = token_rows + jnp.dot(
        attended_rows, out_weight, preferred_element_type=jnp.float32
    )
    normed_two, norm_two_back = jax.vjp(layer_norm, residual_two, gain_two, bias_two)
    normed_two_b = normed_two.astype(jnp.bfloat16)
    logits = jnp.dot(normed_two_b, router_weight, preferred_element_type=jnp.float32)
    route_rows = routes.reshape(row_count, 2)
    chosen = (route_rows[:, :, None] == jnp.arange(expert_count)[None, None, :]) & valid_rows[
        :, None, None
    ]
    chosen_f = chosen.astype(jnp.float32)

    def gate_pick(logit_rows):
        return jnp.sum(jax.nn.softmax(logit_rows, axis=-1)[:, None, :] * chosen_f, axis=-1)

    gate_values, gate_back = jax.vjp(gate_pick, logits)
    pick_count = chosen.astype(jnp.int32).reshape(image_count, slot_count * 2, expert_count)
    before = jnp.cumsum(pick_count, axis=1) - pick_count
    place_hit = (before[..., None] == jnp.arange(slot_limit)) & (pick_count[..., None] > 0)
    dispatch = place_hit.astype(jnp.bfloat16).reshape(
        image_count, slot_count, 2, expert_count, slot_limit
    )
    normed_img = normed_two_b.reshape(image_count, slot_count, model_width)
    sent_rows = jnp.einsum(
        "bskem,bsd->ebmd", dispatch, normed_img, preferred_element_type=jnp.float32
    ).astype(jnp.bfloat16)
    received = send_experts(sent_rows.reshape(expert_count, image_count * slot_limit, model_width))
    weights_in, weights_out = (
        lax.all_gather(expert_in, "seq", axis=2, tiled=True),
        lax.all_gather(expert_out, "seq", axis=1, tiled=True),
    )
    total_rows = received.shape[1]
    block_rows = pick_block(total_rows)
    block_count = total_rows // block_rows

    def expert_step(block_index, produced):
        row_piece = lax.dynamic_slice_in_dim(received, block_index * block_rows, block_rows, 1)
        hidden_pre = jnp.einsum(
            "erd,edf->erf", row_piece, weights_in, preferred_element_type=jnp.float32
        )
        activated = jax.nn.gelu(hidden_pre).astype(jnp.bfloat16)
        result = jnp.einsum(
            "erf,efd->erd", activated, weights_out, preferred_element_type=jnp.float32
        ).astype(jnp.bfloat16)
        return lax.dynamic_update_slice_in_dim(produced, result, block_index * block_rows, 1)

    produced = lax.fori_loop(
        0,
        block_count,
        expert_step,
        jnp.zeros((local_experts, total_rows, model_width), jnp.bfloat16),
    )
    returned = send_tokens(produced).reshape(expert_count, image_count, slot_limit, model_width)
    per_choice = jnp.einsum(
        "bskem,ebmd->bskd", dispatch, returned, preferred_element_type=jnp.float32
    ).reshape(row_count, 2, model_width)
    mixed_rows = (
        residual_two
        + gate_values[:, 0:1] * per_choice[:, 0]
        + gate_values[:, 1:2] * per_choice[:, 1]
    )
    target_rows = targets.reshape(row_count, model_width).astype(jnp.float32)
    grad_mixed = (mixed_rows - target_rows) * valid_rows[:, None].astype(jnp.float32)
    grad_gates = jnp.sum(grad_mixed[:, None, :] * per_choice, axis=-1)
    grad_choice = (
        (gate_values[:, :, None] * grad_mixed[:, None, :])
        .astype(jnp.bfloat16)
        .reshape(image_count, slot_count, 2, model_width)
    )
    grad_sent = jnp.einsum(
        "bskem,bskd->ebmd", dispatch, grad_choice, preferred_element_type=jnp.float32
    ).astype(jnp.bfloat16)
    grad_received = send_experts(
        grad_sent.reshape(expert_count, image_count * slot_limit, model_width)
    )
    back_in, back_out = (
        lax.all_gather(expert_in, "seq", axis=2, tiled=True),
        lax.all_gather(expert_out, "seq", axis=1, tiled=True),
    )

    def expert_back(block_index, loop_carry):
        grad_in_sum, grad_out_sum, grad_rows = loop_carry
        row_piece = lax.dynamic_slice_in_dim(received, block_index * block_rows, block_rows, 1)
        grad_piece = lax.dynamic_slice_in_dim(
            grad_received, block_index * block_rows, block_rows, 1
        )
        hidden_pre = jnp.einsum(
            "erd,edf->erf", row_piece, back_in, preferred_element_type=jnp.float32
        )
        activated, gelu_back = jax.vjp(jax.nn.gelu, hidden_pre)
        grad_act = jnp.einsum(
            "erd,efd->erf", grad_piece, back_out, preferred_element_type=jnp.float32
        )
        grad_pre = gelu_back(grad_act)[0].astype(jnp.bfloat16)
        grad_out_sum = grad_out_sum + jnp.einsum(
            "erf,erd->efd",
            activated.astype(jnp.bfloat16),
            grad_piece,
            preferred_element_type=jnp.float32,
        )
        grad_in_sum = grad_in_sum + jnp.einsum(
            "erd,erf->edf", row_piece, grad_pre, preferred_element_type=jnp.float32
        )
        rows_back = jnp.einsum(
            "erf,edf->erd", grad_pre, back_in, preferred_element_type=jnp.float32
        ).astype(jnp.bfloat16)
        grad_rows = lax.dynamic_update_slice_in_dim(
            grad_rows, rows_back, block_index * block_rows, 1
        )
        return (grad_in_sum, grad_out_sum, grad_rows)

    start_carry = (
        jnp.zeros(back_in.shape, jnp.float32),
        jnp.zeros(back_out.shape, jnp.float32),
        jnp.zeros((local_experts, total_rows, model_width), jnp.bfloat16),
    )
    grad_in_sum, grad_out_sum, grad_rows = lax.fori_loop(0, block_count, expert_back, start_carry)
    grad_returned = send_tokens(grad_rows).reshape(
        expert_count, image_count, slot_limit, model_width
    )
    grad_normed_two = jnp.einsum(
        "bskem,ebmd->bsd", dispatch, grad_returned, preferred_element_type=jnp.float32
    ).reshape(row_count, model_width)
    grad_logits = gate_back(grad_gates)[0].astype(jnp.bfloat16)
    grad_router = jnp.einsum(
        "rd,re->de", normed_two_b, grad_logits, preferred_element_type=jnp.float32
    )
    grad_normed_two = grad_normed_two + jnp.einsum(
        "re,de->rd", grad_logits, router_weight, preferred_element_type=jnp.float32
    )
    grad_res_two, grad_gain_two, grad_bias_two = norm_two_back(grad_normed_two)
    grad_residual = grad_mixed + grad_res_two
    grad_branch = grad_residual.astype(jnp.bfloat16)
    grad_out_weight = jnp.einsum(
        "rd,re->de", attended_rows, grad_branch, preferred_element_type=jnp.float32
    )
    grad_attended = jnp.einsum(
        "re,de->rd", grad_branch, out_weight, preferred_element_type=jnp.float32
    ).astype(jnp.bfloat16)
    grad_heads = regroup_heads(grad_attended.reshape(image_count, slot_count, 1, H, head_size))[
        :, :, 0
    ]
    grad_qkv_heads = attention_backward(
        queries, keys_in, values, log_total, grad_heads, key_valid
    ).astype(jnp.bfloat16)
    grad_qkv_rows = regroup_slots(grad_qkv_heads).reshape(row_count, 3 * model_width)
    grad_qkv_weight = jnp.einsum(
        "rd,rf->df", normed_one_b, grad_qkv_rows, preferred_element_type=jnp.float32
    )
    grad_normed_one = jnp.einsum(
        "rf,df->rd", grad_qkv_rows, qkv_weight, preferred_element_type=jnp.float32
    )
    grad_token_ln, grad_gain_one, grad_bias_one = norm_one_back(grad_normed_one)
    grad_tokens = grad_residual + grad_token_ln
    dense_grads = (
        grad_gain_one,
        grad_bias_one,
        grad_qkv_weight,
        grad_out_weight,
        grad_gain_two,
        grad_bias_two,
        grad_router,
    )
    dense_grads = (
        lax.psum(dense_grads[0].astype(jnp.bfloat16), "seq").astype(jnp.float32),
        lax.psum(dense_grads[1].astype(jnp.bfloat16), "seq").astype(jnp.float32),
        lax.psum(dense_grads[2].astype(jnp.bfloat16), "seq").astype(jnp.float32),
        lax.psum(dense_grads[3].astype(jnp.bfloat16), "seq").astype(jnp.float32),
        lax.psum(dense_grads[4].astype(jnp.bfloat16), "seq").astype(jnp.float32),
        lax.psum(dense_grads[5].astype(jnp.bfloat16), "seq").astype(jnp.float32),
        lax.psum(dense_grads[6].astype(jnp.bfloat16), "seq").astype(jnp.float32),
    )
    dense_grads = (
        lax.psum_scatter(
            dense_grads[0].astype(jnp.bfloat16), "dp", scatter_dimension=0, tiled=True
        ).astype(jnp.float32),
        lax.psum_scatter(
            dense_grads[1].astype(jnp.bfloat16), "dp", scatter_dimension=0, tiled=True
        ).astype(jnp.float32),
        lax.psum_scatter(
            dense_grads[2].astype(jnp.bfloat16), "dp", scatter_dimension=0, tiled=True
        ).astype(jnp.float32),
        lax.psum_scatter(
            dense_grads[3].astype(jnp.bfloat16), "dp", scatter_dimension=0, tiled=True
        ).astype(jnp.float32),
        lax.psum_scatter(
            dense_grads[4].astype(jnp.bfloat16), "dp", scatter_dimension=0, tiled=True
        ).astype(jnp.float32),
        lax.psum_scatter(
            dense_grads[5].astype(jnp.bfloat16), "dp", scatter_dimension=0, tiled=True
        ).astype(jnp.float32),
        lax.psum_scatter(
            dense_grads[6].astype(jnp.bfloat16), "dp", scatter_dimension=0, tiled=True
        ).astype(jnp.float32),
    )
    expert_in_grad, expert_out_grad = (
        lax.psum_scatter(
            grad_in_sum.astype(jnp.bfloat16), "seq", scatter_dimension=2, tiled=True
        ).astype(jnp.float32),
        lax.psum_scatter(
            grad_out_sum.astype(jnp.bfloat16), "seq", scatter_dimension=1, tiled=True
        ).astype(jnp.float32),
    )
    mixed = mixed_rows.astype(jnp.bfloat16).reshape(image_count, slot_count, model_width)
    return (
        mixed,
        grad_tokens.reshape(image_count, slot_count, model_width),
        dense_grads[0],
        dense_grads[1],
        dense_grads[2],
        dense_grads[3],
        dense_grads[4],
        dense_grads[5],
        dense_grads[6],
        expert_in_grad,
        expert_out_grad,
    )


BF = jnp.bfloat16
F32 = jnp.float32
MESH_ID = pl.DeviceIdType.MESH
NEG = -1e30
BP = 64
VMEM_LIMIT = 67000000
GELU_C = 0.7978845608028654
GELU_K = 0.044715


def nn(a, b):
    return lax.dot_general(a, b, (((1,), (0,)), ((), ())), preferred_element_type=F32)


def nt(a, b):
    return lax.dot_general(a, b, (((1,), (1,)), ((), ())), preferred_element_type=F32)


def tn(a, b):
    return lax.dot_general(a, b, (((0,), (0,)), ((), ())), preferred_element_type=F32)


def remote(src, dst, send_sem, recv_sem, dp, z):
    return pltpu.make_async_remote_copy(
        src_ref=src,
        dst_ref=dst,
        send_sem=send_sem,
        recv_sem=recv_sem,
        device_id=(dp, z),
        device_id_type=MESH_ID,
    )


def rows_of(index, size):
    return pl.ds(pl.multiple_of(index * size, size), size)


def norm_parts(x):
    centre = x - jnp.mean(x, axis=-1, keepdims=True)
    scale = lax.rsqrt(jnp.mean(centre * centre, axis=-1, keepdims=True) + 1e-06)
    return centre * scale, scale


def norm_back(grad_hat, hat, scale):
    return scale * (
        grad_hat
        - jnp.mean(grad_hat, axis=-1, keepdims=True)
        - hat * jnp.mean(grad_hat * hat, axis=-1, keepdims=True)
    )


def half_masks():
    lane = lax.broadcasted_iota(jnp.int32, (1, 128), 1)
    low = jnp.where(lane < 64, 1.0, 0.0)
    return (low.astype(BF), (1.0 - low).astype(BF))


def slot_ok(position, block):
    return (position % BP < block) & ((position // BP) * block + position % BP < VALID)


def block_kernel(
    dims,
    tok, tgt, rts, wq, wo, vec, win, wout,
    mixed, gtok, gqkv, gwo, gsmall, gin, gout,
    xin, rin, tin, vec_all, wq_all, wo_all, vsum, xpad, n2s, qkvs, outs, cols, gts, meta,
    win_all, wout_all, recv, ret, acts, slopes, sbuf,
    drows, dys, dws, arrived,
    gacc, accf, gvec, csend, crecv, cvec, hrecv, hvec, zsend, zrecv, zall, zvec,
    loc_sem, tok_ss, tok_rs, rts_ss, rts_rs, tgt_ss, tgt_rs, den_ss, den_rs, fwd_ss, win_ss, win_rs, wout_ss, wout_rs,
    row_ss, row_rs, u_ss, u_rs, du_ss, du_rs, dn_ss, dn_rs, mix_ss, mix_rs, gt_ss, gt_rs,
    r_ss, r_rs, c_ss, c_rs, cv_ss, cv_rs, h_ss, h_rs, hv_ss, hv_rs, za_ss, za_rs, zb_ss, zb_rs, zv_ss, zv_rs,
):
    n_dp, n_z, counts, block, cap = dims
    firsts = tuple(sum(counts[:h]) for h in range(n_z))
    me, z = lax.axis_index("dp"), lax.axis_index("seq")
    sp = n_z * BP
    half = n_dp // 2
    last = n_z - 1
    core, chip = lax.rem(me, 2), me // 2
    partner = chip * 2 + 1 - core
    inner = (z == 1) | (z == last - 1)
    ends = jnp.logical_not(inner)
    far_end = jnp.where(z < n_z // 2, last, 0)
    near_end = last - far_end
    middle = last - z
    im = jnp.where(inner, counts[1], counts[0])
    sizes = ((counts[1], inner), (counts[0], ends))
    first = jnp.where(z == 0, firsts[0], jnp.where(z == 1, firsts[1], jnp.where(z == 2, firsts[2], firsts[3])))

    barrier = pltpu.get_barrier_semaphore()
    for k in range(1, n_dp):
        pl.semaphore_signal(barrier, inc=1, device_id=(lax.rem(me + k, n_dp), z), device_id_type=MESH_ID)
    for k in range(1, n_z):
        pl.semaphore_signal(barrier, inc=1, device_id=(me, lax.rem(z + k, n_z)), device_id_type=MESH_ID)

    def hosts_own(source, target, sem):
        for h in range(n_z):

            @pl.when(z == h)
            def _():
                pltpu.make_async_copy(
                    source.at[pl.ds(firsts[h], counts[h])], target.at[z, pl.ds(0, counts[h])], sem
                ).start()

    def hosts_own_wait(source, target, sem):
        for h in range(n_z):

            @pl.when(z == h)
            def _():
                pltpu.make_async_copy(
                    source.at[pl.ds(firsts[h], counts[h])], target.at[z, pl.ds(0, counts[h])], sem
                ).wait()

    def hosts_start(source, target, send_sem, recv_sem, hosts, who):
        for h in hosts:

            @pl.when((z != h) & who)
            def _():
                remote(
                    source.at[pl.ds(firsts[h], counts[h])],
                    target.at[z, pl.ds(0, counts[h])],
                    send_sem.at[h],
                    recv_sem.at[z],
                    me,
                    h,
                ).start()

    def hosts_arrive(target, recv_sem):
        for size, there in sizes:

            @pl.when(there)
            def _():
                for k in range(1, n_z):
                    origin = lax.rem(z + k, n_z)
                    spot = target.at[origin, pl.ds(0, size)]
                    remote(spot, spot, loc_sem.at[8], recv_sem.at[origin], me, z).wait_recv()

    def hosts_sent(target, send_sem):
        for h in range(n_z):

            @pl.when(z != h)
            def _():
                spot = target.at[0, pl.ds(0, counts[h])]
                remote(spot, spot, send_sem.at[h], loc_sem.at[8], me, z).wait_send()

    def home_own(source, target, sem):
        return [
            (there, pltpu.make_async_copy(source.at[z, pl.ds(0, size)], target.at[pl.ds(first, size)], sem))
            for size, there in sizes
        ]

    def home_start(source, target, send_sem, recv_sem, who):
        for size, there in who:

            @pl.when(there)
            def _():
                for k in range(1, n_z):
                    peer = lax.rem(z + k, n_z)
                    remote(
                        source.at[peer, pl.ds(0, size)],
                        target.at[pl.ds(first, size)],
                        send_sem.at[k],
                        recv_sem.at[z],
                        me,
                        peer,
                    ).start()

    def home_arrive(target, recv_sem):
        for h in range(n_z):

            @pl.when(z != h)
            def _():
                spot = target.at[pl.ds(firsts[h], counts[h])]
                remote(spot, spot, loc_sem.at[8], recv_sem.at[h], me, z).wait_recv()

    def home_sent(source, send_sem):
        for size, there in sizes:

            @pl.when(there)
            def _():
                for k in range(1, n_z):
                    spot = source.at[0, pl.ds(0, size)]
                    remote(spot, spot, send_sem.at[k], loc_sem.at[8], me, z).wait_send()

    def each(pairs, act):
        for there, copy in pairs:

            @pl.when(there)
            def _():
                getattr(copy, act)()

    own_copies = [
        pltpu.make_async_copy(win, win_all.at[z], loc_sem.at[3]),
        pltpu.make_async_copy(wout, wout_all.at[z], loc_sem.at[4]),
        pltpu.make_async_copy(wq, wq_all.at[rows_of(me, 64)], loc_sem.at[5]),
        pltpu.make_async_copy(wo, wo_all.at[rows_of(me, 64)], loc_sem.at[6]),
        pltpu.make_async_copy(vec, vec_all.at[me], loc_sem.at[7]),
    ]
    for copy in own_copies:
        copy.start()
    hosts_own(tok, xin, loc_sem.at[0])
    hosts_own(rts, rin, loc_sem.at[1])
    hosts_own(tgt, tin, loc_sem.at[2])
    for buffer in (xpad, gvec, recv, ret, drows):
        buffer[...] = jnp.zeros_like(buffer)
    pl.semaphore_wait(barrier, n_dp + n_z - 2)
    hosts_start(tok, xin, tok_ss, tok_rs, range(n_z), z >= 0)
    hosts_start(rts, rin, rts_ss, rts_rs, range(n_z), z >= 0)

    def dense_slot(array, index):
        if array == 0:
            return wq_all.at[rows_of(index, 64)]
        if array == 1:
            return wo_all.at[rows_of(index, 64)]
        return vec_all.at[index]

    dense_in = (wq, wo, vec)
    for array in range(3):
        for k in range(1, half):
            peer = lax.rem(chip + k, half) * 2 + core
            remote(
                dense_in[array], dense_slot(array, me), den_ss.at[array, k], den_rs.at[array, me], peer, z
            ).start()
        remote(
            dense_in[array], dense_slot(array, me), den_ss.at[array, 0], den_rs.at[array, me], partner, z
        ).start()

    experts = ((win, win_all, win_ss, win_rs), (wout, wout_all, wout_ss, wout_rs))

    def gather_hop(array, step):
        source, full, send_sem, recv_sem = experts[array]
        for way, there, slot in ((0, z >= step, z - step), (1, z + step < n_z, z + step)):

            @pl.when(there)
            def _():
                at = full.at[slot]
                if step > 0:
                    remote(at, at, send_sem.at[way, step], recv_sem.at[slot], me, z).wait_recv()

                @pl.when((z < last) if way == 0 else (z > 0))
                def _():
                    remote(
                        at if step > 0 else source,
                        at,
                        send_sem.at[way, step],
                        recv_sem.at[slot],
                        me,
                        z + 1 if way == 0 else z - 1,
                    ).start()

    def weights_sent():
        for step in range(n_z - 1):
            for way, there in ((0, (z >= step) & (z < last)), (1, (z + step < n_z) & (z > 0))):

                @pl.when(there)
                def _():
                    for source, full, send_sem, recv_sem in experts:
                        remote(
                            full.at[0], full.at[0], send_sem.at[way, step], recv_sem.at[0], me, z
                        ).wait_send()

    gather_hop(0, 0)
    gather_hop(1, 0)

    for k in range(1, half):
        origin = lax.rem(chip + k, half) * 2 + core
        for array in range(3):
            slot = dense_slot(array, origin)
            remote(slot, slot, den_ss.at[array, 0], den_rs.at[array, origin], me, z).wait_recv()
            remote(slot, slot, fwd_ss.at[array, k], den_rs.at[array, origin], partner, z).start()
    for k in range(half):
        origin = lax.rem(chip + k, half) * 2 + 1 - core
        for array in range(3):
            slot = dense_slot(array, origin)
            remote(slot, slot, den_ss.at[array, 0], den_rs.at[array, origin], me, z).wait_recv()
    for copy in own_copies:
        copy.wait()
    hosts_own_wait(tok, xin, loc_sem.at[0])
    hosts_own_wait(rts, rin, loc_sem.at[1])
    hosts_own_wait(tgt, tin, loc_sem.at[2])
    total = vec_all[0].astype(F32)
    for k in range(1, n_dp):
        total = total + vec_all[k].astype(F32)
    vsum[...] = total
    hosts_arrive(xin, tok_rs)
    hosts_arrive(rin, rts_rs)

    masks = half_masks()
    eighths = [mask * 0.125 for mask in masks]
    keys_ok = slot_ok(lax.broadcasted_iota(jnp.int32, (1, sp), 1), block)
    rows_ok = slot_ok(lax.broadcasted_iota(jnp.int32, (sp, 1), 0), block)
    gain_one, bias_one = vsum[0:1, :], vsum[1:2, :]
    gain_two, bias_two = vsum[2:3, :], vsum[3:4, :]
    router_t = vsum[8:16, :].astype(BF)
    lane_id = lax.broadcasted_iota(jnp.int32, (sp, 128), 1)
    lane_low = lane_id < 64
    row_id = lax.broadcasted_iota(jnp.int32, (512, sp), 0).astype(F32)

    def lanes_of(target):
        return pl.ds(pl.multiple_of(target * 512, 512), 512)

    def rows_at(index):
        return pl.ds(pl.multiple_of(index * 64, 64), n_z * cap)

    def send_rows(i, target, send_sem, recv_sem):
        def step(s, carry):
            j, c = lax.rem(s // 2 + 1, half), lax.rem(s, 2)
            index = 2 * j + c
            peer = lax.rem(chip + j, half) * 2 + lax.rem(core + c, 2)

            @pl.when(index > 0)
            def _():
                remote(
                    sbuf.at[i, rows_at(peer)],
                    target.at[i, rows_at(me)],
                    send_sem.at[i, index],
                    recv_sem.at[i, me],
                    peer,
                    z,
                ).start()

            return carry

        lax.fori_loop(0, n_dp, step, 0)
        target[i, rows_of(me, 64)] = sbuf[i, rows_of(me, 64)]

    def arrive(i, target, recv_sem):
        def step(k, carry):
            origin = lax.rem(me + k, n_dp)
            spot = target.at[i, rows_at(origin)]
            remote(spot, spot, loc_sem.at[8], recv_sem.at[i, origin], me, z).wait_recv()
            return carry

        lax.fori_loop(1, n_dp, step, 0)

    def sent(i, send_sem):
        def step(index, carry):
            spot = sbuf.at[i, rows_at(0)]
            remote(spot, spot, send_sem.at[i, index], loc_sem.at[8], me, z).wait_send()
            return carry

        lax.fori_loop(1, n_dp, step, 0)

    def front(i, carry):
        before = lax.broadcasted_iota(jnp.int32, (sp, sp), 0)
        after = lax.broadcasted_iota(jnp.int32, (sp, sp), 1)
        prefix = jnp.where((before < after) & (before // BP == after // BP), 1.0, 0.0).astype(BF)
        expert_id = lax.broadcasted_iota(jnp.int32, (8, sp), 0)
        slot_lane = lax.broadcasted_iota(jnp.int32, (8, sp), 1)
        for b in range(n_z):
            xpad[i, b * BP : b * BP + block, :] = xin[b, i]
        x = xpad[i].astype(F32)
        hat, _ = norm_parts(x)
        normed = (hat * gain_one + bias_one).astype(BF)
        qkvs[i] = nn(normed, wq_all[...]).astype(BF)
        lse_all = jnp.zeros((sp, 128), F32)
        for pair in range(4):
            q2 = qkvs[i, :, pair * 128 : pair * 128 + 128]
            k2 = qkvs[i, :, 512 + pair * 128 : 512 + pair * 128 + 128]
            v2 = qkvs[i, :, 1024 + pair * 128 : 1024 + pair * 128 + 128]
            parts = []
            for side in range(2):
                scores = nt(q2 * eighths[side], k2)
                scores = jnp.where(keys_ok, scores, NEG)
                top = jnp.max(scores, axis=-1, keepdims=True)
                exponent = jnp.exp(scores - top)
                whole = jnp.sum(exponent, axis=-1, keepdims=True)
                lse_all = jnp.where(lane_id == pair * 2 + side, top + jnp.log(whole), lse_all)
                parts.append(nn((exponent / whole).astype(BF), v2))
            outs[i, :, pair * 128 : pair * 128 + 128] = jnp.where(lane_low, parts[0], parts[1]).astype(BF)
        x2 = x + nn(outs[i], wo_all[...])
        hat2, _ = norm_parts(x2)
        n2 = (hat2 * gain_two + bias_two).astype(BF)
        n2s[i] = n2
        logits = nt(router_t, n2)
        raised = jnp.exp(logits - jnp.max(logits, axis=0, keepdims=True))
        share = raised / jnp.sum(raised, axis=0, keepdims=True)
        gts[i] = share
        wide = jnp.concatenate([rin[0, i] + rin[1, i], rin[2, i] + rin[3, i]], axis=1)
        hits = [(expert_id + 1) == wide[j : j + 1, :] for j in range(2)]
        any_hit = jnp.where(hits[0] | hits[1], 1.0, 0.0)
        place = nn(any_hit.astype(BF), prefix)
        base = place + (expert_id * 64 + (slot_lane // BP) * cap + 1).astype(F32)
        lines = [jnp.sum(jnp.where(hit, base, 0.0), axis=0, keepdims=True) - 1.0 for hit in hits]
        lines += [jnp.sum(jnp.where(hit, share, 0.0), axis=0, keepdims=True) for hit in hits]
        lines = jnp.concatenate(lines + [jnp.zeros((4, sp), F32)], axis=0)
        meta[i] = lines
        table = jnp.concatenate([jnp.zeros((8, sp), F32), lines, jnp.zeros((112, sp), F32)], axis=0)
        cols[i] = jnp.transpose(table) + lse_all
        pick = (row_id == lines[0:1, :]) | (row_id == lines[1:2, :])
        sbuf[i] = nn(jnp.where(pick, 1.0, 0.0).astype(BF), n2).astype(BF)
        send_rows(i, recv, row_ss, row_rs)

        @pl.when(i == 1)
        def _():
            gather_hop(0, 1)

        return carry

    lax.fori_loop(0, im, front, 0)


    def hidden(shard):
        def image(i, carry):
            x = recv[i]
            for side in range(2):
                pre = nn(x, win_all[shard, :, side * 256 : side * 256 + 256])
                square = pre * pre
                tanh = jnp.tanh(pre * (GELU_C + (GELU_C * GELU_K) * square))
                gate = 0.5 + 0.5 * tanh
                acts[shard, i, :, side * 256 : side * 256 + 256] = (pre * gate).astype(BF)
                slope = gate + pre * (0.5 - 0.5 * tanh * tanh) * (GELU_C + (3.0 * GELU_C * GELU_K) * square)
                slopes[shard, i, :, side * 256 : side * 256 + 256] = slope.astype(BF)
            return carry

        lax.fori_loop(0, im, image, 0)

    def hidden_step(s, carry):
        for at_step, hop in ((1, 2), (3, 3)):

            @pl.when(s == at_step)
            def _():
                gather_hop(0, hop)

        for way in range(2):
            shard = z - s if way == 0 else z + s

            @pl.when((shard >= 0) & (shard < n_z) & ((s > 0) | (way == 0)))
            def _():
                hidden(shard)

        @pl.when(s == 2)
        def _():
            gather_hop(1, 2)
            hosts_start(tgt, tin, tgt_ss, tgt_rs, (1, 2), z >= 0)

        return carry

    gather_hop(1, 1)

    def rows_here(i, carry):
        arrive(i, recv, row_rs)
        return carry

    lax.fori_loop(0, im, rows_here, 0)
    lax.fori_loop(0, n_z, hidden_step, 0)

    def early_results(i, carry):
        for k in range(1, n_z):
            shard = lax.rem(far_end + k, n_z)
            part = nn(acts[shard, i], wout_all[shard])
            if k == 1:
                gacc[:, lanes_of(i)] = part
            else:
                gacc[:, lanes_of(i)] += part
        return carry

    lax.fori_loop(0, im, early_results, 0)
    gather_hop(1, 3)
    hosts_start(tgt, tin, tgt_ss, tgt_rs, (0, last), ends)

    def results(i, carry):
        sent(i, row_ss)
        sbuf[i] = (gacc[:, lanes_of(i)] + nn(acts[far_end, i], wout_all[far_end])).astype(BF)
        send_rows(i, ret, u_ss, u_rs)
        return carry

    lax.fori_loop(0, im, results, 0)
    gacc[...] = jnp.zeros_like(gacc)

    def mix(i, carry):
        @pl.when(i == 0)
        def _():
            hosts_start(tgt, tin, tgt_ss, tgt_rs, (0, last), inner)

        arrive(i, ret, u_rs)

        @pl.when(i == 0)
        def _():
            hosts_arrive(tin, tgt_rs)

        line = lax.broadcasted_iota(jnp.int32, (sp, 512), 1).astype(F32)
        here = cols[i]
        picked = []
        for j in range(2):
            pick = jnp.where(line == here[:, 8 + j : 9 + j], 1.0, 0.0).astype(BF)
            picked.append(nn(pick, ret[i]))
        x2 = xpad[i].astype(F32) + nn(outs[i], wo_all[...])
        mix = x2 + here[:, 10:11] * picked[0] + here[:, 11:12] * picked[1]
        mix_b = mix.astype(BF)
        for b in range(n_z):
            xin[b, i] = mix_b[b * BP : b * BP + block]
            dys[i, b * BP : b * BP + block, :] = tin[b, i].astype(F32)
        dy = jnp.where(rows_ok, mix - dys[i], 0.0)
        dys[i] = dy
        total = jnp.zeros((512, 512), F32)
        for j in range(2):
            pick = jnp.where(row_id == meta[i, j : j + 1, :], 1.0, 0.0).astype(BF)
            total = total + nn(pick, (here[:, 10 + j : 11 + j] * dy).astype(BF))
        sent(i, u_ss)
        sbuf[i] = total.astype(BF)
        send_rows(i, drows, du_ss, du_rs)
        for j in range(2):
            here = jnp.where(lane_id == 12 + j, jnp.sum(dy * picked[j], axis=-1, keepdims=True), here)
        cols[i] = here
        return carry

    lax.fori_loop(0, im, mix, 0)
    home_start(xin, mixed, mix_ss, mix_rs, sizes)
    own_mixed = home_own(xin, mixed, loc_sem.at[0])
    each(own_mixed, "start")
    expert_row = lax.broadcasted_iota(jnp.int32, (8, sp), 0).astype(F32)

    def gates_back(i, carry):
        flat = jnp.transpose(cols[i])
        share = gts[i]
        grad = jnp.zeros((8, sp), F32)
        for j in range(2):
            at = meta[i, j : j + 1, :]
            inside = (at >= expert_row * 64) & (at < expert_row * 64 + 64)
            grad = grad + jnp.where(inside, flat[12 + j : 13 + j, :], 0.0)
        dlog = share * (grad - jnp.sum(share * grad, axis=0, keepdims=True))
        gts[i] = dlog
        gvec[8:16, :] += nn(dlog.astype(BF), n2s[i])
        return carry

    lax.fori_loop(0, im, gates_back, 0)

    def turn(i, carry):
        recv[i] = jnp.transpose(recv[i])
        for shard in range(n_z):
            acts[shard, i] = jnp.transpose(acts[shard, i])
        return carry

    lax.fori_loop(0, im, turn, 0)

    def reduce_start(target, piece):
        peer = jnp.where(z == 0, 1, last - 1)
        slot = jnp.where(target == peer, 0, jnp.where(target == far_end, 2, 1))
        remote(
            dws.at[target, piece], arrived.at[slot, piece], r_ss.at[target, piece], r_rs.at[slot, piece], me, peer
        ).start()

    def reduce_forward(piece, steps):
        @pl.when(inner)
        def _():
            for target, slot, peer, there in steps:
                here = arrived.at[slot, piece]
                remote(here, here, r_ss.at[target, piece], r_rs.at[slot, piece], me, z).wait_recv()

                def add(c, carry):
                    at = rows_of(c, 128)
                    dws[target, piece, at] = (
                        dws[target, piece, at].astype(F32) + arrived[slot, piece, at].astype(F32)
                    ).astype(BF)
                    return carry

                lax.fori_loop(0, 4, add, 0)
                remote(
                    dws.at[target, piece],
                    arrived.at[there, piece],
                    r_ss.at[target, piece],
                    r_rs.at[there, piece],
                    me,
                    peer,
                ).start()

    first_steps = ((far_end, 2, middle, 4),)
    second_steps = ((middle, 1, middle, 3), (near_end, 4, near_end, 0))

    def owner(s):
        return jnp.where(z < n_z // 2, lax.rem(z + 2 * n_z - 1 - s, n_z), lax.rem(z + 1 + s, n_z))

    def out_ready(s, carry):
        target = owner(s)
        dws[target, 0] = gacc[:, lanes_of(target)].astype(BF)

        @pl.when(ends & (s < 2))
        def _():
            reduce_start(target, 0)

        return carry

    def experts_back(i, carry):
        arrive(i, drows, du_rs)
        du = drows[i]
        for target in range(n_z):
            gacc[:, target * 512 : target * 512 + 512] += nn(acts[target, i], du)

        @pl.when(i == im - 1)
        def _():
            lax.fori_loop(0, n_z, out_ready, 0)

        total = jnp.zeros((512, 512), F32)
        for shard in range(n_z):
            dpre = (nt(du, wout_all[shard]) * slopes[shard, i].astype(F32)).astype(BF)
            slopes[shard, i] = dpre
            total = total + nt(dpre, win_all[shard])
        sent(i, du_ss)
        sbuf[i] = total.astype(BF)
        send_rows(i, ret, dn_ss, dn_rs)
        return carry

    lax.fori_loop(0, im, experts_back, 0)

    def in_grads(target):
        accf[...] = nn(recv[0], slopes[target, 0])

        def more(i, carry):
            accf[...] += nn(recv[i], slopes[target, i])
            return carry

        lax.fori_loop(1, im, more, 0)
        dws[target, 1] = accf[...].astype(BF)

    def end_in_grads(s, carry):
        target = owner(s)
        in_grads(target)

        @pl.when(s < 2)
        def _():
            reduce_start(target, 1)

        return carry

    def inner_in_grads(s, carry):
        in_grads(jnp.where(s == 0, far_end, jnp.where(s == 1, middle, jnp.where(s == 2, near_end, z))))
        return carry

    @pl.when(ends)
    def _():
        lax.fori_loop(0, n_z, end_in_grads, 0)

    gacc[...] = jnp.zeros_like(gacc)
    each(own_mixed, "wait")
    home_sent(xin, mix_ss)

    reduce_forward(0, first_steps)

    def back(i, carry):
        arrive(i, ret, dn_rs)
        line = lax.broadcasted_iota(jnp.int32, (sp, 512), 1).astype(F32)
        here = cols[i]
        pick = jnp.where((line == here[:, 8:9]) | (line == here[:, 9:10]), 1.0, 0.0).astype(BF)
        dn2 = nn(pick, ret[i]) + tn(gts[i].astype(BF), router_t)
        hat2, scale2 = norm_parts(xpad[i].astype(F32) + nn(outs[i], wo_all[...]))
        gvec[2:3, :] += jnp.sum(dn2 * hat2, axis=0, keepdims=True)
        gvec[3:4, :] += jnp.sum(dn2, axis=0, keepdims=True)
        dx2 = dys[i] + norm_back(dn2 * gain_two, hat2, scale2)
        da = dx2.astype(BF)
        gacc[:, 1536:2048] += tn(outs[i], da)
        do = nt(da, wo_all[...]).astype(BF)
        hat1, scale1 = norm_parts(xpad[i].astype(F32))
        n1 = (hat1 * gain_one + bias_one).astype(BF)
        for pair in range(4):
            at = pair * 128
            q2 = qkvs[i, :, at : at + 128]
            k2 = qkvs[i, :, 512 + at : 512 + at + 128]
            v2 = qkvs[i, :, 1024 + at : 1024 + at + 128]
            do2 = do[:, at : at + 128]
            grads = ([], [], [])
            for side in range(2):
                head = pair * 2 + side
                scores = nt(q2 * eighths[side], k2)
                scores = jnp.where(keys_ok, scores, NEG)
                prob = jnp.exp(scores - here[:, head : head + 1])
                dprob = nt(do2 * masks[side], v2)
                weighted = jnp.sum(prob * dprob, axis=-1, keepdims=True)
                ds = (prob * (dprob - weighted)).astype(BF)
                grads[0].append(nn(ds, k2))
                grads[1].append(tn(ds, q2))
                grads[2].append(tn(prob.astype(BF), do2))
            for part in range(3):
                grad = jnp.where(lane_low, grads[part][0], grads[part][1])
                if part < 2:
                    grad = grad * 0.125
                qkvs[i, :, part * 512 + at : part * 512 + at + 128] = grad.astype(BF)
        dqkv = qkvs[i]
        gacc[:, 0:1536] += tn(n1, dqkv)
        dn1 = nt(dqkv, wq_all[...])
        gvec[0:1, :] += jnp.sum(dn1 * hat1, axis=0, keepdims=True)
        gvec[1:2, :] += jnp.sum(dn1, axis=0, keepdims=True)
        dx = (dx2 + norm_back(dn1 * gain_one, hat1, scale1)).astype(BF)
        for b in range(n_z):
            xin[b, i] = dx[b * BP : b * BP + block]

        @pl.when(i == 1)
        def _():
            reduce_forward(0, second_steps)

        @pl.when(i == 2)
        def _():

            @pl.when(inner)
            def _():
                lax.fori_loop(0, 1, inner_in_grads, 0)

            reduce_forward(1, first_steps)

        return carry

    lax.fori_loop(0, im, back, 0)

    def inner_tokens(near):
        @pl.when(inner)
        def _():
            for k in range(1, n_z):
                peer = lax.rem(z + k, n_z)

                @pl.when((peer == near_end) if near else (peer != near_end))
                def _():
                    remote(
                        xin.at[peer, pl.ds(0, counts[1])],
                        gtok.at[pl.ds(first, counts[1])],
                        gt_ss.at[k],
                        gt_rs.at[z],
                        me,
                        peer,
                    ).start()

    inner_tokens(True)
    own_gtok = home_own(xin, gtok, loc_sem.at[1])
    each(own_gtok, "start")

    for q in range(half):
        csend[q] = gacc[rows_of(2 * q + 1 - core, 64)].astype(BF)
        remote(csend.at[q], crecv.at[q], c_ss.at[q], c_rs.at[q], partner, z).start()
    remote(gvec, cvec, cv_ss.at[0], cv_rs.at[0], partner, z).start()

    @pl.when(inner)
    def _():
        lax.fori_loop(1, 3, inner_in_grads, 0)

    for q in range(half):
        remote(crecv.at[q], crecv.at[q], c_ss.at[q], c_rs.at[q], me, z).wait_recv()
    for k in range(1, half):
        q = lax.rem(chip + k, half)
        crecv[q] = (gacc[rows_of(2 * q + core, 64)] + crecv[q].astype(F32)).astype(BF)
        remote(crecv.at[q], hrecv.at[chip], h_ss.at[k], h_rs.at[chip], q * 2 + core, z).start()
    remote(cvec, cvec, cv_ss.at[0], cv_rs.at[0], me, z).wait_recv()
    hvec[chip] = gvec[...] + cvec[...]
    for k in range(1, half):
        q = lax.rem(chip + k, half)
        remote(hvec.at[chip], hvec.at[chip], hv_ss.at[k], hv_rs.at[chip], q * 2 + core, z).start()
    reduce_forward(1, second_steps)

    @pl.when(inner)
    def _():
        lax.fori_loop(3, n_z, inner_in_grads, 0)

    dense = gacc[rows_of(me, 64)] + crecv[chip].astype(F32)
    for k in range(1, half):
        q = lax.rem(chip + k, half)
        remote(hrecv.at[q], hrecv.at[q], h_ss.at[0], h_rs.at[q], me, z).wait_recv()
        dense = dense + hrecv[q].astype(F32)
    gacc[0:64] = dense
    for k in range(1, half):
        q = lax.rem(chip + k, half)
        remote(hvec.at[q], hvec.at[q], hv_ss.at[0], hv_rs.at[q], me, z).wait_recv()
    zvec[0] = hvec[0] + hvec[1] + hvec[2] + hvec[3]

    @pl.when(ends)
    def _():
        zsend[...] = gacc[0:64].astype(BF)
        peer = jnp.where(z == 0, 1, last - 1)
        remote(zsend, zrecv.at[0], za_ss.at[0], za_rs.at[0], me, peer).start()
        remote(zvec.at[0], zvec.at[1], zv_ss.at[0], zv_rs.at[1], me, peer).start()

    @pl.when(ends)
    def _():
        reduce_start(owner(2), 0)
        reduce_start(owner(2), 1)

    home_start(xin, gtok, gt_ss, gt_rs, sizes[1:])

    @pl.when(inner)
    def _():
        remote(zrecv.at[0], zrecv.at[0], za_ss.at[0], za_rs.at[0], me, z).wait_recv()
        zsend[...] = (gacc[0:64] + zrecv[0].astype(F32)).astype(BF)
        remote(zsend, zrecv.at[1], za_ss.at[1], za_rs.at[1], me, middle).start()
        remote(zvec.at[1], zvec.at[1], zv_ss.at[0], zv_rs.at[1], me, z).wait_recv()
        zvec[2] = zvec[0] + zvec[1]
        remote(zvec.at[2], zvec.at[3], zv_ss.at[1], zv_rs.at[3], me, middle).start()
        remote(zrecv.at[1], zrecv.at[1], za_ss.at[0], za_rs.at[1], me, z).wait_recv()
        zall[...] = (zsend[...].astype(F32) + zrecv[1].astype(F32)).astype(BF)
        remote(zall, zall, zb_ss.at[0], zb_rs.at[0], me, near_end).start()
        remote(zvec.at[3], zvec.at[3], zv_ss.at[0], zv_rs.at[3], me, z).wait_recv()
        zvec[4] = zvec[2] + zvec[3]
        remote(zvec.at[4], zvec.at[4], zv_ss.at[2], zv_rs.at[4], me, near_end).start()
        inner_tokens(False)

    final_copies = [
        pltpu.make_async_copy(gacc.at[:, pl.ds(piece * 512, 512)], out, loc_sem.at[2 + piece])
        for piece, out in ((0, gout), (1, gin))
    ]
    for piece in range(2):
        for slot, there in ((0, z >= 0), (3, inner)):

            @pl.when(there)
            def _():
                here = arrived.at[slot, piece]
                remote(here, here, r_ss.at[0, piece], r_rs.at[slot, piece], me, z).wait_recv()

        def finish(c, carry):
            at = rows_of(c, 128)
            gacc[at, piece * 512 : piece * 512 + 512] = (
                dws[z, piece, at].astype(F32)
                + arrived[0, piece, at].astype(F32)
                + jnp.where(inner, arrived[3, piece, at].astype(F32), 0.0)
            )
            return carry

        lax.fori_loop(0, 4, finish, 0)
        final_copies[piece].start()
    @pl.when(ends)
    def _():
        remote(zvec.at[4], zvec.at[4], zv_ss.at[0], zv_rs.at[4], me, z).wait_recv()
        remote(zall, zall, zb_ss.at[0], zb_rs.at[0], me, z).wait_recv()

    gsmall[...] = zvec[4]
    gqkv[...] = zall[:, 0:1536].astype(F32)
    gwo[...] = zall[:, 1536:2048].astype(F32)
    each(own_gtok, "wait")
    home_arrive(gtok, gt_rs)
    home_arrive(mixed, mix_rs)
    for copy in final_copies:
        copy.wait()

    hosts_sent(xin, tok_ss)
    hosts_sent(rin, rts_ss)
    hosts_sent(tin, tgt_ss)
    home_sent(xin, gt_ss)
    @pl.when(ends)
    def _():
        remote(zsend, zsend, za_ss.at[0], loc_sem.at[8], me, z).wait_send()
        remote(zvec.at[0], zvec.at[0], zv_ss.at[0], loc_sem.at[8], me, z).wait_send()

    @pl.when(inner)
    def _():
        remote(zsend, zsend, za_ss.at[1], loc_sem.at[8], me, z).wait_send()
        remote(zall, zall, zb_ss.at[0], loc_sem.at[8], me, z).wait_send()
        for k in (1, 2):
            remote(zvec.at[0], zvec.at[0], zv_ss.at[k], loc_sem.at[8], me, z).wait_send()


    def rows_sent(i, carry):
        sent(i, dn_ss)
        return carry

    lax.fori_loop(0, im, rows_sent, 0)
    weights_sent()
    for array in range(3):
        slot = dense_slot(array, 0)
        for k in range(half):
            remote(slot, slot, den_ss.at[array, k], loc_sem.at[8], me, z).wait_send()
        for k in range(1, half):
            remote(slot, slot, fwd_ss.at[array, k], loc_sem.at[8], me, z).wait_send()
    for piece in range(2):
        for target in range(n_z):
            here = dws.at[0, 0]

            @pl.when(z != target)
            def _():
                remote(here, here, r_ss.at[target, piece], loc_sem.at[8], me, z).wait_send()

    for q in range(half):
        remote(crecv.at[q], crecv.at[q], c_ss.at[q], loc_sem.at[8], me, z).wait_send()
    remote(cvec, cvec, cv_ss.at[0], loc_sem.at[8], me, z).wait_send()
    for k in range(1, half):
        remote(crecv.at[0], crecv.at[0], h_ss.at[k], loc_sem.at[8], me, z).wait_send()
        remote(cvec, cvec, hv_ss.at[k], loc_sem.at[8], me, z).wait_send()


def finish_kernel(mixed, gtok, gqkv, gwo, gsmall, gin, gout, *outs):
    me = lax.axis_index("dp")
    outs[0][...] = mixed[...]
    outs[1][...] = gtok[...].astype(F32)
    for source, target in ((gqkv, outs[2]), (gwo, outs[3]), (gin, outs[4]), (gout, outs[5])):
        target[...] = source[...]

    lanes = gsmall[:, pl.ds(pl.multiple_of((me // 2) * 128, 128), 128)]
    lanes = jnp.where(lax.rem(me, 2) == 1, pltpu.roll(lanes, 64, 1), lanes)
    for row in range(4):
        outs[6 + row][...] = lanes[row, 0:64]
    outs[10][...] = lanes[8:16, 0:64]


def whole_images(
    tokens, ln1_gain, ln1_bias, w_qkv, w_out, ln2_gain, ln2_bias, w_router, expert_in, expert_out, routes, targets
):
    n_dp, n_z = lax.axis_size("dp"), lax.axis_size("seq")
    image_count, block, width = tokens.shape
    im = image_count // 3
    cap = 2 * S // (n_z * w_router.shape[1]) + 2
    dims = (n_dp, n_z, (image_count // 6, im, im, image_count // 6), block, cap)
    sp, half = n_z * BP, n_dp // 2
    me, z = lax.axis_index("dp"), lax.axis_index("seq")
    dma, vm = pltpu.SemaphoreType.DMA, pltpu.VMEM

    valid = z * block + jnp.arange(block) < VALID
    lines = jnp.where(valid[None, None, :], jnp.transpose(routes, (0, 2, 1)) + 1, 0)
    lines = jnp.pad(lines, ((0, 0), (0, 6), (0, BP - block)))
    odd = lax.rem(z, 2) == 1
    lines = jnp.concatenate([jnp.where(odd, 0, lines), jnp.where(odd, lines, 0)], axis=-1)
    vec = jnp.concatenate(
        [
            jnp.stack([ln1_gain, ln1_bias, ln2_gain, ln2_bias]),
            jnp.zeros((4, ln1_gain.shape[0]), BF),
            jnp.transpose(w_router),
        ],
        axis=0,
    )
    vec = lax.dynamic_update_slice(jnp.zeros((16, width), BF), vec, (0, me * ln1_gain.shape[0]))
    blocks = (n_z, im, block, width)
    in_any, in_vmem = pl.BlockSpec(memory_space=pl.ANY), pl.BlockSpec(memory_space=pltpu.VMEM)
    mixed, gtok, gqkv, gwo, gsmall, gin, gout = pl.pallas_call(
        functools.partial(block_kernel, dims),
        out_shape=[
            jax.ShapeDtypeStruct((image_count, block, width), BF),
            jax.ShapeDtypeStruct((image_count, block, width), BF),
            jax.ShapeDtypeStruct((64, 1536), F32),
            jax.ShapeDtypeStruct((64, width), F32),
            jax.ShapeDtypeStruct((16, width), F32),
            jax.ShapeDtypeStruct((512, 512), F32),
            jax.ShapeDtypeStruct((512, 512), F32),
        ],
        in_specs=[in_any, in_any, in_vmem, in_any, in_any, in_vmem, in_any, in_any],
        out_specs=[in_any, in_any] + [in_vmem] * 3 + [in_any] * 2,
        scratch_shapes=[
            vm(blocks, BF), vm((n_z, im, 8, 128), jnp.int32), vm(blocks, BF), vm((n_dp, 16, width), BF),
            vm((width, 1536), BF), vm((width, width), BF), vm((16, width), F32), vm((im, sp, width), BF),
            vm((im, sp, width), BF), vm((im, sp, 1536), BF), vm((im, sp, width), BF),
            vm((im, sp, 128), F32), vm((im, 8, sp), F32), vm((im, 8, sp), F32),
            vm((n_z, 512, 512), BF), vm((n_z, 512, 512), BF), vm((im, 512, 512), BF), vm((im, 512, 512), BF),
            vm((n_z, im, 512, 512), BF), vm((n_z, im, 512, 512), BF), vm((im, 512, 512), BF),
            vm((im, 512, 512), BF), vm((im, sp, width), F32), vm((n_z, 2, 512, 512), BF), vm((5, 2, 512, 512), BF),
            vm((width, 2048), F32), vm((512, 512), F32), vm((16, width), F32), vm((half, 64, 2048), BF), vm((half, 64, 2048), BF),
            vm((16, width), F32), vm((half, 64, 2048), BF), vm((half, 16, width), F32),
            vm((64, 2048), BF), vm((2, 64, 2048), BF), vm((64, 2048), BF), vm((5, 16, width), F32),
            dma((9,)), dma((n_z,)), dma((n_z,)), dma((n_z,)), dma((n_z,)), dma((n_z,)), dma((n_z,)),
            dma((3, half)), dma((3, n_dp)), dma((3, half)), dma((2, n_z)), dma((n_z,)), dma((2, n_z)), dma((n_z,)),
            dma((im, n_dp)), dma((im, n_dp)), dma((im, n_dp)), dma((im, n_dp)), dma((im, n_dp)), dma((im, n_dp)),
            dma((im, n_dp)), dma((im, n_dp)),
            dma((n_z,)), dma((n_z,)), dma((n_z,)), dma((n_z,)),
            dma((n_z, 2)), dma((5, 2)), dma((half,)), dma((half,)), dma((1,)), dma((1,)),
            dma((half,)), dma((half,)), dma((half,)), dma((half,)), dma((2,)), dma((2,)), dma((1,)), dma((1,)),
            dma((3,)), dma((5,)),
        ],
        compiler_params=pltpu.CompilerParams(
            collective_id=1, has_side_effects=True, vmem_limit_bytes=VMEM_LIMIT
        ),
        name="block",
    )(tokens, targets, lines, w_qkv, w_out, vec, expert_in[0], expert_out[0])
    whole = pl.BlockSpec(memory_space=pltpu.VMEM)
    mixed, gtok, gqkv, gwo, gin, gout, g1, b1, g2, b2, grouter = pl.pallas_call(
        finish_kernel,
        out_shape=[
            jax.ShapeDtypeStruct((image_count, block, width), BF),
            jax.ShapeDtypeStruct((image_count, block, width), F32),
            jax.ShapeDtypeStruct((64, 1536), F32),
            jax.ShapeDtypeStruct((64, width), F32),
            jax.ShapeDtypeStruct((512, 512), F32),
            jax.ShapeDtypeStruct((512, 512), F32),
        ]
        + [jax.ShapeDtypeStruct((64,), F32)] * 4
        + [jax.ShapeDtypeStruct((8, 64), F32)],
        in_specs=[whole] * 7,
        out_specs=[whole] * 11,
        name="finish",
    )(mixed, gtok, gqkv, gwo, gsmall, gin, gout)
    return (mixed, gtok, g1, b1, gqkv, gwo, g2, b2, jnp.transpose(grouter), gin[None], gout[None])


def fits(tokens, w_qkv, w_router, expert_in):
    n_dp, n_z = lax.axis_size("dp"), lax.axis_size("seq")
    return (
        n_dp == 8
        and n_z == 4
        and tokens.shape[0] % 6 == 0
        and tokens.shape[1] <= BP
        and tokens.shape[2] == 512
        and w_qkv.shape == (64, 1536)
        and w_router.shape[1] == n_dp
        and expert_in.shape == (1, 512, 512)
    )


def local(*args):
    if fits(args[0], args[3], args[7], args[8]):
        return whole_images(*args)
    return by_heads(*args)


def solution(mesh):
    placed = (
        P("dp", "seq", None),
        P("dp"),
        P("dp"),
        P("dp", None),
        P("dp", None),
        P("dp"),
        P("dp"),
        P("dp", None),
        P("dp", None, "seq"),
        P("dp", "seq", None),
        P("dp", "seq", None),
        P("dp", "seq", None),
    )
    return jax.shard_map(
        local,
        mesh=mesh,
        in_specs=placed,
        out_specs=(
            P("dp", "seq", None),
            P("dp", "seq", None),
            P("dp"),
            P("dp"),
            P("dp", None),
            P("dp", None),
            P("dp"),
            P("dp"),
            P("dp", None),
            P("dp", None, "seq"),
            P("dp", "seq", None),
        ),
        check_vma=False,
    )
```
